32 devices in a mesh: dp: 8 (over z, y), fsdp: 4 (over x, core).
Axes of the slice: x: 2, y: 2, z: 4, core: 2. Of those that a mesh axis runs over, the one named last changes fastest.
Arguments:
- tokens: bfloat16 [64, 1024, 1280], P(('dp', 'fsdp')), may hold values from -8 to 8
- out_grad: bfloat16 [64, 1024, 1280], P(('dp', 'fsdp')), may hold values from -6 to 6
- lengths: int32 [64], P(('dp', 'fsdp')), may hold values from 30 to 1024, as said below
- ln1_gain: bfloat16 [1280], P(('dp', 'fsdp')), may hold values from 0.5 to 1.5
- ln1_bias: bfloat16 [1280], P(('dp', 'fsdp')), may hold values from -1.5 to 1.5
- w_in: bfloat16 [1280, 640], P(('dp', 'fsdp')), may hold values from -0.15625 to 0.15625
- b_in: bfloat16 [640], P(('dp', 'fsdp')), may hold values from -1.5 to 1.5
- ln2_gain: bfloat16 [640], P(('dp', 'fsdp')), may hold values from 0.5 to 1.5
- ln2_bias: bfloat16 [640], P(('dp', 'fsdp')), may hold values from -1.5 to 1.5
- w_conv: bfloat16 [5, 640, 640], P(None, ('dp', 'fsdp')), may hold values from -0.109375 to 0.109375
- b_conv: bfloat16 [640], P(('dp', 'fsdp')), may hold values from -1.5 to 1.5
- ln3_gain: bfloat16 [640], P(('dp', 'fsdp')), may hold values from 0.5 to 1.5
- ln3_bias: bfloat16 [640], P(('dp', 'fsdp')), may hold values from -1.5 to 1.5
- w_out: bfloat16 [640, 1280], P(('dp', 'fsdp')), may hold values from -0.3125 to 0.3125
- b_out: bfloat16 [1280], P(('dp', 'fsdp')), may hold values from -1.5 to 1.5
Outputs:
- out: bfloat16 [64, 1024, 1280], P(('dp', 'fsdp'))
- grad_tokens: bfloat16 [64, 1024, 1280], P(('dp', 'fsdp'))
- grad_ln1_gain: float32 [1280], P(('dp', 'fsdp'))
- grad_ln1_bias: float32 [1280], P(('dp', 'fsdp'))
- grad_w_in: float32 [1280, 640], P(('dp', 'fsdp'))
- grad_b_in: float32 [640], P(('dp', 'fsdp'))
- grad_ln2_gain: float32 [640], P(('dp', 'fsdp'))
- grad_ln2_bias: float32 [640], P(('dp', 'fsdp'))
- grad_w_conv: float32 [5, 640, 640], P(None, ('dp', 'fsdp'))
- grad_b_conv: float32 [640], P(('dp', 'fsdp'))
- grad_ln3_gain: float32 [640], P(('dp', 'fsdp'))
- grad_ln3_bias: float32 [640], P(('dp', 'fsdp'))
- grad_w_out: float32 [640, 1280], P(('dp', 'fsdp'))
- grad_b_out: float32 [1280], P(('dp', 'fsdp'))
The draws below stay inside these ranges and needn't reach their ends.
Inputs may be any that keep to these rules, and one draw needn't show every extreme that they name: `lengths`: each protein's count of live residues; in every draw one protein has exactly 1024.
All inputs are finite; a program needn't handle non-finite values.
Results may differ from the reference program's by a relative error of at most 0.0085.
Values may be sent and summed in bfloat16 or wider, within the bound.
A program may use at most 256 MiB of HBM per device.

```python
import math
import jax
import jax.numpy as jnp
from jax import lax

D = 1280
INNER = 640
KSIZE = 5
DILATION = 8
LEN = 1024
MIN_LEN = 30
P_DEV = 2
PROTEINS = 64


def draw_tokens(key, part):
    key_base, key_rows, key_cols = jax.random.split(jax.random.fold_in(key, 11), 3)
    base = jax.random.normal(key_base, (PROTEINS, LEN, D), jnp.float32)
    row_scale = jnp.exp(jax.random.uniform(key_rows, (PROTEINS, LEN, 1), jnp.float32, math.log(0.4), math.log(4.0)))
    col_scale = jnp.exp(jax.random.uniform(key_cols, (D,), jnp.float32, math.log(0.5), math.log(2.0)))
    return jnp.clip(base * row_scale * col_scale, -8.0, 8.0).astype(jnp.bfloat16)


def draw_lengths(key, part):
    key_first, key_second, key_pick = jax.random.split(jax.random.fold_in(key, 23), 3)
    first = jax.random.randint(key_first, (PROTEINS,), MIN_LEN, LEN + 1)
    second = jax.random.randint(key_second, (PROTEINS,), MIN_LEN, LEN + 1)
    shorter = jnp.minimum(first, second)
    chosen = jax.random.randint(key_pick, (), 0, PROTEINS)
    slots = jnp.arange(PROTEINS, dtype=jnp.int32)
    return jnp.where(slots == chosen, LEN, shorter).astype(jnp.int32)


def shard_levels(key, shape, shards, smallest, top_value):
    loudness, own = 1.0, jax.random.fold_in(key, 6)
    for position, parts in shards:
        steps = jnp.exp(jax.random.uniform(jax.random.fold_in(own, position), (parts,), jnp.float32, smallest / len(shards), top_value / len(shards)))
        loudness = loudness * jnp.repeat(steps, shape[position] // parts).reshape([-1 if axis == position else 1 for axis in range(len(shape))])
    return loudness


def gaussian(rng, shape, deviation, bound, cuts=(), kind=jnp.bfloat16):
    level = shard_levels(rng, shape, cuts, -0.22, 0.18) if cuts else 1.0
    result = jax.random.normal(rng, shape, jnp.float32) * deviation * level
    return jnp.minimum(jnp.maximum(result, -bound), bound).astype(kind)


def setup_inputs(seed: int = 0) -> dict:
    splits = jax.random.split(jax.random.key(seed), 16)
    return {
        "tokens": draw_tokens(jax.random.fold_in(splits[15], 71), 0),
        "out_grad": gaussian(splits[1], (PROTEINS, LEN, D), 1.0, 6.0, ((0, 32),)),
        "lengths": draw_lengths(jax.random.fold_in(splits[15], 71), 0),
        "ln1_gain": jnp.clip(1.0 + 0.1 * jax.random.normal(splits[3], (D,), jnp.float32), 0.5, 1.5).astype(jnp.bfloat16),
        "ln1_bias": gaussian(splits[4], (D,), 0.3, 1.5, ((0, 32),)),
        "w_in": gaussian(splits[5], (D, INNER), D ** -0.5, 0.15625, ((0, 32),)),
        "b_in": gaussian(splits[6], (INNER,), 0.3, 1.5, ((0, 32),)),
        "ln2_gain": jnp.clip(1.0 + 0.1 * jax.random.normal(splits[7], (INNER,), jnp.float32), 0.5, 1.5).astype(jnp.bfloat16),
        "ln2_bias": gaussian(splits[8], (INNER,), 0.3, 1.5, ((0, 32),)),
        "w_conv": gaussian(splits[9], (KSIZE, INNER, INNER), (KSIZE * INNER) ** -0.5, 0.109375, ((1, 32),)),
        "b_conv": gaussian(splits[10], (INNER,), 0.3, 1.5, ((0, 32),)),
        "ln3_gain": jnp.clip(1.0 + 0.1 * jax.random.normal(splits[11], (INNER,), jnp.float32), 0.5, 1.5).astype(jnp.bfloat16),
        "ln3_bias": gaussian(splits[12], (INNER,), 0.3, 1.5, ((0, 32),)),
        "w_out": gaussian(splits[13], (INNER, D), (INNER // 2) ** -0.5, 0.3125, ((0, 32),)),
        "b_out": gaussian(splits[14], (D,), 0.3, 1.5, ((0, 32),)),
    }


@jax.custom_vjp
def low(v):
    return lax.optimization_barrier(v.astype(jnp.bfloat16)).astype(jnp.float32)

@jax.custom_vjp
def low_back(v):
    return v

def low_keep(v):
    return (low(v), None)

def low_pass(kept, grad):
    return (grad,)

def back_keep(v):
    return (v, None)

def back_low(kept, grad):
    return (low(grad),)
low.defvjp(low_keep, low_pass)
low_back.defvjp(back_keep, back_low)
EPS = 1e-05

def layer_norm(values, gain, bias):
    center = values - lax.optimization_barrier(jnp.mean(values, axis=-1, keepdims=True))
    var_rows = lax.optimization_barrier(jnp.mean(center * center, axis=-1, keepdims=True))
    return center * lax.rsqrt(var_rows + EPS) * gain + bias

def norm_gelu(values, gain, bias):
    return jax.nn.gelu(layer_norm(values, gain, bias), approximate=False)

def dilate(values, kernel):
    reach = KSIZE // 2 * DILATION
    padded = jnp.pad(values, ((0, 0), (reach, reach), (0, 0)))
    total = jnp.zeros(values.shape[:2] + (kernel.shape[2],), jnp.float32)
    for kernel_tap in range(KSIZE):
        window = padded[:, kernel_tap * DILATION:kernel_tap * DILATION + LEN]
        total = total + jnp.einsum('gli,io->glo', window, kernel[kernel_tap], precision=lax.Precision.HIGHEST)
    return total

def block(tokens, live, params):
    ln1_gain, ln1_bias, w_in, b_in, ln2_gain, ln2_bias, w_conv, b_conv, ln3_gain, ln3_bias, w_out, b_out = params
    highest = lax.Precision.HIGHEST
    inner_one = low(norm_gelu(tokens, ln1_gain, ln1_bias))
    hidden_one = low_back(jnp.einsum('gld,di->gli', inner_one, w_in, precision=highest) + b_in)
    inner_two = low(norm_gelu(hidden_one, ln2_gain, ln2_bias) * live)
    hidden_two = low_back(dilate(inner_two, w_conv) + b_conv)
    inner_three = low(norm_gelu(hidden_two, ln3_gain, ln3_bias))
    branch = (jnp.einsum('gli,id->gld', inner_three, w_out, precision=highest) + b_out) * live
    return tokens + branch

def add_pair(first, second):
    return first + second

def reference(tokens, out_grad, lengths, ln1_gain, ln1_bias, w_in, b_in, ln2_gain, ln2_bias, w_conv, b_conv, ln3_gain, ln3_bias, w_out, b_out):
    params = tuple((weight.astype(jnp.float32) for weight in (ln1_gain, ln1_bias, w_in, b_in, ln2_gain, ln2_bias, w_conv, b_conv, ln3_gain, ln3_bias, w_out, b_out)))
    groups = PROTEINS // P_DEV
    group_toks = tokens.reshape(groups, P_DEV, LEN, D)
    group_cots = out_grad.reshape(groups, P_DEV, LEN, D)
    group_lens = lengths.reshape(groups, P_DEV)

    def step(totals, inputs):
        these_tokens, these_grads, these_lengths = inputs
        positions = jnp.arange(LEN, dtype=jnp.int32)
        live = (positions[None, :] < these_lengths[:, None]).astype(jnp.float32)[:, :, None]

        def forward(values, weights):
            return block(values, live, weights)
        output, pullback = jax.vjp(forward, these_tokens.astype(jnp.float32), params)
        d_tokens, d_params = pullback(these_grads.astype(jnp.float32))
        totals = jax.tree.map(add_pair, totals, d_params)
        return (totals, (output.astype(jnp.bfloat16), d_tokens.astype(jnp.bfloat16)))
    zeros_init = tuple((jnp.zeros_like(weight) for weight in params))
    totals, (outputs, d_tokens) = lax.scan(step, zeros_init, (group_toks, group_cots, group_lens))
    return (outputs.reshape(PROTEINS, LEN, D), d_tokens.reshape(PROTEINS, LEN, D), totals[0], totals[1], totals[2], totals[3], totals[4], totals[5], totals[6], totals[7], totals[8], totals[9], totals[10], totals[11])
```

```python
import functools

import jax
import jax.numpy as jnp
from jax import lax
from jax.experimental import pallas as pl
from jax.experimental.pallas import tpu as pltpu
from jax.sharding import PartitionSpec as P

KSIZE = 5
DILATION = 8
EPS = 1e-05
HALF_ROOT = 0.7071067811865476
PHI_SCALE = 0.3989422804014327
F32 = jnp.float32
BF16 = jnp.bfloat16
MESH = pl.DeviceIdType.MESH
VMEM_BYTES = 62 * 2**20
HBM = pl.BlockSpec(memory_space=pl.ANY)
LEVELS = 4
CHIPS = 16
DEVICES = 32
TILE = 256
CONV_COLS = ((0, 384), (384, 256))
OUT_COLS = ((0, 384), (384, 896))
WIDE_OFFSETS = (0, 40, 80)
SLIM_OFFSETS = (0, 20, 40, 60, 80, 100)


def place():
    dp = lax.axis_index("dp")
    fs = lax.axis_index("fsdp")
    return lax.div(dp, 2), lax.rem(dp, 2), lax.div(fs, 2), lax.rem(fs, 2)


def device(z, y, x, core):
    return (z * 2 + y, x * 2 + core)


def chip(z, y, x):
    return (z * 2 + y) * 2 + x


def peer_of(step):
    mine = lax.axis_index("dp") * 4 + lax.axis_index("fsdp")
    other = lax.rem(mine + step, DEVICES)
    return mine, other, (lax.div(other, 4), lax.rem(other, 4))


def greet_all():
    barrier = pltpu.get_barrier_semaphore()

    def greet(step, _):
        _, _, target = peer_of(step)
        pl.semaphore_signal(barrier, inc=1, device_id=target, device_id_type=MESH)
        return 0

    lax.fori_loop(1, DEVICES, greet, 0)
    pl.semaphore_wait(barrier, DEVICES - 1)


def chunk_masks(width, chunk):
    scale = -(-65536 // chunk)
    column = lax.broadcasted_iota(jnp.int32, (DEVICES, width), 1)
    row = lax.broadcasted_iota(jnp.int32, (DEVICES, width), 0)
    owner = lax.shift_right_logical(column * scale, 16) == row
    place_col = lax.broadcasted_iota(jnp.int32, (128, width), 1)
    place_row = lax.broadcasted_iota(jnp.int32, (128, width), 0)
    slot = place_col - lax.shift_right_logical(place_col * scale, 16) * chunk
    return owner, slot, place_row


def unpack_vectors(packed_ref, vectors_ref):
    for plane, (width, chunk, offsets) in enumerate(
        ((1280, 40, WIDE_OFFSETS), (640, 20, SLIM_OFFSETS))
    ):
        owner, slot, row = chunk_masks(width, chunk)
        packed = packed_ref[:, plane, :].astype(BF16)
        for index, offset in enumerate(offsets):
            pick = (slot + offset == row).astype(F32).astype(BF16)
            spread = jnp.dot(packed, pick, preferred_element_type=F32)
            line = jnp.sum(jnp.where(owner, spread, 0.0), axis=0, keepdims=True)
            vectors_ref[pl.ds(plane * 3 + index, 1), pl.ds(0, width)] = line


def lanes(column, width):
    return jnp.concatenate([column] * (width // 128), axis=1)


def norm_parts(values):
    width = values.shape[1]
    mean = jnp.sum(values, axis=1, keepdims=True) * (1.0 / width)
    center = values - mean
    var = jnp.sum(center * center, axis=1, keepdims=True) * (1.0 / width)
    scale = lax.rsqrt(var + EPS)
    return center * scale, scale


def gelu_parts(arg):
    normal = 0.5 + 0.5 * lax.erf(arg * HALF_ROOT)
    slope = normal + arg * (PHI_SCALE * jnp.exp(-0.5 * (arg * arg)))
    return arg * normal, slope


def gather_kernel(
    tokens, vec, w_in, w_conv, w_out,
    u1_out, slope1_out, xh1_out, scale1_out, xh2_out, slope2_out, scale2_out, u2_out, vectors_out,
    in_full, conv_full, out_full,
    packed, in_vmem, conv_twin, out_twin, conv_own, out_own, u1_keep,
    vec_send, vec_recv, link_send, link_recv, twin_recv, pair_send, pair_recv, own_sem, load_sem,
):
    step = pl.program_id(0)
    z, y, x, core = place()
    here = chip(z, y, x)
    steps = TILE and 2048 // TILE

    def piece(part, source, side):
        if part == 0:
            return in_vmem.at[pl.ds(pl.multiple_of(source * 80 + side * 40, 8), 40), :]
        if part == 1:
            start, width = CONV_COLS[side]
            return conv_full.at[:, pl.ds(pl.multiple_of(source * 40, 8), 40), pl.ds(start, width)]
        start, width = OUT_COLS[side]
        return out_full.at[pl.ds(pl.multiple_of(source * 40, 8), 40), pl.ds(start, width)]

    def own_piece(part, side):
        if part == 0:
            return w_in
        if part == 1:
            start, width = CONV_COLS[side]
            return conv_own.at[:, :, pl.ds(start, width)]
        start, width = OUT_COLS[side]
        return out_own.at[:, pl.ds(start, width)]

    def target(link, side):
        return (
            device(z, y, 1 - x, side),
            device(z, 1 - y, x, side),
            device(z + 1, y, x, side),
            device(z - 1, y, x, side),
            device(z, y, x, 1 - side),
        )[link]

    def send_of(side, part, source, link, own):
        recv = twin_recv if link == 4 else link_recv
        return pltpu.make_async_remote_copy(
            src_ref=own_piece(part, side) if own else piece(part, source, side),
            dst_ref=piece(part, source, side),
            send_sem=link_send.at[link, source, part],
            recv_sem=recv.at[source, part],
            device_id=target(link, side),
            device_id_type=MESH,
        )

    def guarded(link):
        if link == 2:
            return z < LEVELS - 1
        if link == 3:
            return z > 0
        return None

    def forward(side, part, source, links, own=False, wait=False):
        for link in links:
            def act(link=link):
                copy = send_of(side, part, source, link, own)
                if wait:
                    copy.wait_send()
                else:
                    copy.start()

            guard = guarded(link)
            if guard is None:
                act()
            else:
                pl.when(guard)(act)

    def arrive(side, part, source):
        pltpu.make_async_remote_copy(
            src_ref=piece(part, source, side),
            dst_ref=piece(part, source, side),
            send_sem=link_send.at[4, source, part],
            recv_sem=link_recv.at[source, part],
            device_id=target(4, side),
            device_id_type=MESH,
        ).wait_recv()

    def twin_arrive(side, part, source):
        pltpu.make_async_remote_copy(
            src_ref=piece(part, source, 1 - side),
            dst_ref=piece(part, source, 1 - side),
            send_sem=link_send.at[4, source, part],
            recv_sem=twin_recv.at[source, part],
            device_id=target(4, side),
            device_id_type=MESH,
        ).wait_recv()

    def levels(distance, act):
        if distance == 0:
            act(z, 0)
            return
        if distance < LEVELS:
            pl.when(z + distance < LEVELS)(lambda: act(z + distance, 1))
            pl.when(z - distance >= 0)(lambda: act(z - distance, -1))

    by_y = (False, True, False)

    def own_column(side, part, distance, wait=False):
        def act(level, sign):
            source = chip(level, y, x)
            if not wait:
                arrive(side, part, source)
            forward(side, part, source, (3 if sign > 0 else 2, 0, 1, 4), wait=wait)

        levels(distance, act)

    def x_column(side, part, distance, wait=False):
        def act(level, sign):
            source = chip(level, y, 1 - x)
            if not wait:
                arrive(side, part, source)
            forward(side, part, source, (1, 4) if by_y[part] else (4,), wait=wait)

        levels(distance, act)

    def y_column(side, part, distance, wait=False):
        def act(level, sign):
            source = chip(level, 1 - y, x)
            if not wait:
                arrive(side, part, source)
            forward(side, part, source, (4,) if by_y[part] else (0, 4), wait=wait)

        levels(distance, act)

    def far_column(side, part, distance, wait=False):
        def act(level, sign):
            source = chip(level, 1 - y, 1 - x)
            if not wait:
                arrive(side, part, source)
            forward(side, part, source, (4,), wait=wait)

        levels(distance, act)

    def own_sends(side, part, wait=False):
        forward(side, part, here, (0, 1, 2, 3, 4) if part == 0 else (0, 1, 2, 3), own=True, wait=wait)

    def pair_copies(side):
        return [
            pltpu.make_async_remote_copy(
                src_ref=src, dst_ref=dst, send_sem=pair_send.at[index], recv_sem=pair_recv.at[index],
                device_id=target(4, side), device_id_type=MESH,
            )
            for index, (src, dst) in enumerate(((w_conv, conv_twin), (w_out, out_twin)))
        ]

    def own_copies():
        return [
            pltpu.make_async_copy(conv_own, conv_full.at[:, pl.ds(pl.multiple_of(here * 40, 8), 40), :], own_sem.at[0]),
            pltpu.make_async_copy(out_own, out_full.at[pl.ds(pl.multiple_of(here * 40, 8), 40), :], own_sem.at[1]),
            pltpu.make_async_copy(w_in, in_vmem.at[pl.ds(pl.multiple_of(here * 80 + core * 40, 8), 40), :], own_sem.at[2]),
        ]

    def vec_copy(step_):
        mine, other, where = peer_of(step_)
        return mine, other, pltpu.make_async_remote_copy(
            src_ref=vec, dst_ref=packed.at[mine], send_sem=vec_send.at[other], recv_sem=vec_recv.at[mine],
            device_id=where, device_id_type=MESH,
        )

    def begin(side):
        own_sends(side, 0)
        for copy in pair_copies(side):
            copy.start()

    def assemble(side):
        for copy in pair_copies(side):
            copy.wait()
        first_conv, second_conv = (w_conv, conv_twin) if side == 0 else (conv_twin, w_conv)
        first_out, second_out = (w_out, out_twin) if side == 0 else (out_twin, w_out)
        conv_own[...] = jnp.concatenate(
            [first_conv[...].astype(F32), second_conv[...].astype(F32)], axis=1
        ).astype(BF16)
        out_own[...] = jnp.concatenate(
            [first_out[...].astype(F32), second_out[...].astype(F32)], axis=0
        ).astype(BF16)
        for copy in own_copies():
            copy.start()
        own_sends(side, 1)

    def finish(side):
        for part in range(3):
            for source_z in range(LEVELS):
                for source_y in range(2):
                    for source_x in range(2):
                        source = chip(source_z, source_y, source_x)
                        if part > 0:
                            pl.when(source != here)(functools.partial(twin_arrive, side, part, source))
        for part in range(3):
            own_sends(side, part, wait=True)
            for distance in range(LEVELS):
                if distance:
                    own_column(side, part, distance, wait=True)
                x_column(side, part, distance, wait=True)
                y_column(side, part, distance, wait=True)
                far_column(side, part, distance, wait=True)
        for copy in own_copies()[:2]:
            copy.wait()
        save_in().wait()

    def save_in():
        return pltpu.make_async_copy(in_vmem, in_full, load_sem.at[0])

    def both(*acts):
        for side in range(2):

            @pl.when(core == side)
            def _(side=side):
                for act in acts:
                    act(side)

    @pl.when(step == 0)
    def _():
        greet_all()

        def send_vec(step_, _):
            vec_copy(step_)[2].start()
            return 0

        lax.fori_loop(1, DEVICES, send_vec, 0)
        both(begin)
        packed[pl.ds(lax.axis_index("dp") * 4 + lax.axis_index("fsdp"), 1)] = vec[...][None]
        both(assemble)

        def take_vec(step_, _):
            _, other, copy = vec_copy(step_)
            copy.wait_send()
            pltpu.make_async_remote_copy(
                src_ref=vec, dst_ref=packed.at[other], send_sem=vec_send.at[other], recv_sem=vec_recv.at[other],
                device_id=peer_of(step_)[2], device_id_type=MESH,
            ).wait_recv()
            return 0

        lax.fori_loop(1, DEVICES, take_vec, 0)
        unpack_vectors(packed, vectors_out)

    def run(at, *acts):
        @pl.when(step == at)
        def _():
            both(*acts)

    run(
        1,
        lambda s: own_column(s, 0, 1), lambda s: x_column(s, 0, 0), lambda s: y_column(s, 0, 0),
        lambda s: own_sends(s, 2),
    )
    run(
        2,
        lambda s: own_column(s, 0, 2), lambda s: x_column(s, 0, 1), lambda s: y_column(s, 0, 1),
        lambda s: far_column(s, 0, 0),
        lambda s: own_column(s, 1, 1),
    )
    run(
        4,
        lambda s: own_column(s, 0, 3), lambda s: x_column(s, 0, 2), lambda s: y_column(s, 0, 2),
        lambda s: far_column(s, 0, 1), lambda s: x_column(s, 1, 0), lambda s: y_column(s, 1, 0),
    )
    run(
        5,
        lambda s: x_column(s, 0, 3), lambda s: y_column(s, 0, 3), lambda s: far_column(s, 0, 2),
        lambda s: own_column(s, 2, 1),
    )
    run(7, lambda s: far_column(s, 0, 3), lambda s: own_column(s, 1, 2))

    def wait_in(side):
        for source_z in range(LEVELS):
            for source_y in range(2):
                for source_x in range(2):
                    twin_arrive(side, 0, chip(source_z, source_y, source_x))
        own_copies()[2].wait()
        save_in().start()

    run(
        8,
        wait_in,
        lambda s: x_column(s, 1, 1), lambda s: y_column(s, 1, 1), lambda s: far_column(s, 1, 0),
    )
    run(
        9,
        lambda s: own_column(s, 1, 3), lambda s: x_column(s, 2, 0), lambda s: y_column(s, 2, 0),
        lambda s: own_column(s, 2, 2),
    )
    run(
        11,
        lambda s: x_column(s, 1, 2), lambda s: y_column(s, 1, 2), lambda s: far_column(s, 1, 1),
        lambda s: own_column(s, 2, 3),
    )
    run(
        13,
        lambda s: x_column(s, 2, 1), lambda s: y_column(s, 2, 1), lambda s: far_column(s, 2, 0),
        lambda s: x_column(s, 1, 3), lambda s: y_column(s, 1, 3),
    )

    @pl.when(step < steps)
    def _():
        gain, bias = vectors_out[pl.ds(0, 1), :], vectors_out[pl.ds(1, 1), :]
        norm, scale = norm_parts(tokens[...].astype(F32))
        act, slope = gelu_parts(norm * gain + bias)
        u1 = act.astype(BF16)
        u1_out[...] = u1
        u1_keep[pl.ds(pl.multiple_of(step * TILE, TILE), TILE), :] = u1
        slope1_out[...] = slope.astype(BF16)
        xh1_out[...] = norm.astype(BF16)
        scale1_out[...] = jnp.broadcast_to(scale, (TILE, 128))

    @pl.when(step >= steps)
    def _():
        row = pl.multiple_of((step - steps) * TILE, TILE)
        hidden = jnp.dot(u1_keep[pl.ds(row, TILE), :], in_vmem[...], preferred_element_type=F32)
        hidden = hidden + vectors_out[pl.ds(3, 1), pl.ds(0, 640)]
        norm, scale = norm_parts(hidden)
        act, slope = gelu_parts(norm * vectors_out[pl.ds(4, 1), pl.ds(0, 640)] + vectors_out[pl.ds(5, 1), pl.ds(0, 640)])
        u2_out[...] = act.astype(BF16)
        slope2_out[...] = slope.astype(BF16)
        xh2_out[...] = norm.astype(BF16)
        scale2_out[...] = jnp.broadcast_to(scale, (TILE, 128))

    run(
        2 * steps - 1,
        lambda s: x_column(s, 2, 2), lambda s: y_column(s, 2, 2), lambda s: far_column(s, 1, 2),
        lambda s: x_column(s, 2, 3), lambda s: y_column(s, 2, 3), lambda s: far_column(s, 1, 3),
        lambda s: far_column(s, 2, 1), lambda s: far_column(s, 2, 2), lambda s: far_column(s, 2, 3),
        finish,
    )


def gather_stage(tokens, vec, w_in, w_conv, w_out):
    rows = tokens.shape[0]
    steps = rows // TILE
    first = lambda i: (jnp.minimum(i, steps - 1), 0)
    second = lambda i: (jnp.maximum(i - steps, 0), 0)
    whole = lambda shape: pl.BlockSpec(shape, lambda i: (0,) * len(shape))
    wide = pl.BlockSpec((TILE, 1280), first)
    slim = pl.BlockSpec((TILE, 640), second)
    shape = jax.ShapeDtypeStruct
    return pl.pallas_call(
        gather_kernel,
        grid=(2 * steps,),
        in_specs=[wide, whole((2, 128)), whole((40, 640)), whole((KSIZE, 20, 640)), whole((20, 1280))],
        out_specs=[
            wide, wide, wide, pl.BlockSpec((TILE, 128), first),
            slim, slim, pl.BlockSpec((TILE, 128), second), slim, whole((16, 1280)),
            HBM, HBM, HBM,
        ],
        out_shape=[
            shape((rows, 1280), BF16), shape((rows, 1280), BF16), shape((rows, 1280), BF16), shape((rows, 128), F32),
            shape((rows, 640), BF16), shape((rows, 640), BF16), shape((rows, 128), F32), shape((rows, 640), BF16),
            shape((16, 1280), F32),
            shape((1280, 640), BF16), shape((KSIZE, 640, 640), BF16), shape((640, 1280), BF16),
        ],
        scratch_shapes=[
            pltpu.VMEM((DEVICES, 2, 128), F32),
            pltpu.VMEM((1280, 640), BF16),
            pltpu.VMEM((KSIZE, 20, 640), BF16),
            pltpu.VMEM((20, 1280), BF16),
            pltpu.VMEM((KSIZE, 40, 640), BF16),
            pltpu.VMEM((40, 1280), BF16),
            pltpu.VMEM((rows, 1280), BF16),
            pltpu.SemaphoreType.DMA((DEVICES,)),
            pltpu.SemaphoreType.DMA((DEVICES,)),
            pltpu.SemaphoreType.DMA((5, CHIPS, 3)),
            pltpu.SemaphoreType.DMA((CHIPS, 3)),
            pltpu.SemaphoreType.DMA((CHIPS, 3)),
            pltpu.SemaphoreType.DMA((2,)),
            pltpu.SemaphoreType.DMA((2,)),
            pltpu.SemaphoreType.DMA((3,)),
            pltpu.SemaphoreType.DMA((1,)),
        ],
        compiler_params=pltpu.CompilerParams(
            collective_id=0, has_side_effects=True, vmem_limit_bytes=VMEM_BYTES,
            dimension_semantics=("arbitrary",),
        ),
        name="gather_stage",
    )(tokens, vec, w_in, w_conv, w_out)


def pack_vectors(ln1_gain, ln1_bias, b_in, ln2_gain, ln2_bias, b_conv, ln3_gain, ln3_bias, b_out):
    wide = jnp.concatenate([ln1_gain, ln1_bias, b_out, jnp.zeros((8,), BF16)])
    slim = jnp.concatenate([b_in, ln2_gain, ln2_bias, b_conv, ln3_gain, ln3_bias, jnp.zeros((8,), BF16)])
    return jnp.stack([wide, slim]).astype(F32)


PAD = 32
SPAN = 1024 + 2 * PAD


def middle_kernel(
    lengths, vectors, u2_hbm, xh2_hbm, slope2_hbm, scale2_hbm, grads_hbm, tokens_hbm, conv_hbm, last_hbm,
    out_hbm, dh1_hbm, d_conv_hbm, d_last_hbm, sums_out,
    conv, conv_t, last, last_t, u2, dh2, grads, tokens, xh2, slope2, scale2, dh1, d_conv, d_last, zeros,
    u2_sem, row_sem, back_sem, weight_sem, out_sem, dh1_sem, flush_sem,
):
    proteins = 2
    tiles = 1024 // TILE
    wide, slim = 1280, 640

    def tile_count(protein):
        return lax.div(lengths[protein] + TILE - 1, TILE)

    def rows_of(protein, tile):
        return pl.ds(pl.multiple_of(protein * 1024 + tile * TILE, TILE), TILE)

    def padded(protein, tile, shift=0):
        return pl.ds(pl.multiple_of(protein * SPAN + PAD + tile * TILE, 8) + shift, TILE)

    def u2_load(protein, tile):
        return pltpu.make_async_copy(
            u2_hbm.at[rows_of(protein, tile), :], u2.at[padded(protein, tile), :], u2_sem.at[protein, tile]
        )

    def row_loads(protein, tile):
        rows = rows_of(protein, tile)
        return [
            pltpu.make_async_copy(grads_hbm.at[rows, :], grads.at[rows, :], row_sem.at[0, protein, tile]),
            pltpu.make_async_copy(tokens_hbm.at[rows, :], tokens.at[rows, :], row_sem.at[1, protein, tile]),
        ]

    def back_loads(protein, tile):
        rows = rows_of(protein, tile)
        return [
            pltpu.make_async_copy(xh2_hbm.at[rows, :], xh2.at[rows, :], back_sem.at[0, protein, tile]),
            pltpu.make_async_copy(slope2_hbm.at[rows, :], slope2.at[rows, :], back_sem.at[1, protein, tile]),
            pltpu.make_async_copy(scale2_hbm.at[rows, :], scale2.at[rows, :], back_sem.at[2, protein, tile]),
        ]

    def out_store(protein, tile):
        rows = rows_of(protein, tile)
        return pltpu.make_async_copy(tokens.at[rows, :], out_hbm.at[rows, :], out_sem.at[protein, tile])

    def dh1_store(protein, tile, source):
        return pltpu.make_async_copy(source, dh1_hbm.at[rows_of(protein, tile), :], dh1_sem.at[protein, tile])

    conv_load = pltpu.make_async_copy(conv_hbm, conv, weight_sem.at[0])
    last_load = pltpu.make_async_copy(last_hbm, last, weight_sem.at[1])

    def each_tile(protein, act):
        def step(tile, _):
            act(protein, tile)
            return 0

        lax.fori_loop(0, tile_count(protein), step, 0)

    def start_all(copies):
        for copy in copies:
            copy.start()

    each_tile(0, lambda p, t: u2_load(p, t).start())
    conv_load.start()
    last_load.start()
    each_tile(0, lambda p, t: start_all(row_loads(p, t)))
    each_tile(1, lambda p, t: u2_load(p, t).start())
    each_tile(1, lambda p, t: start_all(row_loads(p, t)))
    for protein in range(proteins):
        each_tile(protein, lambda p, t: start_all(back_loads(p, t)))
    zeros[...] = jnp.zeros_like(zeros)
    for protein in range(proteins):

        def dead_load(tile, _, protein=protein):
            row_loads(protein, tile)[1].start()
            dh1_store(protein, tile, zeros).start()
            return 0

        lax.fori_loop(tile_count(protein), tiles, dead_load, 0)

    sums_out[...] = jnp.zeros_like(sums_out)
    for tap in range(KSIZE):
        d_conv[tap] = jnp.zeros((slim, slim), F32)
    d_last[...] = jnp.zeros_like(d_last)

    def vector(index, width=slim):
        return vectors[pl.ds(index, 1), pl.ds(0, width)]

    def add_sum(index, values):
        width = values.shape[1]
        sums_out[pl.ds(index * 8, 8), pl.ds(0, width)] += jnp.sum(
            values.reshape(values.shape[0] // 8, 8, width), axis=0
        )

    def live_rows(protein, tile):
        position = lax.broadcasted_iota(jnp.int32, (TILE, 128), 0) + tile * TILE
        return (position < lengths[protein]).astype(F32)

    edge = jnp.zeros((PAD, slim), BF16)
    for protein in range(proteins):
        base = protein * SPAN
        u2[pl.ds(base, PAD), :] = edge
        dh2[pl.ds(base, PAD), :] = edge

        def prepare(tile, _, protein=protein, base=base):
            u2_load(protein, tile).wait()
            return 0

        count = tile_count(protein)
        lax.fori_loop(0, count, prepare, 0)
        last_tile = count - 1
        u2[padded(protein, last_tile), :] = (
            u2[padded(protein, last_tile), :].astype(F32) * lanes(live_rows(protein, last_tile), slim)
        ).astype(BF16)
        after = pl.ds(pl.multiple_of(base + PAD + count * TILE, 8), PAD)
        u2[after, :] = edge
        dh2[after, :] = edge
        if protein == 0:
            conv_load.wait()
            last_load.wait()
            last_t[...] = last[...].T
            for tap in range(KSIZE):
                conv_t[tap] = conv[tap].T

        def forward(tile, _, protein=protein):
            for copy in row_loads(protein, tile):
                copy.wait()
            rows = rows_of(protein, tile)
            live = live_rows(protein, tile)
            hidden = jnp.dot(u2[padded(protein, tile, -16), :], conv[0], preferred_element_type=F32)
            for tap in range(1, KSIZE):
                hidden += jnp.dot(
                    u2[padded(protein, tile, (tap - 2) * DILATION), :], conv[tap], preferred_element_type=F32
                )
            gz = (grads[rows, :].astype(F32) * lanes(live, wide)).astype(BF16)
            back = jnp.dot(gz, last_t[...], preferred_element_type=F32)
            norm, scale = norm_parts(hidden + vector(6))
            act, slope = gelu_parts(norm * vector(7) + vector(8))
            u3 = act.astype(BF16)
            branch = jnp.dot(u3, last[...], preferred_element_type=F32) + vector(2, wide)
            tokens[rows, :] = (tokens[rows, :].astype(F32) + lanes(live, wide) * branch).astype(BF16)
            out_store(protein, tile).start()
            d_last[...] += lax.dot_general(u3, gz, (((0,), (0,)), ((), ())), preferred_element_type=F32)
            add_sum(2, gz.astype(F32))
            slope_grad = back * slope
            add_sum(7, slope_grad * norm)
            add_sum(8, slope_grad)
            err = slope_grad * vector(7)
            mean = jnp.sum(err, axis=1, keepdims=True) * (1.0 / slim)
            along = jnp.sum(err * norm, axis=1, keepdims=True) * (1.0 / slim)
            low = (scale * (err - mean - norm * along)).astype(BF16)
            add_sum(6, low.astype(F32))
            dh2[padded(protein, tile), :] = low
            return 0

        lax.fori_loop(0, count, forward, 0)

        def backward(tile, _, protein=protein):
            for copy in back_loads(protein, tile):
                copy.wait()
            rows = rows_of(protein, tile)
            live = lanes(live_rows(protein, tile), slim)
            source_t = u2[padded(protein, tile), :].T
            total = None
            for tap in range(KSIZE):
                window = dh2[padded(protein, tile, (2 - tap) * DILATION), :]
                term = jnp.dot(window, conv_t[tap], preferred_element_type=F32)
                total = term if total is None else total + term
                d_conv[tap] += jnp.dot(source_t, window, preferred_element_type=F32)
            norm = xh2[rows, :].astype(F32)
            slope_grad = total * live * slope2[rows, :].astype(F32)
            add_sum(4, slope_grad * norm)
            add_sum(5, slope_grad)
            err = slope_grad * vector(4)
            mean = jnp.sum(err, axis=1, keepdims=True) * (1.0 / slim)
            along = jnp.sum(err * norm, axis=1, keepdims=True) * (1.0 / slim)
            low = (lanes(scale2[rows, :], slim) * (err - mean - norm * along)).astype(BF16)
            add_sum(3, low.astype(F32))
            dh1[rows, :] = low
            dh1_store(protein, tile, dh1.at[rows, :]).start()
            return 0

        lax.fori_loop(0, count, backward, 0)

    last[...] = d_last[...].astype(BF16)
    flushes = [pltpu.make_async_copy(last, d_last_hbm, flush_sem.at[0])]
    flushes[0].start()
    for tap in range(KSIZE):
        conv[tap] = d_conv[tap].astype(BF16)
        flushes.append(pltpu.make_async_copy(conv.at[tap], d_conv_hbm.at[tap], flush_sem.at[tap + 1]))
        flushes[-1].start()
    for protein in range(proteins):

        def dead_store(tile, _, protein=protein):
            row_loads(protein, tile)[1].wait()
            out_store(protein, tile).start()
            return 0

        lax.fori_loop(tile_count(protein), tiles, dead_store, 0)
    for protein in range(proteins):
        for tile in range(tiles):
            out_store(protein, tile).wait()
            dh1_store(protein, tile, zeros).wait()
    for copy in flushes:
        copy.wait()


def middle_stage(lengths, vectors, u2, xh2, slope2, scale2, grads, tokens, w_conv, w_out):
    rows = u2.shape[0]
    shape = jax.ShapeDtypeStruct
    vmem = pl.BlockSpec(memory_space=pltpu.VMEM)
    tiles = 1024 // TILE
    return pl.pallas_call(
        middle_kernel,
        in_specs=[pl.BlockSpec(memory_space=pltpu.SMEM), vmem] + [HBM] * 8,
        out_specs=[HBM, HBM, HBM, HBM, vmem],
        out_shape=[
            shape((rows, 1280), BF16), shape((rows, 640), BF16), shape((KSIZE, 640, 640), BF16),
            shape((640, 1280), BF16), shape((72, 1280), F32),
        ],
        scratch_shapes=[
            pltpu.VMEM((KSIZE, 640, 640), BF16),
            pltpu.VMEM((KSIZE, 640, 640), BF16),
            pltpu.VMEM((640, 1280), BF16),
            pltpu.VMEM((1280, 640), BF16),
            pltpu.VMEM((2 * SPAN, 640), BF16),
            pltpu.VMEM((2 * SPAN, 640), BF16),
            pltpu.VMEM((rows, 1280), BF16),
            pltpu.VMEM((rows, 1280), BF16),
            pltpu.VMEM((rows, 640), BF16),
            pltpu.VMEM((rows, 640), BF16),
            pltpu.VMEM((rows, 128), F32),
            pltpu.VMEM((rows, 640), BF16),
            pltpu.VMEM((KSIZE, 640, 640), F32),
            pltpu.VMEM((640, 1280), F32),
            pltpu.VMEM((TILE, 640), BF16),
            pltpu.SemaphoreType.DMA((2, tiles)),
            pltpu.SemaphoreType.DMA((2, 2, tiles)),
            pltpu.SemaphoreType.DMA((3, 2, tiles)),
            pltpu.SemaphoreType.DMA((2,)),
            pltpu.SemaphoreType.DMA((2, tiles)),
            pltpu.SemaphoreType.DMA((2, tiles)),
            pltpu.SemaphoreType.DMA((6,)),
        ],
        compiler_params=pltpu.CompilerParams(vmem_limit_bytes=VMEM_BYTES),
        name="middle_stage",
    )(lengths, vectors, u2, xh2, slope2, scale2, grads, tokens, w_conv, w_out)


def pack_sums(lines, packed_ref):
    for plane, (width, chunk, offsets) in enumerate(
        ((1280, 40, WIDE_OFFSETS), (640, 20, SLIM_OFFSETS))
    ):
        owner, slot, row = chunk_masks(width, chunk)
        total = None
        for line, offset in zip(lines[plane], offsets):
            pick = (slot + offset == row).astype(F32)
            term = lax.dot_general(
                jnp.where(owner, jnp.broadcast_to(line, owner.shape), 0.0), pick, (((1,), (1,)), ((), ())),
                precision=lax.Precision.HIGHEST, preferred_element_type=F32,
            )
            total = term if total is None else total + term
        packed_ref[:, plane, :] = total


def scatter_kernel(
    u1, dh1, slope1, xh1, scale1, grads, w_in, vectors, sums, d_conv_hbm, d_last_hbm,
    grad_tokens, g_in, g_conv, g_last, g_vec,
    w_in_t, d_in_sum, d_in, own_sums, packed, packed_in,
    conv_own, conv_twin, conv_far, conv_x, conv_y, conv_up, conv_down, conv_done, conv_swap,
    last_own, last_twin, last_far, last_x, last_y, last_up, last_down, last_done, last_swap,
    in_twin, in_far, in_x, in_y, in_up, in_down,
    vec_send, vec_recv, load_sem, twin_send, twin_recv, move_send, move_recv, line_send, line_recv, swap_send, swap_recv,
):
    step = pl.program_id(0)
    steps = 2048 // TILE
    z, y, x, core = place()
    columns = {"own": 2 * y + x, "x": 2 * y + (1 - x), "y": 2 * (1 - y) + x, "far": 2 * (1 - y) + (1 - x)}

    def cut(side, part):
        if part == 1:
            return CONV_COLS[side]
        if part == 2:
            return OUT_COLS[side]
        return (0, 640)

    def own_at(side, part, level, column):
        width = cut(side, part)[1]
        if part == 0:
            return d_in.at[level, column, side]
        if part == 1:
            return conv_own.at[:, level, column, :, pl.ds(0, width)]
        return last_own.at[level, column, :, pl.ds(0, width)]

    def twin_at(side, part, level, column):
        width = cut(side, part)[1]
        if part == 0:
            return in_twin.at[level, column]
        if part == 1:
            return conv_twin.at[:, level, column, :, pl.ds(0, width)]
        return last_twin.at[level, column, :, pl.ds(0, width)]

    boxes = {
        "far": (in_far, conv_far, last_far),
        "x": (in_x, conv_x, last_x),
        "y": (in_y, conv_y, last_y),
        "up": (in_up, conv_up, last_up),
        "down": (in_down, conv_down, last_down),
    }

    def box_at(side, part, name, level):
        width = cut(side, part)[1]
        box = boxes[name][part]
        if part == 0:
            return box.at[level]
        if part == 1:
            return box.at[level, :, :, pl.ds(0, width)]
        return box.at[level, :, pl.ds(0, width)]

    twin_id = device(z, y, x, 1 - core)
    link_ids = {"x": device(z, y, 1 - x, core), "y": device(z, 1 - y, x, core),
                "up": device(z + 1, y, x, core), "down": device(z - 1, y, x, core)}
    names = ("own", "x", "y", "far")
    by_y = (False, True, False)

    def loads(side):
        start, width = cut(side, 1)
        first = pltpu.make_async_copy(
            d_conv_hbm.at[:, :, :, :, pl.ds(start, width)], conv_own.at[:, :, :, :, pl.ds(0, width)], load_sem.at[0]
        )
        start, width = cut(side, 2)
        second = pltpu.make_async_copy(
            d_last_hbm.at[:, :, :, pl.ds(start, width)], last_own.at[:, :, :, pl.ds(0, width)], load_sem.at[1]
        )
        return first, second

    def twin_copy(side, part, name, to_side):
        column = columns[name]
        start, width = cut(to_side, part)
        if part == 0:
            src, dst = d_in.at[:, column, to_side], in_twin.at[:, column]
        elif part == 1:
            src = d_conv_hbm.at[:, :, column, :, pl.ds(start, width)]
            dst = conv_twin.at[:, :, column, :, pl.ds(0, width)]
        else:
            src = d_last_hbm.at[:, column, :, pl.ds(start, width)]
            dst = last_twin.at[:, column, :, pl.ds(0, width)]
        index = names.index(name)
        return pltpu.make_async_remote_copy(
            src_ref=src, dst_ref=dst, send_sem=twin_send.at[part, index], recv_sem=twin_recv.at[part, index],
            device_id=twin_id, device_id_type=MESH,
        )

    def exchange(part):
        def act(side):
            for name in ("far", "y", "x", "own"):
                twin_copy(side, part, name, 1 - side).start()

        return act

    kinds = ("far", "x", "y")

    def move(side, part, column, level, link, box):
        return pltpu.make_async_remote_copy(
            src_ref=own_at(side, part, level, columns[column]), dst_ref=box_at(side, part, box, level),
            send_sem=move_send.at[kinds.index(box), part, level], recv_sem=move_recv.at[kinds.index(box), part, level],
            device_id=link_ids[link], device_id_type=MESH,
        )

    def line(side, part, level, link):
        box = "down" if link == "up" else "up"
        index = 0 if link == "up" else 1
        return pltpu.make_async_remote_copy(
            src_ref=own_at(side, part, level, columns["own"]), dst_ref=box_at(side, part, box, level),
            send_sem=line_send.at[index, part, level], recv_sem=line_recv.at[index, part, level],
            device_id=link_ids[link], device_id_type=MESH,
        )

    def levels(distance, act):
        if distance == 0:
            act(z, 0)
            return
        pl.when(z + distance < LEVELS)(lambda: act(z + distance, 1))
        pl.when(z - distance >= 0)(lambda: act(z - distance, -1))

    def read(ref):
        return ref[...].astype(F32)

    def both_terms(side, part, level, column):
        return read(own_at(side, part, level, columns[column])) + read(twin_at(side, part, level, columns[column]))

    def put(side, part, level, column, value):
        own_at(side, part, level, columns[column])[...] = value.astype(BF16)

    def first_hop(part, distances=(3, 2, 1, 0)):
        link = "y" if by_y[part] else "x"

        def act(side):
            if part and distances[0] == 3:
                loads(side)[part - 1].wait()
            if distances[0] == 3:
                twin_copy(side, part, "far", side).wait_recv()
            for distance in distances:

                def one(level, sign):
                    put(side, part, level, "far", both_terms(side, part, level, "far"))
                    move(side, part, "far", level, link, "far").start()

                levels(distance, one)

        return act

    def direct_hop(part, distances=(3, 2, 1, 0)):
        name = "y" if by_y[part] else "x"

        def act(side):
            if distances[0] == 3:
                twin_copy(side, part, name, side).wait_recv()
            for distance in distances:

                def one(level, sign):
                    put(side, part, level, name, both_terms(side, part, level, name))
                    move(side, part, name, level, name, name).start()

                levels(distance, one)

        return act

    def second_hop(part, distances=(3, 2, 1, 0)):
        name = "x" if by_y[part] else "y"
        link = "y" if by_y[part] else "x"

        def act(side):
            if distances[0] == 3:
                twin_copy(side, part, name, side).wait_recv()
            for distance in distances:

                def one(level, sign):
                    move(side, part, "far", level, link, "far").wait_recv()
                    put(
                        side, part, level, name,
                        both_terms(side, part, level, name) + read(box_at(side, part, "far", level)),
                    )
                    move(side, part, name, level, name, name).start()

                levels(distance, one)

        return act

    def line_hop(part, distances=(3, 2, 1)):
        def act(side):
            if distances[0] == 3:
                twin_copy(side, part, "own", side).wait_recv()
            for distance in distances:

                def one(level, sign):
                    move(side, part, "x", level, "x", "x").wait_recv()
                    move(side, part, "y", level, "y", "y").wait_recv()
                    total = both_terms(side, part, level, "own")
                    total += read(box_at(side, part, "x", level)) + read(box_at(side, part, "y", level))
                    behind, box, link = (z > 0, "down", "up") if sign > 0 else (z < LEVELS - 1, "up", "down")

                    @pl.when(behind)
                    def _():
                        line(side, part, level, link).wait_recv()
                        put(side, part, level, "own", total + read(box_at(side, part, box, level)))

                    @pl.when(jnp.logical_not(behind))
                    def _():
                        put(side, part, level, "own", total)

                    line(side, part, level, link).start()

                levels(distance, one)

        return act

    def arrive(part):
        def act(side):
            move(side, part, "x", z, "x", "x").wait_recv()
            move(side, part, "y", z, "y", "y").wait_recv()
            width = cut(side, part)[1]
            if part == 0:
                done = g_in
            elif part == 1:
                done = conv_done.at[:, :, pl.ds(0, width)]
            else:
                done = last_done.at[:, pl.ds(0, width)]
            total = both_terms(side, part, z, "own")
            done[...] = total + read(box_at(side, part, "x", z)) + read(box_at(side, part, "y", z))
            for link, box, guard in (("up", "down", z > 0), ("down", "up", z < LEVELS - 1)):

                @pl.when(guard)
                def _(link=link, box=box):
                    line(side, part, z, link).wait_recv()
                    done[...] += read(box_at(side, part, box, z))

            if part:
                swap(side, part, side).start()

        return act

    def swap(side, part, from_side):
        width = cut(from_side, part)[1]
        if part == 1:
            src, dst = conv_done.at[:, :, pl.ds(0, width)], conv_swap.at[:, :, pl.ds(0, width)]
        else:
            src, dst = last_done.at[:, pl.ds(0, width)], last_swap.at[:, pl.ds(0, width)]
        return pltpu.make_async_remote_copy(
            src_ref=src, dst_ref=dst, send_sem=swap_send.at[part - 1], recv_sem=swap_recv.at[part - 1],
            device_id=twin_id, device_id_type=MESH,
        )

    def deliver(side):
        first, count = side * 20, 20
        for part, done, other, target in ((1, conv_done, conv_swap, g_conv), (2, last_done, last_swap, g_last)):
            swap(side, part, 1 - side).wait_recv()
            for refs, owner in ((done, side), (other, 1 - side)):
                start, width = cut(owner, part)
                if part == 1:
                    target[:, :, pl.ds(start, width)] = refs[:, pl.ds(first, count), pl.ds(0, width)]
                else:
                    target[:, pl.ds(start, width)] = refs[pl.ds(first, count), pl.ds(0, width)]

    def finish(side):
        for part in range(3):
            if part:
                swap(side, part, side).wait_send()
            for name in names:
                twin_copy(side, part, name, 1 - side).wait_send()
            link, other = ("y", "x") if by_y[part] else ("x", "y")
            for level in range(LEVELS):
                move(side, part, "far", level, link, "far").wait_send()
                move(side, part, link, level, link, link).wait_send()
                move(side, part, other, level, other, other).wait_send()
                pl.when(level > z)(lambda level=level: line(side, part, level, "up").wait_send())
                pl.when(level < z)(lambda level=level: line(side, part, level, "down").wait_send())

    def vec_copy(step_):
        mine, other, where = peer_of(step_)
        return mine, other, pltpu.make_async_remote_copy(
            src_ref=packed.at[other], dst_ref=packed_in.at[mine], send_sem=vec_send.at[other],
            recv_sem=vec_recv.at[mine], device_id=where, device_id_type=MESH,
        )

    def vectors_out(side):
        lines = [
            [jnp.sum(own_sums[pl.ds(8 * index, 8), :], axis=0, keepdims=True) for index in range(2)]
            + [jnp.sum(sums[pl.ds(16, 8), :], axis=0, keepdims=True)],
            [jnp.sum(sums[pl.ds(8 * index, 8), pl.ds(0, 640)], axis=0, keepdims=True) for index in range(3, 9)],
        ]
        pack_sums(lines, packed)

        def send(step_, _):
            vec_copy(step_)[2].start()
            return 0

        lax.fori_loop(1, DEVICES, send, 0)
        mine = lax.axis_index("dp") * 4 + lax.axis_index("fsdp")
        packed_in[pl.ds(mine, 1)] = packed[pl.ds(mine, 1)]

    def vectors_in():
        def take(step_, _):
            _, other, copy = vec_copy(step_)
            copy.wait_send()
            pltpu.make_async_remote_copy(
                src_ref=packed.at[other], dst_ref=packed_in.at[other], send_sem=vec_send.at[other],
                recv_sem=vec_recv.at[other], device_id=peer_of(step_)[2], device_id_type=MESH,
            ).wait_recv()
            return 0

        lax.fori_loop(1, DEVICES, take, 0)
        g_vec[...] = jnp.sum(packed_in[...], axis=0)

    def run(at, *acts):
        @pl.when(step == at)
        def _():
            for side in range(2):

                @pl.when(core == side)
                def _(side=side):
                    for act in acts:
                        act(side)

    @pl.when(step == 0)
    def _():
        own_sums[...] = jnp.zeros_like(own_sums)
        greet_all()

    def start_loads(side):
        for copy in loads(side):
            copy.start()

    run(0, start_loads, exchange(1), exchange(2), first_hop(1), first_hop(2))
    run(1, direct_hop(2), direct_hop(1))
    run(5, second_hop(2))

    @pl.when(step < steps)
    def _():
        term = lax.dot_general(u1[...], dh1[...], (((0,), (0,)), ((), ())), preferred_element_type=F32)

        @pl.when(step == 0)
        def _():
            d_in_sum[...] = term

        @pl.when(step > 0)
        def _():
            d_in_sum[...] += term

    @pl.when(step == steps - 1)
    def _():
        d_in[...] = d_in_sum[...].astype(BF16).reshape(d_in.shape)
        w_in_t[...] = w_in[...].T

    run(7, exchange(0))
    run(8, second_hop(1, (3, 2)))
    run(9, first_hop(0), direct_hop(0), second_hop(1, (1, 0)))
    run(11, second_hop(0))
    run(12, line_hop(2))
    run(13, line_hop(1, (3, 2)))

    @pl.when(step >= steps)
    def _():
        back = jnp.dot(dh1[...], w_in_t[...], preferred_element_type=F32)
        norm = xh1[...].astype(F32)
        slope_grad = back * slope1[...].astype(F32)
        for index, values in enumerate((slope_grad * norm, slope_grad)):
            own_sums[pl.ds(8 * index, 8), :] += jnp.sum(values.reshape(TILE // 8, 8, 1280), axis=0)
        err = slope_grad * vectors[pl.ds(0, 1), :]
        mean = jnp.sum(err, axis=1, keepdims=True) * (1.0 / 1280)
        along = jnp.sum(err * norm, axis=1, keepdims=True) * (1.0 / 1280)
        grad_tokens[...] = (
            grads[...].astype(F32) + lanes(scale1[...], 1280) * (err - mean - norm * along)
        ).astype(BF16)

    run(
        2 * steps - 1,
        vectors_out, line_hop(1, (1,)), arrive(2), line_hop(0), arrive(1), arrive(0), deliver, finish,
    )

    @pl.when(step == 2 * steps - 1)
    def _():
        vectors_in()


def scatter_stage(u1, dh1, slope1, xh1, scale1, grads, w_in, vectors, sums, d_conv, d_last):
    rows = u1.shape[0]
    steps = rows // TILE
    first = lambda i: (jnp.minimum(i, steps - 1), 0)
    second = lambda i: (jnp.maximum(i - steps, 0), 0)
    again = lambda i: (lax.rem(i, steps), 0)
    whole = lambda shape: pl.BlockSpec(shape, lambda i: (0,) * len(shape))
    wide = pl.BlockSpec((TILE, 1280), second)
    shape = jax.ShapeDtypeStruct
    conv_box = pltpu.VMEM((LEVELS, KSIZE, 40, 384), BF16)
    last_box = pltpu.VMEM((LEVELS, 40, 896), BF16)
    in_box = pltpu.VMEM((LEVELS, 40, 640), BF16)
    dma = pltpu.SemaphoreType.DMA
    return pl.pallas_call(
        scatter_kernel,
        grid=(2 * steps,),
        in_specs=[
            pl.BlockSpec((TILE, 1280), first), pl.BlockSpec((TILE, 640), again), wide, wide,
            pl.BlockSpec((TILE, 128), second), wide, whole((1280, 640)), whole((16, 1280)), whole((72, 1280)), HBM, HBM,
        ],
        out_specs=[wide, whole((40, 640)), whole((KSIZE, 20, 640)), whole((20, 1280)), whole((2, 128))],
        out_shape=[
            shape((rows, 1280), BF16), shape((40, 640), F32), shape((KSIZE, 20, 640), F32), shape((20, 1280), F32),
            shape((2, 128), F32),
        ],
        scratch_shapes=[
            pltpu.VMEM((640, 1280), BF16),
            pltpu.VMEM((1280, 640), F32),
            pltpu.VMEM((LEVELS, 4, 2, 40, 640), BF16),
            pltpu.VMEM((16, 1280), F32),
            pltpu.VMEM((DEVICES, 2, 128), F32),
            pltpu.VMEM((DEVICES, 2, 128), F32),
            pltpu.VMEM((KSIZE, LEVELS, 4, 40, 384), BF16),
            pltpu.VMEM((KSIZE, LEVELS, 4, 40, 384), BF16),
            conv_box, conv_box, conv_box, conv_box, conv_box,
            pltpu.VMEM((KSIZE, 40, 384), F32),
            pltpu.VMEM((KSIZE, 40, 384), F32),
            pltpu.VMEM((LEVELS, 4, 40, 896), BF16),
            pltpu.VMEM((LEVELS, 4, 40, 896), BF16),
            last_box, last_box, last_box, last_box, last_box,
            pltpu.VMEM((40, 896), F32),
            pltpu.VMEM((40, 896), F32),
            pltpu.VMEM((LEVELS, 4, 40, 640), BF16),
            in_box, in_box, in_box, in_box, in_box,
            dma((DEVICES,)), dma((DEVICES,)), dma((2,)), dma((3, 4)), dma((3, 4)),
            dma((3, 3, LEVELS)), dma((3, 3, LEVELS)), dma((2, 3, LEVELS)), dma((2, 3, LEVELS)), dma((2,)), dma((2,)),
        ],
        compiler_params=pltpu.CompilerParams(
            collective_id=1, has_side_effects=True, vmem_limit_bytes=VMEM_BYTES,
            dimension_semantics=("arbitrary",),
        ),
        name="scatter_stage",
    )(
        u1, dh1, slope1, xh1, scale1, grads, w_in, vectors, sums,
        d_conv.reshape(KSIZE, LEVELS, 4, 40, 640), d_last.reshape(LEVELS, 4, 40, 1280),
    )


def kernel_body(
    tokens, out_grad, lengths, ln1_gain, ln1_bias, w_in, b_in, ln2_gain, ln2_bias,
    w_conv, b_conv, ln3_gain, ln3_bias, w_out, b_out,
):
    proteins, length_pad, width = tokens.shape
    rows = tokens.reshape(proteins * length_pad, width)
    grads = out_grad.reshape(proteins * length_pad, width)
    vec = pack_vectors(ln1_gain, ln1_bias, b_in, ln2_gain, ln2_bias, b_conv, ln3_gain, ln3_bias, b_out)
    u1, slope1, xh1, scale1, xh2, slope2, scale2, u2, vectors, in_full, conv_full, out_full = gather_stage(
        rows, vec, w_in, w_conv, w_out
    )
    result, dh1, d_conv, d_last, sums = middle_stage(
        lengths, vectors, u2, xh2, slope2, scale2, grads, rows, conv_full, out_full
    )
    grad_rows, g_in, g_conv, g_last, g_vec = scatter_stage(
        u1, dh1, slope1, xh1, scale1, grads, in_full, vectors, sums, d_conv, d_last
    )
    wide = [g_vec[0, start : start + 40] for start in WIDE_OFFSETS]
    slim = [g_vec[1, start : start + 20] for start in SLIM_OFFSETS]
    return (
        result.reshape(tokens.shape), grad_rows.reshape(tokens.shape),
        wide[0], wide[1], g_in, slim[0], slim[1], slim[2], g_conv, slim[3], slim[4], slim[5], g_last, wide[2],
    )


def layer_norm(values, gain, bias):
    center = values - jnp.mean(values, axis=-1, keepdims=True)
    var_rows = jnp.mean(center * center, axis=-1, keepdims=True)
    return center * lax.rsqrt(var_rows + EPS) * gain + bias


def norm_gelu(values, gain, bias):
    return jax.nn.gelu(layer_norm(values, gain, bias), approximate=False)


def collect(
    ln1_gain,
    ln1_bias,
    w_in,
    b_in,
    ln2_gain,
    ln2_bias,
    w_conv,
    b_conv,
    ln3_gain,
    ln3_bias,
    w_out,
    b_out,
):
    return (
        lax.all_gather(ln1_gain, ("dp", "fsdp"), axis=0, tiled=True),
        lax.all_gather(ln1_bias, ("dp", "fsdp"), axis=0, tiled=True),
        lax.all_gather(w_in, ("dp", "fsdp"), axis=0, tiled=True),
        lax.all_gather(b_in, ("dp", "fsdp"), axis=0, tiled=True),
        lax.all_gather(ln2_gain, ("dp", "fsdp"), axis=0, tiled=True),
        lax.all_gather(ln2_bias, ("dp", "fsdp"), axis=0, tiled=True),
        lax.all_gather(w_conv, ("dp", "fsdp"), axis=1, tiled=True),
        lax.all_gather(b_conv, ("dp", "fsdp"), axis=0, tiled=True),
        lax.all_gather(ln3_gain, ("dp", "fsdp"), axis=0, tiled=True),
        lax.all_gather(ln3_bias, ("dp", "fsdp"), axis=0, tiled=True),
        lax.all_gather(w_out, ("dp", "fsdp"), axis=0, tiled=True),
        lax.all_gather(b_out, ("dp", "fsdp"), axis=0, tiled=True),
    )


def spread(
    term_g1,
    term_b1,
    term_wi,
    term_bi,
    term_g2,
    term_b2,
    term_wc,
    term_bc,
    term_g3,
    term_b3,
    term_wo,
    term_bo,
):
    return (
        lax.psum_scatter(term_g1, ("dp", "fsdp"), scatter_dimension=0, tiled=True),
        lax.psum_scatter(term_b1, ("dp", "fsdp"), scatter_dimension=0, tiled=True),
        lax.psum_scatter(term_wi, ("dp", "fsdp"), scatter_dimension=0, tiled=True),
        lax.psum_scatter(term_bi, ("dp", "fsdp"), scatter_dimension=0, tiled=True),
        lax.psum_scatter(term_g2, ("dp", "fsdp"), scatter_dimension=0, tiled=True),
        lax.psum_scatter(term_b2, ("dp", "fsdp"), scatter_dimension=0, tiled=True),
        lax.psum_scatter(term_wc, ("dp", "fsdp"), scatter_dimension=1, tiled=True),
        lax.psum_scatter(term_bc, ("dp", "fsdp"), scatter_dimension=0, tiled=True),
        lax.psum_scatter(term_g3, ("dp", "fsdp"), scatter_dimension=0, tiled=True),
        lax.psum_scatter(term_b3, ("dp", "fsdp"), scatter_dimension=0, tiled=True),
        lax.psum_scatter(term_wo, ("dp", "fsdp"), scatter_dimension=0, tiled=True),
        lax.psum_scatter(term_bo, ("dp", "fsdp"), scatter_dimension=0, tiled=True),
    )


def dilate(padded, kernel, length_pad):
    total = jnp.zeros((padded.shape[0], length_pad, kernel.shape[2]), jnp.float32)
    for kernel_tap in range(kernel.shape[0]):
        window = padded[:, kernel_tap * DILATION : kernel_tap * DILATION + length_pad]
        total = total + jnp.einsum(
            "pli,io->plo", window, kernel[kernel_tap], preferred_element_type=jnp.float32
        )
    return total


def plain_body(
    tokens,
    out_grad,
    lengths,
    ln1_gain,
    ln1_bias,
    w_in,
    b_in,
    ln2_gain,
    ln2_bias,
    w_conv,
    b_conv,
    ln3_gain,
    ln3_bias,
    w_out,
    b_out,
):
    proteins, length_pad, width = tokens.shape
    row_count = proteins * length_pad
    reach = KSIZE // 2 * DILATION
    positions = lax.broadcasted_iota(jnp.int32, (proteins, length_pad), 1)
    live = (positions < lengths[:, None]).astype(jnp.float32).reshape(row_count, 1)
    full = collect(
        ln1_gain,
        ln1_bias,
        w_in,
        b_in,
        ln2_gain,
        ln2_bias,
        w_conv,
        b_conv,
        ln3_gain,
        ln3_bias,
        w_out,
        b_out,
    )
    (
        gain_one,
        bias_one,
        first_matrix,
        first_bias,
        gain_two,
        bias_two,
        conv_kernel,
        conv_bias,
        gain_three,
        bias_three,
        last_matrix,
        last_bias,
    ) = full
    inner = first_matrix.shape[1]
    row_tokens = tokens.reshape(row_count, width).astype(jnp.float32)
    act_one, pull_one = jax.vjp(
        norm_gelu, row_tokens, gain_one.astype(jnp.float32), bias_one.astype(jnp.float32)
    )
    inner_one = act_one.astype(jnp.bfloat16)
    hidden_one = jnp.dot(
        inner_one, first_matrix, preferred_element_type=jnp.float32
    ) + first_bias.astype(jnp.float32)
    act_two, pull_two = jax.vjp(
        norm_gelu, hidden_one, gain_two.astype(jnp.float32), bias_two.astype(jnp.float32)
    )
    inner_two = (act_two * live).astype(jnp.bfloat16)
    padded_two = jnp.pad(
        inner_two.reshape(proteins, length_pad, inner), ((0, 0), (reach, reach), (0, 0))
    )
    hidden_two = dilate(padded_two, conv_kernel, length_pad).reshape(
        row_count, inner
    ) + conv_bias.astype(jnp.float32)
    act_three, pull_three = jax.vjp(
        norm_gelu, hidden_two, gain_three.astype(jnp.float32), bias_three.astype(jnp.float32)
    )
    inner_three = act_three.astype(jnp.bfloat16)
    branch = jnp.dot(
        inner_three, last_matrix, preferred_element_type=jnp.float32
    ) + last_bias.astype(jnp.float32)
    result = (row_tokens + live * branch).astype(jnp.bfloat16).reshape(proteins, length_pad, width)
    again = collect(
        ln1_gain,
        ln1_bias,
        w_in,
        b_in,
        ln2_gain,
        ln2_bias,
        w_conv,
        b_conv,
        ln3_gain,
        ln3_bias,
        w_out,
        b_out,
    )
    (
        again_g1,
        again_b1,
        back_first,
        again_bi,
        again_g2,
        again_b2,
        back_kernel,
        again_bc,
        again_g3,
        again_b3,
        back_last,
        again_bo,
    ) = again
    pull_one = jax.vjp(
        norm_gelu, row_tokens, again_g1.astype(jnp.float32), again_b1.astype(jnp.float32)
    )[1]
    pull_two = jax.vjp(
        norm_gelu, hidden_one, again_g2.astype(jnp.float32), again_b2.astype(jnp.float32)
    )[1]
    pull_three = jax.vjp(
        norm_gelu, hidden_two, again_g3.astype(jnp.float32), again_b3.astype(jnp.float32)
    )[1]
    grad_rows = out_grad.reshape(row_count, width)
    grad_branch = grad_rows * live.astype(jnp.bfloat16)
    term_wo = jnp.einsum("ri,rd->id", inner_three, grad_branch, preferred_element_type=jnp.float32)
    term_bo = jnp.sum(grad_branch.astype(jnp.float32), axis=0)
    grad_three = jnp.einsum("rd,id->ri", grad_branch, back_last, preferred_element_type=jnp.float32)
    d_hidden_two, term_g3, term_b3 = pull_three(grad_three)
    low_two = d_hidden_two.astype(jnp.bfloat16)
    term_bc = jnp.sum(low_two.astype(jnp.float32), axis=0)
    padded_grad = jnp.pad(
        low_two.reshape(proteins, length_pad, inner), ((0, 0), (reach, reach), (0, 0))
    )
    grad_view = low_two.reshape(proteins, length_pad, inner)
    kernel_terms = []
    grad_two = jnp.zeros((proteins, length_pad, inner), jnp.float32)
    taps = back_kernel.shape[0]
    for kernel_tap in range(taps):
        window = padded_two[:, kernel_tap * DILATION : kernel_tap * DILATION + length_pad]
        kernel_terms.append(
            jnp.einsum("pli,plo->io", window, grad_view, preferred_element_type=jnp.float32)
        )
        mirror = (taps - 1 - kernel_tap) * DILATION
        grad_window = padded_grad[:, mirror : mirror + length_pad]
        grad_two = grad_two + jnp.einsum(
            "plo,io->pli", grad_window, back_kernel[kernel_tap], preferred_element_type=jnp.float32
        )
    term_wc = jnp.stack(kernel_terms, axis=0)
    grad_two = grad_two.reshape(row_count, inner) * live
    d_hidden_one, term_g2, term_b2 = pull_two(grad_two)
    low_one = d_hidden_one.astype(jnp.bfloat16)
    term_wi = jnp.einsum("rd,ri->di", inner_one, low_one, preferred_element_type=jnp.float32)
    term_bi = jnp.sum(low_one.astype(jnp.float32), axis=0)
    grad_one = jnp.einsum("ri,di->rd", low_one, back_first, preferred_element_type=jnp.float32)
    d_tokens, term_g1, term_b1 = pull_one(grad_one)
    grad_tokens = (
        (grad_rows.astype(jnp.float32) + d_tokens)
        .astype(jnp.bfloat16)
        .reshape(proteins, length_pad, width)
    )
    owned = spread(
        term_g1,
        term_b1,
        term_wi,
        term_bi,
        term_g2,
        term_b2,
        term_wc,
        term_bc,
        term_g3,
        term_b3,
        term_wo,
        term_bo,
    )
    return (
        result,
        grad_tokens,
        owned[0],
        owned[1],
        owned[2],
        owned[3],
        owned[4],
        owned[5],
        owned[6],
        owned[7],
        owned[8],
        owned[9],
        owned[10],
        owned[11],
    )


def solution(mesh):
    both = ("dp", "fsdp")
    by_row = P(both)
    in_specs = (
        P(both, None, None), P(both, None, None), by_row, by_row, by_row, P(both, None), by_row, by_row, by_row,
        P(None, both, None), by_row, by_row, by_row, P(both, None), by_row,
    )
    out_specs = (
        P(both, None, None), P(both, None, None), by_row, by_row, P(both, None), by_row, by_row, by_row,
        P(None, both, None), by_row, by_row, by_row, P(both, None), by_row,
    )
    body = kernel_body if (mesh.shape["dp"], mesh.shape["fsdp"]) == (8, 4) else plain_body
    return jax.shard_map(body, mesh=mesh, in_specs=in_specs, out_specs=out_specs, check_vma=False)
```

```python
import functools
import itertools

import jax
import jax.numpy as jnp
from jax import lax
from jax.experimental import pallas as pl
from jax.experimental.pallas import tpu as pltpu
from jax.sharding import PartitionSpec as P

KSIZE = 5
DILATION = 8
EPS = 1e-05
HALF_ROOT = 0.7071067811865476
PHI_SCALE = 0.3989422804014327
F32 = jnp.float32
BF16 = jnp.bfloat16
MESH = pl.DeviceIdType.MESH
VMEM_BYTES = 62 * 2**20
HBM = pl.BlockSpec(memory_space=pl.ANY)
LEVELS = 4
CHIPS = 16
DEVICES = 32
TILE = 256
CONV_COLS = ((0, 384), (384, 256))
OUT_COLS = ((0, 384), (384, 896))
WIDE_OFFSETS = (0, 40, 80)
SLIM_OFFSETS = (0, 20, 40, 60, 80, 100)


def place():
    dp = lax.axis_index("dp")
    fs = lax.axis_index("fsdp")
    return lax.div(dp, 2), lax.rem(dp, 2), lax.div(fs, 2), lax.rem(fs, 2)


def device(z, y, x, core):
    return (z * 2 + y, x * 2 + core)


def chip(z, y, x):
    return (z * 2 + y) * 2 + x


def peer_of(step):
    mine = lax.axis_index("dp") * 4 + lax.axis_index("fsdp")
    other = lax.rem(mine + step, DEVICES)
    return mine, other, (lax.div(other, 4), lax.rem(other, 4))


def greet_all():
    barrier = pltpu.get_barrier_semaphore()

    def greet(step, _):
        _, _, target = peer_of(step)
        pl.semaphore_signal(barrier, inc=1, device_id=target, device_id_type=MESH)
        return 0

    lax.fori_loop(1, DEVICES, greet, 0)
    pl.semaphore_wait(barrier, DEVICES - 1)


def chunk_masks(width, chunk):
    scale = -(-65536 // chunk)
    column = lax.broadcasted_iota(jnp.int32, (DEVICES, width), 1)
    row = lax.broadcasted_iota(jnp.int32, (DEVICES, width), 0)
    owner = lax.shift_right_logical(column * scale, 16) == row
    place_col = lax.broadcasted_iota(jnp.int32, (128, width), 1)
    place_row = lax.broadcasted_iota(jnp.int32, (128, width), 0)
    slot = place_col - lax.shift_right_logical(place_col * scale, 16) * chunk
    return owner, slot, place_row


def unpack_vectors(packed_ref, vectors_ref):
    for plane, (width, chunk, offsets) in enumerate(
        ((1280, 40, WIDE_OFFSETS), (640, 20, SLIM_OFFSETS))
    ):
        owner, slot, row = chunk_masks(width, chunk)
        packed = packed_ref[:, plane, :].astype(BF16)
        for index, offset in enumerate(offsets):
            pick = (slot + offset == row).astype(F32).astype(BF16)
            spread = jnp.dot(packed, pick, preferred_element_type=F32)
            line = jnp.sum(jnp.where(owner, spread, 0.0), axis=0, keepdims=True)
            vectors_ref[pl.ds(plane * 3 + index, 1), pl.ds(0, width)] = line


def lanes(column, width):
    return jnp.concatenate([column] * (width // 128), axis=1)


def norm_parts(values):
    width = values.shape[1]
    mean = jnp.sum(values, axis=1, keepdims=True) * (1.0 / width)
    center = values - mean
    var = jnp.sum(center * center, axis=1, keepdims=True) * (1.0 / width)
    scale = lax.rsqrt(var + EPS)
    return center * scale, scale


def gelu_parts(arg):
    normal = 0.5 + 0.5 * lax.erf(arg * HALF_ROOT)
    slope = normal + arg * (PHI_SCALE * jnp.exp(-0.5 * (arg * arg)))
    return arg * normal, slope


PART_COUNT = 4
CONV_TAPS = {1: (0, 3), 2: (3, 2)}
BY_Y = (False, True, False, True)
PLANE_FIRST = (False, False, False, True)
KINDS = ("own", "x", "y", "far")
GATHER_PLAN = (
    (
        ("vec_begin",), ("send", 0), ("begin",), ("assemble",), ("send", 3), ("vec_plane",), ("y", 0, 0),
        ("own", 0, 1), ("send", 1), ("vec_pass", 1), ("own", 0, 2), ("send", 2), ("vec_pass", 2), ("y", 3, 0),
        ("x", 3, 0), ("x", 0, 0), ("own", 1, 1), ("own", 0, 3), ("share", "own", 0), ("y", 0, 1), ("vec_pass", 3),
        ("vectors",), ("x", 1, 0), ("x", 0, 1),
    ),
    (),
    (
        ("y", 0, 2), ("own", 2, 1), ("far", 3, 0),
    ),
    (),
    (
        ("y", 0, 3), ("share", "y", 0), ("x", 0, 2), ("own", 1, 2), ("y", 1, 0), ("y", 3, 1),
    ),
    (
        ("own", 2, 2), ("x", 3, 1), ("x", 2, 0),
    ),
    (),
    (
        ("y", 2, 0), ("own", 3, 1), ("x", 1, 1),
    ),
    (
        ("far", 3, 1), ("far", 0, 1), ("y", 1, 1), ("x", 0, 3), ("share", "x", 0), ("far", 0, 2), ("far", 0, 0),
        ("own", 1, 3), ("share", "own", 1), ("far", 0, 3), ("share", "far", 0), ("far", 1, 0), ("y", 2, 1),
        ("y", 3, 2), ("w_in",),
    ),
    (
        ("own", 2, 3), ("share", "own", 2),
    ),
    (),
    (
        ("x", 3, 2), ("x", 1, 2),
    ),
    (
        ("x", 2, 1), ("y", 1, 2), ("y", 2, 2), ("own", 3, 2), ("far", 3, 2), ("x", 1, 3), ("share", "x", 1),
        ("x", 2, 2), ("y", 2, 3), ("share", "y", 2),
    ),
    (),
    (
        ("y", 1, 3), ("share", "y", 1), ("far", 2, 0),
    ),
    (
        ("far", 1, 1), ("x", 2, 3), ("share", "x", 2),
    ),
    (
        ("y", 3, 3), ("share", "y", 3), ("far", 2, 1), ("own", 3, 3), ("share", "own", 3), ("far", 1, 2), ("x", 3, 3),
        ("share", "x", 3), ("far", 1, 3), ("share", "far", 1), ("far", 2, 2), ("far", 2, 3), ("share", "far", 2),
        ("far", 3, 3), ("share", "far", 3), ("finish",),
    ),
)


def plane_peer(offset):
    z, y, x, core = place()
    other = lax.rem(y * 4 + x * 2 + core + offset, 8)
    return other, (z * 2 + lax.div(other, 4), lax.rem(other, 4))


def greet_near(z, y, x, core):
    barrier = pltpu.get_barrier_semaphore()

    def greet(target):
        pl.semaphore_signal(barrier, inc=1, device_id=target, device_id_type=MESH)

    for offset in range(1, 8):
        greet(plane_peer(offset)[1])
    pl.when(z > 0)(lambda: greet(device(z - 1, y, x, core)))
    pl.when(z < LEVELS - 1)(lambda: greet(device(z + 1, y, x, core)))
    pl.semaphore_wait(barrier, 7 + (z > 0).astype(jnp.int32) + (z < LEVELS - 1).astype(jnp.int32))


def each_level(z, distance, act):
    if distance == 0:
        act(z, 0)
        return
    pl.when(z + distance < LEVELS)(lambda: act(z + distance, 1))
    pl.when(z - distance >= 0)(lambda: act(z - distance, -1))


def gather_kernel(
    tokens_hbm, vec, w_in, w_conv, w_out,
    u1_hbm, slope1_hbm, xh1_hbm, scale1_hbm, xh2_hbm, slope2_hbm, scale2_hbm, u2_hbm, vectors_out,
    in_full, conv_full, out_full,
    packed, in_vmem, conv_twin, out_twin, conv_own, out_own,
    tokens, u1, slope1, xh1, scale1, xh2, slope2, scale2, u2, token_sem, store_sem,
    vec_send, vec_recv, link_send, link_recv, twin_recv, pair_send, pair_recv, own_sem, load_sem,
):
    z, y, x, core = place()
    here = 2 * y + x
    steps = 2048 // TILE
    columns = {"own": here, "x": 2 * y + (1 - x), "y": 2 * (1 - y) + x, "far": 2 * (1 - y) + (1 - x)}

    def piece(part, level, column, side):
        if part == 0:
            return in_vmem.at[pl.ds(pl.multiple_of((level * 4 + column) * 80 + side * 40, 8), 40), :]
        if part in CONV_TAPS:
            return conv_full.at[pl.ds(*CONV_TAPS[part]), level, column, :, pl.ds(*CONV_COLS[side])]
        return out_full.at[level, column, :, pl.ds(*OUT_COLS[side])]

    def pieces(part, column, side):
        if part in CONV_TAPS:
            return conv_full.at[pl.ds(*CONV_TAPS[part]), :, column, :, pl.ds(*CONV_COLS[side])]
        return out_full.at[:, column, :, pl.ds(*OUT_COLS[side])]

    def span(part, side, count):
        if part == 0:
            return in_vmem.at[pl.ds(0, 40 * count), :]
        rows, columns_ = (LEVELS, count // LEVELS) if count % LEVELS == 0 else (count, 1)
        if part in CONV_TAPS:
            return conv_full.at[
                pl.ds(*CONV_TAPS[part]), pl.ds(0, rows), pl.ds(0, columns_), :, pl.ds(*CONV_COLS[side])
            ]
        return out_full.at[pl.ds(0, rows), pl.ds(0, columns_), :, pl.ds(*OUT_COLS[side])]

    def own_piece(part, side):
        if part == 0:
            return w_in
        if part in CONV_TAPS:
            return conv_own.at[pl.ds(*CONV_TAPS[part]), :, pl.ds(*CONV_COLS[side])]
        return out_own.at[:, pl.ds(*OUT_COLS[side])]

    def target(link, side):
        return (
            device(z, y, 1 - x, side),
            device(z, 1 - y, x, side),
            device(z + 1, y, x, side),
            device(z - 1, y, x, side),
            device(z, y, x, 1 - side),
        )[link]

    def remote(src, dst, send_sem, recv_sem, where):
        return pltpu.make_async_remote_copy(
            src_ref=src, dst_ref=dst, send_sem=send_sem, recv_sem=recv_sem, device_id=where, device_id_type=MESH
        )

    def wait_sent(side, part, link, count):
        view = span(part, side, count)
        remote(view, view, link_send.at[link, part], twin_recv.at[0, part], target(4, side)).wait_send()

    def guarded(link, act):
        if link == 2:
            pl.when(z < LEVELS - 1)(act)
        elif link == 3:
            pl.when(z > 0)(act)
        else:
            act()

    def forward(side, part, level, column, links, own=False):
        place_ref = piece(part, level, column, side)
        for link in links:

            def act(link=link):
                remote(
                    own_piece(part, side) if own else place_ref, place_ref,
                    link_send.at[link, part], link_recv.at[level, column, part], target(link, side),
                ).start()

            guarded(link, act)

    def pass_on(side, kind, part, distance):
        def act(level, sign):
            column = columns[kind]
            place_ref = piece(part, level, column, side)
            remote(
                place_ref, place_ref, link_send.at[4, part], link_recv.at[level, column, part], target(4, side)
            ).wait_recv()
            along = {1: (3,), -1: (2,), 0: (2, 3)}[sign]
            links = ()
            if kind == "own":
                links = along if PLANE_FIRST[part] else along + (0, 1)
            else:
                if kind == "x" and BY_Y[part] and (distance == 0 or not PLANE_FIRST[part]):
                    links += (1,)
                if kind == "y" and not BY_Y[part] and (distance == 0 or not PLANE_FIRST[part]):
                    links += (0,)
                if PLANE_FIRST[part]:
                    links += along
            forward(side, part, level, column, links)

        each_level(z, distance, act)

    def own_sends(side, part):
        forward(side, part, z, here, (0, 1, 2, 3), own=True)

    def twin_copy(side, kind, part, level=None):
        if level is None:
            view = pieces(part, columns[kind], side)
        else:
            view = piece(part, level, columns[kind], side)
        return remote(view, view, link_send.at[4, part], twin_recv.at[KINDS.index(kind), part], target(4, side))

    def share(side, kind, part):
        if kind == "own":
            own_copy(side, part).wait()
        if part:
            twin_copy(side, kind, part).start()
        else:
            for level in range(LEVELS):
                twin_copy(side, kind, part, level).start()

    def take_twin(side, part):
        for kind in KINDS:
            if part:
                twin_copy(1 - side, kind, part).wait_recv()
            else:
                view = span(part, side, LEVELS)
                remote(
                    view, view, link_send.at[4, part], twin_recv.at[KINDS.index(kind), part], target(4, side)
                ).wait_recv()

    def pair_copies(side):
        return [
            remote(src, dst, pair_send.at[index], pair_recv.at[index], target(4, side))
            for index, (src, dst) in enumerate(((w_conv, conv_twin), (w_out, out_twin)))
        ]

    def own_copy(side, part):
        return pltpu.make_async_copy(own_piece(part, side), piece(part, z, here, side), own_sem.at[part])

    def vec_copy(offset):
        mine = z * 8 + y * 4 + x * 2 + core
        return remote(vec, packed.at[mine], vec_send.at[0], vec_recv.at[0], plane_peer(offset)[1])

    def level_rows(level):
        return packed.at[pl.ds(pl.multiple_of(level * 8, 8), 8)]

    def vec_line(side, level, link):
        rows = level_rows(level)
        return remote(rows, rows, vec_send.at[link - 1], vec_recv.at[1 + level], target(link, side))

    def vec_begin(side):
        for offset in range(1, 8):
            vec_copy(offset).start()
        packed[pl.ds(z * 8 + y * 4 + x * 2 + side, 1)] = vec[...][None]

    def vec_plane(side):
        rows = packed.at[pl.ds(0, 7)]
        remote(rows, rows, vec_send.at[0], vec_recv.at[0], target(4, side)).wait()
        for link in (2, 3):
            guarded(link, lambda link=link: vec_line(side, z, link).start())

    def vec_pass(side, distance):
        def act(level, sign):
            link = 3 if sign > 0 else 2
            vec_line(side, level, link).wait_recv()
            guarded(link, lambda: vec_line(side, level, link).start())

        each_level(z, distance, act)

    def vec_finish(side):
        for level in range(LEVELS):

            @pl.when(z == level)
            def _(level=level):
                for link, count in ((2, level + 1 if level < LEVELS - 1 else 0), (3, LEVELS - level if level else 0)):
                    if count:
                        rows = packed.at[pl.ds(0, 8 * count)]
                        remote(rows, rows, vec_send.at[link - 1], vec_recv.at[0], target(4, side)).wait_send()

    def begin(side):
        own_copy(side, 0).start()
        for copy in pair_copies(side):
            copy.start()

    def assemble(side):
        for copy in pair_copies(side):
            copy.wait()
        first_conv, second_conv = (w_conv, conv_twin) if side == 0 else (conv_twin, w_conv)
        first_out, second_out = (w_out, out_twin) if side == 0 else (out_twin, w_out)
        conv_own[...] = jnp.concatenate(
            [first_conv[...].astype(F32), second_conv[...].astype(F32)], axis=1
        ).astype(BF16)
        out_own[...] = jnp.concatenate(
            [first_out[...].astype(F32), second_out[...].astype(F32)], axis=0
        ).astype(BF16)
        for part in range(1, PART_COUNT):
            own_copy(side, part).start()

    def save_in():
        return pltpu.make_async_copy(in_vmem, in_full, load_sem.at[0])

    def take_in(side):
        take_twin(side, 0)
        save_in().start()

    def finish(side):
        vec_finish(side)
        for part in range(1, PART_COUNT):
            take_twin(side, part)
        for part in range(PART_COUNT):
            plane, along = (1, 4) if PLANE_FIRST[part] else (4, 1)
            wait_sent(side, part, 0, plane if BY_Y[part] else 2 * plane)
            wait_sent(side, part, 1, 2 * plane if BY_Y[part] else plane)
            wait_sent(side, part, 4, CHIPS)
            for level in range(LEVELS):

                @pl.when(z == level)
                def _(part=part, along=along, level=level):
                    if level < LEVELS - 1:
                        wait_sent(side, part, 2, along * (level + 1))
                    if level > 0:
                        wait_sent(side, part, 3, along * (LEVELS - level))

        save_in().wait()

    actions = {
        "send": own_sends, "begin": begin, "assemble": assemble, "w_in": take_in, "finish": finish,
        "vec_begin": vec_begin, "vec_plane": vec_plane, "vec_pass": vec_pass,
        "vectors": lambda side: unpack_vectors(packed, vectors_out),
        "share": share,
    }

    def perform(events):
        for side in range(2):

            @pl.when(core == side)
            def _(side=side):
                for event in events:
                    if event[0] in actions:
                        actions[event[0]](side, *event[1:])
                    else:
                        pass_on(side, *event)

    def rows_of(tile, count=1):
        return pl.ds(pl.multiple_of(tile * TILE, TILE), count * TILE)

    def token_load(tile):
        return pltpu.make_async_copy(tokens_hbm.at[rows_of(tile), :], tokens.at[rows_of(tile), :], token_sem.at[tile])

    first = ((u1, u1_hbm), (slope1, slope1_hbm), (xh1, xh1_hbm), (scale1, scale1_hbm))
    second = ((u2, u2_hbm), (xh2, xh2_hbm), (slope2, slope2_hbm), (scale2, scale2_hbm))

    def stores(pairs, phase, half):
        rows = rows_of(half * (steps // 2), steps // 2)
        return [
            pltpu.make_async_copy(src.at[rows, :], dst.at[rows, :], store_sem.at[phase, half, index])
            for index, (src, dst) in enumerate(pairs)
        ]

    def start_stores(pairs, phase, half):
        for copy in stores(pairs, phase, half):
            copy.start()

    greet_near(z, y, x, core)
    for tile in range(steps):
        token_load(tile).start()

    def wide_tile(tile, _):
        for index in range(steps):
            if GATHER_PLAN[index]:
                pl.when(tile == index)(functools.partial(perform, GATHER_PLAN[index]))
        token_load(tile).wait()
        rows = rows_of(tile)
        gain, bias = vectors_out[pl.ds(0, 1), :], vectors_out[pl.ds(1, 1), :]
        norm, scale = norm_parts(tokens[rows, :].astype(F32))
        act, slope = gelu_parts(norm * gain + bias)
        u1[rows, :] = act.astype(BF16)
        slope1[rows, :] = slope.astype(BF16)
        xh1[rows, :] = norm.astype(BF16)
        scale1[rows, :] = jnp.broadcast_to(scale, (TILE, 128))
        return 0

    lax.fori_loop(0, steps, wide_tile, 0)

    def slim_tile(tile, _):
        for index in range(steps):
            events = GATHER_PLAN[steps + index]
            if index == 0:
                pl.when(tile == 0)(lambda: start_stores(first, 0, 0))
                pl.when(tile == 0)(lambda: start_stores(first, 0, 1))
            if index == steps // 2:
                pl.when(tile == index)(lambda: start_stores(second, 1, 0))
            if events:
                pl.when(tile == index)(functools.partial(perform, events))
        rows = rows_of(tile)
        hidden = jnp.dot(u1[rows, :], in_vmem[...], preferred_element_type=F32)
        hidden = hidden + vectors_out[pl.ds(3, 1), pl.ds(0, 640)]
        norm, scale = norm_parts(hidden)
        act, slope = gelu_parts(norm * vectors_out[pl.ds(4, 1), pl.ds(0, 640)] + vectors_out[pl.ds(5, 1), pl.ds(0, 640)])
        u2[rows, :] = act.astype(BF16)
        slope2[rows, :] = slope.astype(BF16)
        xh2[rows, :] = norm.astype(BF16)
        scale2[rows, :] = jnp.broadcast_to(scale, (TILE, 128))
        return 0

    lax.fori_loop(0, steps, slim_tile, 0)
    start_stores(second, 1, 1)
    perform(GATHER_PLAN[2 * steps])
    for phase, pairs in enumerate((first, second)):
        for half in range(2):
            for copy in stores(pairs, phase, half):
                copy.wait()


def gather_stage(tokens, vec, w_in, w_conv, w_out):
    rows = tokens.shape[0]
    shape = jax.ShapeDtypeStruct
    vmem = pl.BlockSpec(memory_space=pltpu.VMEM)
    wide, slim, column = (rows, 1280), (rows, 640), (rows, 128)
    *results, conv_full, out_full = pl.pallas_call(
        gather_kernel,
        in_specs=[HBM] + [vmem] * 4,
        out_specs=[HBM] * 8 + [vmem] + [HBM] * 3,
        out_shape=[
            shape(wide, BF16), shape(wide, BF16), shape(wide, BF16), shape(column, F32),
            shape(slim, BF16), shape(slim, BF16), shape(column, F32), shape(slim, BF16),
            shape((16, 1280), F32),
            shape((1280, 640), BF16), shape((KSIZE, LEVELS, 4, 40, 640), BF16), shape((LEVELS, 4, 40, 1280), BF16),
        ],
        scratch_shapes=[
            pltpu.VMEM((DEVICES, 2, 128), F32),
            pltpu.VMEM((1280, 640), BF16),
            pltpu.VMEM((KSIZE, 20, 640), BF16),
            pltpu.VMEM((20, 1280), BF16),
            pltpu.VMEM((KSIZE, 40, 640), BF16),
            pltpu.VMEM((40, 1280), BF16),
            pltpu.VMEM(wide, BF16),
            pltpu.VMEM(wide, BF16),
            pltpu.VMEM(wide, BF16),
            pltpu.VMEM(wide, BF16),
            pltpu.VMEM(column, F32),
            pltpu.VMEM(slim, BF16),
            pltpu.VMEM(slim, BF16),
            pltpu.VMEM(column, F32),
            pltpu.VMEM(slim, BF16),
            pltpu.SemaphoreType.DMA((rows // TILE,)),
            pltpu.SemaphoreType.DMA((2, 2, 4)),
            pltpu.SemaphoreType.DMA((3,)),
            pltpu.SemaphoreType.DMA((1 + LEVELS,)),
            pltpu.SemaphoreType.DMA((5, PART_COUNT)),
            pltpu.SemaphoreType.DMA((LEVELS, 4, PART_COUNT)),
            pltpu.SemaphoreType.DMA((4, PART_COUNT)),
            pltpu.SemaphoreType.DMA((2,)),
            pltpu.SemaphoreType.DMA((2,)),
            pltpu.SemaphoreType.DMA((PART_COUNT,)),
            pltpu.SemaphoreType.DMA((1,)),
        ],
        compiler_params=pltpu.CompilerParams(
            collective_id=0, has_side_effects=True, vmem_limit_bytes=VMEM_BYTES,
        ),
        name="gather_stage",
    )(tokens, vec, w_in, w_conv, w_out)
    return *results, conv_full.reshape(KSIZE, 640, 640), out_full.reshape(640, 1280)


def pack_vectors(ln1_gain, ln1_bias, b_in, ln2_gain, ln2_bias, b_conv, ln3_gain, ln3_bias, b_out):
    total = None
    for plane, pieces in enumerate(
        (
            zip((ln1_gain, ln1_bias, b_out), WIDE_OFFSETS),
            zip((b_in, ln2_gain, ln2_bias, b_conv, ln3_gain, ln3_bias), SLIM_OFFSETS),
        )
    ):
        for piece, offset in pieces:
            line = piece.astype(F32)[None]
            placed = lax.pad(line, jnp.float32(0), ((plane, 1 - plane, 0), (offset, 128 - offset - piece.shape[0], 0)))
            total = placed if total is None else total + placed
    return total


PAD = 32
SPAN = 1024 + 2 * PAD


def middle_kernel(
    lengths, vectors, u2_hbm, xh2_hbm, slope2_hbm, scale2_hbm, grads_hbm, tokens_hbm, conv_hbm, last_hbm,
    out_hbm, dh1_hbm, d_conv_hbm, d_last_hbm, sums_out,
    conv, conv_t, last, last_t, u2, dh2, grads, tokens, xh2, slope2, scale2, dh1, d_conv, d_last, zeros,
    u2_sem, row_sem, back_sem, weight_sem, out_sem, dh1_sem, flush_sem,
):
    proteins = 2
    tiles = 1024 // TILE
    wide, slim = 1280, 640

    def tile_count(protein):
        return lax.div(lengths[protein] + TILE - 1, TILE)

    def rows_of(protein, tile):
        return pl.ds(pl.multiple_of(protein * 1024 + tile * TILE, TILE), TILE)

    def padded(protein, tile, shift=0):
        return pl.ds(pl.multiple_of(protein * SPAN + PAD + tile * TILE, 8) + shift, TILE)

    def u2_load(protein, tile):
        return pltpu.make_async_copy(
            u2_hbm.at[rows_of(protein, tile), :], u2.at[padded(protein, tile), :], u2_sem.at[protein, tile]
        )

    def row_loads(protein, tile):
        rows = rows_of(protein, tile)
        return [
            pltpu.make_async_copy(grads_hbm.at[rows, :], grads.at[rows, :], row_sem.at[0, protein, tile]),
            pltpu.make_async_copy(tokens_hbm.at[rows, :], tokens.at[rows, :], row_sem.at[1, protein, tile]),
        ]

    def back_loads(protein, tile):
        rows = rows_of(protein, tile)
        return [
            pltpu.make_async_copy(xh2_hbm.at[rows, :], xh2.at[rows, :], back_sem.at[0, protein, tile]),
            pltpu.make_async_copy(slope2_hbm.at[rows, :], slope2.at[rows, :], back_sem.at[1, protein, tile]),
            pltpu.make_async_copy(scale2_hbm.at[rows, :], scale2.at[rows, :], back_sem.at[2, protein, tile]),
        ]

    def out_store(protein, tile):
        rows = rows_of(protein, tile)
        return pltpu.make_async_copy(tokens.at[rows, :], out_hbm.at[rows, :], out_sem.at[protein, tile])

    def dh1_store(protein, tile, source):
        return pltpu.make_async_copy(source, dh1_hbm.at[rows_of(protein, tile), :], dh1_sem.at[protein, tile])

    conv_load = pltpu.make_async_copy(conv_hbm, conv, weight_sem.at[0])
    last_load = pltpu.make_async_copy(last_hbm, last, weight_sem.at[1])

    def each_tile(protein, act):
        def step(tile, _):
            act(protein, tile)
            return 0

        lax.fori_loop(0, tile_count(protein), step, 0)

    def start_all(copies):
        for copy in copies:
            copy.start()

    each_tile(0, lambda p, t: u2_load(p, t).start())
    conv_load.start()
    last_load.start()

    def load_rows(protein, _):
        pl.when(protein > 0)(lambda: each_tile(protein, lambda p, t: u2_load(p, t).start()))
        each_tile(protein, lambda p, t: start_all(row_loads(p, t)))
        return 0

    def load_back(protein, _):
        each_tile(protein, lambda p, t: start_all(back_loads(p, t)))
        return 0

    lax.fori_loop(0, proteins, load_rows, 0)
    lax.fori_loop(0, proteins, load_back, 0)
    zeros[...] = jnp.zeros_like(zeros)
    for protein in range(proteins):

        def dead_load(tile, _, protein=protein):
            row_loads(protein, tile)[1].start()
            dh1_store(protein, tile, zeros).start()
            return 0

        lax.fori_loop(tile_count(protein), tiles, dead_load, 0)

    sums_out[...] = jnp.zeros_like(sums_out)

    def clear(index, _):
        rows = pl.ds(pl.multiple_of(index * 64, 64), 64)
        d_last[rows, :] = jnp.zeros((64, wide), F32)
        for tap in range(KSIZE):
            d_conv[tap, rows, :] = jnp.zeros((64, slim), F32)
        return 0

    lax.fori_loop(0, slim // 64, clear, 0)

    def vector(index, width=slim):
        return vectors[pl.ds(index, 1), pl.ds(0, width)]

    def add_sum(index, values):
        width = values.shape[1]
        sums_out[pl.ds(index * 8, 8), pl.ds(0, width)] += jnp.sum(
            values.reshape(values.shape[0] // 8, 8, width), axis=0
        )

    def live_rows(protein, tile):
        position = lax.broadcasted_iota(jnp.int32, (TILE, 128), 0) + tile * TILE
        return (position < lengths[protein]).astype(F32)

    edge = jnp.zeros((PAD, slim), BF16)
    def one_protein(protein, _):
        base = pl.multiple_of(protein * SPAN, 8)
        u2[pl.ds(base, PAD), :] = edge
        dh2[pl.ds(base, PAD), :] = edge

        def prepare(tile, _):
            u2_load(protein, tile).wait()
            return 0

        count = tile_count(protein)
        lax.fori_loop(0, count, prepare, 0)
        last_tile = count - 1
        u2[padded(protein, last_tile), :] = (
            u2[padded(protein, last_tile), :].astype(F32) * lanes(live_rows(protein, last_tile), slim)
        ).astype(BF16)
        after = pl.ds(pl.multiple_of(base + PAD + count * TILE, 8), PAD)
        u2[after, :] = edge
        dh2[after, :] = edge

        @pl.when(protein == 0)
        def _():
            conv_load.wait()
            last_load.wait()
            last_t[...] = last[...].T

            def turn(tap, _):
                conv_t[tap] = conv[tap].T
                return 0

            lax.fori_loop(0, KSIZE, turn, 0)

        def forward(tile, _):
            for copy in row_loads(protein, tile):
                copy.wait()
            rows = rows_of(protein, tile)
            live = live_rows(protein, tile)
            hidden = jnp.dot(u2[padded(protein, tile, -16), :], conv[0], preferred_element_type=F32)
            for tap in range(1, KSIZE):
                hidden += jnp.dot(
                    u2[padded(protein, tile, (tap - 2) * DILATION), :], conv[tap], preferred_element_type=F32
                )
            gz = (grads[rows, :].astype(F32) * lanes(live, wide)).astype(BF16)
            back = jnp.dot(gz, last_t[...], preferred_element_type=F32)
            norm, scale = norm_parts(hidden + vector(6))
            act, slope = gelu_parts(norm * vector(7) + vector(8))
            u3 = act.astype(BF16)
            branch = jnp.dot(u3, last[...], preferred_element_type=F32) + vector(2, wide)
            tokens[rows, :] = (tokens[rows, :].astype(F32) + lanes(live, wide) * branch).astype(BF16)
            out_store(protein, tile).start()
            d_last[...] += lax.dot_general(u3, gz, (((0,), (0,)), ((), ())), preferred_element_type=F32)
            add_sum(2, gz.astype(F32))
            slope_grad = back * slope
            add_sum(7, slope_grad * norm)
            add_sum(8, slope_grad)
            err = slope_grad * vector(7)
            mean = jnp.sum(err, axis=1, keepdims=True) * (1.0 / slim)
            along = jnp.sum(err * norm, axis=1, keepdims=True) * (1.0 / slim)
            low = (scale * (err - mean - norm * along)).astype(BF16)
            add_sum(6, low.astype(F32))
            dh2[padded(protein, tile), :] = low
            return 0

        lax.fori_loop(0, count, forward, 0)

        def backward(tile, _):
            for copy in back_loads(protein, tile):
                copy.wait()
            rows = rows_of(protein, tile)
            live = lanes(live_rows(protein, tile), slim)
            source_t = u2[padded(protein, tile), :].T
            total = None
            for tap in range(KSIZE):
                window = dh2[padded(protein, tile, (2 - tap) * DILATION), :]
                term = jnp.dot(window, conv_t[tap], preferred_element_type=F32)
                total = term if total is None else total + term
                d_conv[tap] += jnp.dot(source_t, window, preferred_element_type=F32)
            norm = xh2[rows, :].astype(F32)
            slope_grad = total * live * slope2[rows, :].astype(F32)
            add_sum(4, slope_grad * norm)
            add_sum(5, slope_grad)
            err = slope_grad * vector(4)
            mean = jnp.sum(err, axis=1, keepdims=True) * (1.0 / slim)
            along = jnp.sum(err * norm, axis=1, keepdims=True) * (1.0 / slim)
            low = (lanes(scale2[rows, :], slim) * (err - mean - norm * along)).astype(BF16)
            add_sum(3, low.astype(F32))
            dh1[rows, :] = low
            dh1_store(protein, tile, dh1.at[rows, :]).start()
            return 0

        lax.fori_loop(0, count, backward, 0)
        return 0

    lax.fori_loop(0, proteins, one_protein, 0)

    last[...] = d_last[...].astype(BF16)
    flushes = [pltpu.make_async_copy(last, d_last_hbm, flush_sem.at[0])]
    flushes[0].start()

    def conv_flush(tap):
        return pltpu.make_async_copy(conv.at[tap], d_conv_hbm.at[tap], flush_sem.at[tap + 1])

    def flush(tap, _):
        conv[tap] = d_conv[tap].astype(BF16)
        conv_flush(tap).start()
        return 0

    lax.fori_loop(0, KSIZE, flush, 0)
    flushes += [conv_flush(tap) for tap in range(KSIZE)]
    for protein in range(proteins):

        def dead_store(tile, _, protein=protein):
            row_loads(protein, tile)[1].wait()
            out_store(protein, tile).start()
            return 0

        lax.fori_loop(tile_count(protein), tiles, dead_store, 0)
    for protein in range(proteins):
        for tile in range(tiles):
            out_store(protein, tile).wait()
            dh1_store(protein, tile, zeros).wait()
    for copy in flushes:
        copy.wait()


def middle_stage(lengths, vectors, u2, xh2, slope2, scale2, grads, tokens, w_conv, w_out):
    rows = u2.shape[0]
    shape = jax.ShapeDtypeStruct
    vmem = pl.BlockSpec(memory_space=pltpu.VMEM)
    tiles = 1024 // TILE
    return pl.pallas_call(
        middle_kernel,
        in_specs=[pl.BlockSpec(memory_space=pltpu.SMEM), vmem] + [HBM] * 8,
        out_specs=[HBM, HBM, HBM, HBM, vmem],
        out_shape=[
            shape((rows, 1280), BF16), shape((rows, 640), BF16), shape((KSIZE, 640, 640), BF16),
            shape((640, 1280), BF16), shape((72, 1280), F32),
        ],
        scratch_shapes=[
            pltpu.VMEM((KSIZE, 640, 640), BF16),
            pltpu.VMEM((KSIZE, 640, 640), BF16),
            pltpu.VMEM((640, 1280), BF16),
            pltpu.VMEM((1280, 640), BF16),
            pltpu.VMEM((2 * SPAN, 640), BF16),
            pltpu.VMEM((2 * SPAN, 640), BF16),
            pltpu.VMEM((rows, 1280), BF16),
            pltpu.VMEM((rows, 1280), BF16),
            pltpu.VMEM((rows, 640), BF16),
            pltpu.VMEM((rows, 640), BF16),
            pltpu.VMEM((rows, 128), F32),
            pltpu.VMEM((rows, 640), BF16),
            pltpu.VMEM((KSIZE, 640, 640), F32),
            pltpu.VMEM((640, 1280), F32),
            pltpu.VMEM((TILE, 640), BF16),
            pltpu.SemaphoreType.DMA((2, tiles)),
            pltpu.SemaphoreType.DMA((2, 2, tiles)),
            pltpu.SemaphoreType.DMA((3, 2, tiles)),
            pltpu.SemaphoreType.DMA((2,)),
            pltpu.SemaphoreType.DMA((2, tiles)),
            pltpu.SemaphoreType.DMA((2, tiles)),
            pltpu.SemaphoreType.DMA((6,)),
        ],
        compiler_params=pltpu.CompilerParams(vmem_limit_bytes=VMEM_BYTES),
        name="middle_stage",
    )(lengths, vectors, u2, xh2, slope2, scale2, grads, tokens, w_conv, w_out)


def pack_sums(lines, packed_ref):
    for plane, (width, chunk, offsets) in enumerate(
        ((1280, 40, WIDE_OFFSETS), (640, 20, SLIM_OFFSETS))
    ):
        owner, slot, row = chunk_masks(width, chunk)
        total = None
        for line, offset in zip(lines[plane], offsets):
            pick = (slot + offset == row).astype(F32)
            term = lax.dot_general(
                jnp.where(owner, jnp.broadcast_to(line, owner.shape), 0.0), pick, (((1,), (1,)), ((), ())),
                precision=lax.Precision.HIGHEST, preferred_element_type=F32,
            )
            total = term if total is None else total + term
        packed_ref[:, :, plane, :] = total.reshape(LEVELS, 8, 128)


SCATTER_BY_Y = (False, True, False)
LINE_FIRST = (False, False, True)
SCATTER_PLAN = (
    (),
    (),
    (),
    (),
    (),
    (
        ("load", 1), ("twin", 1, "far"), ("first", 1, 3), ("first", 1, 2),
    ),
    (
        ("load", 2), ("twin", 2, "x"), ("line", 2, "x", 3), ("twin", 2, "far"), ("line", 2, "far", 3),
        ("twin", 2, "y"), ("line", 2, "y", 3), ("twin", 1, "y"), ("direct", 1, 3),
    ),
    (),
    (
        ("twin", 2, "own"), ("line", 2, "own", 3), ("ready",), ("twin", 1, "x"), ("second", 1, 3), ("first", 1, 1),
    ),
    (
        ("direct", 1, 2), ("line", 2, "x", 2), ("twin", 0, "far"), ("first", 0, 3), ("first", 0, 2),
        ("line", 2, "far", 2), ("twin", 0, "x"), ("direct", 0, 3), ("first", 0, 1), ("line", 2, "y", 2),
    ),
    (
        ("twin", 1, "own"), ("line", 1, "own", 3), ("second", 1, 2),
    ),
    (
        ("twin", 0, "y"), ("second", 0, 3), ("second", 0, 2), ("line", 2, "own", 2), ("first", 1, 0),
        ("line", 2, "x", 1), ("direct", 1, 1), ("direct", 0, 2), ("direct", 0, 1), ("second", 1, 1),
        ("line", 2, "far", 1),
    ),
    (
        ("twin", 0, "own"), ("line", 0, "own", 3), ("line", 1, "own", 2), ("second", 0, 1), ("first", 0, 0),
    ),
    (),
    (
        ("line", 2, "y", 1), ("line", 2, "own", 1), ("plane", 2, "F"), ("line", 0, "own", 2), ("direct", 1, 0),
        ("second", 1, 0),
    ),
    (
        ("line", 1, "own", 1), ("plane", 2, "D"), ("direct", 0, 0),
    ),
    (
        ("plane", 2, "S"), ("second", 0, 0), ("line", 0, "own", 1), ("vec_start",), ("done", 2), ("vec_middle",),
        ("done", 1), ("done", 0), ("vec_end",), ("finish",),
    ),
)


def scatter_kernel(
    u1_hbm, dh1_hbm, slope1_hbm, xh1_hbm, scale1_hbm, grads_hbm, w_in_hbm, vectors, sums, d_conv_hbm, d_last_hbm, d_conv_flat, d_last_flat,
    grad_tokens, g_in, g_conv, g_last, g_vec,
    u1, dh1, slope1, xh1, scale1, grads, w_in, w_in_t, d_in_sum, d_in, own_sums, packed, plane_box, level_box,
    conv_own, conv_twin, conv_far, conv_x, conv_y, conv_line, conv_done, conv_swap,
    last_own, last_twin, last_far, last_x, last_y, last_line, last_done, last_swap,
    in_twin, in_far, in_x, in_y, in_line,
    tile_sem, weight_sem, store_sem, vec_sem, load_sem, twin_send, twin_recv, send_sem, move_recv, line_recv,
    swap_send, swap_recv,
):
    steps = 2048 // TILE
    z, y, x, core = place()
    columns = {"own": 2 * y + x, "x": 2 * y + (1 - x), "y": 2 * (1 - y) + x, "far": 2 * (1 - y) + (1 - x)}
    boxes = {"far": (in_far, conv_far, last_far), "x": (in_x, conv_x, last_x), "y": (in_y, conv_y, last_y)}
    line_boxes = (in_line, conv_line, last_line)
    links = {
        "x": lambda: device(z, y, 1 - x, core), "y": lambda: device(z, 1 - y, x, core),
        "twin": lambda: device(z, y, x, 1 - core),
    }

    def remote(src, dst, send, recv, link):
        return pltpu.make_async_remote_copy(
            src_ref=src, dst_ref=dst, send_sem=send, recv_sem=recv, device_id=links[link]() if isinstance(link, str) else device(z + link, y, x, core), device_id_type=MESH
        )

    def cut(side, part):
        return (None, CONV_COLS[side], OUT_COLS[side])[part]

    def narrow(side, part):
        return pl.ds(0, 640 if part == 0 else cut(side, part)[1])

    def own_at(side, part, level, column):
        if part == 0:
            return d_in.at[level, column, side]
        if part == 1:
            return conv_own.at[:, level, column, :, narrow(side, part)]
        return last_own.at[level, column, :, narrow(side, part)]

    def twin_at(side, part, level, column):
        if part == 0:
            return in_twin.at[level, column]
        if part == 1:
            return conv_twin.at[:, level, column, :, narrow(side, part)]
        return last_twin.at[level, column, :, narrow(side, part)]

    def box_at(side, part, name, level):
        box = boxes[name][part]
        if part == 0:
            return box.at[level]
        if part == 1:
            return box.at[level, :, :, narrow(side, part)]
        return box.at[level, :, narrow(side, part)]

    def way_of(sign):
        return lax.shift_right_logical(1 - sign, 1) if not isinstance(sign, int) else (1 - sign) // 2

    def line_at(side, part, kind, sign, level):
        way = way_of(sign)
        if part == 0:
            return in_line.at[way, level]
        if part == 1:
            return conv_line.at[way, level, :, :, narrow(side, part)]
        return last_line.at[KINDS.index(kind), way, level, :, narrow(side, part)]

    def all_units(side, part, count):
        rows = pl.ds(0, 40 * count)
        if part == 0:
            return w_in_hbm.at[rows, :]
        if part == 1:
            return d_conv_flat.at[:, rows, pl.ds(*cut(side, part))]
        return d_last_flat.at[rows, pl.ds(*cut(side, part))]

    def load(side, part):
        source = (d_conv_hbm.at[:, :, :, :, pl.ds(*cut(side, 1))], d_last_hbm.at[:, :, :, pl.ds(*cut(side, 2))])
        target = (conv_own.at[:, :, :, :, narrow(side, 1)], last_own.at[:, :, :, narrow(side, 2)])
        return pltpu.make_async_copy(source[part - 1], target[part - 1], load_sem.at[part - 1])

    def twin_copy(part, kind, to_side):
        column = columns[kind]
        if part == 0:
            src, dst = d_in.at[:, column, to_side], in_twin.at[:, column]
        elif part == 1:
            src = d_conv_hbm.at[:, :, column, :, pl.ds(*cut(to_side, part))]
            dst = conv_twin.at[:, :, column, :, narrow(to_side, part)]
        else:
            src = d_last_hbm.at[:, column, :, pl.ds(*cut(to_side, part))]
            dst = last_twin.at[:, column, :, narrow(to_side, part)]
        return remote(src, dst, twin_send.at[part], twin_recv.at[part, KINDS.index(kind)], "twin")

    def exchange(side, part):
        for kind in ("far", "y", "x", "own"):
            twin_copy(part, kind, 1 - side).start()

    def take_twin(side, part, kind):
        twin_copy(part, kind, side).wait_recv()

    def move(side, part, kind, level, link, box):
        return remote(
            own_at(side, part, level, columns[kind]), box_at(side, part, box, level),
            send_sem.at[part], move_recv.at[("far", "x", "y").index(box), part, level], link,
        )

    def line(side, part, kind, level, sign):
        return remote(
            own_at(side, part, level, columns[kind]), line_at(side, part, kind, sign, level),
            send_sem.at[part], line_recv.at[KINDS.index(kind), way_of(sign), part, level], sign,
        )

    def read(ref):
        return ref[...].astype(F32)

    def each_level(distance, act):
        if distance == 0:
            act(z, 0)
            return

        def one(index, _):
            sign = 1 - 2 * index
            level = z + sign * distance
            pl.when(jnp.logical_and(level >= 0, level < LEVELS))(lambda: act(level, sign))
            return 0

        lax.fori_loop(0, 2, one, 0)

    def both_terms(side, part, level, kind):
        column = columns[kind]
        return read(own_at(side, part, level, column)) + read(twin_at(side, part, level, column))

    def put(side, part, level, kind, value):
        own_at(side, part, level, columns[kind])[...] = value.astype(BF16)

    def roles(part):
        return ("y", "x") if SCATTER_BY_Y[part] else ("x", "y")

    def first(side, part, distance):
        def one(level, sign):
            put(side, part, level, "far", both_terms(side, part, level, "far"))
            move(side, part, "far", level, roles(part)[0], "far").start()

        each_level(distance, one)

    def direct(side, part, distance):
        name = roles(part)[0]

        def one(level, sign):
            put(side, part, level, name, both_terms(side, part, level, name))
            move(side, part, name, level, name, name).start()

        each_level(distance, one)

    def second(side, part, distance):
        link, name = roles(part)

        def one(level, sign):
            move(side, part, "far", level, link, "far").wait_recv()
            put(side, part, level, name, both_terms(side, part, level, name) + read(box_at(side, part, "far", level)))
            move(side, part, name, level, name, name).start()

        each_level(distance, one)

    def line_hop(side, part, kind, distance):
        def one(level, sign):
            total = None
            if not LINE_FIRST[part]:
                for name in ("x", "y"):
                    move(side, part, name, level, name, name).wait_recv()
                total = read(box_at(side, part, "x", level)) + read(box_at(side, part, "y", level))
            terms = both_terms(side, part, level, kind)
            total = terms if total is None else terms + total
            behind = jnp.logical_and(z - sign >= 0, z - sign < LEVELS)

            @pl.when(behind)
            def _():
                line(side, part, kind, level, sign).wait_recv()
                put(side, part, level, kind, total + read(line_at(side, part, kind, sign, level)))

            @pl.when(jnp.logical_not(behind))
            def _():
                put(side, part, level, kind, total)

            line(side, part, kind, level, sign).start()

        each_level(distance, one)

    def add_lines(side, part, kind, target):
        for sign, guard in ((1, z > 0), (-1, z < LEVELS - 1)):

            @pl.when(guard)
            def _(sign=sign):
                line(side, part, kind, z, sign).wait_recv()
                target[...] = (
                    target[...].astype(F32) + read(line_at(side, part, kind, sign, z))
                ).astype(target.dtype)

    def plane(side, part, what):
        link, other = roles(part)
        kind = {"F": "far", "D": link, "S": other}[what]
        own = own_at(side, part, z, columns[kind])
        keep = last_done.at[:, narrow(side, part)]
        keep[...] = both_terms(side, part, z, kind)
        add_lines(side, part, kind, keep)
        if what == "S":
            move(side, part, "far", z, link, "far").wait_recv()
            keep[...] += read(box_at(side, part, "far", z))
        own[...] = keep[...].astype(BF16)
        if what == "F":
            move(side, part, "far", z, link, "far").start()
        else:
            move(side, part, kind, z, kind, kind).start()

    def done(side, part):
        if part == 0:
            target = g_in
        elif part == 1:
            target = conv_done.at[:, :, narrow(side, part)]
        else:
            target = last_done.at[:, narrow(side, part)]
        for name in ("x", "y"):
            move(side, part, name, z, name, name).wait_recv()
        target[...] = (
            both_terms(side, part, z, "own") + read(box_at(side, part, "x", z)) + read(box_at(side, part, "y", z))
        )
        add_lines(side, part, "own", target)
        if part:
            swap(part, side).start()

    def swap(part, from_side):
        lanes_ = narrow(from_side, part)
        if part == 1:
            src, dst = conv_done.at[:, :, lanes_], conv_swap.at[:, :, lanes_]
        else:
            src, dst = last_done.at[:, lanes_], last_swap.at[:, lanes_]
        return remote(src, dst, swap_send.at[part - 1], swap_recv.at[part - 1], "twin")

    def finish(side):
        first_row, count = side * 20, 20
        for part, mine, other, target in ((2, last_done, last_swap, g_last), (1, conv_done, conv_swap, g_conv)):
            swap(part, 1 - side).wait_recv()
            for refs, owner in ((mine, side), (other, 1 - side)):
                start, width = cut(owner, part)
                if part == 1:
                    target[:, :, pl.ds(start, width)] = refs[:, pl.ds(first_row, count), pl.ds(0, width)]
                else:
                    target[:, pl.ds(start, width)] = refs[pl.ds(first_row, count), pl.ds(0, width)]
        for part in range(3):
            if part:
                swap(part, side).wait_send()
            view = all_units(1 - side, part, CHIPS)
            remote(view, view, twin_send.at[part], twin_recv.at[part, 0], "twin").wait_send()
            view = all_units(side, part, CHIPS - 1)
            remote(view, view, send_sem.at[part], twin_recv.at[part, 0], "twin").wait_send()


    def in_plane():
        return y * 4 + x * 2 + core

    def plane_copy(offset):
        other, where = plane_peer(offset)
        return pltpu.make_async_remote_copy(
            src_ref=packed.at[:, other], dst_ref=plane_box.at[in_plane()], send_sem=vec_sem.at[0],
            recv_sem=vec_sem.at[1], device_id=where, device_id_type=MESH,
        )

    def level_copy(step):
        level = lax.rem(z + step, LEVELS)
        return pltpu.make_async_remote_copy(
            src_ref=plane_box.at[0, level], dst_ref=level_box.at[z], send_sem=vec_sem.at[2], recv_sem=vec_sem.at[3],
            device_id=device(level, y, x, core), device_id_type=MESH,
        )

    def vec_start(side):
        lines = [
            [jnp.sum(own_sums[pl.ds(8 * index, 8), :], axis=0, keepdims=True) for index in range(2)]
            + [jnp.sum(sums[pl.ds(16, 8), :], axis=0, keepdims=True)],
            [jnp.sum(sums[pl.ds(8 * index, 8), pl.ds(0, 640)], axis=0, keepdims=True) for index in range(3, 9)],
        ]
        pack_sums(lines, packed)
        for offset in range(1, 8):
            plane_copy(offset).start()
        for level in range(LEVELS):
            plane_box[pl.ds(in_plane(), 1), level] = packed[level, pl.ds(in_plane(), 1)]

    def vec_middle(side):
        view = plane_box.at[pl.ds(0, 7)]
        remote(view, view, vec_sem.at[0], vec_sem.at[1], "twin").wait()
        total = jnp.sum(plane_box[...], axis=0)
        plane_box[0] = total
        level_box[pl.ds(z, 1)] = plane_box[0, pl.ds(z, 1)]
        for step in range(1, LEVELS):
            level_copy(step).start()

    def vec_end(side):
        view = level_box.at[pl.ds(0, LEVELS - 1)]
        remote(view, view, vec_sem.at[2], vec_sem.at[3], "twin").wait()
        g_vec[...] = jnp.sum(level_box[...], axis=0)

    def ready(side):
        d_in[...] = d_in_sum[...].astype(BF16).reshape(d_in.shape)
        exchange(side, 0)

    actions = {
        "load": lambda side, part: load(side, part).wait(), "twin": take_twin, "first": first, "direct": direct,
        "second": second, "line": line_hop, "plane": plane, "done": done, "ready": ready, "vec_start": vec_start,
        "vec_middle": vec_middle, "vec_end": vec_end, "finish": finish,
    }

    def either(event):
        return event[0] in ("ready", "vec_start", "vec_middle", "vec_end") or event[1:2] == (0,)

    def perform(events):
        for alike, group in itertools.groupby(events, either):
            group = tuple(group)
            if alike:
                for event in group:
                    actions[event[0]](core, *event[1:])
                continue
            for side in range(2):

                @pl.when(core == side)
                def _(side=side, group=group):
                    for event in group:
                        actions[event[0]](side, *event[1:])

    def rows_of(tile):
        return pl.ds(pl.multiple_of(tile * TILE, TILE), TILE)

    tiles_of = ((u1, u1_hbm), (dh1, dh1_hbm), (slope1, slope1_hbm), (xh1, xh1_hbm), (scale1, scale1_hbm), (grads, grads_hbm))

    def tile_load(index, tile):
        target, source = tiles_of[index]
        return pltpu.make_async_copy(source.at[rows_of(tile), :], target.at[rows_of(tile), :], tile_sem.at[index, tile])

    def store(tile):
        return pltpu.make_async_copy(grads.at[rows_of(tile), :], grad_tokens.at[rows_of(tile), :], store_sem.at[tile])

    weight_load = pltpu.make_async_copy(w_in_hbm, w_in, weight_sem.at[0])

    barrier = pltpu.get_barrier_semaphore()
    for offset in range(1, 8):
        pl.semaphore_signal(barrier, inc=1, device_id=plane_peer(offset)[1], device_id_type=MESH)
    for step in range(1, LEVELS):
        pl.semaphore_signal(
            barrier, inc=1, device_id=device(lax.rem(z + step, LEVELS), y, x, core), device_id_type=MESH
        )
    for side in range(2):

        @pl.when(core == side)
        def _(side=side):
            for part in (1, 2):
                load(side, part).start()

    weight_load.start()
    for tile in range(steps):
        tile_load(0, tile).start()
        tile_load(1, tile).start()
    own_sums[...] = jnp.zeros_like(own_sums)
    pl.semaphore_wait(barrier, 7 + LEVELS - 1)
    for side in range(2):

        @pl.when(core == side)
        def _(side=side):
            exchange(side, 1)
            exchange(side, 2)

    for tile in range(steps):
        for index in range(2, 6):
            tile_load(index, tile).start()
    weight_load.wait()
    w_in_t[...] = w_in[...].T

    def weight_tile(tile, _):
        for index in range(steps):
            if SCATTER_PLAN[index]:
                pl.when(tile == index)(functools.partial(perform, SCATTER_PLAN[index]))
        tile_load(0, tile).wait()
        tile_load(1, tile).wait()
        rows = rows_of(tile)
        term = lax.dot_general(u1[rows, :], dh1[rows, :], (((0,), (0,)), ((), ())), preferred_element_type=F32)

        @pl.when(tile == 0)
        def _():
            d_in_sum[...] = term

        @pl.when(tile > 0)
        def _():
            d_in_sum[...] += term

        return 0

    lax.fori_loop(0, steps, weight_tile, 0)

    def token_tile(tile, _):
        for index in range(steps):
            if SCATTER_PLAN[steps + index]:
                pl.when(tile == index)(functools.partial(perform, SCATTER_PLAN[steps + index]))
        for index in range(2, 6):
            tile_load(index, tile).wait()
        rows = rows_of(tile)
        back = jnp.dot(dh1[rows, :], w_in_t[...], preferred_element_type=F32)
        norm = xh1[rows, :].astype(F32)
        slope_grad = back * slope1[rows, :].astype(F32)
        for index, values in enumerate((slope_grad * norm, slope_grad)):
            own_sums[pl.ds(8 * index, 8), :] += jnp.sum(values.reshape(TILE // 8, 8, 1280), axis=0)
        err = slope_grad * vectors[pl.ds(0, 1), :]
        mean = jnp.sum(err, axis=1, keepdims=True) * (1.0 / 1280)
        along = jnp.sum(err * norm, axis=1, keepdims=True) * (1.0 / 1280)
        grads[rows, :] = (
            grads[rows, :].astype(F32) + lanes(scale1[rows, :], 1280) * (err - mean - norm * along)
        ).astype(BF16)
        store(tile).start()
        return 0

    lax.fori_loop(0, steps, token_tile, 0)
    perform(SCATTER_PLAN[2 * steps])
    for tile in range(steps):
        store(tile).wait()


def scatter_stage(u1, dh1, slope1, xh1, scale1, grads, w_in, vectors, sums, d_conv, d_last):
    rows = u1.shape[0]
    steps = rows // TILE
    shape = jax.ShapeDtypeStruct
    vmem = pl.BlockSpec(memory_space=pltpu.VMEM)
    conv_box = (LEVELS, KSIZE, 40, 384)
    last_box = (LEVELS, 40, 896)
    in_box = (LEVELS, 40, 640)
    dma = pltpu.SemaphoreType.DMA
    return pl.pallas_call(
        scatter_kernel,
        in_specs=[HBM] * 7 + [vmem] * 2 + [HBM] * 4,
        out_specs=[HBM] + [vmem] * 4,
        out_shape=[
            shape((rows, 1280), BF16), shape((40, 640), F32), shape((KSIZE, 20, 640), F32), shape((20, 1280), F32),
            shape((2, 128), F32),
        ],
        scratch_shapes=[
            pltpu.VMEM((rows, 1280), BF16),
            pltpu.VMEM((rows, 640), BF16),
            pltpu.VMEM((rows, 1280), BF16),
            pltpu.VMEM((rows, 1280), BF16),
            pltpu.VMEM((rows, 128), F32),
            pltpu.VMEM((rows, 1280), BF16),
            pltpu.VMEM((1280, 640), BF16),
            pltpu.VMEM((640, 1280), BF16),
            pltpu.VMEM((1280, 640), F32),
            pltpu.VMEM((LEVELS, 4, 2, 40, 640), BF16),
            pltpu.VMEM((16, 1280), F32),
            pltpu.VMEM((LEVELS, 8, 2, 128), F32),
            pltpu.VMEM((8, LEVELS, 2, 128), F32),
            pltpu.VMEM((LEVELS, 2, 128), F32),
            pltpu.VMEM((KSIZE, LEVELS, 4, 40, 384), BF16),
            pltpu.VMEM((KSIZE, LEVELS, 4, 40, 384), BF16),
            pltpu.VMEM(conv_box, BF16),
            pltpu.VMEM(conv_box, BF16),
            pltpu.VMEM(conv_box, BF16),
            pltpu.VMEM((2,) + conv_box, BF16),
            pltpu.VMEM((KSIZE, 40, 384), F32),
            pltpu.VMEM((KSIZE, 40, 384), F32),
            pltpu.VMEM((LEVELS, 4, 40, 896), BF16),
            pltpu.VMEM((LEVELS, 4, 40, 896), BF16),
            pltpu.VMEM(last_box, BF16),
            pltpu.VMEM(last_box, BF16),
            pltpu.VMEM(last_box, BF16),
            pltpu.VMEM((4, 2) + last_box, BF16),
            pltpu.VMEM((40, 896), F32),
            pltpu.VMEM((40, 896), F32),
            pltpu.VMEM((LEVELS, 4, 40, 640), BF16),
            pltpu.VMEM(in_box, BF16),
            pltpu.VMEM(in_box, BF16),
            pltpu.VMEM(in_box, BF16),
            pltpu.VMEM((2,) + in_box, BF16),
            dma((6, steps)), dma((1,)), dma((steps,)), dma((4,)), dma((2,)), dma((3,)), dma((3, 4)),
            dma((3,)), dma((3, 3, LEVELS)), dma((4, 2, 3, LEVELS)), dma((2,)), dma((2,)),
        ],
        compiler_params=pltpu.CompilerParams(collective_id=1, has_side_effects=True, vmem_limit_bytes=VMEM_BYTES),
        name="scatter_stage",
    )(
        u1, dh1, slope1, xh1, scale1, grads, w_in, vectors, sums,
        d_conv.reshape(KSIZE, LEVELS, 4, 40, 640), d_last.reshape(LEVELS, 4, 40, 1280), d_conv, d_last,
    )


def settle_kernel(rows_hbm, g_in, g_conv, g_last, g_vec, rows_out, in_out, conv_out, last_out, *rest):
    vectors_out, (buffer, load_sem, store_sem) = rest[:9], rest[9:]
    count = buffer.shape[0]
    chunk = buffer.shape[1]
    loads = [
        pltpu.make_async_copy(rows_hbm.at[pl.ds(index * chunk, chunk), :], buffer.at[index], load_sem.at[index])
        for index in range(count)
    ]
    stores = [
        pltpu.make_async_copy(buffer.at[index], rows_out.at[pl.ds(index * chunk, chunk), :], store_sem.at[index])
        for index in range(count)
    ]
    for copy in loads:
        copy.start()
    in_out[...] = g_in[...]
    conv_out[...] = g_conv[...]
    last_out[...] = g_last[...]
    places = [(0, offset, 40) for offset in WIDE_OFFSETS] + [(1, offset, 20) for offset in SLIM_OFFSETS]
    for target, (plane, offset, width) in zip(vectors_out, places):
        target[...] = g_vec[pl.ds(plane, 1), pl.ds(offset, width)]
    for load, store in zip(loads, stores):
        load.wait()
        store.start()
    for copy in stores:
        copy.wait()


def settle_stage(rows, g_in, g_conv, g_last, g_vec):
    chunks = 8
    shape = jax.ShapeDtypeStruct
    vmem = pl.BlockSpec(memory_space=pltpu.VMEM)
    return pl.pallas_call(
        settle_kernel,
        in_specs=[HBM] + [vmem] * 4,
        out_specs=[HBM] + [vmem] * 12,
        out_shape=[shape(v.shape, v.dtype) for v in (rows, g_in, g_conv, g_last)]
        + [shape((1, 40), F32)] * 3
        + [shape((1, 20), F32)] * 6,
        scratch_shapes=[
            pltpu.VMEM((chunks, rows.shape[0] // chunks, rows.shape[1]), rows.dtype),
            pltpu.SemaphoreType.DMA((chunks,)),
            pltpu.SemaphoreType.DMA((chunks,)),
        ],
        compiler_params=pltpu.CompilerParams(vmem_limit_bytes=VMEM_BYTES),
        name="settle_stage",
    )(rows, g_in, g_conv, g_last, g_vec)


def kernel_body(
    tokens, out_grad, lengths, ln1_gain, ln1_bias, w_in, b_in, ln2_gain, ln2_bias,
    w_conv, b_conv, ln3_gain, ln3_bias, w_out, b_out,
):
    proteins, length_pad, width = tokens.shape
    rows = tokens.reshape(proteins * length_pad, width)
    grads = out_grad.reshape(proteins * length_pad, width)
    vec = pack_vectors(ln1_gain, ln1_bias, b_in, ln2_gain, ln2_bias, b_conv, ln3_gain, ln3_bias, b_out)
    u1, slope1, xh1, scale1, xh2, slope2, scale2, u2, vectors, in_full, conv_full, out_full = gather_stage(
        rows, vec, w_in, w_conv, w_out
    )
    result, dh1, d_conv, d_last, sums = middle_stage(
        lengths, vectors, u2, xh2, slope2, scale2, grads, rows, conv_full, out_full
    )
    grad_rows, g_in, g_conv, g_last, *lines = settle_stage(
        *scatter_stage(u1, dh1, slope1, xh1, scale1, grads, in_full, vectors, sums, d_conv, d_last)
    )
    lines = [line.reshape(line.shape[1]) for line in lines]
    wide, slim = lines[:3], lines[3:]
    return (
        result.reshape(tokens.shape), grad_rows.reshape(tokens.shape),
        wide[0], wide[1], g_in, slim[0], slim[1], slim[2], g_conv, slim[3], slim[4], slim[5], g_last, wide[2],
    )


def layer_norm(values, gain, bias):
    center = values - jnp.mean(values, axis=-1, keepdims=True)
    var_rows = jnp.mean(center * center, axis=-1, keepdims=True)
    return center * lax.rsqrt(var_rows + EPS) * gain + bias


def norm_gelu(values, gain, bias):
    return jax.nn.gelu(layer_norm(values, gain, bias), approximate=False)


def collect(
    ln1_gain,
    ln1_bias,
    w_in,
    b_in,
    ln2_gain,
    ln2_bias,
    w_conv,
    b_conv,
    ln3_gain,
    ln3_bias,
    w_out,
    b_out,
):
    return (
        lax.all_gather(ln1_gain, ("dp", "fsdp"), axis=0, tiled=True),
        lax.all_gather(ln1_bias, ("dp", "fsdp"), axis=0, tiled=True),
        lax.all_gather(w_in, ("dp", "fsdp"), axis=0, tiled=True),
        lax.all_gather(b_in, ("dp", "fsdp"), axis=0, tiled=True),
        lax.all_gather(ln2_gain, ("dp", "fsdp"), axis=0, tiled=True),
        lax.all_gather(ln2_bias, ("dp", "fsdp"), axis=0, tiled=True),
        lax.all_gather(w_conv, ("dp", "fsdp"), axis=1, tiled=True),
        lax.all_gather(b_conv, ("dp", "fsdp"), axis=0, tiled=True),
        lax.all_gather(ln3_gain, ("dp", "fsdp"), axis=0, tiled=True),
        lax.all_gather(ln3_bias, ("dp", "fsdp"), axis=0, tiled=True),
        lax.all_gather(w_out, ("dp", "fsdp"), axis=0, tiled=True),
        lax.all_gather(b_out, ("dp", "fsdp"), axis=0, tiled=True),
    )


def spread(
    term_g1,
    term_b1,
    term_wi,
    term_bi,
    term_g2,
    term_b2,
    term_wc,
    term_bc,
    term_g3,
    term_b3,
    term_wo,
    term_bo,
):
    return (
        lax.psum_scatter(term_g1, ("dp", "fsdp"), scatter_dimension=0, tiled=True),
        lax.psum_scatter(term_b1, ("dp", "fsdp"), scatter_dimension=0, tiled=True),
        lax.psum_scatter(term_wi, ("dp", "fsdp"), scatter_dimension=0, tiled=True),
        lax.psum_scatter(term_bi, ("dp", "fsdp"), scatter_dimension=0, tiled=True),
        lax.psum_scatter(term_g2, ("dp", "fsdp"), scatter_dimension=0, tiled=True),
        lax.psum_scatter(term_b2, ("dp", "fsdp"), scatter_dimension=0, tiled=True),
        lax.psum_scatter(term_wc, ("dp", "fsdp"), scatter_dimension=1, tiled=True),
        lax.psum_scatter(term_bc, ("dp", "fsdp"), scatter_dimension=0, tiled=True),
        lax.psum_scatter(term_g3, ("dp", "fsdp"), scatter_dimension=0, tiled=True),
        lax.psum_scatter(term_b3, ("dp", "fsdp"), scatter_dimension=0, tiled=True),
        lax.psum_scatter(term_wo, ("dp", "fsdp"), scatter_dimension=0, tiled=True),
        lax.psum_scatter(term_bo, ("dp", "fsdp"), scatter_dimension=0, tiled=True),
    )


def dilate(padded, kernel, length_pad):
    total = jnp.zeros((padded.shape[0], length_pad, kernel.shape[2]), jnp.float32)
    for kernel_tap in range(kernel.shape[0]):
        window = padded[:, kernel_tap * DILATION : kernel_tap * DILATION + length_pad]
        total = total + jnp.einsum(
            "pli,io->plo", window, kernel[kernel_tap], preferred_element_type=jnp.float32
        )
    return total


def plain_body(
    tokens,
    out_grad,
    lengths,
    ln1_gain,
    ln1_bias,
    w_in,
    b_in,
    ln2_gain,
    ln2_bias,
    w_conv,
    b_conv,
    ln3_gain,
    ln3_bias,
    w_out,
    b_out,
):
    proteins, length_pad, width = tokens.shape
    row_count = proteins * length_pad
    reach = KSIZE // 2 * DILATION
    positions = lax.broadcasted_iota(jnp.int32, (proteins, length_pad), 1)
    live = (positions < lengths[:, None]).astype(jnp.float32).reshape(row_count, 1)
    full = collect(
        ln1_gain,
        ln1_bias,
        w_in,
        b_in,
        ln2_gain,
        ln2_bias,
        w_conv,
        b_conv,
        ln3_gain,
        ln3_bias,
        w_out,
        b_out,
    )
    (
        gain_one,
        bias_one,
        first_matrix,
        first_bias,
        gain_two,
        bias_two,
        conv_kernel,
        conv_bias,
        gain_three,
        bias_three,
        last_matrix,
        last_bias,
    ) = full
    inner = first_matrix.shape[1]
    row_tokens = tokens.reshape(row_count, width).astype(jnp.float32)
    act_one, pull_one = jax.vjp(
        norm_gelu, row_tokens, gain_one.astype(jnp.float32), bias_one.astype(jnp.float32)
    )
    inner_one = act_one.astype(jnp.bfloat16)
    hidden_one = jnp.dot(
        inner_one, first_matrix, preferred_element_type=jnp.float32
    ) + first_bias.astype(jnp.float32)
    act_two, pull_two = jax.vjp(
        norm_gelu, hidden_one, gain_two.astype(jnp.float32), bias_two.astype(jnp.float32)
    )
    inner_two = (act_two * live).astype(jnp.bfloat16)
    padded_two = jnp.pad(
        inner_two.reshape(proteins, length_pad, inner), ((0, 0), (reach, reach), (0, 0))
    )
    hidden_two = dilate(padded_two, conv_kernel, length_pad).reshape(
        row_count, inner
    ) + conv_bias.astype(jnp.float32)
    act_three, pull_three = jax.vjp(
        norm_gelu, hidden_two, gain_three.astype(jnp.float32), bias_three.astype(jnp.float32)
    )
    inner_three = act_three.astype(jnp.bfloat16)
    branch = jnp.dot(
        inner_three, last_matrix, preferred_element_type=jnp.float32
    ) + last_bias.astype(jnp.float32)
    result = (row_tokens + live * branch).astype(jnp.bfloat16).reshape(proteins, length_pad, width)
    again = collect(
        ln1_gain,
        ln1_bias,
        w_in,
        b_in,
        ln2_gain,
        ln2_bias,
        w_conv,
        b_conv,
        ln3_gain,
        ln3_bias,
        w_out,
        b_out,
    )
    (
        again_g1,
        again_b1,
        back_first,
        again_bi,
        again_g2,
        again_b2,
        back_kernel,
        again_bc,
        again_g3,
        again_b3,
        back_last,
        again_bo,
    ) = again
    pull_one = jax.vjp(
        norm_gelu, row_tokens, again_g1.astype(jnp.float32), again_b1.astype(jnp.float32)
    )[1]
    pull_two = jax.vjp(
        norm_gelu, hidden_one, again_g2.astype(jnp.float32), again_b2.astype(jnp.float32)
    )[1]
    pull_three = jax.vjp(
        norm_gelu, hidden_two, again_g3.astype(jnp.float32), again_b3.astype(jnp.float32)
    )[1]
    grad_rows = out_grad.reshape(row_count, width)
    grad_branch = grad_rows * live.astype(jnp.bfloat16)
    term_wo = jnp.einsum("ri,rd->id", inner_three, grad_branch, preferred_element_type=jnp.float32)
    term_bo = jnp.sum(grad_branch.astype(jnp.float32), axis=0)
    grad_three = jnp.einsum("rd,id->ri", grad_branch, back_last, preferred_element_type=jnp.float32)
    d_hidden_two, term_g3, term_b3 = pull_three(grad_three)
    low_two = d_hidden_two.astype(jnp.bfloat16)
    term_bc = jnp.sum(low_two.astype(jnp.float32), axis=0)
    padded_grad = jnp.pad(
        low_two.reshape(proteins, length_pad, inner), ((0, 0), (reach, reach), (0, 0))
    )
    grad_view = low_two.reshape(proteins, length_pad, inner)
    kernel_terms = []
    grad_two = jnp.zeros((proteins, length_pad, inner), jnp.float32)
    taps = back_kernel.shape[0]
    for kernel_tap in range(taps):
        window = padded_two[:, kernel_tap * DILATION : kernel_tap * DILATION + length_pad]
        kernel_terms.append(
            jnp.einsum("pli,plo->io", window, grad_view, preferred_element_type=jnp.float32)
        )
        mirror = (taps - 1 - kernel_tap) * DILATION
        grad_window = padded_grad[:, mirror : mirror + length_pad]
        grad_two = grad_two + jnp.einsum(
            "plo,io->pli", grad_window, back_kernel[kernel_tap], preferred_element_type=jnp.float32
        )
    term_wc = jnp.stack(kernel_terms, axis=0)
    grad_two = grad_two.reshape(row_count, inner) * live
    d_hidden_one, term_g2, term_b2 = pull_two(grad_two)
    low_one = d_hidden_one.astype(jnp.bfloat16)
    term_wi = jnp.einsum("rd,ri->di", inner_one, low_one, preferred_element_type=jnp.float32)
    term_bi = jnp.sum(low_one.astype(jnp.float32), axis=0)
    grad_one = jnp.einsum("ri,di->rd", low_one, back_first, preferred_element_type=jnp.float32)
    d_tokens, term_g1, term_b1 = pull_one(grad_one)
    grad_tokens = (
        (grad_rows.astype(jnp.float32) + d_tokens)
        .astype(jnp.bfloat16)
        .reshape(proteins, length_pad, width)
    )
    owned = spread(
        term_g1,
        term_b1,
        term_wi,
        term_bi,
        term_g2,
        term_b2,
        term_wc,
        term_bc,
        term_g3,
        term_b3,
        term_wo,
        term_bo,
    )
    return (
        result,
        grad_tokens,
        owned[0],
        owned[1],
        owned[2],
        owned[3],
        owned[4],
        owned[5],
        owned[6],
        owned[7],
        owned[8],
        owned[9],
        owned[10],
        owned[11],
    )


def solution(mesh):
    both = ("dp", "fsdp")
    by_row = P(both)
    in_specs = (
        P(both, None, None), P(both, None, None), by_row, by_row, by_row, P(both, None), by_row, by_row, by_row,
        P(None, both, None), by_row, by_row, by_row, P(both, None), by_row,
    )
    out_specs = (
        P(both, None, None), P(both, None, None), by_row, by_row, P(both, None), by_row, by_row, by_row,
        P(None, both, None), by_row, by_row, by_row, P(both, None), by_row,
    )
    body = kernel_body if (mesh.shape["dp"], mesh.shape["fsdp"]) == (8, 4) else plain_body
    return jax.shard_map(body, mesh=mesh, in_specs=in_specs, out_specs=out_specs, check_vma=False)
```

```python
import functools
import itertools

import jax
import jax.numpy as jnp
from jax import lax
from jax.experimental import pallas as pl
from jax.experimental.pallas import tpu as pltpu
from jax.sharding import PartitionSpec as P

KSIZE = 5
DILATION = 8
EPS = 1e-05
HALF_ROOT = 0.7071067811865476
PHI_SCALE = 0.3989422804014327
F32 = jnp.float32
BF16 = jnp.bfloat16
MESH = pl.DeviceIdType.MESH
VMEM_BYTES = 62 * 2**20
HBM = pl.BlockSpec(memory_space=pl.ANY)
LEVELS = 4
CHIPS = 16
DEVICES = 32
TILE = 256
CONV_COLS = ((0, 384), (384, 256))
OUT_COLS = ((0, 384), (384, 896))
WIDE_OFFSETS = (0, 40, 80)
SLIM_OFFSETS = (0, 20, 40, 60, 80, 100)


def place():
    dp = lax.axis_index("dp")
    fs = lax.axis_index("fsdp")
    return lax.div(dp, 2), lax.rem(dp, 2), lax.div(fs, 2), lax.rem(fs, 2)


def device(z, y, x, core):
    return (z * 2 + y, x * 2 + core)


def chip(z, y, x):
    return (z * 2 + y) * 2 + x


def peer_of(step):
    mine = lax.axis_index("dp") * 4 + lax.axis_index("fsdp")
    other = lax.rem(mine + step, DEVICES)
    return mine, other, (lax.div(other, 4), lax.rem(other, 4))


def greet_all():
    barrier = pltpu.get_barrier_semaphore()

    def greet(step, _):
        _, _, target = peer_of(step)
        pl.semaphore_signal(barrier, inc=1, device_id=target, device_id_type=MESH)
        return 0

    lax.fori_loop(1, DEVICES, greet, 0)
    pl.semaphore_wait(barrier, DEVICES - 1)


def chunk_masks(width, chunk):
    scale = -(-65536 // chunk)
    column = lax.broadcasted_iota(jnp.int32, (DEVICES, width), 1)
    row = lax.broadcasted_iota(jnp.int32, (DEVICES, width), 0)
    owner = lax.shift_right_logical(column * scale, 16) == row
    place_col = lax.broadcasted_iota(jnp.int32, (128, width), 1)
    place_row = lax.broadcasted_iota(jnp.int32, (128, width), 0)
    slot = place_col - lax.shift_right_logical(place_col * scale, 16) * chunk
    return owner, slot, place_row


def unpack_vectors(packed_ref, vectors_ref):
    for plane, (width, chunk, offsets) in enumerate(
        ((1280, 40, WIDE_OFFSETS), (640, 20, SLIM_OFFSETS))
    ):
        owner, slot, row = chunk_masks(width, chunk)
        packed = packed_ref[:, plane, :].astype(BF16)
        for index, offset in enumerate(offsets):
            pick = (slot + offset == row).astype(F32).astype(BF16)
            spread = jnp.dot(packed, pick, preferred_element_type=F32)
            line = jnp.sum(jnp.where(owner, spread, 0.0), axis=0, keepdims=True)
            vectors_ref[pl.ds(plane * 3 + index, 1), pl.ds(0, width)] = line


def lanes(column, width):
    return jnp.concatenate([column] * (width // 128), axis=1)


def norm_parts(values):
    width = values.shape[1]
    mean = jnp.sum(values, axis=1, keepdims=True) * (1.0 / width)
    center = values - mean
    var = jnp.sum(center * center, axis=1, keepdims=True) * (1.0 / width)
    scale = lax.rsqrt(var + EPS)
    return center * scale, scale


def gelu_parts(arg):
    normal = 0.5 + 0.5 * lax.erf(arg * HALF_ROOT)
    slope = normal + arg * (PHI_SCALE * jnp.exp(-0.5 * (arg * arg)))
    return arg * normal, slope


PART_COUNT = 4
CONV_TAPS = {1: (0, 3), 2: (3, 2)}
BY_Y = (False, True, False, True)
PLANE_FIRST = (False, False, False, True)
KINDS = ("own", "x", "y", "far")
GATHER_PLAN = (
    (
        ("vec_begin",), ("send", 0), ("begin",), ("assemble",), ("send", 3), ("vec_plane",), ("y", 0, 0),
        ("own", 0, 1), ("send", 1), ("vec_pass", 1), ("own", 0, 2), ("send", 2), ("vec_pass", 2), ("y", 3, 0),
        ("x", 3, 0), ("x", 0, 0), ("own", 1, 1), ("own", 0, 3), ("share", "own", 0), ("y", 0, 1), ("vec_pass", 3),
        ("vectors",), ("x", 1, 0), ("x", 0, 1),
    ),
    (),
    (
        ("y", 0, 2), ("own", 2, 1), ("far", 3, 0),
    ),
    (),
    (
        ("y", 0, 3), ("share", "y", 0), ("x", 0, 2), ("own", 1, 2), ("y", 1, 0), ("y", 3, 1),
    ),
    (
        ("own", 2, 2), ("x", 3, 1), ("x", 2, 0),
    ),
    (),
    (
        ("y", 2, 0), ("own", 3, 1), ("x", 1, 1),
    ),
    (
        ("far", 3, 1), ("far", 0, 1), ("y", 1, 1), ("x", 0, 3), ("share", "x", 0), ("far", 0, 2), ("far", 0, 0),
        ("own", 1, 3), ("share", "own", 1), ("far", 0, 3), ("share", "far", 0), ("far", 1, 0), ("y", 2, 1),
        ("y", 3, 2), ("w_in",),
    ),
    (
        ("own", 2, 3), ("share", "own", 2),
    ),
    (),
    (
        ("x", 3, 2), ("x", 1, 2),
    ),
    (
        ("x", 2, 1), ("y", 1, 2), ("y", 2, 2), ("own", 3, 2), ("far", 3, 2), ("x", 1, 3), ("share", "x", 1),
        ("x", 2, 2), ("y", 2, 3), ("share", "y", 2),
    ),
    (),
    (
        ("y", 1, 3), ("share", "y", 1), ("far", 2, 0),
    ),
    (
        ("far", 1, 1), ("x", 2, 3), ("share", "x", 2),
    ),
    (
        ("y", 3, 3), ("share", "y", 3), ("far", 2, 1), ("own", 3, 3), ("share", "own", 3), ("far", 1, 2), ("x", 3, 3),
        ("share", "x", 3), ("far", 1, 3), ("share", "far", 1), ("far", 2, 2), ("far", 2, 3), ("share", "far", 2),
        ("far", 3, 3), ("share", "far", 3), ("finish",),
    ),
)


def plane_peer(offset):
    z, y, x, core = place()
    other = lax.rem(y * 4 + x * 2 + core + offset, 8)
    return other, (z * 2 + lax.div(other, 4), lax.rem(other, 4))


def greet_near(z, y, x, core):
    barrier = pltpu.get_barrier_semaphore()

    def greet(target):
        pl.semaphore_signal(barrier, inc=1, device_id=target, device_id_type=MESH)

    for offset in range(1, 8):
        greet(plane_peer(offset)[1])
    pl.when(z > 0)(lambda: greet(device(z - 1, y, x, core)))
    pl.when(z < LEVELS - 1)(lambda: greet(device(z + 1, y, x, core)))
    pl.semaphore_wait(barrier, 7 + (z > 0).astype(jnp.int32) + (z < LEVELS - 1).astype(jnp.int32))


def each_level(z, distance, act):
    if distance == 0:
        act(z, 0)
        return
    pl.when(z + distance < LEVELS)(lambda: act(z + distance, 1))
    pl.when(z - distance >= 0)(lambda: act(z - distance, -1))


def gather_kernel(
    tokens_hbm, grads_hbm, vec, w_in, w_conv, w_out,
    u1_hbm, slope1_hbm, xh1_hbm, scale1_hbm, xh2_hbm, slope2_hbm, scale2_hbm, u2_hbm, vectors_out,
    in_full, conv_full, out_full,
    u2_share, xh2_share, slope2_share, scale2_share, grads_share, tokens_share,
    packed, in_vmem, conv_twin, out_twin, conv_own, out_own,
    tokens, u1, slope1, xh1, scale1, xh2, slope2, scale2, u2, token_sem, store_sem, share_send, share_recv,
    vec_send, vec_recv, link_send, link_recv, twin_recv, pair_send, pair_recv, own_sem, load_sem,
):
    z, y, x, core = place()
    here = 2 * y + x
    steps = 2048 // TILE
    columns = {"own": here, "x": 2 * y + (1 - x), "y": 2 * (1 - y) + x, "far": 2 * (1 - y) + (1 - x)}

    def piece(part, level, column, side):
        if part == 0:
            return in_vmem.at[pl.ds(pl.multiple_of((level * 4 + column) * 80 + side * 40, 8), 40), :]
        if part in CONV_TAPS:
            return conv_full.at[pl.ds(*CONV_TAPS[part]), level, column, :, pl.ds(*CONV_COLS[side])]
        return out_full.at[level, column, :, pl.ds(*OUT_COLS[side])]

    def pieces(part, column, side):
        if part in CONV_TAPS:
            return conv_full.at[pl.ds(*CONV_TAPS[part]), :, column, :, pl.ds(*CONV_COLS[side])]
        return out_full.at[:, column, :, pl.ds(*OUT_COLS[side])]

    def span(part, side, count):
        if part == 0:
            return in_vmem.at[pl.ds(0, 40 * count), :]
        rows, columns_ = (LEVELS, count // LEVELS) if count % LEVELS == 0 else (count, 1)
        if part in CONV_TAPS:
            return conv_full.at[
                pl.ds(*CONV_TAPS[part]), pl.ds(0, rows), pl.ds(0, columns_), :, pl.ds(*CONV_COLS[side])
            ]
        return out_full.at[pl.ds(0, rows), pl.ds(0, columns_), :, pl.ds(*OUT_COLS[side])]

    def own_piece(part, side):
        if part == 0:
            return w_in
        if part in CONV_TAPS:
            return conv_own.at[pl.ds(*CONV_TAPS[part]), :, pl.ds(*CONV_COLS[side])]
        return out_own.at[:, pl.ds(*OUT_COLS[side])]

    def target(link, side):
        return (
            device(z, y, 1 - x, side),
            device(z, 1 - y, x, side),
            device(z + 1, y, x, side),
            device(z - 1, y, x, side),
            device(z, y, x, 1 - side),
        )[link]

    def remote(src, dst, send_sem, recv_sem, where):
        return pltpu.make_async_remote_copy(
            src_ref=src, dst_ref=dst, send_sem=send_sem, recv_sem=recv_sem, device_id=where, device_id_type=MESH
        )

    def wait_sent(side, part, link, count):
        view = span(part, side, count)
        remote(view, view, link_send.at[link, part], twin_recv.at[0, part], target(4, side)).wait_send()

    def guarded(link, act):
        if link == 2:
            pl.when(z < LEVELS - 1)(act)
        elif link == 3:
            pl.when(z > 0)(act)
        else:
            act()

    def forward(side, part, level, column, links, own=False):
        place_ref = piece(part, level, column, side)
        for link in links:

            def act(link=link):
                remote(
                    own_piece(part, side) if own else place_ref, place_ref,
                    link_send.at[link, part], link_recv.at[level, column, part], target(link, side),
                ).start()

            guarded(link, act)

    def pass_on(side, kind, part, distance):
        def act(level, sign):
            column = columns[kind]
            place_ref = piece(part, level, column, side)
            remote(
                place_ref, place_ref, link_send.at[4, part], link_recv.at[level, column, part], target(4, side)
            ).wait_recv()
            along = {1: (3,), -1: (2,), 0: (2, 3)}[sign]
            links = ()
            if kind == "own":
                links = along if PLANE_FIRST[part] else along + (0, 1)
            else:
                if kind == "x" and BY_Y[part] and (distance == 0 or not PLANE_FIRST[part]):
                    links += (1,)
                if kind == "y" and not BY_Y[part] and (distance == 0 or not PLANE_FIRST[part]):
                    links += (0,)
                if PLANE_FIRST[part]:
                    links += along
            forward(side, part, level, column, links)

        each_level(z, distance, act)

    def own_sends(side, part):
        forward(side, part, z, here, (0, 1, 2, 3), own=True)

    def twin_copy(side, kind, part, level=None):
        if level is None:
            view = pieces(part, columns[kind], side)
        else:
            view = piece(part, level, columns[kind], side)
        return remote(view, view, link_send.at[4, part], twin_recv.at[KINDS.index(kind), part], target(4, side))

    def share(side, kind, part):
        if kind == "own":
            own_copy(side, part).wait()
        if part:
            twin_copy(side, kind, part).start()
        else:
            for level in range(LEVELS):
                twin_copy(side, kind, part, level).start()

    def take_twin(side, part):
        for kind in KINDS:
            if part:
                twin_copy(1 - side, kind, part).wait_recv()
            else:
                view = span(part, side, LEVELS)
                remote(
                    view, view, link_send.at[4, part], twin_recv.at[KINDS.index(kind), part], target(4, side)
                ).wait_recv()

    def pair_copies(side):
        return [
            remote(src, dst, pair_send.at[index], pair_recv.at[index], target(4, side))
            for index, (src, dst) in enumerate(((w_conv, conv_twin), (w_out, out_twin)))
        ]

    def own_copy(side, part):
        return pltpu.make_async_copy(own_piece(part, side), piece(part, z, here, side), own_sem.at[part])

    def vec_copy(offset):
        mine = z * 8 + y * 4 + x * 2 + core
        return remote(vec, packed.at[mine], vec_send.at[0], vec_recv.at[0], plane_peer(offset)[1])

    def level_rows(level):
        return packed.at[pl.ds(pl.multiple_of(level * 8, 8), 8)]

    def vec_line(side, level, link):
        rows = level_rows(level)
        return remote(rows, rows, vec_send.at[link - 1], vec_recv.at[1 + level], target(link, side))

    def vec_begin(side):
        for offset in range(1, 8):
            vec_copy(offset).start()
        packed[pl.ds(z * 8 + y * 4 + x * 2 + side, 1)] = vec[...][None]

    def vec_plane(side):
        rows = packed.at[pl.ds(0, 7)]
        remote(rows, rows, vec_send.at[0], vec_recv.at[0], target(4, side)).wait()
        for link in (2, 3):
            guarded(link, lambda link=link: vec_line(side, z, link).start())

    def vec_pass(side, distance):
        def act(level, sign):
            link = 3 if sign > 0 else 2
            vec_line(side, level, link).wait_recv()
            guarded(link, lambda: vec_line(side, level, link).start())

        each_level(z, distance, act)

    def vec_finish(side):
        for level in range(LEVELS):

            @pl.when(z == level)
            def _(level=level):
                for link, count in ((2, level + 1 if level < LEVELS - 1 else 0), (3, LEVELS - level if level else 0)):
                    if count:
                        rows = packed.at[pl.ds(0, 8 * count)]
                        remote(rows, rows, vec_send.at[link - 1], vec_recv.at[0], target(4, side)).wait_send()

    def begin(side):
        own_copy(side, 0).start()
        for copy in pair_copies(side):
            copy.start()
        share_rows(side, slice(4, 6))

    def assemble(side):
        for copy in pair_copies(side):
            copy.wait()
        first_conv, second_conv = (w_conv, conv_twin) if side == 0 else (conv_twin, w_conv)
        first_out, second_out = (w_out, out_twin) if side == 0 else (out_twin, w_out)
        conv_own[...] = jnp.concatenate(
            [first_conv[...].astype(F32), second_conv[...].astype(F32)], axis=1
        ).astype(BF16)
        out_own[...] = jnp.concatenate(
            [first_out[...].astype(F32), second_out[...].astype(F32)], axis=0
        ).astype(BF16)
        for part in range(1, PART_COUNT):
            own_copy(side, part).start()

    def shares(side):
        half = pl.ds(1024, 1024)
        pairs = (
            (u2, u2_share), (xh2, xh2_share), (slope2, slope2_share), (scale2, scale2_share),
            (grads_hbm, grads_share), (tokens_hbm, tokens_share),
        )
        return [
            remote(source.at[half, :], target_, share_send.at[index], share_recv.at[index], target(4, side))
            for index, (source, target_) in enumerate(pairs)
        ]

    def share_rows(side, which):
        for copy in shares(side)[which]:
            copy.start()

    def save_in():
        return pltpu.make_async_copy(in_vmem, in_full, load_sem.at[0])

    def take_in(side):
        take_twin(side, 0)
        save_in().start()

    def finish(side):
        vec_finish(side)
        for part in range(1, PART_COUNT):
            take_twin(side, part)
        for part in range(PART_COUNT):
            plane, along = (1, 4) if PLANE_FIRST[part] else (4, 1)
            wait_sent(side, part, 0, plane if BY_Y[part] else 2 * plane)
            wait_sent(side, part, 1, 2 * plane if BY_Y[part] else plane)
            wait_sent(side, part, 4, CHIPS)
            for level in range(LEVELS):

                @pl.when(z == level)
                def _(part=part, along=along, level=level):
                    if level < LEVELS - 1:
                        wait_sent(side, part, 2, along * (level + 1))
                    if level > 0:
                        wait_sent(side, part, 3, along * (LEVELS - level))

        save_in().wait()
        for copy in shares(side):
            copy.wait()

    def take_vectors(side):
        unpack_vectors(packed, vectors_out)
        mine = z * 8 + y * 4 + x * 2
        for row, owner in ((9, mine + side), (10, mine + 1 - side)):
            vectors_out[pl.ds(row, 1), pl.ds(0, 128)] = packed[owner, pl.ds(0, 1), :]

    actions = {
        "share_rows": share_rows,
        "send": own_sends, "begin": begin, "assemble": assemble, "w_in": take_in, "finish": finish,
        "vec_begin": vec_begin, "vec_plane": vec_plane, "vec_pass": vec_pass,
        "vectors": take_vectors,
        "share": share,
    }

    def perform(events):
        for side in range(2):

            @pl.when(core == side)
            def _(side=side):
                for event in events:
                    if event[0] in actions:
                        actions[event[0]](side, *event[1:])
                    else:
                        pass_on(side, *event)

    def rows_of(tile, count=1):
        return pl.ds(pl.multiple_of(tile * TILE, TILE), count * TILE)

    def token_load(tile):
        return pltpu.make_async_copy(tokens_hbm.at[rows_of(tile), :], tokens.at[rows_of(tile), :], token_sem.at[tile])

    first = ((u1, u1_hbm), (slope1, slope1_hbm), (xh1, xh1_hbm), (scale1, scale1_hbm))
    second = ((u2, u2_hbm), (xh2, xh2_hbm), (slope2, slope2_hbm), (scale2, scale2_hbm))

    def stores(pairs, phase, half):
        rows = rows_of(half * (steps // 2), steps // 2)
        return [
            pltpu.make_async_copy(src.at[rows, :], dst.at[rows, :], store_sem.at[phase, half, index])
            for index, (src, dst) in enumerate(pairs)
        ]

    def start_stores(pairs, phase, half):
        for copy in stores(pairs, phase, half):
            copy.start()

    greet_near(z, y, x, core)
    for tile in range(steps):
        token_load(tile).start()

    def wide_tile(tile, _):
        for index in range(steps):
            if GATHER_PLAN[index]:
                pl.when(tile == index)(functools.partial(perform, GATHER_PLAN[index]))
        token_load(tile).wait()
        rows = rows_of(tile)
        gain, bias = vectors_out[pl.ds(0, 1), :], vectors_out[pl.ds(1, 1), :]
        norm, scale = norm_parts(tokens[rows, :].astype(F32))
        act, slope = gelu_parts(norm * gain + bias)
        u1[rows, :] = act.astype(BF16)
        slope1[rows, :] = slope.astype(BF16)
        xh1[rows, :] = norm.astype(BF16)
        scale1[rows, :] = jnp.broadcast_to(scale, (TILE, 128))
        return 0

    lax.fori_loop(0, steps, wide_tile, 0)

    def slim_tile(tile, _):
        for index in range(steps):
            events = GATHER_PLAN[steps + index]
            if index == 0:
                pl.when(tile == 0)(lambda: start_stores(first, 0, 0))
                pl.when(tile == 0)(lambda: start_stores(first, 0, 1))
            if index == steps // 2:

                @pl.when(tile == index)
                def _():
                    start_stores(second, 1, 1)
                    perform((("share_rows", slice(0, 4)),))

            if events:
                pl.when(tile == index)(functools.partial(perform, events))
        rows = rows_of(lax.rem(tile + steps // 2, steps))
        hidden = jnp.dot(u1[rows, :], in_vmem[...], preferred_element_type=F32)
        hidden = hidden + vectors_out[pl.ds(3, 1), pl.ds(0, 640)]
        norm, scale = norm_parts(hidden)
        act, slope = gelu_parts(norm * vectors_out[pl.ds(4, 1), pl.ds(0, 640)] + vectors_out[pl.ds(5, 1), pl.ds(0, 640)])
        u2[rows, :] = act.astype(BF16)
        slope2[rows, :] = slope.astype(BF16)
        xh2[rows, :] = norm.astype(BF16)
        scale2[rows, :] = jnp.broadcast_to(scale, (TILE, 128))
        return 0

    lax.fori_loop(0, steps, slim_tile, 0)
    start_stores(second, 1, 0)
    perform(GATHER_PLAN[2 * steps])
    for phase, pairs in enumerate((first, second)):
        for half in range(2):
            for copy in stores(pairs, phase, half):
                copy.wait()


def gather_stage(tokens, grads, vec, w_in, w_conv, w_out):
    rows = tokens.shape[0]
    shape = jax.ShapeDtypeStruct
    vmem = pl.BlockSpec(memory_space=pltpu.VMEM)
    wide, slim, column = (rows, 1280), (rows, 640), (rows, 128)
    *results, conv_full, out_full, s0, s1, s2, s3, s4, s5 = pl.pallas_call(
        gather_kernel,
        in_specs=[HBM] * 2 + [vmem] * 4,
        out_specs=[HBM] * 8 + [vmem] + [HBM] * 9,
        out_shape=[
            shape(wide, BF16), shape(wide, BF16), shape(wide, BF16), shape(column, F32),
            shape(slim, BF16), shape(slim, BF16), shape(column, F32), shape(slim, BF16),
            shape((16, 1280), F32),
            shape((1280, 640), BF16), shape((KSIZE, LEVELS, 4, 40, 640), BF16), shape((LEVELS, 4, 40, 1280), BF16),
            shape((1024, 640), BF16), shape((1024, 640), BF16), shape((1024, 640), BF16), shape((1024, 128), F32),
            shape((1024, 1280), BF16), shape((1024, 1280), BF16),
        ],
        scratch_shapes=[
            pltpu.VMEM((DEVICES, 2, 128), F32),
            pltpu.VMEM((1280, 640), BF16),
            pltpu.VMEM((KSIZE, 20, 640), BF16),
            pltpu.VMEM((20, 1280), BF16),
            pltpu.VMEM((KSIZE, 40, 640), BF16),
            pltpu.VMEM((40, 1280), BF16),
            pltpu.VMEM(wide, BF16),
            pltpu.VMEM(wide, BF16),
            pltpu.VMEM(wide, BF16),
            pltpu.VMEM(wide, BF16),
            pltpu.VMEM(column, F32),
            pltpu.VMEM(slim, BF16),
            pltpu.VMEM(slim, BF16),
            pltpu.VMEM(column, F32),
            pltpu.VMEM(slim, BF16),
            pltpu.SemaphoreType.DMA((rows // TILE,)),
            pltpu.SemaphoreType.DMA((2, 2, 4)),
            pltpu.SemaphoreType.DMA((6,)),
            pltpu.SemaphoreType.DMA((6,)),
            pltpu.SemaphoreType.DMA((3,)),
            pltpu.SemaphoreType.DMA((1 + LEVELS,)),
            pltpu.SemaphoreType.DMA((5, PART_COUNT)),
            pltpu.SemaphoreType.DMA((LEVELS, 4, PART_COUNT)),
            pltpu.SemaphoreType.DMA((4, PART_COUNT)),
            pltpu.SemaphoreType.DMA((2,)),
            pltpu.SemaphoreType.DMA((2,)),
            pltpu.SemaphoreType.DMA((PART_COUNT,)),
            pltpu.SemaphoreType.DMA((1,)),
        ],
        compiler_params=pltpu.CompilerParams(
            collective_id=0, has_side_effects=True, vmem_limit_bytes=VMEM_BYTES,
        ),
        name="gather_stage",
    )(tokens, grads, vec, w_in, w_conv, w_out)
    return *results, conv_full.reshape(KSIZE, 640, 640), out_full.reshape(640, 1280), (s0, s1, s2, s3, s4, s5)


def pack_vectors(ln1_gain, ln1_bias, b_in, ln2_gain, ln2_bias, b_conv, ln3_gain, ln3_bias, b_out, lengths):
    total = None
    for plane, pieces in enumerate(
        (
            zip((ln1_gain, ln1_bias, b_out, lengths), WIDE_OFFSETS + (LENGTH_LANE,)),
            zip((b_in, ln2_gain, ln2_bias, b_conv, ln3_gain, ln3_bias), SLIM_OFFSETS),
        )
    ):
        for piece, offset in pieces:
            line = piece.astype(F32)[None]
            placed = lax.pad(line, jnp.float32(0), ((plane, 1 - plane, 0), (offset, 128 - offset - piece.shape[0], 0)))
            total = placed if total is None else total + placed
    return total


PAD = 32
SPAN = 1024 + 2 * PAD
HALO = 16
LENGTH_LANE = 120


def tile_share(lengths):
    own_first, own_second, twin_first, twin_second = (lax.div(length + TILE - 1, TILE) for length in lengths)
    excess = own_first + own_second - twin_first - twin_second
    give = jnp.minimum(lax.div(jnp.maximum(excess, 0), 2), own_second)
    take = jnp.minimum(lax.div(jnp.maximum(-excess, 0), 2), twin_second)
    return own_first, own_second, twin_second, give, take


def read_lengths(vectors):
    lane = lax.broadcasted_iota(jnp.int32, (1, 128), 1)
    return [
        jnp.sum(jnp.where(lane == LENGTH_LANE + index, vectors[pl.ds(row, 1), pl.ds(0, 128)], 0.0)).astype(jnp.int32)
        for row in (9, 10)
        for index in range(2)
    ]


def middle_kernel(
    vectors, u2_hbm, xh2_hbm, slope2_hbm, scale2_hbm, grads_hbm, tokens_hbm, conv_hbm, last_hbm,
    u2_twin, xh2_twin, slope2_twin, scale2_twin, grads_twin, tokens_twin,
    out_hbm, dh1_hbm, out_twin, dh1_twin, d_conv_hbm, d_last_hbm, sums_out,
    conv, conv_t, last, last_t, u2, dh2, grads, tokens, xh2, slope2, scale2, d_conv, d_last, zeros,
    u2_sem, row_sem, back_sem, weight_sem, out_sem, dh1_sem, flush_sem,
):
    segments = 3
    tiles = 1024 // TILE
    wide, slim = 1280, 640
    lengths = read_lengths(vectors)
    first_tiles, second_tiles, twin_tiles, give, take = tile_share(lengths)

    def pick(segment, values):
        return jnp.where(segment == 0, values[0], jnp.where(segment == 1, values[1], values[2]))

    def bounds(segment):
        low = pick(segment, (0, 0, twin_tiles - take))
        high = pick(segment, (first_tiles, second_tiles - give, twin_tiles))
        before = jnp.logical_and(jnp.logical_and(segment == 2, low > 0), high > low).astype(jnp.int32)
        after = jnp.logical_and(jnp.logical_and(segment == 1, give > 0), high > 0).astype(jnp.int32)
        return low, high, before, after

    def live_tiles(segment):
        return pick(segment, (first_tiles, second_tiles, twin_tiles))

    def rows_of(segment, tile):
        return pl.ds(pl.multiple_of(segment * 1024 + tile * TILE, TILE), TILE)

    def padded(segment, row, count, shift=0):
        return pl.ds(pl.multiple_of(segment * SPAN + PAD + row, 8) + shift, count)

    def plain(row, count, shift=0):
        return pl.ds(pl.multiple_of(PAD + row, 8) + shift, count)

    def fetch(segment, tile, own, twin, target, rows, sem):
        @pl.when(segment < 2)
        def _():
            pltpu.make_async_copy(own.at[rows_of(segment, tile), :], target.at[rows, :], sem).start()

        @pl.when(segment == 2)
        def _():
            pltpu.make_async_copy(twin.at[rows_of(0, tile), :], target.at[rows, :], sem).start()

    def fetched(segment, tile, own, target, rows, sem):
        pltpu.make_async_copy(own.at[rows_of(0, tile), :], target.at[rows, :], sem).wait()

    def emit(tile, segment, source, own, twin, sem):
        @pl.when(segment < 2)
        def _():
            pltpu.make_async_copy(source, own.at[rows_of(segment, tile), :], sem).start()

        @pl.when(segment == 2)
        def _():
            pltpu.make_async_copy(source, twin.at[rows_of(0, tile), :], sem).start()

    def u2_at(segment, tile):
        return padded(segment, tile * TILE, TILE)

    row_arrays = ((grads_hbm, grads_twin, grads), (tokens_hbm, tokens_twin, tokens))
    back_arrays = ((xh2_hbm, xh2_twin, xh2), (slope2_hbm, slope2_twin, slope2), (scale2_hbm, scale2_twin, scale2))

    def fetch_rows(segment, tile, index):
        own, twin, target = row_arrays[index]
        fetch(segment, tile, own, twin, target, rows_of(segment, tile), row_sem.at[index, segment, tile])

    def rows_fetched(segment, tile, index):
        own, _, target = row_arrays[index]
        fetched(segment, tile, own, target, rows_of(segment, tile), row_sem.at[index, segment, tile])

    def fetch_u2(segment):
        low, high, before, after = bounds(segment)

        def one(tile, _):
            fetch(segment, tile, u2_hbm, u2_twin, u2, u2_at(segment, tile), u2_sem.at[segment, tile])
            return 0

        lax.fori_loop(low - before, high + after, one, 0)

    def out_store(segment, tile):
        emit(tile, segment, tokens.at[rows_of(segment, tile), :], out_hbm, out_twin, out_sem.at[segment, tile])

    def dh1_store(segment, tile, source):
        emit(tile, segment, source, dh1_hbm, dh1_twin, dh1_sem.at[segment, tile])

    conv_load = pltpu.make_async_copy(conv_hbm, conv, weight_sem.at[0])
    last_load = pltpu.make_async_copy(last_hbm, last, weight_sem.at[1])
    last_flush = pltpu.make_async_copy(last, d_last_hbm, flush_sem.at[0])

    fetch_u2(0)
    conv_load.start()
    last_load.start()

    def load_rows(segment, _):
        pl.when(segment > 0)(lambda: fetch_u2(segment))
        low, high, before, after = bounds(segment)

        def one(tile, _):
            fetch_rows(segment, tile, 0)
            pl.when(jnp.logical_and(tile >= low, tile < high))(lambda: fetch_rows(segment, tile, 1))
            return 0

        lax.fori_loop(low - before, high + after, one, 0)
        return 0

    def load_back(segment, _):
        low, high, _, _ = bounds(segment)

        def one(tile, _):
            for index, (own, twin, target) in enumerate(back_arrays):
                fetch(segment, tile, own, twin, target, rows_of(segment, tile), back_sem.at[index, segment, tile])
            return 0

        lax.fori_loop(low, high, one, 0)
        return 0

    lax.fori_loop(0, segments, load_rows, 0)
    lax.fori_loop(0, segments, load_back, 0)
    zeros[...] = jnp.zeros_like(zeros)

    def idle(segment, _):
        low, high, _, _ = bounds(segment)

        def one(tile, _):
            pl.when(jnp.logical_or(tile < low, tile >= high))(lambda: dh1_store(segment, tile, zeros))
            dead = jnp.logical_and(segment < 2, tile >= live_tiles(segment))
            pl.when(dead)(lambda: fetch_rows(segment, tile, 1))
            return 0

        lax.fori_loop(0, tiles, one, 0)
        return 0

    lax.fori_loop(0, segments, idle, 0)

    sums_out[...] = jnp.zeros_like(sums_out)

    def clear(index, _):
        rows = pl.ds(pl.multiple_of(index * 64, 64), 64)
        d_last[rows, :] = jnp.zeros((64, wide), F32)
        for tap in range(KSIZE):
            d_conv[tap, rows, :] = jnp.zeros((64, slim), F32)
        return 0

    lax.fori_loop(0, slim // 64, clear, 0)

    def vector(index, width=slim):
        return vectors[pl.ds(index, 1), pl.ds(0, width)]

    def add_sum(index, values):
        width = values.shape[1]
        sums_out[pl.ds(index * 8, 8), pl.ds(0, width)] += jnp.sum(
            values.reshape(values.shape[0] // 8, 8, width), axis=0
        )

    edge = jnp.zeros((PAD, slim), BF16)

    def one_segment(segment, _):
        low, high, before, after = bounds(segment)
        count = live_tiles(segment)
        length = pick(segment, (lengths[0], lengths[1], lengths[3]))

        def live_rows(row, size):
            position = lax.broadcasted_iota(jnp.int32, (size, 128), 0) + row
            return (position < length).astype(F32)

        def prepare(tile, _):
            fetched(segment, tile, u2_hbm, u2, u2_at(segment, tile), u2_sem.at[segment, tile])
            return 0

        lax.fori_loop(low - before, high + after, prepare, 0)

        @pl.when(low == 0)
        def _():
            u2[padded(segment, -PAD, PAD), :] = edge

        dh2[plain(low * TILE - PAD, PAD), :] = edge
        dh2[plain(high * TILE, PAD), :] = edge

        @pl.when(jnp.logical_and(high > low, high + after == count))
        def _():
            tail = u2_at(segment, count - 1)
            u2[tail, :] = (u2[tail, :].astype(F32) * lanes(live_rows((count - 1) * TILE, TILE), slim)).astype(BF16)
            u2[padded(segment, count * TILE, PAD), :] = edge

        @pl.when(segment == 0)
        def _():
            conv_load.wait()
            last_load.wait()
            last_t[...] = last[...].T

            def turn(tap, _):
                conv_t[tap] = conv[tap].T
                return 0

            lax.fori_loop(0, KSIZE, turn, 0)

        def forward_rows(row, size, whole):
            rows = pl.ds(pl.multiple_of(segment * 1024 + row, HALO), size)
            live = live_rows(row, size)
            hidden = jnp.dot(u2[padded(segment, row, size, -16), :], conv[0], preferred_element_type=F32)
            for tap in range(1, KSIZE):
                hidden += jnp.dot(
                    u2[padded(segment, row, size, (tap - 2) * DILATION), :], conv[tap], preferred_element_type=F32
                )
            gz = (grads[rows, :].astype(F32) * lanes(live, wide)).astype(BF16)
            back = jnp.dot(gz, last_t[...], preferred_element_type=F32)
            norm, scale = norm_parts(hidden + vector(6))
            act, slope = gelu_parts(norm * vector(7) + vector(8))
            slope_grad = back * slope
            err = slope_grad * vector(7)
            mean = jnp.sum(err, axis=1, keepdims=True) * (1.0 / slim)
            along = jnp.sum(err * norm, axis=1, keepdims=True) * (1.0 / slim)
            low_grad = (scale * (err - mean - norm * along)).astype(BF16)
            dh2[plain(row, size), :] = low_grad
            if whole:
                u3 = act.astype(BF16)
                branch = jnp.dot(u3, last[...], preferred_element_type=F32) + vector(2, wide)
                tokens[rows, :] = (tokens[rows, :].astype(F32) + lanes(live, wide) * branch).astype(BF16)
                d_last[...] += lax.dot_general(u3, gz, (((0,), (0,)), ((), ())), preferred_element_type=F32)
                add_sum(2, gz.astype(F32))
                add_sum(7, slope_grad * norm)
                add_sum(8, slope_grad)
                add_sum(6, low_grad.astype(F32))

        def forward(tile, _):
            rows_fetched(segment, tile, 0)
            rows_fetched(segment, tile, 1)
            forward_rows(tile * TILE, TILE, True)
            out_store(segment, tile)
            return 0

        lax.fori_loop(low, high, forward, 0)

        @pl.when(before + after > 0)
        def _():
            tile = jnp.where(before > 0, low - 1, high)
            rows_fetched(segment, tile, 0)
            forward_rows(jnp.where(before > 0, low * TILE - HALO, high * TILE), HALO, False)

        def dead_store(tile, _):
            rows_fetched(segment, tile, 1)
            out_store(segment, tile)
            return 0

        lax.fori_loop(jnp.where(segment < 2, count, tiles), tiles, dead_store, 0)

        @pl.when(segment == segments - 1)
        def _():
            last[...] = d_last[...].astype(BF16)
            last_flush.start()

        def backward(tile, _):
            rows = rows_of(segment, tile)
            for index, (own, twin, target) in enumerate(back_arrays):
                fetched(segment, tile, own, target, rows, back_sem.at[index, segment, tile])
            live = lanes(live_rows(tile * TILE, TILE), slim)
            source_t = u2[u2_at(segment, tile), :].T
            total = None
            for tap in range(KSIZE):
                window = dh2[plain(tile * TILE, TILE, (2 - tap) * DILATION), :]
                term = jnp.dot(window, conv_t[tap], preferred_element_type=F32)
                total = term if total is None else total + term
                d_conv[tap] += jnp.dot(source_t, window, preferred_element_type=F32)
            norm = xh2[rows, :].astype(F32)
            slope_grad = total * live * slope2[rows, :].astype(F32)
            add_sum(4, slope_grad * norm)
            add_sum(5, slope_grad)
            err = slope_grad * vector(4)
            mean = jnp.sum(err, axis=1, keepdims=True) * (1.0 / slim)
            along = jnp.sum(err * norm, axis=1, keepdims=True) * (1.0 / slim)
            low_grad = (lanes(scale2[rows, :], slim) * (err - mean - norm * along)).astype(BF16)
            add_sum(3, low_grad.astype(F32))
            slope2[rows, :] = low_grad
            dh1_store(segment, tile, slope2.at[rows, :])
            return 0

        lax.fori_loop(low, high, backward, 0)
        return 0

    lax.fori_loop(0, segments, one_segment, 0)

    def conv_flush(tap):
        return pltpu.make_async_copy(conv.at[tap], d_conv_hbm.at[tap], flush_sem.at[tap + 1])

    def flush(tap, _):
        conv[tap] = d_conv[tap].astype(BF16)
        conv_flush(tap).start()
        return 0

    lax.fori_loop(0, KSIZE, flush, 0)

    def stored(segment, _):
        low, high, _, _ = bounds(segment)

        def one(tile, _):
            pltpu.make_async_copy(zeros, dh1_hbm.at[rows_of(0, tile), :], dh1_sem.at[segment, tile]).wait()
            worked = jnp.logical_and(tile >= low, tile < high)
            dead = jnp.logical_and(segment < 2, tile >= live_tiles(segment))

            @pl.when(jnp.logical_or(worked, dead))
            def _():
                pltpu.make_async_copy(
                    tokens.at[rows_of(0, tile), :], out_hbm.at[rows_of(0, tile), :], out_sem.at[segment, tile]
                ).wait()

            return 0

        lax.fori_loop(0, tiles, one, 0)
        return 0

    lax.fori_loop(0, segments, stored, 0)
    for copy in [last_flush] + [conv_flush(tap) for tap in range(KSIZE)]:
        copy.wait()


def middle_stage(vectors, u2, xh2, slope2, scale2, grads, tokens, w_conv, w_out, twins):
    rows = u2.shape[0]
    shape = jax.ShapeDtypeStruct
    vmem = pl.BlockSpec(memory_space=pltpu.VMEM)
    tiles = 1024 // TILE
    held = 3 * 1024
    return pl.pallas_call(
        middle_kernel,
        in_specs=[vmem] + [HBM] * 14,
        out_specs=[HBM] * 6 + [vmem],
        out_shape=[
            shape((rows, 1280), BF16), shape((rows, 640), BF16), shape((1024, 1280), BF16), shape((1024, 640), BF16),
            shape((KSIZE, 640, 640), BF16), shape((640, 1280), BF16), shape((72, 1280), F32),
        ],
        scratch_shapes=[
            pltpu.VMEM((KSIZE, 640, 640), BF16),
            pltpu.VMEM((KSIZE, 640, 640), BF16),
            pltpu.VMEM((640, 1280), BF16),
            pltpu.VMEM((1280, 640), BF16),
            pltpu.VMEM((3 * SPAN, 640), BF16),
            pltpu.VMEM((SPAN, 640), BF16),
            pltpu.VMEM((held, 1280), BF16),
            pltpu.VMEM((held, 1280), BF16),
            pltpu.VMEM((held, 640), BF16),
            pltpu.VMEM((held, 640), BF16),
            pltpu.VMEM((held, 128), F32),
            pltpu.VMEM((KSIZE, 640, 640), F32),
            pltpu.VMEM((640, 1280), F32),
            pltpu.VMEM((TILE, 640), BF16),
            pltpu.SemaphoreType.DMA((3, tiles)),
            pltpu.SemaphoreType.DMA((2, 3, tiles)),
            pltpu.SemaphoreType.DMA((3, 3, tiles)),
            pltpu.SemaphoreType.DMA((2,)),
            pltpu.SemaphoreType.DMA((3, tiles)),
            pltpu.SemaphoreType.DMA((3, tiles)),
            pltpu.SemaphoreType.DMA((6,)),
        ],
        compiler_params=pltpu.CompilerParams(vmem_limit_bytes=VMEM_BYTES),
        name="middle_stage",
    )(vectors, u2, xh2, slope2, scale2, grads, tokens, w_conv, w_out, *twins)


def pack_sums(plane, lines, offsets, packed_ref):
    width, chunk = ((1280, 40), (640, 20))[plane]
    owner, slot, row = chunk_masks(width, chunk)
    total = packed_ref[:, :, plane, :].reshape(DEVICES, 128)
    for line, offset in zip(lines, offsets):
        pick = (slot + offset == row).astype(F32).astype(BF16)
        spread = jnp.where(owner, jnp.broadcast_to(line, owner.shape), 0.0)
        for _ in range(3):
            term = spread.astype(BF16)
            spread = spread - term.astype(F32)
            total += lax.dot_general(term, pick, (((1,), (1,)), ((), ())), preferred_element_type=F32)
    packed_ref[:, :, plane, :] = total.reshape(LEVELS, 8, 128)


SCATTER_BY_Y = (False, True, False)
LINE_FIRST = (False, False, True)
SCATTER_PLAN = (
    (),
    (),
    (),
    (
        ("load", 1), ("twin", 1, "far"), ("first", 1, 3), ("first", 1, 2),
    ),
    (
        ("load", 2), ("twin", 2, "y"), ("line", 2, "y", 3), ("ready",), ("twin", 2, "far"), ("line", 2, "far", 3),
        ("twin", 2, "own"), ("line", 2, "own", 3), ("twin", 2, "x"), ("line", 2, "x", 3), ("twin", 1, "y"),
        ("direct", 1, 3), ("first", 1, 1), ("twin", 1, "x"), ("second", 1, 3),
    ),
    (),
    (
        ("line", 2, "y", 2), ("twin", 0, "far"), ("first", 0, 2), ("twin", 0, "x"), ("direct", 0, 1),
        ("line", 2, "far", 2), ("first", 0, 3), ("direct", 1, 2), ("first", 0, 0), ("twin", 1, "own"),
        ("line", 1, "own", 3), ("direct", 0, 3), ("line", 2, "own", 2),
    ),
    (
        ("second", 1, 2), ("line", 2, "x", 2), ("twin", 0, "y"), ("second", 0, 3), ("first", 0, 1), ("first", 1, 0),
        ("line", 2, "y", 1), ("direct", 0, 2), ("line", 2, "far", 1), ("second", 0, 2), ("twin", 0, "own"),
        ("line", 0, "own", 3), ("second", 1, 1), ("direct", 1, 1), ("direct", 0, 0), ("line", 1, "own", 2),
    ),
    (
        ("line", 2, "x", 1), ("second", 0, 1), ("second", 0, 0), ("line", 2, "own", 1), ("plane", 2, "F"),
        ("line", 0, "own", 2), ("second", 1, 0), ("direct", 1, 0),
    ),
    (
        ("line", 1, "own", 1),
    ),
    (
        ("plane", 2, "D"), ("plane", 2, "S"), ("line", 0, "own", 1),
    ),
    (),
    (
        ("done", 2), ("done", 1), ("done", 0), ("vec_start",), ("vec_middle",), ("vec_end",), ("finish",),
    ),
)


def scatter_kernel(
    u1_hbm, dh1_hbm, slope1_hbm, xh1_hbm, scale1_hbm, grads_hbm, w_in_hbm, vectors, sums, d_conv_hbm, d_last_hbm, d_conv_flat, d_last_flat, dh1_share, out_share,
    grad_tokens, g_in, g_conv, g_last, g_vec, out_back,
    u1, dh1, slope1, xh1, scale1, grads, w_in, w_in_t, dh1_back, d_in_sum, d_in, own_sums, packed, plane_box, level_box,
    conv_own, conv_twin, conv_far, conv_x, conv_y, conv_line, conv_done, conv_swap,
    last_own, last_twin, last_far, last_x, last_y, last_line, last_done, last_swap,
    in_twin, in_far, in_x, in_y, in_line,
    tile_sem, weight_sem, store_sem, vec_sem, load_sem, twin_send, twin_recv, send_sem, move_recv, line_recv,
    swap_send, swap_recv, back_send, back_recv,
):
    steps, weight_steps = 2048 // TILE, 4
    z, y, x, core = place()
    columns = {"own": 2 * y + x, "x": 2 * y + (1 - x), "y": 2 * (1 - y) + x, "far": 2 * (1 - y) + (1 - x)}
    boxes = {"far": (in_far, conv_far, last_far), "x": (in_x, conv_x, last_x), "y": (in_y, conv_y, last_y)}
    line_boxes = (in_line, conv_line, last_line)
    links = {
        "x": lambda: device(z, y, 1 - x, core), "y": lambda: device(z, 1 - y, x, core),
        "twin": lambda: device(z, y, x, 1 - core),
    }

    def remote(src, dst, send, recv, link):
        return pltpu.make_async_remote_copy(
            src_ref=src, dst_ref=dst, send_sem=send, recv_sem=recv, device_id=links[link]() if isinstance(link, str) else device(z + link, y, x, core), device_id_type=MESH
        )

    def cut(side, part):
        return (None, CONV_COLS[side], OUT_COLS[side])[part]

    def narrow(side, part):
        return pl.ds(0, 640 if part == 0 else cut(side, part)[1])

    def own_at(side, part, level, column):
        if part == 0:
            return d_in.at[level, column, side]
        if part == 1:
            return conv_own.at[:, level, column, :, narrow(side, part)]
        return last_own.at[level, column, :, narrow(side, part)]

    def twin_at(side, part, level, column):
        if part == 0:
            return in_twin.at[level, column]
        if part == 1:
            return conv_twin.at[:, level, column, :, narrow(side, part)]
        return last_twin.at[level, column, :, narrow(side, part)]

    def box_at(side, part, name, level):
        box = boxes[name][part]
        if part == 0:
            return box.at[level]
        if part == 1:
            return box.at[level, :, :, narrow(side, part)]
        return box.at[level, :, narrow(side, part)]

    def way_of(sign):
        return lax.shift_right_logical(1 - sign, 1) if not isinstance(sign, int) else (1 - sign) // 2

    def line_at(side, part, kind, sign, level):
        way = way_of(sign)
        if part == 0:
            return in_line.at[way, level]
        if part == 1:
            return conv_line.at[way, level, :, :, narrow(side, part)]
        return last_line.at[KINDS.index(kind), way, level, :, narrow(side, part)]

    def all_units(side, part, count):
        rows = pl.ds(0, 40 * count)
        if part == 0:
            return w_in_hbm.at[rows, :]
        if part == 1:
            return d_conv_flat.at[:, rows, pl.ds(*cut(side, part))]
        return d_last_flat.at[rows, pl.ds(*cut(side, part))]

    def load(side, part):
        source = (d_conv_hbm.at[:, :, :, :, pl.ds(*cut(side, 1))], d_last_hbm.at[:, :, :, pl.ds(*cut(side, 2))])
        target = (conv_own.at[:, :, :, :, narrow(side, 1)], last_own.at[:, :, :, narrow(side, 2)])
        return pltpu.make_async_copy(source[part - 1], target[part - 1], load_sem.at[part - 1])

    def twin_copy(part, kind, to_side):
        column = columns[kind]
        if part == 0:
            src, dst = d_in.at[:, column, to_side], in_twin.at[:, column]
        elif part == 1:
            src = d_conv_hbm.at[:, :, column, :, pl.ds(*cut(to_side, part))]
            dst = conv_twin.at[:, :, column, :, narrow(to_side, part)]
        else:
            src = d_last_hbm.at[:, column, :, pl.ds(*cut(to_side, part))]
            dst = last_twin.at[:, column, :, narrow(to_side, part)]
        return remote(src, dst, twin_send.at[part], twin_recv.at[part, KINDS.index(kind)], "twin")

    def exchange(side, part):
        for kind in ("far", "y", "x", "own"):
            twin_copy(part, kind, 1 - side).start()

    def take_twin(side, part, kind):
        twin_copy(part, kind, side).wait_recv()

    def move(side, part, kind, level, link, box):
        return remote(
            own_at(side, part, level, columns[kind]), box_at(side, part, box, level),
            send_sem.at[part], move_recv.at[("far", "x", "y").index(box), part, level], link,
        )

    def line(side, part, kind, level, sign):
        return remote(
            own_at(side, part, level, columns[kind]), line_at(side, part, kind, sign, level),
            send_sem.at[part], line_recv.at[KINDS.index(kind), way_of(sign), part, level], sign,
        )

    def read(ref):
        return ref[...].astype(F32)

    def each_level(distance, act):
        if distance == 0:
            act(z, 0)
            return

        def one(index, _):
            sign = 1 - 2 * index
            level = z + sign * distance
            pl.when(jnp.logical_and(level >= 0, level < LEVELS))(lambda: act(level, sign))
            return 0

        lax.fori_loop(0, 2, one, 0)

    def both_terms(side, part, level, kind):
        column = columns[kind]
        return read(own_at(side, part, level, column)) + read(twin_at(side, part, level, column))

    def put(side, part, level, kind, value):
        own_at(side, part, level, columns[kind])[...] = value.astype(BF16)

    def roles(part):
        return ("y", "x") if SCATTER_BY_Y[part] else ("x", "y")

    def first(side, part, distance):
        def one(level, sign):
            put(side, part, level, "far", both_terms(side, part, level, "far"))
            move(side, part, "far", level, roles(part)[0], "far").start()

        each_level(distance, one)

    def direct(side, part, distance):
        name = roles(part)[0]

        def one(level, sign):
            put(side, part, level, name, both_terms(side, part, level, name))
            move(side, part, name, level, name, name).start()

        each_level(distance, one)

    def second(side, part, distance):
        link, name = roles(part)

        def one(level, sign):
            move(side, part, "far", level, link, "far").wait_recv()
            put(side, part, level, name, both_terms(side, part, level, name) + read(box_at(side, part, "far", level)))
            move(side, part, name, level, name, name).start()

        each_level(distance, one)

    def line_hop(side, part, kind, distance):
        def one(level, sign):
            total = None
            if not LINE_FIRST[part]:
                for name in ("x", "y"):
                    move(side, part, name, level, name, name).wait_recv()
                total = read(box_at(side, part, "x", level)) + read(box_at(side, part, "y", level))
            terms = both_terms(side, part, level, kind)
            total = terms if total is None else terms + total
            behind = jnp.logical_and(z - sign >= 0, z - sign < LEVELS)

            @pl.when(behind)
            def _():
                line(side, part, kind, level, sign).wait_recv()
                put(side, part, level, kind, total + read(line_at(side, part, kind, sign, level)))

            @pl.when(jnp.logical_not(behind))
            def _():
                put(side, part, level, kind, total)

            line(side, part, kind, level, sign).start()

        each_level(distance, one)

    def add_lines(side, part, kind, target):
        for sign, guard in ((1, z > 0), (-1, z < LEVELS - 1)):

            @pl.when(guard)
            def _(sign=sign):
                line(side, part, kind, z, sign).wait_recv()
                target[...] = (
                    target[...].astype(F32) + read(line_at(side, part, kind, sign, z))
                ).astype(target.dtype)

    def plane(side, part, what):
        link, other = roles(part)
        kind = {"F": "far", "D": link, "S": other}[what]
        own = own_at(side, part, z, columns[kind])
        keep = last_done.at[:, narrow(side, part)]
        keep[...] = both_terms(side, part, z, kind)
        add_lines(side, part, kind, keep)
        if what == "S":
            move(side, part, "far", z, link, "far").wait_recv()
            keep[...] += read(box_at(side, part, "far", z))
        own[...] = keep[...].astype(BF16)
        if what == "F":
            move(side, part, "far", z, link, "far").start()
        else:
            move(side, part, kind, z, kind, kind).start()

    def done(side, part):
        if part == 0:
            target = g_in
        elif part == 1:
            target = conv_done.at[:, :, narrow(side, part)]
        else:
            target = last_done.at[:, narrow(side, part)]
        for name in ("x", "y"):
            move(side, part, name, z, name, name).wait_recv()
        target[...] = (
            both_terms(side, part, z, "own") + read(box_at(side, part, "x", z)) + read(box_at(side, part, "y", z))
        )
        add_lines(side, part, "own", target)
        if part:
            swap(part, side).start()

    def swap(part, from_side):
        lanes_ = narrow(from_side, part)
        if part == 1:
            src, dst = conv_done.at[:, :, lanes_], conv_swap.at[:, :, lanes_]
        else:
            src, dst = last_done.at[:, lanes_], last_swap.at[:, lanes_]
        return remote(src, dst, swap_send.at[part - 1], swap_recv.at[part - 1], "twin")

    def finish(side):
        first_row, count = side * 20, 20
        for part, mine, other, target in ((2, last_done, last_swap, g_last), (1, conv_done, conv_swap, g_conv)):
            swap(part, 1 - side).wait_recv()
            for refs, owner in ((mine, side), (other, 1 - side)):
                start, width = cut(owner, part)
                if part == 1:
                    target[:, :, pl.ds(start, width)] = refs[:, pl.ds(first_row, count), pl.ds(0, width)]
                else:
                    target[:, pl.ds(start, width)] = refs[pl.ds(first_row, count), pl.ds(0, width)]
        for part in range(3):
            if part:
                swap(part, side).wait_send()
            view = all_units(1 - side, part, CHIPS)
            remote(view, view, twin_send.at[part], twin_recv.at[part, 0], "twin").wait_send()
            view = all_units(side, part, CHIPS - 1)
            remote(view, view, send_sem.at[part], twin_recv.at[part, 0], "twin").wait_send()


    def in_plane():
        return y * 4 + x * 2 + core

    def plane_copy(offset):
        other, where = plane_peer(offset)
        return pltpu.make_async_remote_copy(
            src_ref=packed.at[:, other], dst_ref=plane_box.at[in_plane()], send_sem=vec_sem.at[0],
            recv_sem=vec_sem.at[1], device_id=where, device_id_type=MESH,
        )

    def level_copy(step):
        level = lax.rem(z + step, LEVELS)
        return pltpu.make_async_remote_copy(
            src_ref=plane_box.at[0, level], dst_ref=level_box.at[z], send_sem=vec_sem.at[2], recv_sem=vec_sem.at[3],
            device_id=device(level, y, x, core), device_id_type=MESH,
        )

    def sum_lines(ref, indices, width):
        return [jnp.sum(ref[pl.ds(8 * index, 8), pl.ds(0, width)], axis=0, keepdims=True) for index in indices]

    def vec_early():
        packed[...] = jnp.zeros_like(packed)
        pack_sums(0, sum_lines(sums, (2,), 1280), WIDE_OFFSETS[2:], packed)
        pack_sums(1, sum_lines(sums, range(3, 9), 640), SLIM_OFFSETS, packed)

    def vec_start(side):
        pack_sums(0, sum_lines(own_sums, (0, 1), 1280), WIDE_OFFSETS[:2], packed)
        for offset in range(1, 8):
            plane_copy(offset).start()
        for level in range(LEVELS):
            plane_box[pl.ds(in_plane(), 1), level] = packed[level, pl.ds(in_plane(), 1)]

    def vec_middle(side):
        view = plane_box.at[pl.ds(0, 7)]
        remote(view, view, vec_sem.at[0], vec_sem.at[1], "twin").wait()
        total = jnp.sum(plane_box[...], axis=0)
        plane_box[0] = total
        level_box[pl.ds(z, 1)] = plane_box[0, pl.ds(z, 1)]
        for step in range(1, LEVELS):
            level_copy(step).start()

    def vec_end(side):
        view = level_box.at[pl.ds(0, LEVELS - 1)]
        remote(view, view, vec_sem.at[2], vec_sem.at[3], "twin").wait()
        g_vec[...] = jnp.sum(level_box[...], axis=0)

    def ready(side):
        d_in[...] = d_in_sum[...].astype(BF16).reshape(d_in.shape)
        exchange(side, 0)

    actions = {
        "load": lambda side, part: load(side, part).wait(), "twin": take_twin, "first": first, "direct": direct,
        "second": second, "line": line_hop, "plane": plane, "done": done, "ready": ready, "vec_start": vec_start,
        "vec_middle": vec_middle, "vec_end": vec_end, "finish": finish,
    }

    def either(event):
        return event[0] in ("ready", "vec_start", "vec_middle", "vec_end") or event[1:2] == (0,)

    def perform(events):
        for alike, group in itertools.groupby(events, either):
            group = tuple(group)
            if alike:
                for event in group:
                    actions[event[0]](core, *event[1:])
                continue
            for side in range(2):

                @pl.when(core == side)
                def _(side=side, group=group):
                    for event in group:
                        actions[event[0]](side, *event[1:])

    def rows_of(tile):
        return pl.ds(pl.multiple_of(tile * TILE, TILE), TILE)

    tiles_of = ((u1, u1_hbm), (dh1, dh1_hbm), (slope1, slope1_hbm), (xh1, xh1_hbm), (scale1, scale1_hbm), (grads, grads_hbm))

    def half_load(index, half):
        target, source = tiles_of[index]
        rows = pl.ds(half * 1024, 1024)
        return pltpu.make_async_copy(source.at[rows, :], target.at[rows, :], tile_sem.at[index, half])

    def store(tile):
        return pltpu.make_async_copy(grads.at[rows_of(tile), :], grad_tokens.at[rows_of(tile), :], store_sem.at[tile])

    weight_load = pltpu.make_async_copy(w_in_hbm, w_in, weight_sem.at[0])

    barrier = pltpu.get_barrier_semaphore()
    for offset in range(1, 8):
        pl.semaphore_signal(barrier, inc=1, device_id=plane_peer(offset)[1], device_id_type=MESH)
    for step in range(1, LEVELS):
        pl.semaphore_signal(
            barrier, inc=1, device_id=device(lax.rem(z + step, LEVELS), y, x, core), device_id_type=MESH
        )
    for side in range(2):

        @pl.when(core == side)
        def _(side=side):
            for part in (1, 2):
                load(side, part).start()

    for half in range(2):
        half_load(0, half).start()
        half_load(1, half).start()
    weight_load.start()
    pl.semaphore_wait(barrier, 7 + LEVELS - 1)
    back_copies = [
        remote(dh1_share, dh1_back, back_send.at[0], back_recv.at[0], "twin"),
        remote(out_share, out_back, back_send.at[1], back_recv.at[1], "twin"),
    ]
    for side in range(2):

        @pl.when(core == side)
        def _(side=side):
            for kind in ("far", "y", "x", "own"):
                for part in (1, 2):
                    twin_copy(part, kind, 1 - side).start()
                if kind == "far":
                    back_copies[0].start()

    for half in range(2):
        for index in range(2, 6):
            half_load(index, half).start()
    own_sums[...] = jnp.zeros_like(own_sums)
    vec_early()

    def weight_tile(tile, _):
        for index in range(weight_steps):
            if SCATTER_PLAN[index]:
                pl.when(tile == index)(functools.partial(perform, SCATTER_PLAN[index]))
            if index in (0, weight_steps // 2):
                for array in range(2):
                    pl.when(tile == index)(half_load(array, 0 if index == 0 else 1).wait)
        rows = pl.ds(pl.multiple_of(tile * 512, 512), 512)
        pl.when(tile == weight_steps // 2)(back_copies[0].wait)

        @pl.when(tile >= weight_steps // 2)
        def _():
            again = pl.ds(pl.multiple_of(tile * 512 - 1024, 512), 512)
            dh1[rows, :] = dh1[rows, :] + dh1_back[again, :]

        term = lax.dot_general(u1[rows, :], dh1[rows, :], (((0,), (0,)), ((), ())), preferred_element_type=F32)

        @pl.when(tile == 0)
        def _():
            d_in_sum[...] = term

        @pl.when(tile > 0)
        def _():
            d_in_sum[...] += term

        return 0

    lax.fori_loop(0, weight_steps, weight_tile, 0)
    weight_load.wait()
    w_in_t[...] = w_in[...].T

    def token_tile(tile, _):
        for index in range(steps):
            if SCATTER_PLAN[weight_steps + index]:
                pl.when(tile == index)(functools.partial(perform, SCATTER_PLAN[weight_steps + index]))
            if index == 1:
                pl.when(tile == index)(back_copies[1].start)
            if index in (0, steps // 2):
                for array in range(2, 6):
                    pl.when(tile == index)(half_load(array, 0 if index == 0 else 1).wait)
        rows = rows_of(tile)
        back = jnp.dot(dh1[rows, :], w_in_t[...], preferred_element_type=F32)
        norm = xh1[rows, :].astype(F32)
        slope_grad = back * slope1[rows, :].astype(F32)
        for index, values in enumerate((slope_grad * norm, slope_grad)):
            own_sums[pl.ds(8 * index, 8), :] += jnp.sum(values.reshape(TILE // 8, 8, 1280), axis=0)
        err = slope_grad * vectors[pl.ds(0, 1), :]
        mean = jnp.sum(err, axis=1, keepdims=True) * (1.0 / 1280)
        along = jnp.sum(err * norm, axis=1, keepdims=True) * (1.0 / 1280)
        grads[rows, :] = (
            grads[rows, :].astype(F32) + lanes(scale1[rows, :], 1280) * (err - mean - norm * along)
        ).astype(BF16)
        store(tile).start()
        return 0

    lax.fori_loop(0, steps, token_tile, 0)
    perform(SCATTER_PLAN[weight_steps + steps])
    back_copies[1].wait()
    for tile in range(steps):
        store(tile).wait()


def scatter_stage(u1, dh1, slope1, xh1, scale1, grads, w_in, vectors, sums, d_conv, d_last, dh1_share, out_share):
    rows = u1.shape[0]
    steps = rows // TILE
    shape = jax.ShapeDtypeStruct
    vmem = pl.BlockSpec(memory_space=pltpu.VMEM)
    conv_box = (LEVELS, KSIZE, 40, 384)
    last_box = (LEVELS, 40, 896)
    in_box = (LEVELS, 40, 640)
    dma = pltpu.SemaphoreType.DMA
    return pl.pallas_call(
        scatter_kernel,
        in_specs=[HBM] * 7 + [vmem] * 2 + [HBM] * 6,
        out_specs=[HBM] + [vmem] * 4 + [HBM],
        out_shape=[
            shape((rows, 1280), BF16), shape((40, 640), F32), shape((KSIZE, 20, 640), F32), shape((20, 1280), F32),
            shape((2, 128), F32), shape((1024, 1280), BF16),
        ],
        scratch_shapes=[
            pltpu.VMEM((rows, 1280), BF16),
            pltpu.VMEM((rows, 640), BF16),
            pltpu.VMEM((rows, 1280), BF16),
            pltpu.VMEM((rows, 1280), BF16),
            pltpu.VMEM((rows, 128), F32),
            pltpu.VMEM((rows, 1280), BF16),
            pltpu.VMEM((1280, 640), BF16),
            pltpu.VMEM((640, 1280), BF16),
            pltpu.VMEM((1024, 640), BF16),
            pltpu.VMEM((1280, 640), F32),
            pltpu.VMEM((LEVELS, 4, 2, 40, 640), BF16),
            pltpu.VMEM((16, 1280), F32),
            pltpu.VMEM((LEVELS, 8, 2, 128), F32),
            pltpu.VMEM((8, LEVELS, 2, 128), F32),
            pltpu.VMEM((LEVELS, 2, 128), F32),
            pltpu.VMEM((KSIZE, LEVELS, 4, 40, 384), BF16),
            pltpu.VMEM((KSIZE, LEVELS, 4, 40, 384), BF16),
            pltpu.VMEM(conv_box, BF16),
            pltpu.VMEM(conv_box, BF16),
            pltpu.VMEM(conv_box, BF16),
            pltpu.VMEM((2,) + conv_box, BF16),
            pltpu.VMEM((KSIZE, 40, 384), F32),
            pltpu.VMEM((KSIZE, 40, 384), F32),
            pltpu.VMEM((LEVELS, 4, 40, 896), BF16),
            pltpu.VMEM((LEVELS, 4, 40, 896), BF16),
            pltpu.VMEM(last_box, BF16),
            pltpu.VMEM(last_box, BF16),
            pltpu.VMEM(last_box, BF16),
            pltpu.VMEM((4, 2) + last_box, BF16),
            pltpu.VMEM((40, 896), F32),
            pltpu.VMEM((40, 896), F32),
            pltpu.VMEM((LEVELS, 4, 40, 640), BF16),
            pltpu.VMEM(in_box, BF16),
            pltpu.VMEM(in_box, BF16),
            pltpu.VMEM(in_box, BF16),
            pltpu.VMEM((2,) + in_box, BF16),
            dma((6, 2)), dma((1,)), dma((steps,)), dma((4,)), dma((2,)), dma((3,)), dma((3, 4)),
            dma((3,)), dma((3, 3, LEVELS)), dma((4, 2, 3, LEVELS)), dma((2,)), dma((2,)), dma((2,)), dma((2,)),
        ],
        compiler_params=pltpu.CompilerParams(collective_id=1, has_side_effects=True, vmem_limit_bytes=VMEM_BYTES),
        name="scatter_stage",
    )(
        u1, dh1, slope1, xh1, scale1, grads, w_in, vectors, sums,
        d_conv.reshape(KSIZE, LEVELS, 4, 40, 640), d_last.reshape(LEVELS, 4, 40, 1280), d_conv, d_last, dh1_share, out_share,
    )


def settle_kernel(
    vectors, result_in, out_back, rows_hbm, g_in, g_conv, g_last, g_vec,
    result, rows_out, in_out, conv_out, last_out, *rest
):
    vectors_out, (buffer, moved, load_sem, store_sem, moved_sem) = rest[:9], rest[9:]
    count = buffer.shape[0]
    chunk = buffer.shape[1]
    loads = [
        pltpu.make_async_copy(rows_hbm.at[pl.ds(index * chunk, chunk), :], buffer.at[index], load_sem.at[index])
        for index in range(count)
    ]
    stores = [
        pltpu.make_async_copy(buffer.at[index], rows_out.at[pl.ds(index * chunk, chunk), :], store_sem.at[index])
        for index in range(count)
    ]
    for copy in loads:
        copy.start()
    in_out[...] = g_in[...]
    conv_out[...] = g_conv[...]
    last_out[...] = g_last[...]
    places = [(0, offset, 40) for offset in WIDE_OFFSETS] + [(1, offset, 20) for offset in SLIM_OFFSETS]
    for target, (plane, offset, width) in zip(vectors_out, places):
        target[...] = g_vec[pl.ds(plane, 1), pl.ds(offset, width)]
    _, second_tiles, _, give, _ = tile_share(read_lengths(vectors))
    kept = second_tiles - give

    def moved_load(tile):
        rows = pl.ds(pl.multiple_of(tile * TILE, TILE), TILE)
        return pltpu.make_async_copy(out_back.at[rows, :], moved.at[rows, :], moved_sem.at[0, tile])

    def moved_store(tile):
        rows = pl.ds(pl.multiple_of(tile * TILE, TILE), TILE)
        target = pl.ds(pl.multiple_of(1024 + tile * TILE, TILE), TILE)
        return pltpu.make_async_copy(moved.at[rows, :], result.at[target, :], moved_sem.at[1, tile])

    def each(act):
        def one(tile, _):
            act(tile)
            return 0

        lax.fori_loop(kept, second_tiles, one, 0)

    def pass_moved(tile):
        moved_load(tile).wait()
        moved_store(tile).start()

    each(lambda tile: moved_load(tile).start())
    for load, store in zip(loads, stores):
        load.wait()
        store.start()
    each(pass_moved)
    each(lambda tile: moved_store(tile).wait())
    for copy in stores:
        copy.wait()


def settle_stage(vectors, result, out_back, rows, g_in, g_conv, g_last, g_vec):
    chunks = 8
    shape = jax.ShapeDtypeStruct
    vmem = pl.BlockSpec(memory_space=pltpu.VMEM)
    return pl.pallas_call(
        settle_kernel,
        in_specs=[vmem] + [HBM] * 3 + [vmem] * 4,
        out_specs=[HBM] * 2 + [vmem] * 12,
        out_shape=[shape(v.shape, v.dtype) for v in (result, rows, g_in, g_conv, g_last)]
        + [shape((1, 40), F32)] * 3
        + [shape((1, 20), F32)] * 6,
        scratch_shapes=[
            pltpu.VMEM((chunks, rows.shape[0] // chunks, rows.shape[1]), rows.dtype),
            pltpu.VMEM((1024, 1280), BF16),
            pltpu.SemaphoreType.DMA((chunks,)),
            pltpu.SemaphoreType.DMA((chunks,)),
            pltpu.SemaphoreType.DMA((2, 1024 // TILE)),
        ],
        input_output_aliases={1: 0},
        compiler_params=pltpu.CompilerParams(vmem_limit_bytes=VMEM_BYTES),
        name="settle_stage",
    )(vectors, result, out_back, rows, g_in, g_conv, g_last, g_vec)


def kernel_body(
    tokens, out_grad, lengths, ln1_gain, ln1_bias, w_in, b_in, ln2_gain, ln2_bias,
    w_conv, b_conv, ln3_gain, ln3_bias, w_out, b_out,
):
    proteins, length_pad, width = tokens.shape
    rows = tokens.reshape(proteins * length_pad, width)
    grads = out_grad.reshape(proteins * length_pad, width)
    vec = pack_vectors(
        ln1_gain, ln1_bias, b_in, ln2_gain, ln2_bias, b_conv, ln3_gain, ln3_bias, b_out, lengths
    )
    u1, slope1, xh1, scale1, xh2, slope2, scale2, u2, vectors, in_full, conv_full, out_full, twins = gather_stage(
        rows, grads, vec, w_in, w_conv, w_out
    )
    result, dh1, out_share, dh1_share, d_conv, d_last, sums = middle_stage(
        vectors, u2, xh2, slope2, scale2, grads, rows, conv_full, out_full, twins
    )
    *owned, out_back = scatter_stage(
        u1, dh1, slope1, xh1, scale1, grads, in_full, vectors, sums, d_conv, d_last, dh1_share, out_share
    )
    result, grad_rows, g_in, g_conv, g_last, *lines = settle_stage(vectors, result, out_back, *owned)
    lines = [line.reshape(line.shape[1]) for line in lines]
    wide, slim = lines[:3], lines[3:]
    return (
        result.reshape(tokens.shape), grad_rows.reshape(tokens.shape),
        wide[0], wide[1], g_in, slim[0], slim[1], slim[2], g_conv, slim[3], slim[4], slim[5], g_last, wide[2],
    )


def layer_norm(values, gain, bias):
    center = values - jnp.mean(values, axis=-1, keepdims=True)
    var_rows = jnp.mean(center * center, axis=-1, keepdims=True)
    return center * lax.rsqrt(var_rows + EPS) * gain + bias


def norm_gelu(values, gain, bias):
    return jax.nn.gelu(layer_norm(values, gain, bias), approximate=False)


def collect(
    ln1_gain,
    ln1_bias,
    w_in,
    b_in,
    ln2_gain,
    ln2_bias,
    w_conv,
    b_conv,
    ln3_gain,
    ln3_bias,
    w_out,
    b_out,
):
    return (
        lax.all_gather(ln1_gain, ("dp", "fsdp"), axis=0, tiled=True),
        lax.all_gather(ln1_bias, ("dp", "fsdp"), axis=0, tiled=True),
        lax.all_gather(w_in, ("dp", "fsdp"), axis=0, tiled=True),
        lax.all_gather(b_in, ("dp", "fsdp"), axis=0, tiled=True),
        lax.all_gather(ln2_gain, ("dp", "fsdp"), axis=0, tiled=True),
        lax.all_gather(ln2_bias, ("dp", "fsdp"), axis=0, tiled=True),
        lax.all_gather(w_conv, ("dp", "fsdp"), axis=1, tiled=True),
        lax.all_gather(b_conv, ("dp", "fsdp"), axis=0, tiled=True),
        lax.all_gather(ln3_gain, ("dp", "fsdp"), axis=0, tiled=True),
        lax.all_gather(ln3_bias, ("dp", "fsdp"), axis=0, tiled=True),
        lax.all_gather(w_out, ("dp", "fsdp"), axis=0, tiled=True),
        lax.all_gather(b_out, ("dp", "fsdp"), axis=0, tiled=True),
    )


def spread(
    term_g1,
    term_b1,
    term_wi,
    term_bi,
    term_g2,
    term_b2,
    term_wc,
    term_bc,
    term_g3,
    term_b3,
    term_wo,
    term_bo,
):
    return (
        lax.psum_scatter(term_g1, ("dp", "fsdp"), scatter_dimension=0, tiled=True),
        lax.psum_scatter(term_b1, ("dp", "fsdp"), scatter_dimension=0, tiled=True),
        lax.psum_scatter(term_wi, ("dp", "fsdp"), scatter_dimension=0, tiled=True),
        lax.psum_scatter(term_bi, ("dp", "fsdp"), scatter_dimension=0, tiled=True),
        lax.psum_scatter(term_g2, ("dp", "fsdp"), scatter_dimension=0, tiled=True),
        lax.psum_scatter(term_b2, ("dp", "fsdp"), scatter_dimension=0, tiled=True),
        lax.psum_scatter(term_wc, ("dp", "fsdp"), scatter_dimension=1, tiled=True),
        lax.psum_scatter(term_bc, ("dp", "fsdp"), scatter_dimension=0, tiled=True),
        lax.psum_scatter(term_g3, ("dp", "fsdp"), scatter_dimension=0, tiled=True),
        lax.psum_scatter(term_b3, ("dp", "fsdp"), scatter_dimension=0, tiled=True),
        lax.psum_scatter(term_wo, ("dp", "fsdp"), scatter_dimension=0, tiled=True),
        lax.psum_scatter(term_bo, ("dp", "fsdp"), scatter_dimension=0, tiled=True),
    )


def dilate(padded, kernel, length_pad):
    total = jnp.zeros((padded.shape[0], length_pad, kernel.shape[2]), jnp.float32)
    for kernel_tap in range(kernel.shape[0]):
        window = padded[:, kernel_tap * DILATION : kernel_tap * DILATION + length_pad]
        total = total + jnp.einsum(
            "pli,io->plo", window, kernel[kernel_tap], preferred_element_type=jnp.float32
        )
    return total


def plain_body(
    tokens,
    out_grad,
    lengths,
    ln1_gain,
    ln1_bias,
    w_in,
    b_in,
    ln2_gain,
    ln2_bias,
    w_conv,
    b_conv,
    ln3_gain,
    ln3_bias,
    w_out,
    b_out,
):
    proteins, length_pad, width = tokens.shape
    row_count = proteins * length_pad
    reach = KSIZE // 2 * DILATION
    positions = lax.broadcasted_iota(jnp.int32, (proteins, length_pad), 1)
    live = (positions < lengths[:, None]).astype(jnp.float32).reshape(row_count, 1)
    full = collect(
        ln1_gain,
        ln1_bias,
        w_in,
        b_in,
        ln2_gain,
        ln2_bias,
        w_conv,
        b_conv,
        ln3_gain,
        ln3_bias,
        w_out,
        b_out,
    )
    (
        gain_one,
        bias_one,
        first_matrix,
        first_bias,
        gain_two,
        bias_two,
        conv_kernel,
        conv_bias,
        gain_three,
        bias_three,
        last_matrix,
        last_bias,
    ) = full
    inner = first_matrix.shape[1]
    row_tokens = tokens.reshape(row_count, width).astype(jnp.float32)
    act_one, pull_one = jax.vjp(
        norm_gelu, row_tokens, gain_one.astype(jnp.float32), bias_one.astype(jnp.float32)
    )
    inner_one = act_one.astype(jnp.bfloat16)
    hidden_one = jnp.dot(
        inner_one, first_matrix, preferred_element_type=jnp.float32
    ) + first_bias.astype(jnp.float32)
    act_two, pull_two = jax.vjp(
        norm_gelu, hidden_one, gain_two.astype(jnp.float32), bias_two.astype(jnp.float32)
    )
    inner_two = (act_two * live).astype(jnp.bfloat16)
    padded_two = jnp.pad(
        inner_two.reshape(proteins, length_pad, inner), ((0, 0), (reach, reach), (0, 0))
    )
    hidden_two = dilate(padded_two, conv_kernel, length_pad).reshape(
        row_count, inner
    ) + conv_bias.astype(jnp.float32)
    act_three, pull_three = jax.vjp(
        norm_gelu, hidden_two, gain_three.astype(jnp.float32), bias_three.astype(jnp.float32)
    )
    inner_three = act_three.astype(jnp.bfloat16)
    branch = jnp.dot(
        inner_three, last_matrix, preferred_element_type=jnp.float32
    ) + last_bias.astype(jnp.float32)
    result = (row_tokens + live * branch).astype(jnp.bfloat16).reshape(proteins, length_pad, width)
    again = collect(
        ln1_gain,
        ln1_bias,
        w_in,
        b_in,
        ln2_gain,
        ln2_bias,
        w_conv,
        b_conv,
        ln3_gain,
        ln3_bias,
        w_out,
        b_out,
    )
    (
        again_g1,
        again_b1,
        back_first,
        again_bi,
        again_g2,
        again_b2,
        back_kernel,
        again_bc,
        again_g3,
        again_b3,
        back_last,
        again_bo,
    ) = again
    pull_one = jax.vjp(
        norm_gelu, row_tokens, again_g1.astype(jnp.float32), again_b1.astype(jnp.float32)
    )[1]
    pull_two = jax.vjp(
        norm_gelu, hidden_one, again_g2.astype(jnp.float32), again_b2.astype(jnp.float32)
    )[1]
    pull_three = jax.vjp(
        norm_gelu, hidden_two, again_g3.astype(jnp.float32), again_b3.astype(jnp.float32)
    )[1]
    grad_rows = out_grad.reshape(row_count, width)
    grad_branch = grad_rows * live.astype(jnp.bfloat16)
    term_wo = jnp.einsum("ri,rd->id", inner_three, grad_branch, preferred_element_type=jnp.float32)
    term_bo = jnp.sum(grad_branch.astype(jnp.float32), axis=0)
    grad_three = jnp.einsum("rd,id->ri", grad_branch, back_last, preferred_element_type=jnp.float32)
    d_hidden_two, term_g3, term_b3 = pull_three(grad_three)
    low_two = d_hidden_two.astype(jnp.bfloat16)
    term_bc = jnp.sum(low_two.astype(jnp.float32), axis=0)
    padded_grad = jnp.pad(
        low_two.reshape(proteins, length_pad, inner), ((0, 0), (reach, reach), (0, 0))
    )
    grad_view = low_two.reshape(proteins, length_pad, inner)
    kernel_terms = []
    grad_two = jnp.zeros((proteins, length_pad, inner), jnp.float32)
    taps = back_kernel.shape[0]
    for kernel_tap in range(taps):
        window = padded_two[:, kernel_tap * DILATION : kernel_tap * DILATION + length_pad]
        kernel_terms.append(
            jnp.einsum("pli,plo->io", window, grad_view, preferred_element_type=jnp.float32)
        )
        mirror = (taps - 1 - kernel_tap) * DILATION
        grad_window = padded_grad[:, mirror : mirror + length_pad]
        grad_two = grad_two + jnp.einsum(
            "plo,io->pli", grad_window, back_kernel[kernel_tap], preferred_element_type=jnp.float32
        )
    term_wc = jnp.stack(kernel_terms, axis=0)
    grad_two = grad_two.reshape(row_count, inner) * live
    d_hidden_one, term_g2, term_b2 = pull_two(grad_two)
    low_one = d_hidden_one.astype(jnp.bfloat16)
    term_wi = jnp.einsum("rd,ri->di", inner_one, low_one, preferred_element_type=jnp.float32)
    term_bi = jnp.sum(low_one.astype(jnp.float32), axis=0)
    grad_one = jnp.einsum("ri,di->rd", low_one, back_first, preferred_element_type=jnp.float32)
    d_tokens, term_g1, term_b1 = pull_one(grad_one)
    grad_tokens = (
        (grad_rows.astype(jnp.float32) + d_tokens)
        .astype(jnp.bfloat16)
        .reshape(proteins, length_pad, width)
    )
    owned = spread(
        term_g1,
        term_b1,
        term_wi,
        term_bi,
        term_g2,
        term_b2,
        term_wc,
        term_bc,
        term_g3,
        term_b3,
        term_wo,
        term_bo,
    )
    return (
        result,
        grad_tokens,
        owned[0],
        owned[1],
        owned[2],
        owned[3],
        owned[4],
        owned[5],
        owned[6],
        owned[7],
        owned[8],
        owned[9],
        owned[10],
        owned[11],
    )


def solution(mesh):
    both = ("dp", "fsdp")
    by_row = P(both)
    in_specs = (
        P(both, None, None), P(both, None, None), by_row, by_row, by_row, P(both, None), by_row, by_row, by_row,
        P(None, both, None), by_row, by_row, by_row, P(both, None), by_row,
    )
    out_specs = (
        P(both, None, None), P(both, None, None), by_row, by_row, P(both, None), by_row, by_row, by_row,
        P(None, both, None), by_row, by_row, by_row, P(both, None), by_row,
    )
    body = kernel_body if (mesh.shape["dp"], mesh.shape["fsdp"]) == (8, 4) else plain_body
    return jax.shard_map(body, mesh=mesh, in_specs=in_specs, out_specs=out_specs, check_vma=False)
```

```python
import functools
import itertools

import jax
import jax.numpy as jnp
from jax import lax
from jax.experimental import pallas as pl
from jax.experimental.pallas import tpu as pltpu
from jax.sharding import PartitionSpec as P

KSIZE = 5
DILATION = 8
EPS = 1e-05
HALF_ROOT = 0.7071067811865476
PHI_SCALE = 0.3989422804014327
F32 = jnp.float32
BF16 = jnp.bfloat16
MESH = pl.DeviceIdType.MESH
VMEM_BYTES = 62 * 2**20
HBM = pl.BlockSpec(memory_space=pl.ANY)
LEVELS = 4
CHIPS = 16
DEVICES = 32
TILE = 256
CONV_COLS = ((0, 384), (384, 256))
OUT_COLS = ((0, 384), (384, 896))
WIDE_OFFSETS = (0, 40, 80)
SLIM_OFFSETS = (0, 20, 40, 60, 80, 100)


def place():
    dp = lax.axis_index("dp")
    fs = lax.axis_index("fsdp")
    return lax.div(dp, 2), lax.rem(dp, 2), lax.div(fs, 2), lax.rem(fs, 2)


def device(z, y, x, core):
    return (z * 2 + y, x * 2 + core)


def chip(z, y, x):
    return (z * 2 + y) * 2 + x


def peer_of(step):
    mine = lax.axis_index("dp") * 4 + lax.axis_index("fsdp")
    other = lax.rem(mine + step, DEVICES)
    return mine, other, (lax.div(other, 4), lax.rem(other, 4))


def greet_all():
    barrier = pltpu.get_barrier_semaphore()

    def greet(step, _):
        _, _, target = peer_of(step)
        pl.semaphore_signal(barrier, inc=1, device_id=target, device_id_type=MESH)
        return 0

    lax.fori_loop(1, DEVICES, greet, 0)
    pl.semaphore_wait(barrier, DEVICES - 1)


def chunk_masks(width, chunk):
    scale = -(-65536 // chunk)
    column = lax.broadcasted_iota(jnp.int32, (DEVICES, width), 1)
    row = lax.broadcasted_iota(jnp.int32, (DEVICES, width), 0)
    owner = lax.shift_right_logical(column * scale, 16) == row
    place_col = lax.broadcasted_iota(jnp.int32, (128, width), 1)
    place_row = lax.broadcasted_iota(jnp.int32, (128, width), 0)
    slot = place_col - lax.shift_right_logical(place_col * scale, 16) * chunk
    return owner, slot, place_row


def unpack_vectors(packed_ref, vectors_ref):
    for plane, (width, chunk, offsets) in enumerate(
        ((1280, 40, WIDE_OFFSETS), (640, 20, SLIM_OFFSETS))
    ):
        owner, slot, row = chunk_masks(width, chunk)
        packed = packed_ref[:, plane, :].astype(BF16)
        for index, offset in enumerate(offsets):
            pick = (slot + offset == row).astype(F32).astype(BF16)
            spread = jnp.dot(packed, pick, preferred_element_type=F32)
            line = jnp.sum(jnp.where(owner, spread, 0.0), axis=0, keepdims=True)
            vectors_ref[pl.ds(plane * 3 + index, 1), pl.ds(0, width)] = line


def lanes(column, width):
    return jnp.concatenate([column] * (width // 128), axis=1)


def norm_parts(values):
    width = values.shape[1]
    mean = jnp.sum(values, axis=1, keepdims=True) * (1.0 / width)
    center = values - mean
    var = jnp.sum(center * center, axis=1, keepdims=True) * (1.0 / width)
    scale = lax.rsqrt(var + EPS)
    return center * scale, scale


def gelu_parts(arg):
    normal = 0.5 + 0.5 * lax.erf(arg * HALF_ROOT)
    slope = normal + arg * (PHI_SCALE * jnp.exp(-0.5 * (arg * arg)))
    return arg * normal, slope


PART_COUNT = 4
CONV_TAPS = {1: (0, 3), 2: (3, 2)}
BY_Y = (False, True, False, True)
PLANE_FIRST = (False, False, False, True)
KINDS = ("own", "x", "y", "far")
GATHER_PLAN = (
    (
        ("vec_begin",), ("send", 0), ("begin",), ("assemble",), ("send", 3), ("vec_plane",), ("y", 0, 0),
        ("own", 0, 1), ("send", 1), ("vec_pass", 1), ("own", 0, 2), ("send", 2), ("vec_pass", 2), ("y", 3, 0),
        ("x", 3, 0), ("x", 0, 0), ("own", 1, 1), ("own", 0, 3), ("share", "own", 0), ("y", 0, 1), ("vec_pass", 3),
        ("vectors",), ("x", 1, 0), ("x", 0, 1),
    ),
    (),
    (
        ("y", 0, 2), ("own", 2, 1), ("far", 3, 0),
    ),
    (),
    (
        ("y", 0, 3), ("share", "y", 0), ("x", 0, 2), ("own", 1, 2), ("y", 1, 0), ("y", 3, 1),
    ),
    (
        ("own", 2, 2), ("x", 3, 1), ("x", 2, 0),
    ),
    (),
    (
        ("y", 2, 0), ("own", 3, 1), ("x", 1, 1),
    ),
    (
        ("far", 3, 1), ("far", 0, 1), ("y", 1, 1), ("x", 0, 3), ("share", "x", 0), ("far", 0, 2), ("far", 0, 0),
        ("own", 1, 3), ("share", "own", 1), ("far", 0, 3), ("share", "far", 0), ("far", 1, 0), ("y", 2, 1),
        ("y", 3, 2), ("w_in",),
    ),
    (
        ("own", 2, 3), ("share", "own", 2),
    ),
    (),
    (
        ("x", 3, 2), ("x", 1, 2),
    ),
    (
        ("x", 2, 1), ("y", 1, 2), ("y", 2, 2), ("own", 3, 2), ("far", 3, 2), ("x", 1, 3), ("share", "x", 1),
        ("x", 2, 2), ("y", 2, 3), ("share", "y", 2),
    ),
    (),
    (
        ("y", 1, 3), ("share", "y", 1), ("far", 2, 0),
    ),
    (
        ("far", 1, 1), ("x", 2, 3), ("share", "x", 2),
    ),
    (
        ("y", 3, 3), ("share", "y", 3), ("far", 2, 1), ("own", 3, 3), ("share", "own", 3), ("far", 1, 2), ("x", 3, 3),
        ("share", "x", 3), ("far", 1, 3), ("share", "far", 1), ("far", 2, 2), ("far", 2, 3), ("share", "far", 2),
        ("far", 3, 3), ("share", "far", 3), ("finish",),
    ),
)


def plane_peer(offset):
    z, y, x, core = place()
    other = lax.rem(y * 4 + x * 2 + core + offset, 8)
    return other, (z * 2 + lax.div(other, 4), lax.rem(other, 4))


def greet_near(z, y, x, core):
    barrier = pltpu.get_barrier_semaphore()

    def greet(target):
        pl.semaphore_signal(barrier, inc=1, device_id=target, device_id_type=MESH)

    for offset in range(1, 8):
        greet(plane_peer(offset)[1])
    pl.when(z > 0)(lambda: greet(device(z - 1, y, x, core)))
    pl.when(z < LEVELS - 1)(lambda: greet(device(z + 1, y, x, core)))
    pl.semaphore_wait(barrier, 7 + (z > 0).astype(jnp.int32) + (z < LEVELS - 1).astype(jnp.int32))


def each_level(z, distance, act):
    if distance == 0:
        act(z, 0)
        return
    pl.when(z + distance < LEVELS)(lambda: act(z + distance, 1))
    pl.when(z - distance >= 0)(lambda: act(z - distance, -1))


def gather_kernel(
    tokens_hbm, grads_hbm, vec, w_in, w_conv, w_out,
    u1_hbm, slope1_hbm, xh1_hbm, scale1_hbm, xh2_hbm, slope2_hbm, scale2_hbm, u2_hbm, vectors_out,
    in_full, conv_full, out_full,
    u2_share, xh2_share, slope2_share, scale2_share, grads_share, tokens_share,
    packed, in_vmem, conv_twin, out_twin, conv_own, out_own,
    tokens, u1, slope1, xh1, scale1, xh2, slope2, scale2, u2, token_sem, store_sem, share_send, share_recv,
    vec_send, vec_recv, link_send, link_recv, twin_recv, pair_send, pair_recv, own_sem, load_sem,
):
    z, y, x, core = place()
    here = 2 * y + x
    steps = 2048 // TILE
    columns = {"own": here, "x": 2 * y + (1 - x), "y": 2 * (1 - y) + x, "far": 2 * (1 - y) + (1 - x)}

    def piece(part, level, column, side):
        if part == 0:
            return in_vmem.at[pl.ds(pl.multiple_of((level * 4 + column) * 80 + side * 40, 8), 40), :]
        if part in CONV_TAPS:
            return conv_full.at[pl.ds(*CONV_TAPS[part]), level, column, :, pl.ds(*CONV_COLS[side])]
        return out_full.at[level, column, :, pl.ds(*OUT_COLS[side])]

    def pieces(part, column, side):
        if part in CONV_TAPS:
            return conv_full.at[pl.ds(*CONV_TAPS[part]), :, column, :, pl.ds(*CONV_COLS[side])]
        return out_full.at[:, column, :, pl.ds(*OUT_COLS[side])]

    def span(part, side, count):
        if part == 0:
            return in_vmem.at[pl.ds(0, 40 * count), :]
        rows, columns_ = (LEVELS, count // LEVELS) if count % LEVELS == 0 else (count, 1)
        if part in CONV_TAPS:
            return conv_full.at[
                pl.ds(*CONV_TAPS[part]), pl.ds(0, rows), pl.ds(0, columns_), :, pl.ds(*CONV_COLS[side])
            ]
        return out_full.at[pl.ds(0, rows), pl.ds(0, columns_), :, pl.ds(*OUT_COLS[side])]

    def own_piece(part, side):
        if part == 0:
            return w_in
        if part in CONV_TAPS:
            return conv_own.at[pl.ds(*CONV_TAPS[part]), :, pl.ds(*CONV_COLS[side])]
        return out_own.at[:, pl.ds(*OUT_COLS[side])]

    def target(link, side):
        return (
            device(z, y, 1 - x, side),
            device(z, 1 - y, x, side),
            device(z + 1, y, x, side),
            device(z - 1, y, x, side),
            device(z, y, x, 1 - side),
        )[link]

    def remote(src, dst, send_sem, recv_sem, where):
        return pltpu.make_async_remote_copy(
            src_ref=src, dst_ref=dst, send_sem=send_sem, recv_sem=recv_sem, device_id=where, device_id_type=MESH
        )

    def wait_sent(side, part, link, count):
        view = span(part, side, count)
        remote(view, view, link_send.at[link, part], twin_recv.at[0, part], target(4, side)).wait_send()

    def guarded(link, act):
        if link == 2:
            pl.when(z < LEVELS - 1)(act)
        elif link == 3:
            pl.when(z > 0)(act)
        else:
            act()

    def forward(side, part, level, column, links, own=False):
        place_ref = piece(part, level, column, side)
        for link in links:

            def act(link=link):
                remote(
                    own_piece(part, side) if own else place_ref, place_ref,
                    link_send.at[link, part], link_recv.at[level, column, part], target(link, side),
                ).start()

            guarded(link, act)

    def pass_on(side, kind, part, distance):
        def act(level, sign):
            column = columns[kind]
            place_ref = piece(part, level, column, side)
            remote(
                place_ref, place_ref, link_send.at[4, part], link_recv.at[level, column, part], target(4, side)
            ).wait_recv()
            along = {1: (3,), -1: (2,), 0: (2, 3)}[sign]
            links = ()
            if kind == "own":
                links = along if PLANE_FIRST[part] else along + (0, 1)
            else:
                if kind == "x" and BY_Y[part] and (distance == 0 or not PLANE_FIRST[part]):
                    links += (1,)
                if kind == "y" and not BY_Y[part] and (distance == 0 or not PLANE_FIRST[part]):
                    links += (0,)
                if PLANE_FIRST[part]:
                    links += along
            forward(side, part, level, column, links)

        each_level(z, distance, act)

    def own_sends(side, part):
        forward(side, part, z, here, (0, 1, 2, 3), own=True)

    def twin_copy(side, kind, part, level=None):
        if level is None:
            view = pieces(part, columns[kind], side)
        else:
            view = piece(part, level, columns[kind], side)
        return remote(view, view, link_send.at[4, part], twin_recv.at[KINDS.index(kind), part], target(4, side))

    def share(side, kind, part):
        if kind == "own":
            own_copy(side, part).wait()
        if part:
            twin_copy(side, kind, part).start()
        else:
            for level in range(LEVELS):
                twin_copy(side, kind, part, level).start()

    def take_twin(side, part):
        for kind in KINDS:
            if part:
                twin_copy(1 - side, kind, part).wait_recv()
            else:
                view = span(part, side, LEVELS)
                remote(
                    view, view, link_send.at[4, part], twin_recv.at[KINDS.index(kind), part], target(4, side)
                ).wait_recv()

    def pair_copies(side):
        return [
            remote(src, dst, pair_send.at[index], pair_recv.at[index], target(4, side))
            for index, (src, dst) in enumerate(((w_conv, conv_twin), (w_out, out_twin)))
        ]

    def own_copy(side, part):
        return pltpu.make_async_copy(own_piece(part, side), piece(part, z, here, side), own_sem.at[part])

    def vec_copy(offset):
        mine = z * 8 + y * 4 + x * 2 + core
        return remote(vec, packed.at[mine], vec_send.at[0], vec_recv.at[0], plane_peer(offset)[1])

    def level_rows(level):
        return packed.at[pl.ds(pl.multiple_of(level * 8, 8), 8)]

    def vec_line(side, level, link):
        rows = level_rows(level)
        return remote(rows, rows, vec_send.at[link - 1], vec_recv.at[1 + level], target(link, side))

    def vec_begin(side):
        for offset in range(1, 8):
            vec_copy(offset).start()
        packed[pl.ds(z * 8 + y * 4 + x * 2 + side, 1)] = vec[...][None]

    def vec_plane(side):
        rows = packed.at[pl.ds(0, 7)]
        remote(rows, rows, vec_send.at[0], vec_recv.at[0], target(4, side)).wait()
        for link in (2, 3):
            guarded(link, lambda link=link: vec_line(side, z, link).start())

    def vec_pass(side, distance):
        def act(level, sign):
            link = 3 if sign > 0 else 2
            vec_line(side, level, link).wait_recv()
            guarded(link, lambda: vec_line(side, level, link).start())

        each_level(z, distance, act)

    def vec_finish(side):
        for level in range(LEVELS):

            @pl.when(z == level)
            def _(level=level):
                for link, count in ((2, level + 1 if level < LEVELS - 1 else 0), (3, LEVELS - level if level else 0)):
                    if count:
                        rows = packed.at[pl.ds(0, 8 * count)]
                        remote(rows, rows, vec_send.at[link - 1], vec_recv.at[0], target(4, side)).wait_send()

    def begin(side):
        own_copy(side, 0).start()
        for copy in pair_copies(side):
            copy.start()
        share_rows(side, slice(4, 6))

    def assemble(side):
        for copy in pair_copies(side):
            copy.wait()
        first_conv, second_conv = (w_conv, conv_twin) if side == 0 else (conv_twin, w_conv)
        first_out, second_out = (w_out, out_twin) if side == 0 else (out_twin, w_out)
        conv_own[...] = jnp.concatenate(
            [first_conv[...].astype(F32), second_conv[...].astype(F32)], axis=1
        ).astype(BF16)
        out_own[...] = jnp.concatenate(
            [first_out[...].astype(F32), second_out[...].astype(F32)], axis=0
        ).astype(BF16)
        for part in range(1, PART_COUNT):
            own_copy(side, part).start()

    def shares(side):
        half = pl.ds(1024, 1024)
        pairs = (
            (u2, u2_share), (xh2, xh2_share), (slope2, slope2_share), (scale2, scale2_share),
            (grads_hbm, grads_share), (tokens_hbm, tokens_share),
        )
        return [
            remote(source.at[half, :], target_, share_send.at[index], share_recv.at[index], target(4, side))
            for index, (source, target_) in enumerate(pairs)
        ]

    def share_rows(side, which):
        for copy in shares(side)[which]:
            copy.start()

    def save_in():
        return pltpu.make_async_copy(in_vmem, in_full, load_sem.at[0])

    def take_in(side):
        take_twin(side, 0)
        save_in().start()

    def finish(side):
        vec_finish(side)
        for part in range(1, PART_COUNT):
            take_twin(side, part)
        for part in range(PART_COUNT):
            plane, along = (1, 4) if PLANE_FIRST[part] else (4, 1)
            wait_sent(side, part, 0, plane if BY_Y[part] else 2 * plane)
            wait_sent(side, part, 1, 2 * plane if BY_Y[part] else plane)
            wait_sent(side, part, 4, CHIPS)
            for level in range(LEVELS):

                @pl.when(z == level)
                def _(part=part, along=along, level=level):
                    if level < LEVELS - 1:
                        wait_sent(side, part, 2, along * (level + 1))
                    if level > 0:
                        wait_sent(side, part, 3, along * (LEVELS - level))

        save_in().wait()
        for copy in shares(side):
            copy.wait()

    def take_vectors(side):
        unpack_vectors(packed, vectors_out)
        mine = z * 8 + y * 4 + x * 2
        for row, owner in ((9, mine + side), (10, mine + 1 - side)):
            vectors_out[pl.ds(row, 1), pl.ds(0, 128)] = packed[owner, pl.ds(0, 1), :]

    actions = {
        "share_rows": share_rows,
        "send": own_sends, "begin": begin, "assemble": assemble, "w_in": take_in, "finish": finish,
        "vec_begin": vec_begin, "vec_plane": vec_plane, "vec_pass": vec_pass,
        "vectors": take_vectors,
        "share": share,
    }

    def perform(events):
        for side in range(2):

            @pl.when(core == side)
            def _(side=side):
                for event in events:
                    if event[0] in actions:
                        actions[event[0]](side, *event[1:])
                    else:
                        pass_on(side, *event)

    def rows_of(tile, count=1):
        return pl.ds(pl.multiple_of(tile * TILE, TILE), count * TILE)

    def token_load(tile):
        return pltpu.make_async_copy(tokens_hbm.at[rows_of(tile), :], tokens.at[rows_of(tile), :], token_sem.at[tile])

    first = ((u1, u1_hbm), (slope1, slope1_hbm), (xh1, xh1_hbm), (scale1, scale1_hbm))
    second = ((u2, u2_hbm), (xh2, xh2_hbm), (slope2, slope2_hbm), (scale2, scale2_hbm))

    def stores(pairs, phase, half):
        rows = rows_of(half * (steps // 2), steps // 2)
        return [
            pltpu.make_async_copy(src.at[rows, :], dst.at[rows, :], store_sem.at[phase, half, index])
            for index, (src, dst) in enumerate(pairs)
        ]

    def start_stores(pairs, phase, half):
        for copy in stores(pairs, phase, half):
            copy.start()

    greet_near(z, y, x, core)
    for tile in range(steps):
        token_load(tile).start()

    def wide_tile(tile, _):
        for index in range(steps):
            if GATHER_PLAN[index]:
                pl.when(tile == index)(functools.partial(perform, GATHER_PLAN[index]))
        token_load(tile).wait()
        rows = rows_of(tile)
        gain, bias = vectors_out[pl.ds(0, 1), :], vectors_out[pl.ds(1, 1), :]
        norm, scale = norm_parts(tokens[rows, :].astype(F32))
        act, slope = gelu_parts(norm * gain + bias)
        u1[rows, :] = act.astype(BF16)
        slope1[rows, :] = slope.astype(BF16)
        xh1[rows, :] = norm.astype(BF16)
        scale1[rows, :] = jnp.broadcast_to(scale, (TILE, 128))
        return 0

    lax.fori_loop(0, steps, wide_tile, 0)

    def slim_tile(tile, _):
        for index in range(steps):
            events = GATHER_PLAN[steps + index]
            if index == 0:
                pl.when(tile == 0)(lambda: start_stores(first, 0, 0))
                pl.when(tile == 0)(lambda: start_stores(first, 0, 1))
            if index == steps // 2:

                @pl.when(tile == index)
                def _():
                    start_stores(second, 1, 1)
                    perform((("share_rows", slice(0, 4)),))

            if events:
                pl.when(tile == index)(functools.partial(perform, events))
        rows = rows_of(lax.rem(tile + steps // 2, steps))
        hidden = jnp.dot(u1[rows, :], in_vmem[...], preferred_element_type=F32)
        hidden = hidden + vectors_out[pl.ds(3, 1), pl.ds(0, 640)]
        norm, scale = norm_parts(hidden)
        act, slope = gelu_parts(norm * vectors_out[pl.ds(4, 1), pl.ds(0, 640)] + vectors_out[pl.ds(5, 1), pl.ds(0, 640)])
        u2[rows, :] = act.astype(BF16)
        slope2[rows, :] = slope.astype(BF16)
        xh2[rows, :] = norm.astype(BF16)
        scale2[rows, :] = jnp.broadcast_to(scale, (TILE, 128))
        return 0

    lax.fori_loop(0, steps, slim_tile, 0)
    start_stores(second, 1, 0)
    perform(GATHER_PLAN[2 * steps])
    for phase, pairs in enumerate((first, second)):
        for half in range(2):
            for copy in stores(pairs, phase, half):
                copy.wait()


def gather_stage(tokens, grads, vec, w_in, w_conv, w_out):
    rows = tokens.shape[0]
    shape = jax.ShapeDtypeStruct
    vmem = pl.BlockSpec(memory_space=pltpu.VMEM)
    wide, slim, column = (rows, 1280), (rows, 640), (rows, 128)
    *results, conv_full, out_full, s0, s1, s2, s3, s4, s5 = pl.pallas_call(
        gather_kernel,
        in_specs=[HBM] * 2 + [vmem] * 4,
        out_specs=[HBM] * 8 + [vmem] + [HBM] * 9,
        out_shape=[
            shape(wide, BF16), shape(wide, BF16), shape(wide, BF16), shape(column, F32),
            shape(slim, BF16), shape(slim, BF16), shape(column, F32), shape(slim, BF16),
            shape((16, 1280), F32),
            shape((1280, 640), BF16), shape((KSIZE, LEVELS, 4, 40, 640), BF16), shape((LEVELS, 4, 40, 1280), BF16),
            shape((1024, 640), BF16), shape((1024, 640), BF16), shape((1024, 640), BF16), shape((1024, 128), F32),
            shape((1024, 1280), BF16), shape((1024, 1280), BF16),
        ],
        scratch_shapes=[
            pltpu.VMEM((DEVICES, 2, 128), F32),
            pltpu.VMEM((1280, 640), BF16),
            pltpu.VMEM((KSIZE, 20, 640), BF16),
            pltpu.VMEM((20, 1280), BF16),
            pltpu.VMEM((KSIZE, 40, 640), BF16),
            pltpu.VMEM((40, 1280), BF16),
            pltpu.VMEM(wide, BF16),
            pltpu.VMEM(wide, BF16),
            pltpu.VMEM(wide, BF16),
            pltpu.VMEM(wide, BF16),
            pltpu.VMEM(column, F32),
            pltpu.VMEM(slim, BF16),
            pltpu.VMEM(slim, BF16),
            pltpu.VMEM(column, F32),
            pltpu.VMEM(slim, BF16),
            pltpu.SemaphoreType.DMA((rows // TILE,)),
            pltpu.SemaphoreType.DMA((2, 2, 4)),
            pltpu.SemaphoreType.DMA((6,)),
            pltpu.SemaphoreType.DMA((6,)),
            pltpu.SemaphoreType.DMA((3,)),
            pltpu.SemaphoreType.DMA((1 + LEVELS,)),
            pltpu.SemaphoreType.DMA((5, PART_COUNT)),
            pltpu.SemaphoreType.DMA((LEVELS, 4, PART_COUNT)),
            pltpu.SemaphoreType.DMA((4, PART_COUNT)),
            pltpu.SemaphoreType.DMA((2,)),
            pltpu.SemaphoreType.DMA((2,)),
            pltpu.SemaphoreType.DMA((PART_COUNT,)),
            pltpu.SemaphoreType.DMA((1,)),
        ],
        compiler_params=pltpu.CompilerParams(
            collective_id=0, has_side_effects=True, vmem_limit_bytes=VMEM_BYTES,
        ),
        name="gather_stage",
    )(tokens, grads, vec, w_in, w_conv, w_out)
    return *results, conv_full.reshape(KSIZE, 640, 640), out_full.reshape(640, 1280), (s0, s1, s2, s3, s4, s5)


def pack_vectors(ln1_gain, ln1_bias, b_in, ln2_gain, ln2_bias, b_conv, ln3_gain, ln3_bias, b_out, lengths):
    total = None
    for plane, pieces in enumerate(
        (
            zip((ln1_gain, ln1_bias, b_out, lengths), WIDE_OFFSETS + (LENGTH_LANE,)),
            zip((b_in, ln2_gain, ln2_bias, b_conv, ln3_gain, ln3_bias), SLIM_OFFSETS),
        )
    ):
        for piece, offset in pieces:
            line = piece[None]
            room = ((plane, 1 - plane, 0), (offset, 128 - offset - piece.shape[0], 0))
            placed = lax.pad(line, jnp.zeros((), line.dtype), room).astype(F32)
            total = placed if total is None else total + placed
    return total


PAD = 32
SPAN = 1024 + 2 * PAD
HALO = 16
UNIT = 128
LENGTH_LANE = 120


def unit_share(lengths):
    own_first, own_second, twin_first, twin_second = (lax.div(length + UNIT - 1, UNIT) for length in lengths)
    excess = own_first + own_second - twin_first - twin_second
    give = jnp.minimum(lax.div(jnp.maximum(excess, 0), 2), own_second)
    take = jnp.minimum(lax.div(jnp.maximum(-excess, 0), 2), twin_second)
    return own_first, own_second, twin_second, give, take


def read_lengths(vectors):
    lane = lax.broadcasted_iota(jnp.int32, (1, 128), 1)
    return [
        jnp.sum(jnp.where(lane == LENGTH_LANE + index, vectors[pl.ds(row, 1), pl.ds(0, 128)], 0.0)).astype(jnp.int32)
        for row in (9, 10)
        for index in range(2)
    ]


def middle_kernel(
    vectors, u2_hbm, xh2_hbm, slope2_hbm, scale2_hbm, grads_hbm, tokens_hbm, conv_hbm, last_hbm,
    u2_twin, xh2_twin, slope2_twin, scale2_twin, grads_twin, tokens_twin,
    out_hbm, dh1_hbm, out_twin, dh1_twin, d_conv_hbm, d_last_hbm, sums_out,
    conv, conv_t, last, last_t, u2, dh2, grads, tokens, xh2, slope2, scale2, d_conv, d_last, zeros,
    u2_sem, row_sem, back_sem, weight_sem, out_sem, dh1_sem, flush_sem,
):
    segments = 3
    tiles = 1024 // TILE
    wide, slim = 1280, 640
    lengths = read_lengths(vectors)
    first_units, second_units, twin_units, give, take = unit_share(lengths)

    def pick(segment, values):
        return jnp.where(segment == 0, values[0], jnp.where(segment == 1, values[1], values[2]))

    def bounds(segment):
        low = pick(segment, (0, 0, twin_units - take))
        high = pick(segment, (first_units, second_units - give, twin_units))
        before = jnp.logical_and(jnp.logical_and(segment == 2, low > 0), high > low).astype(jnp.int32)
        after = jnp.logical_and(jnp.logical_and(segment == 1, give > 0), high > 0).astype(jnp.int32)
        return low, high, before, after

    def tile_range(low, high):
        return lax.div(low, 2), jnp.where(high > low, lax.div(high + 1, 2), lax.div(low, 2))

    def worked_tiles(segment):
        low, high, _, _ = bounds(segment)
        return tile_range(low, high)

    def held_tiles(segment):
        low, high, before, after = bounds(segment)
        return tile_range(low - before, high + after)

    def live_units(segment):
        return pick(segment, (first_units, second_units, twin_units))

    def live_tiles(segment):
        return lax.div(live_units(segment) + 1, 2)

    def rows_of(segment, tile):
        return pl.ds(pl.multiple_of(segment * 1024 + tile * TILE, TILE), TILE)

    def padded(segment, row, count, shift=0):
        return pl.ds(pl.multiple_of(segment * SPAN + PAD + row, 8) + shift, count)

    def plain(row, count, shift=0):
        return pl.ds(pl.multiple_of(PAD + row, 8) + shift, count)

    def fetch(segment, tile, own, twin, target, rows, sem):
        @pl.when(segment < 2)
        def _():
            pltpu.make_async_copy(own.at[rows_of(segment, tile), :], target.at[rows, :], sem).start()

        @pl.when(segment == 2)
        def _():
            pltpu.make_async_copy(twin.at[rows_of(0, tile), :], target.at[rows, :], sem).start()

    def fetched(segment, tile, own, target, rows, sem):
        pltpu.make_async_copy(own.at[rows_of(0, tile), :], target.at[rows, :], sem).wait()

    def emit(tile, segment, source, own, twin, sem):
        @pl.when(segment < 2)
        def _():
            pltpu.make_async_copy(source, own.at[rows_of(segment, tile), :], sem).start()

        @pl.when(segment == 2)
        def _():
            pltpu.make_async_copy(source, twin.at[rows_of(0, tile), :], sem).start()

    def u2_at(segment, tile):
        return padded(segment, tile * TILE, TILE)

    row_arrays = ((grads_hbm, grads_twin, grads), (tokens_hbm, tokens_twin, tokens))
    back_arrays = ((xh2_hbm, xh2_twin, xh2), (slope2_hbm, slope2_twin, slope2), (scale2_hbm, scale2_twin, scale2))

    def fetch_rows(segment, tile, index):
        own, twin, target = row_arrays[index]
        fetch(segment, tile, own, twin, target, rows_of(segment, tile), row_sem.at[index, segment, tile])

    def rows_fetched(segment, tile, index):
        own, _, target = row_arrays[index]
        fetched(segment, tile, own, target, rows_of(segment, tile), row_sem.at[index, segment, tile])

    def fetch_u2(segment):
        low, high = held_tiles(segment)

        def one(tile, _):
            fetch(segment, tile, u2_hbm, u2_twin, u2, u2_at(segment, tile), u2_sem.at[segment, tile])
            return 0

        lax.fori_loop(low, high, one, 0)

    def out_store(segment, tile):
        emit(tile, segment, tokens.at[rows_of(segment, tile), :], out_hbm, out_twin, out_sem.at[segment, tile])

    def dh1_store(segment, tile, source):
        emit(tile, segment, source, dh1_hbm, dh1_twin, dh1_sem.at[segment, tile])

    conv_load = pltpu.make_async_copy(conv_hbm, conv, weight_sem.at[0])
    last_load = pltpu.make_async_copy(last_hbm, last, weight_sem.at[1])
    last_flush = pltpu.make_async_copy(last, d_last_hbm, flush_sem.at[0])

    fetch_u2(0)
    conv_load.start()
    last_load.start()

    def load_rows(segment, _):
        pl.when(segment > 0)(lambda: fetch_u2(segment))
        low, high = worked_tiles(segment)
        held = held_tiles(segment)

        def one(tile, _):
            fetch_rows(segment, tile, 0)
            pl.when(jnp.logical_and(tile >= low, tile < high))(lambda: fetch_rows(segment, tile, 1))
            return 0

        lax.fori_loop(held[0], held[1], one, 0)
        return 0

    def load_back(segment, _):
        low, high = worked_tiles(segment)

        def one(tile, _):
            for index, (own, twin, target) in enumerate(back_arrays):
                fetch(segment, tile, own, twin, target, rows_of(segment, tile), back_sem.at[index, segment, tile])
            return 0

        lax.fori_loop(low, high, one, 0)
        return 0

    lax.fori_loop(0, segments, load_rows, 0)
    lax.fori_loop(0, segments, load_back, 0)
    zeros[...] = jnp.zeros_like(zeros)

    def idle(segment, _):
        low, high = worked_tiles(segment)

        def one(tile, _):
            pl.when(jnp.logical_or(tile < low, tile >= high))(lambda: dh1_store(segment, tile, zeros))
            dead = jnp.logical_and(segment < 2, tile >= live_tiles(segment))
            pl.when(dead)(lambda: fetch_rows(segment, tile, 1))
            return 0

        lax.fori_loop(0, tiles, one, 0)
        return 0

    lax.fori_loop(0, segments, idle, 0)

    sums_out[...] = jnp.zeros_like(sums_out)

    def clear(index, _):
        rows = pl.ds(pl.multiple_of(index * 64, 64), 64)
        d_last[rows, :] = jnp.zeros((64, wide), F32)
        for tap in range(KSIZE):
            d_conv[tap, rows, :] = jnp.zeros((64, slim), F32)
        return 0

    lax.fori_loop(0, slim // 64, clear, 0)

    def vector(index, width=slim):
        return vectors[pl.ds(index, 1), pl.ds(0, width)]

    def add_sum(index, values):
        width = values.shape[1]
        sums_out[pl.ds(index * 8, 8), pl.ds(0, width)] += jnp.sum(
            values.reshape(values.shape[0] // 8, 8, width), axis=0
        )

    edge = jnp.zeros((PAD, slim), BF16)

    def one_segment(segment, _):
        low, high, before, after = bounds(segment)
        first_tile, end_tile = worked_tiles(segment)
        held = held_tiles(segment)
        count = live_units(segment)
        length = pick(segment, (lengths[0], lengths[1], lengths[3]))

        def live_rows(row, size):
            position = lax.broadcasted_iota(jnp.int32, (size, 128), 0) + row
            return (position < length).astype(F32)

        def prepare(tile, _):
            fetched(segment, tile, u2_hbm, u2, u2_at(segment, tile), u2_sem.at[segment, tile])
            return 0

        lax.fori_loop(held[0], held[1], prepare, 0)

        @pl.when(low == 0)
        def _():
            u2[padded(segment, -PAD, PAD), :] = edge

        dh2[plain(low * UNIT - PAD, PAD), :] = edge
        dh2[plain(high * UNIT, PAD), :] = edge

        @pl.when(jnp.logical_and(high > low, high + after == count))
        def _():
            tail = padded(segment, (count - 1) * UNIT, UNIT)
            u2[tail, :] = (u2[tail, :].astype(F32) * lanes(live_rows((count - 1) * UNIT, UNIT), slim)).astype(BF16)
            u2[padded(segment, count * UNIT, PAD), :] = edge

        @pl.when(segment == 0)
        def _():
            conv_load.wait()
            last_load.wait()
            last_t[...] = last[...].T

            def turn(tap, _):
                conv_t[tap] = conv[tap].T
                return 0

            lax.fori_loop(0, KSIZE, turn, 0)

        def forward_rows(row, size, whole):
            rows = pl.ds(pl.multiple_of(segment * 1024 + row, HALO), size)
            live = live_rows(row, size)
            hidden = jnp.dot(u2[padded(segment, row, size, -16), :], conv[0], preferred_element_type=F32)
            for tap in range(1, KSIZE):
                hidden += jnp.dot(
                    u2[padded(segment, row, size, (tap - 2) * DILATION), :], conv[tap], preferred_element_type=F32
                )
            gz = (grads[rows, :].astype(F32) * lanes(live, wide)).astype(BF16)
            back = jnp.dot(gz, last_t[...], preferred_element_type=F32)
            norm, scale = norm_parts(hidden + vector(6))
            act, slope = gelu_parts(norm * vector(7) + vector(8))
            slope_grad = back * slope
            err = slope_grad * vector(7)
            mean = jnp.sum(err, axis=1, keepdims=True) * (1.0 / slim)
            along = jnp.sum(err * norm, axis=1, keepdims=True) * (1.0 / slim)
            low_grad = (scale * (err - mean - norm * along)).astype(BF16)
            dh2[plain(row, size), :] = low_grad
            if whole:
                u3 = act.astype(BF16)
                branch = jnp.dot(u3, last[...], preferred_element_type=F32) + vector(2, wide)
                tokens[rows, :] = (tokens[rows, :].astype(F32) + lanes(live, wide) * branch).astype(BF16)
                d_last[...] += lax.dot_general(u3, gz, (((0,), (0,)), ((), ())), preferred_element_type=F32)
                add_sum(2, gz.astype(F32))
                add_sum(7, slope_grad * norm)
                add_sum(8, slope_grad)
                add_sum(6, low_grad.astype(F32))

        def by_size(tile, act):
            whole = jnp.logical_and(2 * tile >= low, 2 * tile + 2 <= high)
            pl.when(whole)(lambda: act(tile * TILE, TILE))
            pl.when(jnp.logical_not(whole))(lambda: act(jnp.maximum(2 * tile, low) * UNIT, UNIT))

        def forward(tile, _):
            rows_fetched(segment, tile, 0)
            rows_fetched(segment, tile, 1)
            by_size(tile, lambda row, size: forward_rows(row, size, True))
            out_store(segment, tile)
            return 0

        lax.fori_loop(first_tile, end_tile, forward, 0)

        @pl.when(before + after > 0)
        def _():
            tile = jnp.where(before > 0, held[0], held[1] - 1)
            pl.when(jnp.logical_or(tile < first_tile, tile >= end_tile))(lambda: rows_fetched(segment, tile, 0))
            forward_rows(jnp.where(before > 0, low * UNIT - HALO, high * UNIT), HALO, False)

        def dead_store(tile, _):
            rows_fetched(segment, tile, 1)
            out_store(segment, tile)
            return 0

        lax.fori_loop(jnp.where(segment < 2, live_tiles(segment), tiles), tiles, dead_store, 0)

        @pl.when(segment == segments - 1)
        def _():
            last[...] = d_last[...].astype(BF16)
            last_flush.start()

        def backward_rows(row, size):
            rows = pl.ds(pl.multiple_of(segment * 1024 + row, UNIT), size)
            live = lanes(live_rows(row, size), slim)
            source_t = u2[padded(segment, row, size), :].T
            total = None
            for tap in range(KSIZE):
                window = dh2[plain(row, size, (2 - tap) * DILATION), :]
                term = jnp.dot(window, conv_t[tap], preferred_element_type=F32)
                total = term if total is None else total + term
                d_conv[tap] += jnp.dot(source_t, window, preferred_element_type=F32)
            norm = xh2[rows, :].astype(F32)
            slope_grad = total * live * slope2[rows, :].astype(F32)
            add_sum(4, slope_grad * norm)
            add_sum(5, slope_grad)
            err = slope_grad * vector(4)
            mean = jnp.sum(err, axis=1, keepdims=True) * (1.0 / slim)
            along = jnp.sum(err * norm, axis=1, keepdims=True) * (1.0 / slim)
            low_grad = (lanes(scale2[rows, :], slim) * (err - mean - norm * along)).astype(BF16)
            add_sum(3, low_grad.astype(F32))
            slope2[rows, :] = low_grad
            if size == UNIT:
                other = 2 * lax.div(row, TILE) * TILE + UNIT - row
                slope2[pl.ds(pl.multiple_of(segment * 1024 + other, UNIT), UNIT), :] = jnp.zeros((UNIT, slim), BF16)

        def backward(tile, _):
            rows = rows_of(segment, tile)
            for index, (own, twin, target) in enumerate(back_arrays):
                fetched(segment, tile, own, target, rows, back_sem.at[index, segment, tile])
            by_size(tile, backward_rows)
            dh1_store(segment, tile, slope2.at[rows, :])
            return 0

        lax.fori_loop(first_tile, end_tile, backward, 0)
        return 0

    lax.fori_loop(0, segments, one_segment, 0)

    def conv_flush(tap):
        return pltpu.make_async_copy(conv.at[tap], d_conv_hbm.at[tap], flush_sem.at[tap + 1])

    def flush(tap, _):
        conv[tap] = d_conv[tap].astype(BF16)
        conv_flush(tap).start()
        return 0

    lax.fori_loop(0, KSIZE, flush, 0)

    def stored(segment, _):
        low, high = worked_tiles(segment)

        def one(tile, _):
            pltpu.make_async_copy(zeros, dh1_hbm.at[rows_of(0, tile), :], dh1_sem.at[segment, tile]).wait()
            worked = jnp.logical_and(tile >= low, tile < high)
            dead = jnp.logical_and(segment < 2, tile >= live_tiles(segment))

            @pl.when(jnp.logical_or(worked, dead))
            def _():
                pltpu.make_async_copy(
                    tokens.at[rows_of(0, tile), :], out_hbm.at[rows_of(0, tile), :], out_sem.at[segment, tile]
                ).wait()

            return 0

        lax.fori_loop(0, tiles, one, 0)
        return 0

    lax.fori_loop(0, segments, stored, 0)
    for copy in [last_flush] + [conv_flush(tap) for tap in range(KSIZE)]:
        copy.wait()


def middle_stage(vectors, u2, xh2, slope2, scale2, grads, tokens, w_conv, w_out, twins):
    rows = u2.shape[0]
    shape = jax.ShapeDtypeStruct
    vmem = pl.BlockSpec(memory_space=pltpu.VMEM)
    tiles = 1024 // TILE
    held = 3 * 1024
    return pl.pallas_call(
        middle_kernel,
        in_specs=[vmem] + [HBM] * 14,
        out_specs=[HBM] * 6 + [vmem],
        out_shape=[
            shape((rows, 1280), BF16), shape((rows, 640), BF16), shape((1024, 1280), BF16), shape((1024, 640), BF16),
            shape((KSIZE, 640, 640), BF16), shape((640, 1280), BF16), shape((72, 1280), F32),
        ],
        scratch_shapes=[
            pltpu.VMEM((KSIZE, 640, 640), BF16),
            pltpu.VMEM((KSIZE, 640, 640), BF16),
            pltpu.VMEM((640, 1280), BF16),
            pltpu.VMEM((1280, 640), BF16),
            pltpu.VMEM((3 * SPAN, 640), BF16),
            pltpu.VMEM((SPAN, 640), BF16),
            pltpu.VMEM((held, 1280), BF16),
            pltpu.VMEM((held, 1280), BF16),
            pltpu.VMEM((held, 640), BF16),
            pltpu.VMEM((held, 640), BF16),
            pltpu.VMEM((held, 128), F32),
            pltpu.VMEM((KSIZE, 640, 640), F32),
            pltpu.VMEM((640, 1280), F32),
            pltpu.VMEM((TILE, 640), BF16),
            pltpu.SemaphoreType.DMA((3, tiles)),
            pltpu.SemaphoreType.DMA((2, 3, tiles)),
            pltpu.SemaphoreType.DMA((3, 3, tiles)),
            pltpu.SemaphoreType.DMA((2,)),
            pltpu.SemaphoreType.DMA((3, tiles)),
            pltpu.SemaphoreType.DMA((3, tiles)),
            pltpu.SemaphoreType.DMA((6,)),
        ],
        compiler_params=pltpu.CompilerParams(vmem_limit_bytes=VMEM_BYTES),
        name="middle_stage",
    )(vectors, u2, xh2, slope2, scale2, grads, tokens, w_conv, w_out, *twins)


def pack_sums(plane, lines, offsets, packed_ref):
    width, chunk = ((1280, 40), (640, 20))[plane]
    owner, slot, row = chunk_masks(width, chunk)
    total = packed_ref[:, :, plane, :].reshape(DEVICES, 128)
    for line, offset in zip(lines, offsets):
        pick = (slot + offset == row).astype(F32).astype(BF16)
        spread = jnp.where(owner, jnp.broadcast_to(line, owner.shape), 0.0)
        for _ in range(3):
            term = spread.astype(BF16)
            spread = spread - term.astype(F32)
            total += lax.dot_general(term, pick, (((1,), (1,)), ((), ())), preferred_element_type=F32)
    packed_ref[:, :, plane, :] = total.reshape(LEVELS, 8, 128)


SCATTER_BY_Y = (False, True, False)
LINE_FIRST = (False, False, True)
SCATTER_PLAN = (
    (),
    (),
    (),
    (
        ("load", 1), ("twin", 1, "far"), ("first", 1, 3), ("first", 1, 2),
    ),
    (
        ("load", 2), ("twin", 2, "y"), ("line", 2, "y", 3), ("ready",), ("twin", 2, "far"), ("line", 2, "far", 3),
        ("twin", 2, "own"), ("line", 2, "own", 3), ("twin", 2, "x"), ("line", 2, "x", 3), ("twin", 1, "y"),
        ("direct", 1, 3), ("first", 1, 1), ("twin", 1, "x"), ("second", 1, 3),
    ),
    (),
    (
        ("line", 2, "y", 2), ("twin", 0, "far"), ("first", 0, 2), ("twin", 0, "x"), ("direct", 0, 1),
        ("line", 2, "far", 2), ("first", 0, 3), ("direct", 1, 2), ("first", 0, 0), ("twin", 1, "own"),
        ("line", 1, "own", 3), ("direct", 0, 3), ("line", 2, "own", 2),
    ),
    (
        ("second", 1, 2), ("line", 2, "x", 2), ("twin", 0, "y"), ("second", 0, 3), ("first", 0, 1), ("first", 1, 0),
        ("line", 2, "y", 1), ("direct", 0, 2), ("line", 2, "far", 1), ("second", 0, 2), ("twin", 0, "own"),
        ("line", 0, "own", 3), ("second", 1, 1), ("direct", 1, 1), ("direct", 0, 0), ("line", 1, "own", 2),
    ),
    (
        ("line", 2, "x", 1), ("second", 0, 1), ("second", 0, 0), ("line", 2, "own", 1), ("plane", 2, "F"),
        ("line", 0, "own", 2), ("second", 1, 0), ("direct", 1, 0),
    ),
    (
        ("line", 1, "own", 1),
    ),
    (
        ("plane", 2, "D"), ("plane", 2, "S"), ("line", 0, "own", 1),
    ),
    (),
    (
        ("done", 2), ("done", 1), ("done", 0), ("vec_start",), ("vec_middle",), ("vec_end",), ("finish",),
    ),
)


def scatter_kernel(
    u1_hbm, dh1_hbm, slope1_hbm, xh1_hbm, scale1_hbm, grads_hbm, w_in_hbm, vectors, sums, d_conv_hbm, d_last_hbm, d_conv_flat, d_last_flat, dh1_share, out_share,
    grad_tokens, g_in, g_conv, g_last, g_vec, out_back,
    u1, dh1, slope1, xh1, scale1, grads, w_in, w_in_t, dh1_back, d_in_sum, d_in, own_sums, packed, plane_box, level_box,
    conv_own, conv_twin, conv_far, conv_x, conv_y, conv_line, conv_done, conv_swap,
    last_own, last_twin, last_far, last_x, last_y, last_line, last_done, last_swap,
    in_twin, in_far, in_x, in_y, in_line,
    tile_sem, weight_sem, store_sem, vec_sem, load_sem, twin_send, twin_recv, send_sem, move_recv, line_recv,
    swap_send, swap_recv, back_send, back_recv,
):
    steps, weight_steps = 2048 // TILE, 4
    z, y, x, core = place()
    columns = {"own": 2 * y + x, "x": 2 * y + (1 - x), "y": 2 * (1 - y) + x, "far": 2 * (1 - y) + (1 - x)}
    boxes = {"far": (in_far, conv_far, last_far), "x": (in_x, conv_x, last_x), "y": (in_y, conv_y, last_y)}
    line_boxes = (in_line, conv_line, last_line)
    links = {
        "x": lambda: device(z, y, 1 - x, core), "y": lambda: device(z, 1 - y, x, core),
        "twin": lambda: device(z, y, x, 1 - core),
    }

    def remote(src, dst, send, recv, link):
        return pltpu.make_async_remote_copy(
            src_ref=src, dst_ref=dst, send_sem=send, recv_sem=recv, device_id=links[link]() if isinstance(link, str) else device(z + link, y, x, core), device_id_type=MESH
        )

    def cut(side, part):
        return (None, CONV_COLS[side], OUT_COLS[side])[part]

    def narrow(side, part):
        return pl.ds(0, 640 if part == 0 else cut(side, part)[1])

    def own_at(side, part, level, column):
        if part == 0:
            return d_in.at[level, column, side]
        if part == 1:
            return conv_own.at[:, level, column, :, narrow(side, part)]
        return last_own.at[level, column, :, narrow(side, part)]

    def twin_at(side, part, level, column):
        if part == 0:
            return in_twin.at[level, column]
        if part == 1:
            return conv_twin.at[:, level, column, :, narrow(side, part)]
        return last_twin.at[level, column, :, narrow(side, part)]

    def box_at(side, part, name, level):
        box = boxes[name][part]
        if part == 0:
            return box.at[level]
        if part == 1:
            return box.at[level, :, :, narrow(side, part)]
        return box.at[level, :, narrow(side, part)]

    def way_of(sign):
        return lax.shift_right_logical(1 - sign, 1) if not isinstance(sign, int) else (1 - sign) // 2

    def line_at(side, part, kind, sign, level):
        way = way_of(sign)
        if part == 0:
            return in_line.at[way, level]
        if part == 1:
            return conv_line.at[way, level, :, :, narrow(side, part)]
        return last_line.at[KINDS.index(kind), way, level, :, narrow(side, part)]

    def all_units(side, part, count):
        rows = pl.ds(0, 40 * count)
        if part == 0:
            return w_in_hbm.at[rows, :]
        if part == 1:
            return d_conv_flat.at[:, rows, pl.ds(*cut(side, part))]
        return d_last_flat.at[rows, pl.ds(*cut(side, part))]

    def load(side, part):
        source = (d_conv_hbm.at[:, :, :, :, pl.ds(*cut(side, 1))], d_last_hbm.at[:, :, :, pl.ds(*cut(side, 2))])
        target = (conv_own.at[:, :, :, :, narrow(side, 1)], last_own.at[:, :, :, narrow(side, 2)])
        return pltpu.make_async_copy(source[part - 1], target[part - 1], load_sem.at[part - 1])

    def twin_copy(part, kind, to_side):
        column = columns[kind]
        if part == 0:
            src, dst = d_in.at[:, column, to_side], in_twin.at[:, column]
        elif part == 1:
            src = d_conv_hbm.at[:, :, column, :, pl.ds(*cut(to_side, part))]
            dst = conv_twin.at[:, :, column, :, narrow(to_side, part)]
        else:
            src = d_last_hbm.at[:, column, :, pl.ds(*cut(to_side, part))]
            dst = last_twin.at[:, column, :, narrow(to_side, part)]
        return remote(src, dst, twin_send.at[part], twin_recv.at[part, KINDS.index(kind)], "twin")

    def exchange(side, part):
        for kind in ("far", "y", "x", "own"):
            twin_copy(part, kind, 1 - side).start()

    def take_twin(side, part, kind):
        twin_copy(part, kind, side).wait_recv()

    def move(side, part, kind, level, link, box):
        return remote(
            own_at(side, part, level, columns[kind]), box_at(side, part, box, level),
            send_sem.at[part], move_recv.at[("far", "x", "y").index(box), part, level], link,
        )

    def line(side, part, kind, level, sign):
        return remote(
            own_at(side, part, level, columns[kind]), line_at(side, part, kind, sign, level),
            send_sem.at[part], line_recv.at[KINDS.index(kind), way_of(sign), part, level], sign,
        )

    def read(ref):
        return ref[...].astype(F32)

    def each_level(distance, act):
        if distance == 0:
            act(z, 0)
            return

        def one(index, _):
            sign = 1 - 2 * index
            level = z + sign * distance
            pl.when(jnp.logical_and(level >= 0, level < LEVELS))(lambda: act(level, sign))
            return 0

        lax.fori_loop(0, 2, one, 0)

    def both_terms(side, part, level, kind):
        column = columns[kind]
        return read(own_at(side, part, level, column)) + read(twin_at(side, part, level, column))

    def put(side, part, level, kind, value):
        own_at(side, part, level, columns[kind])[...] = value.astype(BF16)

    def roles(part):
        return ("y", "x") if SCATTER_BY_Y[part] else ("x", "y")

    def first(side, part, distance):
        def one(level, sign):
            put(side, part, level, "far", both_terms(side, part, level, "far"))
            move(side, part, "far", level, roles(part)[0], "far").start()

        each_level(distance, one)

    def direct(side, part, distance):
        name = roles(part)[0]

        def one(level, sign):
            put(side, part, level, name, both_terms(side, part, level, name))
            move(side, part, name, level, name, name).start()

        each_level(distance, one)

    def second(side, part, distance):
        link, name = roles(part)

        def one(level, sign):
            move(side, part, "far", level, link, "far").wait_recv()
            put(side, part, level, name, both_terms(side, part, level, name) + read(box_at(side, part, "far", level)))
            move(side, part, name, level, name, name).start()

        each_level(distance, one)

    def line_hop(side, part, kind, distance):
        def one(level, sign):
            total = None
            if not LINE_FIRST[part]:
                for name in ("x", "y"):
                    move(side, part, name, level, name, name).wait_recv()
                total = read(box_at(side, part, "x", level)) + read(box_at(side, part, "y", level))
            terms = both_terms(side, part, level, kind)
            total = terms if total is None else terms + total
            behind = jnp.logical_and(z - sign >= 0, z - sign < LEVELS)

            @pl.when(behind)
            def _():
                line(side, part, kind, level, sign).wait_recv()
                put(side, part, level, kind, total + read(line_at(side, part, kind, sign, level)))

            @pl.when(jnp.logical_not(behind))
            def _():
                put(side, part, level, kind, total)

            line(side, part, kind, level, sign).start()

        each_level(distance, one)

    def add_lines(side, part, kind, target):
        for sign, guard in ((1, z > 0), (-1, z < LEVELS - 1)):

            @pl.when(guard)
            def _(sign=sign):
                line(side, part, kind, z, sign).wait_recv()
                target[...] = (
                    target[...].astype(F32) + read(line_at(side, part, kind, sign, z))
                ).astype(target.dtype)

    def plane(side, part, what):
        link, other = roles(part)
        kind = {"F": "far", "D": link, "S": other}[what]
        own = own_at(side, part, z, columns[kind])
        keep = last_done.at[:, narrow(side, part)]
        keep[...] = both_terms(side, part, z, kind)
        add_lines(side, part, kind, keep)
        if what == "S":
            move(side, part, "far", z, link, "far").wait_recv()
            keep[...] += read(box_at(side, part, "far", z))
        own[...] = keep[...].astype(BF16)
        if what == "F":
            move(side, part, "far", z, link, "far").start()
        else:
            move(side, part, kind, z, kind, kind).start()

    def done(side, part):
        if part == 0:
            target = g_in
        elif part == 1:
            target = conv_done.at[:, :, narrow(side, part)]
        else:
            target = last_done.at[:, narrow(side, part)]
        for name in ("x", "y"):
            move(side, part, name, z, name, name).wait_recv()
        target[...] = (
            both_terms(side, part, z, "own") + read(box_at(side, part, "x", z)) + read(box_at(side, part, "y", z))
        )
        add_lines(side, part, "own", target)
        if part:
            swap(part, side).start()

    def swap(part, from_side):
        lanes_ = narrow(from_side, part)
        if part == 1:
            src, dst = conv_done.at[:, :, lanes_], conv_swap.at[:, :, lanes_]
        else:
            src, dst = last_done.at[:, lanes_], last_swap.at[:, lanes_]
        return remote(src, dst, swap_send.at[part - 1], swap_recv.at[part - 1], "twin")

    def finish(side):
        first_row, count = side * 20, 20
        for part, mine, other, target in ((2, last_done, last_swap, g_last), (1, conv_done, conv_swap, g_conv)):
            swap(part, 1 - side).wait_recv()
            for refs, owner in ((mine, side), (other, 1 - side)):
                start, width = cut(owner, part)
                if part == 1:
                    target[:, :, pl.ds(start, width)] = refs[:, pl.ds(first_row, count), pl.ds(0, width)]
                else:
                    target[:, pl.ds(start, width)] = refs[pl.ds(first_row, count), pl.ds(0, width)]
        for part in range(3):
            if part:
                swap(part, side).wait_send()
            view = all_units(1 - side, part, CHIPS)
            remote(view, view, twin_send.at[part], twin_recv.at[part, 0], "twin").wait_send()
            view = all_units(side, part, CHIPS - 1)
            remote(view, view, send_sem.at[part], twin_recv.at[part, 0], "twin").wait_send()


    def in_plane():
        return y * 4 + x * 2 + core

    def plane_copy(offset):
        other, where = plane_peer(offset)
        return pltpu.make_async_remote_copy(
            src_ref=packed.at[:, other], dst_ref=plane_box.at[in_plane()], send_sem=vec_sem.at[0],
            recv_sem=vec_sem.at[1], device_id=where, device_id_type=MESH,
        )

    def level_copy(step):
        level = lax.rem(z + step, LEVELS)
        return pltpu.make_async_remote_copy(
            src_ref=plane_box.at[0, level], dst_ref=level_box.at[z], send_sem=vec_sem.at[2], recv_sem=vec_sem.at[3],
            device_id=device(level, y, x, core), device_id_type=MESH,
        )

    def sum_lines(ref, indices, width):
        return [jnp.sum(ref[pl.ds(8 * index, 8), pl.ds(0, width)], axis=0, keepdims=True) for index in indices]

    def vec_early():
        packed[...] = jnp.zeros_like(packed)
        pack_sums(0, sum_lines(sums, (2,), 1280), WIDE_OFFSETS[2:], packed)
        pack_sums(1, sum_lines(sums, range(3, 9), 640), SLIM_OFFSETS, packed)

    def vec_start(side):
        pack_sums(0, sum_lines(own_sums, (0, 1), 1280), WIDE_OFFSETS[:2], packed)
        for offset in range(1, 8):
            plane_copy(offset).start()
        for level in range(LEVELS):
            plane_box[pl.ds(in_plane(), 1), level] = packed[level, pl.ds(in_plane(), 1)]

    def vec_middle(side):
        view = plane_box.at[pl.ds(0, 7)]
        remote(view, view, vec_sem.at[0], vec_sem.at[1], "twin").wait()
        total = jnp.sum(plane_box[...], axis=0)
        plane_box[0] = total
        level_box[pl.ds(z, 1)] = plane_box[0, pl.ds(z, 1)]
        for step in range(1, LEVELS):
            level_copy(step).start()

    def vec_end(side):
        view = level_box.at[pl.ds(0, LEVELS - 1)]
        remote(view, view, vec_sem.at[2], vec_sem.at[3], "twin").wait()
        g_vec[...] = jnp.sum(level_box[...], axis=0)

    def ready(side):
        d_in[...] = d_in_sum[...].astype(BF16).reshape(d_in.shape)
        exchange(side, 0)

    actions = {
        "load": lambda side, part: load(side, part).wait(), "twin": take_twin, "first": first, "direct": direct,
        "second": second, "line": line_hop, "plane": plane, "done": done, "ready": ready, "vec_start": vec_start,
        "vec_middle": vec_middle, "vec_end": vec_end, "finish": finish,
    }

    def either(event):
        return event[0] in ("ready", "vec_start", "vec_middle", "vec_end") or event[1:2] == (0,)

    def perform(events):
        for alike, group in itertools.groupby(events, either):
            group = tuple(group)
            if alike:
                for event in group:
                    actions[event[0]](core, *event[1:])
                continue
            for side in range(2):

                @pl.when(core == side)
                def _(side=side, group=group):
                    for event in group:
                        actions[event[0]](side, *event[1:])

    def rows_of(tile):
        return pl.ds(pl.multiple_of(tile * TILE, TILE), TILE)

    tiles_of = ((u1, u1_hbm), (dh1, dh1_hbm), (slope1, slope1_hbm), (xh1, xh1_hbm), (scale1, scale1_hbm), (grads, grads_hbm))

    def half_load(index, half):
        target, source = tiles_of[index]
        rows = pl.ds(half * 1024, 1024)
        return pltpu.make_async_copy(source.at[rows, :], target.at[rows, :], tile_sem.at[index, half])

    def store(tile):
        return pltpu.make_async_copy(grads.at[rows_of(tile), :], grad_tokens.at[rows_of(tile), :], store_sem.at[tile])

    weight_load = pltpu.make_async_copy(w_in_hbm, w_in, weight_sem.at[0])

    barrier = pltpu.get_barrier_semaphore()
    for offset in range(1, 8):
        pl.semaphore_signal(barrier, inc=1, device_id=plane_peer(offset)[1], device_id_type=MESH)
    for step in range(1, LEVELS):
        pl.semaphore_signal(
            barrier, inc=1, device_id=device(lax.rem(z + step, LEVELS), y, x, core), device_id_type=MESH
        )
    for side in range(2):

        @pl.when(core == side)
        def _(side=side):
            for part in (1, 2):
                load(side, part).start()

    for half in range(2):
        half_load(0, half).start()
        half_load(1, half).start()
    weight_load.start()
    pl.semaphore_wait(barrier, 7 + LEVELS - 1)
    back_copies = [
        remote(dh1_share, dh1_back, back_send.at[0], back_recv.at[0], "twin"),
        remote(out_share, out_back, back_send.at[1], back_recv.at[1], "twin"),
    ]
    for side in range(2):

        @pl.when(core == side)
        def _(side=side):
            for kind in ("far", "y", "x", "own"):
                for part in (1, 2):
                    twin_copy(part, kind, 1 - side).start()
                if kind == "far":
                    back_copies[0].start()

    for half in range(2):
        for index in range(2, 6):
            half_load(index, half).start()
    own_sums[...] = jnp.zeros_like(own_sums)
    vec_early()

    def weight_tile(tile, _):
        for index in range(weight_steps):
            if SCATTER_PLAN[index]:
                pl.when(tile == index)(functools.partial(perform, SCATTER_PLAN[index]))
            if index in (0, weight_steps // 2):
                for array in range(2):
                    pl.when(tile == index)(half_load(array, 0 if index == 0 else 1).wait)
        rows = pl.ds(pl.multiple_of(tile * 512, 512), 512)
        pl.when(tile == weight_steps // 2)(back_copies[0].wait)

        @pl.when(tile >= weight_steps // 2)
        def _():
            again = pl.ds(pl.multiple_of(tile * 512 - 1024, 512), 512)
            dh1[rows, :] = dh1[rows, :] + dh1_back[again, :]

        term = lax.dot_general(u1[rows, :], dh1[rows, :], (((0,), (0,)), ((), ())), preferred_element_type=F32)

        @pl.when(tile == 0)
        def _():
            d_in_sum[...] = term

        @pl.when(tile > 0)
        def _():
            d_in_sum[...] += term

        return 0

    lax.fori_loop(0, weight_steps, weight_tile, 0)
    weight_load.wait()
    w_in_t[...] = w_in[...].T

    def token_tile(tile, _):
        for index in range(steps):
            if SCATTER_PLAN[weight_steps + index]:
                pl.when(tile == index)(functools.partial(perform, SCATTER_PLAN[weight_steps + index]))
            if index == 1:
                pl.when(tile == index)(back_copies[1].start)
            if index in (0, steps // 2):
                for array in range(2, 6):
                    pl.when(tile == index)(half_load(array, 0 if index == 0 else 1).wait)
        rows = rows_of(tile)
        back = jnp.dot(dh1[rows, :], w_in_t[...], preferred_element_type=F32)
        norm = xh1[rows, :].astype(F32)
        slope_grad = back * slope1[rows, :].astype(F32)
        for index, values in enumerate((slope_grad * norm, slope_grad)):
            own_sums[pl.ds(8 * index, 8), :] += jnp.sum(values.reshape(TILE // 8, 8, 1280), axis=0)
        err = slope_grad * vectors[pl.ds(0, 1), :]
        mean = jnp.sum(err, axis=1, keepdims=True) * (1.0 / 1280)
        along = jnp.sum(err * norm, axis=1, keepdims=True) * (1.0 / 1280)
        grads[rows, :] = (
            grads[rows, :].astype(F32) + lanes(scale1[rows, :], 1280) * (err - mean - norm * along)
        ).astype(BF16)
        store(tile).start()
        return 0

    lax.fori_loop(0, steps, token_tile, 0)
    perform(SCATTER_PLAN[weight_steps + steps])
    back_copies[1].wait()
    for tile in range(steps):
        store(tile).wait()


def scatter_stage(u1, dh1, slope1, xh1, scale1, grads, w_in, vectors, sums, d_conv, d_last, dh1_share, out_share):
    rows = u1.shape[0]
    steps = rows // TILE
    shape = jax.ShapeDtypeStruct
    vmem = pl.BlockSpec(memory_space=pltpu.VMEM)
    conv_box = (LEVELS, KSIZE, 40, 384)
    last_box = (LEVELS, 40, 896)
    in_box = (LEVELS, 40, 640)
    dma = pltpu.SemaphoreType.DMA
    return pl.pallas_call(
        scatter_kernel,
        in_specs=[HBM] * 7 + [vmem] * 2 + [HBM] * 6,
        out_specs=[HBM] + [vmem] * 4 + [HBM],
        out_shape=[
            shape((rows, 1280), BF16), shape((40, 640), F32), shape((KSIZE, 20, 640), F32), shape((20, 1280), F32),
            shape((2, 128), F32), shape((1024, 1280), BF16),
        ],
        scratch_shapes=[
            pltpu.VMEM((rows, 1280), BF16),
            pltpu.VMEM((rows, 640), BF16),
            pltpu.VMEM((rows, 1280), BF16),
            pltpu.VMEM((rows, 1280), BF16),
            pltpu.VMEM((rows, 128), F32),
            pltpu.VMEM((rows, 1280), BF16),
            pltpu.VMEM((1280, 640), BF16),
            pltpu.VMEM((640, 1280), BF16),
            pltpu.VMEM((1024, 640), BF16),
            pltpu.VMEM((1280, 640), F32),
            pltpu.VMEM((LEVELS, 4, 2, 40, 640), BF16),
            pltpu.VMEM((16, 1280), F32),
            pltpu.VMEM((LEVELS, 8, 2, 128), F32),
            pltpu.VMEM((8, LEVELS, 2, 128), F32),
            pltpu.VMEM((LEVELS, 2, 128), F32),
            pltpu.VMEM((KSIZE, LEVELS, 4, 40, 384), BF16),
            pltpu.VMEM((KSIZE, LEVELS, 4, 40, 384), BF16),
            pltpu.VMEM(conv_box, BF16),
            pltpu.VMEM(conv_box, BF16),
            pltpu.VMEM(conv_box, BF16),
            pltpu.VMEM((2,) + conv_box, BF16),
            pltpu.VMEM((KSIZE, 40, 384), F32),
            pltpu.VMEM((KSIZE, 40, 384), F32),
            pltpu.VMEM((LEVELS, 4, 40, 896), BF16),
            pltpu.VMEM((LEVELS, 4, 40, 896), BF16),
            pltpu.VMEM(last_box, BF16),
            pltpu.VMEM(last_box, BF16),
            pltpu.VMEM(last_box, BF16),
            pltpu.VMEM((4, 2) + last_box, BF16),
            pltpu.VMEM((40, 896), F32),
            pltpu.VMEM((40, 896), F32),
            pltpu.VMEM((LEVELS, 4, 40, 640), BF16),
            pltpu.VMEM(in_box, BF16),
            pltpu.VMEM(in_box, BF16),
            pltpu.VMEM(in_box, BF16),
            pltpu.VMEM((2,) + in_box, BF16),
            dma((6, 2)), dma((1,)), dma((steps,)), dma((4,)), dma((2,)), dma((3,)), dma((3, 4)),
            dma((3,)), dma((3, 3, LEVELS)), dma((4, 2, 3, LEVELS)), dma((2,)), dma((2,)), dma((2,)), dma((2,)),
        ],
        compiler_params=pltpu.CompilerParams(collective_id=1, has_side_effects=True, vmem_limit_bytes=VMEM_BYTES),
        name="scatter_stage",
    )(
        u1, dh1, slope1, xh1, scale1, grads, w_in, vectors, sums,
        d_conv.reshape(KSIZE, LEVELS, 4, 40, 640), d_last.reshape(LEVELS, 4, 40, 1280), d_conv, d_last, dh1_share, out_share,
    )


def settle_kernel(
    vectors, result_in, out_back, rows_hbm, g_in, g_conv, g_last, g_vec,
    result, rows_out, in_out, conv_out, last_out, *rest
):
    vectors_out, (buffer, moved, load_sem, store_sem, moved_sem) = rest[:9], rest[9:]
    count = buffer.shape[0]
    chunk = buffer.shape[1]
    loads = [
        pltpu.make_async_copy(rows_hbm.at[pl.ds(index * chunk, chunk), :], buffer.at[index], load_sem.at[index])
        for index in range(count)
    ]
    stores = [
        pltpu.make_async_copy(buffer.at[index], rows_out.at[pl.ds(index * chunk, chunk), :], store_sem.at[index])
        for index in range(count)
    ]
    for copy in loads:
        copy.start()
    in_out[...] = g_in[...]
    conv_out[...] = g_conv[...]
    last_out[...] = g_last[...]
    places = [(0, offset, 40) for offset in WIDE_OFFSETS] + [(1, offset, 20) for offset in SLIM_OFFSETS]
    for target, (plane, offset, width) in zip(vectors_out, places):
        target[...] = g_vec[pl.ds(plane, 1), pl.ds(offset, width)]
    _, second_units, _, give, _ = unit_share(read_lengths(vectors))
    kept = second_units - give
    end = jnp.where(give > 0, 2 * lax.div(second_units + 1, 2), kept)

    def moved_load(unit):
        rows = pl.ds(pl.multiple_of(unit * UNIT, UNIT), UNIT)
        return pltpu.make_async_copy(out_back.at[rows, :], moved.at[rows, :], moved_sem.at[0, unit])

    def moved_store(unit):
        rows = pl.ds(pl.multiple_of(unit * UNIT, UNIT), UNIT)
        target = pl.ds(pl.multiple_of(1024 + unit * UNIT, UNIT), UNIT)
        return pltpu.make_async_copy(moved.at[rows, :], result.at[target, :], moved_sem.at[1, unit])

    def each(act):
        def one(unit, _):
            act(unit)
            return 0

        lax.fori_loop(kept, end, one, 0)

    def pass_moved(unit):
        moved_load(unit).wait()
        moved_store(unit).start()

    each(lambda unit: moved_load(unit).start())
    for load, store in zip(loads, stores):
        load.wait()
        store.start()
    each(pass_moved)
    each(lambda unit: moved_store(unit).wait())
    for copy in stores:
        copy.wait()


def settle_stage(vectors, result, out_back, rows, g_in, g_conv, g_last, g_vec):
    chunks = 8
    shape = jax.ShapeDtypeStruct
    vmem = pl.BlockSpec(memory_space=pltpu.VMEM)
    return pl.pallas_call(
        settle_kernel,
        in_specs=[vmem] + [HBM] * 3 + [vmem] * 4,
        out_specs=[HBM] * 2 + [vmem] * 12,
        out_shape=[shape(v.shape, v.dtype) for v in (result, rows, g_in, g_conv, g_last)]
        + [shape((1, 40), F32)] * 3
        + [shape((1, 20), F32)] * 6,
        scratch_shapes=[
            pltpu.VMEM((chunks, rows.shape[0] // chunks, rows.shape[1]), rows.dtype),
            pltpu.VMEM((1024, 1280), BF16),
            pltpu.SemaphoreType.DMA((chunks,)),
            pltpu.SemaphoreType.DMA((chunks,)),
            pltpu.SemaphoreType.DMA((2, 1024 // UNIT)),
        ],
        input_output_aliases={1: 0},
        compiler_params=pltpu.CompilerParams(vmem_limit_bytes=VMEM_BYTES),
        name="settle_stage",
    )(vectors, result, out_back, rows, g_in, g_conv, g_last, g_vec)


def kernel_body(
    tokens, out_grad, lengths, ln1_gain, ln1_bias, w_in, b_in, ln2_gain, ln2_bias,
    w_conv, b_conv, ln3_gain, ln3_bias, w_out, b_out,
):
    proteins, length_pad, width = tokens.shape
    rows = tokens.reshape(proteins * length_pad, width)
    grads = out_grad.reshape(proteins * length_pad, width)
    vec = pack_vectors(
        ln1_gain, ln1_bias, b_in, ln2_gain, ln2_bias, b_conv, ln3_gain, ln3_bias, b_out, lengths
    )
    u1, slope1, xh1, scale1, xh2, slope2, scale2, u2, vectors, in_full, conv_full, out_full, twins = gather_stage(
        rows, grads, vec, w_in, w_conv, w_out
    )
    result, dh1, out_share, dh1_share, d_conv, d_last, sums = middle_stage(
        vectors, u2, xh2, slope2, scale2, grads, rows, conv_full, out_full, twins
    )
    *owned, out_back = scatter_stage(
        u1, dh1, slope1, xh1, scale1, grads, in_full, vectors, sums, d_conv, d_last, dh1_share, out_share
    )
    result, grad_rows, g_in, g_conv, g_last, *lines = settle_stage(vectors, result, out_back, *owned)
    lines = [line.reshape(line.shape[1]) for line in lines]
    wide, slim = lines[:3], lines[3:]
    return (
        result.reshape(tokens.shape), grad_rows.reshape(tokens.shape),
        wide[0], wide[1], g_in, slim[0], slim[1], slim[2], g_conv, slim[3], slim[4], slim[5], g_last, wide[2],
    )


def layer_norm(values, gain, bias):
    center = values - jnp.mean(values, axis=-1, keepdims=True)
    var_rows = jnp.mean(center * center, axis=-1, keepdims=True)
    return center * lax.rsqrt(var_rows + EPS) * gain + bias


def norm_gelu(values, gain, bias):
    return jax.nn.gelu(layer_norm(values, gain, bias), approximate=False)


def collect(
    ln1_gain,
    ln1_bias,
    w_in,
    b_in,
    ln2_gain,
    ln2_bias,
    w_conv,
    b_conv,
    ln3_gain,
    ln3_bias,
    w_out,
    b_out,
):
    return (
        lax.all_gather(ln1_gain, ("dp", "fsdp"), axis=0, tiled=True),
        lax.all_gather(ln1_bias, ("dp", "fsdp"), axis=0, tiled=True),
        lax.all_gather(w_in, ("dp", "fsdp"), axis=0, tiled=True),
        lax.all_gather(b_in, ("dp", "fsdp"), axis=0, tiled=True),
        lax.all_gather(ln2_gain, ("dp", "fsdp"), axis=0, tiled=True),
        lax.all_gather(ln2_bias, ("dp", "fsdp"), axis=0, tiled=True),
        lax.all_gather(w_conv, ("dp", "fsdp"), axis=1, tiled=True),
        lax.all_gather(b_conv, ("dp", "fsdp"), axis=0, tiled=True),
        lax.all_gather(ln3_gain, ("dp", "fsdp"), axis=0, tiled=True),
        lax.all_gather(ln3_bias, ("dp", "fsdp"), axis=0, tiled=True),
        lax.all_gather(w_out, ("dp", "fsdp"), axis=0, tiled=True),
        lax.all_gather(b_out, ("dp", "fsdp"), axis=0, tiled=True),
    )


def spread(
    term_g1,
    term_b1,
    term_wi,
    term_bi,
    term_g2,
    term_b2,
    term_wc,
    term_bc,
    term_g3,
    term_b3,
    term_wo,
    term_bo,
):
    return (
        lax.psum_scatter(term_g1, ("dp", "fsdp"), scatter_dimension=0, tiled=True),
        lax.psum_scatter(term_b1, ("dp", "fsdp"), scatter_dimension=0, tiled=True),
        lax.psum_scatter(term_wi, ("dp", "fsdp"), scatter_dimension=0, tiled=True),
        lax.psum_scatter(term_bi, ("dp", "fsdp"), scatter_dimension=0, tiled=True),
        lax.psum_scatter(term_g2, ("dp", "fsdp"), scatter_dimension=0, tiled=True),
        lax.psum_scatter(term_b2, ("dp", "fsdp"), scatter_dimension=0, tiled=True),
        lax.psum_scatter(term_wc, ("dp", "fsdp"), scatter_dimension=1, tiled=True),
        lax.psum_scatter(term_bc, ("dp", "fsdp"), scatter_dimension=0, tiled=True),
        lax.psum_scatter(term_g3, ("dp", "fsdp"), scatter_dimension=0, tiled=True),
        lax.psum_scatter(term_b3, ("dp", "fsdp"), scatter_dimension=0, tiled=True),
        lax.psum_scatter(term_wo, ("dp", "fsdp"), scatter_dimension=0, tiled=True),
        lax.psum_scatter(term_bo, ("dp", "fsdp"), scatter_dimension=0, tiled=True),
    )


def dilate(padded, kernel, length_pad):
    total = jnp.zeros((padded.shape[0], length_pad, kernel.shape[2]), jnp.float32)
    for kernel_tap in range(kernel.shape[0]):
        window = padded[:, kernel_tap * DILATION : kernel_tap * DILATION + length_pad]
        total = total + jnp.einsum(
            "pli,io->plo", window, kernel[kernel_tap], preferred_element_type=jnp.float32
        )
    return total


def plain_body(
    tokens,
    out_grad,
    lengths,
    ln1_gain,
    ln1_bias,
    w_in,
    b_in,
    ln2_gain,
    ln2_bias,
    w_conv,
    b_conv,
    ln3_gain,
    ln3_bias,
    w_out,
    b_out,
):
    proteins, length_pad, width = tokens.shape
    row_count = proteins * length_pad
    reach = KSIZE // 2 * DILATION
    positions = lax.broadcasted_iota(jnp.int32, (proteins, length_pad), 1)
    live = (positions < lengths[:, None]).astype(jnp.float32).reshape(row_count, 1)
    full = collect(
        ln1_gain,
        ln1_bias,
        w_in,
        b_in,
        ln2_gain,
        ln2_bias,
        w_conv,
        b_conv,
        ln3_gain,
        ln3_bias,
        w_out,
        b_out,
    )
    (
        gain_one,
        bias_one,
        first_matrix,
        first_bias,
        gain_two,
        bias_two,
        conv_kernel,
        conv_bias,
        gain_three,
        bias_three,
        last_matrix,
        last_bias,
    ) = full
    inner = first_matrix.shape[1]
    row_tokens = tokens.reshape(row_count, width).astype(jnp.float32)
    act_one, pull_one = jax.vjp(
        norm_gelu, row_tokens, gain_one.astype(jnp.float32), bias_one.astype(jnp.float32)
    )
    inner_one = act_one.astype(jnp.bfloat16)
    hidden_one = jnp.dot(
        inner_one, first_matrix, preferred_element_type=jnp.float32
    ) + first_bias.astype(jnp.float32)
    act_two, pull_two = jax.vjp(
        norm_gelu, hidden_one, gain_two.astype(jnp.float32), bias_two.astype(jnp.float32)
    )
    inner_two = (act_two * live).astype(jnp.bfloat16)
    padded_two = jnp.pad(
        inner_two.reshape(proteins, length_pad, inner), ((0, 0), (reach, reach), (0, 0))
    )
    hidden_two = dilate(padded_two, conv_kernel, length_pad).reshape(
        row_count, inner
    ) + conv_bias.astype(jnp.float32)
    act_three, pull_three = jax.vjp(
        norm_gelu, hidden_two, gain_three.astype(jnp.float32), bias_three.astype(jnp.float32)
    )
    inner_three = act_three.astype(jnp.bfloat16)
    branch = jnp.dot(
        inner_three, last_matrix, preferred_element_type=jnp.float32
    ) + last_bias.astype(jnp.float32)
    result = (row_tokens + live * branch).astype(jnp.bfloat16).reshape(proteins, length_pad, width)
    again = collect(
        ln1_gain,
        ln1_bias,
        w_in,
        b_in,
        ln2_gain,
        ln2_bias,
        w_conv,
        b_conv,
        ln3_gain,
        ln3_bias,
        w_out,
        b_out,
    )
    (
        again_g1,
        again_b1,
        back_first,
        again_bi,
        again_g2,
        again_b2,
        back_kernel,
        again_bc,
        again_g3,
        again_b3,
        back_last,
        again_bo,
    ) = again
    pull_one = jax.vjp(
        norm_gelu, row_tokens, again_g1.astype(jnp.float32), again_b1.astype(jnp.float32)
    )[1]
    pull_two = jax.vjp(
        norm_gelu, hidden_one, again_g2.astype(jnp.float32), again_b2.astype(jnp.float32)
    )[1]
    pull_three = jax.vjp(
        norm_gelu, hidden_two, again_g3.astype(jnp.float32), again_b3.astype(jnp.float32)
    )[1]
    grad_rows = out_grad.reshape(row_count, width)
    grad_branch = grad_rows * live.astype(jnp.bfloat16)
    term_wo = jnp.einsum("ri,rd->id", inner_three, grad_branch, preferred_element_type=jnp.float32)
    term_bo = jnp.sum(grad_branch.astype(jnp.float32), axis=0)
    grad_three = jnp.einsum("rd,id->ri", grad_branch, back_last, preferred_element_type=jnp.float32)
    d_hidden_two, term_g3, term_b3 = pull_three(grad_three)
    low_two = d_hidden_two.astype(jnp.bfloat16)
    term_bc = jnp.sum(low_two.astype(jnp.float32), axis=0)
    padded_grad = jnp.pad(
        low_two.reshape(proteins, length_pad, inner), ((0, 0), (reach, reach), (0, 0))
    )
    grad_view = low_two.reshape(proteins, length_pad, inner)
    kernel_terms = []
    grad_two = jnp.zeros((proteins, length_pad, inner), jnp.float32)
    taps = back_kernel.shape[0]
    for kernel_tap in range(taps):
        window = padded_two[:, kernel_tap * DILATION : kernel_tap * DILATION + length_pad]
        kernel_terms.append(
            jnp.einsum("pli,plo->io", window, grad_view, preferred_element_type=jnp.float32)
        )
        mirror = (taps - 1 - kernel_tap) * DILATION
        grad_window = padded_grad[:, mirror : mirror + length_pad]
        grad_two = grad_two + jnp.einsum(
            "plo,io->pli", grad_window, back_kernel[kernel_tap], preferred_element_type=jnp.float32
        )
    term_wc = jnp.stack(kernel_terms, axis=0)
    grad_two = grad_two.reshape(row_count, inner) * live
    d_hidden_one, term_g2, term_b2 = pull_two(grad_two)
    low_one = d_hidden_one.astype(jnp.bfloat16)
    term_wi = jnp.einsum("rd,ri->di", inner_one, low_one, preferred_element_type=jnp.float32)
    term_bi = jnp.sum(low_one.astype(jnp.float32), axis=0)
    grad_one = jnp.einsum("ri,di->rd", low_one, back_first, preferred_element_type=jnp.float32)
    d_tokens, term_g1, term_b1 = pull_one(grad_one)
    grad_tokens = (
        (grad_rows.astype(jnp.float32) + d_tokens)
        .astype(jnp.bfloat16)
        .reshape(proteins, length_pad, width)
    )
    owned = spread(
        term_g1,
        term_b1,
        term_wi,
        term_bi,
        term_g2,
        term_b2,
        term_wc,
        term_bc,
        term_g3,
        term_b3,
        term_wo,
        term_bo,
    )
    return (
        result,
        grad_tokens,
        owned[0],
        owned[1],
        owned[2],
        owned[3],
        owned[4],
        owned[5],
        owned[6],
        owned[7],
        owned[8],
        owned[9],
        owned[10],
        owned[11],
    )


def solution(mesh):
    both = ("dp", "fsdp")
    by_row = P(both)
    in_specs = (
        P(both, None, None), P(both, None, None), by_row, by_row, by_row, P(both, None), by_row, by_row, by_row,
        P(None, both, None), by_row, by_row, by_row, P(both, None), by_row,
    )
    out_specs = (
        P(both, None, None), P(both, None, None), by_row, by_row, P(both, None), by_row, by_row, by_row,
        P(None, both, None), by_row, by_row, by_row, P(both, None), by_row,
    )
    body = kernel_body if (mesh.shape["dp"], mesh.shape["fsdp"]) == (8, 4) else plain_body
    return jax.shard_map(body, mesh=mesh, in_specs=in_specs, out_specs=out_specs, check_vma=False)
```

```python
import functools
import itertools

import jax
import jax.numpy as jnp
from jax import lax
from jax.experimental import pallas as pl
from jax.experimental.pallas import tpu as pltpu
from jax.sharding import PartitionSpec as P

KSIZE = 5
DILATION = 8
EPS = 1e-05
HALF_ROOT = 0.7071067811865476
PHI_SCALE = 0.3989422804014327
F32 = jnp.float32
BF16 = jnp.bfloat16
MESH = pl.DeviceIdType.MESH
VMEM_BYTES = 62 * 2**20
HBM = pl.BlockSpec(memory_space=pl.ANY)
LEVELS = 4
CHIPS = 16
DEVICES = 32
TILE = 256
CONV_COLS = ((0, 384), (384, 256))
OUT_COLS = ((0, 384), (384, 896))
WIDE_OFFSETS = (0, 40, 80)
SLIM_OFFSETS = (0, 20, 40, 60, 80, 100)


def place():
    dp = lax.axis_index("dp")
    fs = lax.axis_index("fsdp")
    return lax.div(dp, 2), lax.rem(dp, 2), lax.div(fs, 2), lax.rem(fs, 2)


def device(z, y, x, core):
    return (z * 2 + y, x * 2 + core)


def chip(z, y, x):
    return (z * 2 + y) * 2 + x


def peer_of(step):
    mine = lax.axis_index("dp") * 4 + lax.axis_index("fsdp")
    other = lax.rem(mine + step, DEVICES)
    return mine, other, (lax.div(other, 4), lax.rem(other, 4))


def greet_all():
    barrier = pltpu.get_barrier_semaphore()

    def greet(step, _):
        _, _, target = peer_of(step)
        pl.semaphore_signal(barrier, inc=1, device_id=target, device_id_type=MESH)
        return 0

    lax.fori_loop(1, DEVICES, greet, 0)
    pl.semaphore_wait(barrier, DEVICES - 1)


def chunk_masks(width, chunk):
    scale = -(-65536 // chunk)
    column = lax.broadcasted_iota(jnp.int32, (DEVICES, width), 1)
    row = lax.broadcasted_iota(jnp.int32, (DEVICES, width), 0)
    owner = lax.shift_right_logical(column * scale, 16) == row
    place_col = lax.broadcasted_iota(jnp.int32, (128, width), 1)
    place_row = lax.broadcasted_iota(jnp.int32, (128, width), 0)
    slot = place_col - lax.shift_right_logical(place_col * scale, 16) * chunk
    return owner, slot, place_row


def unpack_vectors(packed_ref, vectors_ref):
    for plane, (width, chunk, offsets) in enumerate(
        ((1280, 40, WIDE_OFFSETS), (640, 20, SLIM_OFFSETS))
    ):
        owner, slot, row = chunk_masks(width, chunk)
        packed = packed_ref[:, plane, :].astype(BF16)
        for index, offset in enumerate(offsets):
            pick = (slot + offset == row).astype(F32).astype(BF16)
            spread = jnp.dot(packed, pick, preferred_element_type=F32)
            line = jnp.sum(jnp.where(owner, spread, 0.0), axis=0, keepdims=True)
            vectors_ref[pl.ds(plane * 3 + index, 1), pl.ds(0, width)] = line


def lanes(column, width):
    return jnp.concatenate([column] * (width // 128), axis=1)


def norm_parts(values):
    width = values.shape[1]
    mean = jnp.sum(values, axis=1, keepdims=True) * (1.0 / width)
    center = values - mean
    var = jnp.sum(center * center, axis=1, keepdims=True) * (1.0 / width)
    scale = lax.rsqrt(var + EPS)
    return center * scale, scale


def gelu_parts(arg):
    normal = 0.5 + 0.5 * lax.erf(arg * HALF_ROOT)
    slope = normal + arg * (PHI_SCALE * jnp.exp(-0.5 * (arg * arg)))
    return arg * normal, slope


PART_COUNT = 4
CONV_TAPS = {1: (0, 3), 2: (3, 2)}
BY_Y = (False, True, False, True)
PLANE_FIRST = (False, False, False, True)
KINDS = ("own", "x", "y", "far")
GATHER_PLAN = (
    (
        ("vec_begin",), ("send", 0), ("begin",), ("assemble",), ("send", 3), ("vec_plane",), ("y", 0, 0),
        ("own", 0, 1), ("send", 1), ("vec_pass", 1), ("own", 0, 2), ("send", 2), ("vec_pass", 2), ("y", 3, 0),
        ("x", 3, 0), ("x", 0, 0), ("own", 1, 1), ("own", 0, 3), ("share", "own", 0), ("y", 0, 1), ("vec_pass", 3),
        ("vectors",), ("x", 1, 0), ("x", 0, 1),
    ),
    (),
    (
        ("y", 0, 2), ("own", 2, 1), ("far", 3, 0),
    ),
    (),
    (
        ("y", 0, 3), ("share", "y", 0), ("x", 0, 2), ("own", 1, 2), ("y", 1, 0), ("y", 3, 1),
    ),
    (
        ("own", 2, 2), ("x", 3, 1), ("x", 2, 0),
    ),
    (),
    (
        ("y", 2, 0), ("own", 3, 1), ("x", 1, 1),
    ),
    (
        ("far", 3, 1), ("far", 0, 1), ("y", 1, 1), ("x", 0, 3), ("share", "x", 0), ("far", 0, 2), ("far", 0, 0),
        ("own", 1, 3), ("share", "own", 1), ("far", 0, 3), ("share", "far", 0), ("far", 1, 0), ("y", 2, 1),
        ("y", 3, 2), ("w_in",),
    ),
    (
        ("own", 2, 3), ("share", "own", 2),
    ),
    (),
    (
        ("x", 3, 2), ("x", 1, 2),
    ),
    (
        ("x", 2, 1), ("y", 1, 2), ("y", 2, 2), ("own", 3, 2), ("far", 3, 2), ("x", 1, 3), ("share", "x", 1),
        ("x", 2, 2), ("y", 2, 3), ("share", "y", 2),
    ),
    (),
    (
        ("y", 1, 3), ("share", "y", 1), ("far", 2, 0),
    ),
    (
        ("far", 1, 1), ("x", 2, 3), ("share", "x", 2),
    ),
    (
        ("y", 3, 3), ("share", "y", 3), ("far", 2, 1), ("own", 3, 3), ("share", "own", 3), ("far", 1, 2), ("x", 3, 3),
        ("share", "x", 3), ("far", 1, 3), ("share", "far", 1), ("far", 2, 2), ("far", 2, 3), ("share", "far", 2),
        ("far", 3, 3), ("share", "far", 3), ("finish",),
    ),
)


def plane_peer(offset):
    z, y, x, core = place()
    other = lax.rem(y * 4 + x * 2 + core + offset, 8)
    return other, (z * 2 + lax.div(other, 4), lax.rem(other, 4))


def greet_near(z, y, x, core):
    barrier = pltpu.get_barrier_semaphore()

    def greet(target):
        pl.semaphore_signal(barrier, inc=1, device_id=target, device_id_type=MESH)

    for offset in range(1, 8):
        greet(plane_peer(offset)[1])
    pl.when(z > 0)(lambda: greet(device(z - 1, y, x, core)))
    pl.when(z < LEVELS - 1)(lambda: greet(device(z + 1, y, x, core)))
    pl.semaphore_wait(barrier, 7 + (z > 0).astype(jnp.int32) + (z < LEVELS - 1).astype(jnp.int32))


def each_level(z, distance, act):
    if distance == 0:
        act(z, 0)
        return
    pl.when(z + distance < LEVELS)(lambda: act(z + distance, 1))
    pl.when(z - distance >= 0)(lambda: act(z - distance, -1))


def gather_kernel(
    tokens_hbm, grads_hbm, vec, w_in, w_conv, w_out,
    u1_hbm, slope1_hbm, xh1_hbm, scale1_hbm, xh2_hbm, slope2_hbm, scale2_hbm, u2_hbm, vectors_out,
    in_full, conv_full, out_full,
    u2_share, xh2_share, slope2_share, scale2_share, grads_share, tokens_share,
    packed, in_vmem, conv_twin, out_twin, conv_own, out_own,
    tokens, u1, slope1, xh1, scale1, xh2, slope2, scale2, u2, token_sem, store_sem, share_send, share_recv,
    vec_send, vec_recv, link_send, link_recv, twin_recv, pair_send, pair_recv, own_sem, load_sem,
):
    z, y, x, core = place()
    here = 2 * y + x
    steps = 2048 // TILE
    columns = {"own": here, "x": 2 * y + (1 - x), "y": 2 * (1 - y) + x, "far": 2 * (1 - y) + (1 - x)}

    def piece(part, level, column, side):
        if part == 0:
            return in_vmem.at[pl.ds(pl.multiple_of((level * 4 + column) * 80 + side * 40, 8), 40), :]
        if part in CONV_TAPS:
            return conv_full.at[pl.ds(*CONV_TAPS[part]), level, column, :, pl.ds(*CONV_COLS[side])]
        return out_full.at[level, column, :, pl.ds(*OUT_COLS[side])]

    def pieces(part, column, side):
        if part in CONV_TAPS:
            return conv_full.at[pl.ds(*CONV_TAPS[part]), :, column, :, pl.ds(*CONV_COLS[side])]
        return out_full.at[:, column, :, pl.ds(*OUT_COLS[side])]

    def span(part, side, count):
        if part == 0:
            return in_vmem.at[pl.ds(0, 40 * count), :]
        rows, columns_ = (LEVELS, count // LEVELS) if count % LEVELS == 0 else (count, 1)
        if part in CONV_TAPS:
            return conv_full.at[
                pl.ds(*CONV_TAPS[part]), pl.ds(0, rows), pl.ds(0, columns_), :, pl.ds(*CONV_COLS[side])
            ]
        return out_full.at[pl.ds(0, rows), pl.ds(0, columns_), :, pl.ds(*OUT_COLS[side])]

    def own_piece(part, side):
        if part == 0:
            return w_in
        if part in CONV_TAPS:
            return conv_own.at[pl.ds(*CONV_TAPS[part]), :, pl.ds(*CONV_COLS[side])]
        return out_own.at[:, pl.ds(*OUT_COLS[side])]

    def target(link, side):
        return (
            device(z, y, 1 - x, side),
            device(z, 1 - y, x, side),
            device(z + 1, y, x, side),
            device(z - 1, y, x, side),
            device(z, y, x, 1 - side),
        )[link]

    def remote(src, dst, send_sem, recv_sem, where):
        return pltpu.make_async_remote_copy(
            src_ref=src, dst_ref=dst, send_sem=send_sem, recv_sem=recv_sem, device_id=where, device_id_type=MESH
        )

    def wait_sent(side, part, link, count):
        view = span(part, side, count)
        remote(view, view, link_send.at[link, part], twin_recv.at[0, part], target(4, side)).wait_send()

    def guarded(link, act):
        if link == 2:
            pl.when(z < LEVELS - 1)(act)
        elif link == 3:
            pl.when(z > 0)(act)
        else:
            act()

    def forward(side, part, level, column, links, own=False):
        place_ref = piece(part, level, column, side)
        for link in links:

            def act(link=link):
                remote(
                    own_piece(part, side) if own else place_ref, place_ref,
                    link_send.at[link, part], link_recv.at[level, column, part], target(link, side),
                ).start()

            guarded(link, act)

    def pass_on(side, kind, part, distance):
        def act(level, sign):
            column = columns[kind]
            place_ref = piece(part, level, column, side)
            remote(
                place_ref, place_ref, link_send.at[4, part], link_recv.at[level, column, part], target(4, side)
            ).wait_recv()
            along = {1: (3,), -1: (2,), 0: (2, 3)}[sign]
            links = ()
            if kind == "own":
                links = along if PLANE_FIRST[part] else along + (0, 1)
            else:
                if kind == "x" and BY_Y[part] and (distance == 0 or not PLANE_FIRST[part]):
                    links += (1,)
                if kind == "y" and not BY_Y[part] and (distance == 0 or not PLANE_FIRST[part]):
                    links += (0,)
                if PLANE_FIRST[part]:
                    links += along
            forward(side, part, level, column, links)

        each_level(z, distance, act)

    def own_sends(side, part):
        forward(side, part, z, here, (0, 1, 2, 3), own=True)

    def twin_copy(side, kind, part, level=None):
        if level is None:
            view = pieces(part, columns[kind], side)
        else:
            view = piece(part, level, columns[kind], side)
        return remote(view, view, link_send.at[4, part], twin_recv.at[KINDS.index(kind), part], target(4, side))

    def share(side, kind, part):
        if kind == "own":
            own_copy(side, part).wait()
        if part:
            twin_copy(side, kind, part).start()
        else:
            for level in range(LEVELS):
                twin_copy(side, kind, part, level).start()

    def take_twin(side, part):
        for kind in KINDS:
            if part:
                twin_copy(1 - side, kind, part).wait_recv()
            else:
                view = span(part, side, LEVELS)
                remote(
                    view, view, link_send.at[4, part], twin_recv.at[KINDS.index(kind), part], target(4, side)
                ).wait_recv()

    def pair_copies(side):
        return [
            remote(src, dst, pair_send.at[index], pair_recv.at[index], target(4, side))
            for index, (src, dst) in enumerate(((w_conv, conv_twin), (w_out, out_twin)))
        ]

    def own_copy(side, part):
        return pltpu.make_async_copy(own_piece(part, side), piece(part, z, here, side), own_sem.at[part])

    def vec_copy(offset):
        mine = z * 8 + y * 4 + x * 2 + core
        return remote(vec, packed.at[mine], vec_send.at[0], vec_recv.at[0], plane_peer(offset)[1])

    def level_rows(level):
        return packed.at[pl.ds(pl.multiple_of(level * 8, 8), 8)]

    def vec_line(side, level, link):
        rows = level_rows(level)
        return remote(rows, rows, vec_send.at[link - 1], vec_recv.at[1 + level], target(link, side))

    def vec_begin(side):
        for offset in range(1, 8):
            vec_copy(offset).start()
        packed[pl.ds(z * 8 + y * 4 + x * 2 + side, 1)] = vec[...][None]

    def vec_plane(side):
        rows = packed.at[pl.ds(0, 7)]
        remote(rows, rows, vec_send.at[0], vec_recv.at[0], target(4, side)).wait()
        for link in (2, 3):
            guarded(link, lambda link=link: vec_line(side, z, link).start())

    def vec_pass(side, distance):
        def act(level, sign):
            link = 3 if sign > 0 else 2
            vec_line(side, level, link).wait_recv()
            guarded(link, lambda: vec_line(side, level, link).start())

        each_level(z, distance, act)

    def vec_finish(side):
        for level in range(LEVELS):

            @pl.when(z == level)
            def _(level=level):
                for link, count in ((2, level + 1 if level < LEVELS - 1 else 0), (3, LEVELS - level if level else 0)):
                    if count:
                        rows = packed.at[pl.ds(0, 8 * count)]
                        remote(rows, rows, vec_send.at[link - 1], vec_recv.at[0], target(4, side)).wait_send()

    def begin(side):
        own_copy(side, 0).start()
        for copy in pair_copies(side):
            copy.start()
        share_rows(side, slice(4, 6))

    def assemble(side):
        for copy in pair_copies(side):
            copy.wait()
        first_conv, second_conv = (w_conv, conv_twin) if side == 0 else (conv_twin, w_conv)
        first_out, second_out = (w_out, out_twin) if side == 0 else (out_twin, w_out)
        conv_own[...] = jnp.concatenate(
            [first_conv[...].astype(F32), second_conv[...].astype(F32)], axis=1
        ).astype(BF16)
        out_own[...] = jnp.concatenate(
            [first_out[...].astype(F32), second_out[...].astype(F32)], axis=0
        ).astype(BF16)
        for part in range(1, PART_COUNT):
            own_copy(side, part).start()

    def shares(side):
        half = pl.ds(1024, 1024)
        pairs = (
            (u2, u2_share), (xh2, xh2_share), (slope2, slope2_share), (scale2, scale2_share),
            (grads_hbm, grads_share), (tokens_hbm, tokens_share),
        )
        return [
            remote(source.at[half, :], target_, share_send.at[index], share_recv.at[index], target(4, side))
            for index, (source, target_) in enumerate(pairs)
        ]

    def share_rows(side, which):
        for copy in shares(side)[which]:
            copy.start()

    def save_in():
        return pltpu.make_async_copy(in_vmem, in_full, load_sem.at[0])

    def take_in(side):
        take_twin(side, 0)
        save_in().start()

    def finish(side):
        vec_finish(side)
        for part in range(1, PART_COUNT):
            take_twin(side, part)
        for part in range(PART_COUNT):
            plane, along = (1, 4) if PLANE_FIRST[part] else (4, 1)
            wait_sent(side, part, 0, plane if BY_Y[part] else 2 * plane)
            wait_sent(side, part, 1, 2 * plane if BY_Y[part] else plane)
            wait_sent(side, part, 4, CHIPS)
            for level in range(LEVELS):

                @pl.when(z == level)
                def _(part=part, along=along, level=level):
                    if level < LEVELS - 1:
                        wait_sent(side, part, 2, along * (level + 1))
                    if level > 0:
                        wait_sent(side, part, 3, along * (LEVELS - level))

        save_in().wait()
        for copy in shares(side):
            copy.wait()

    def take_vectors(side):
        unpack_vectors(packed, vectors_out)
        mine = z * 8 + y * 4 + x * 2
        for row, owner in ((9, mine + side), (10, mine + 1 - side)):
            vectors_out[pl.ds(row, 1), pl.ds(0, 128)] = packed[owner, pl.ds(0, 1), :]

    actions = {
        "share_rows": share_rows,
        "send": own_sends, "begin": begin, "assemble": assemble, "w_in": take_in, "finish": finish,
        "vec_begin": vec_begin, "vec_plane": vec_plane, "vec_pass": vec_pass,
        "vectors": take_vectors,
        "share": share,
    }

    def perform(events):
        for side in range(2):

            @pl.when(core == side)
            def _(side=side):
                for event in events:
                    if event[0] in actions:
                        actions[event[0]](side, *event[1:])
                    else:
                        pass_on(side, *event)

    def rows_of(tile, count=1):
        return pl.ds(pl.multiple_of(tile * TILE, TILE), count * TILE)

    def token_load(tile):
        return pltpu.make_async_copy(tokens_hbm.at[rows_of(tile), :], tokens.at[rows_of(tile), :], token_sem.at[tile])

    first = ((u1, u1_hbm), (slope1, slope1_hbm), (xh1, xh1_hbm), (scale1, scale1_hbm))
    second = ((u2, u2_hbm), (xh2, xh2_hbm), (slope2, slope2_hbm), (scale2, scale2_hbm))

    def stores(pairs, phase, half):
        rows = rows_of(half * (steps // 2), steps // 2)
        return [
            pltpu.make_async_copy(src.at[rows, :], dst.at[rows, :], store_sem.at[phase, half, index])
            for index, (src, dst) in enumerate(pairs)
        ]

    def start_stores(pairs, phase, half):
        for copy in stores(pairs, phase, half):
            copy.start()

    greet_near(z, y, x, core)
    for tile in range(steps):
        token_load(tile).start()

    def wide_tile(tile, _):
        for index in range(steps):
            if GATHER_PLAN[index]:
                pl.when(tile == index)(functools.partial(perform, GATHER_PLAN[index]))
        token_load(tile).wait()
        rows = rows_of(tile)
        gain, bias = vectors_out[pl.ds(0, 1), :], vectors_out[pl.ds(1, 1), :]
        norm, scale = norm_parts(tokens[rows, :].astype(F32))
        act, slope = gelu_parts(norm * gain + bias)
        u1[rows, :] = act.astype(BF16)
        slope1[rows, :] = slope.astype(BF16)
        xh1[rows, :] = norm.astype(BF16)
        scale1[rows, :] = jnp.broadcast_to(scale, (TILE, 128))
        return 0

    lax.fori_loop(0, steps, wide_tile, 0)

    def slim_tile(tile, _):
        for index in range(steps):
            events = GATHER_PLAN[steps + index]
            if index == 0:
                pl.when(tile == 0)(lambda: start_stores(first, 0, 0))
                pl.when(tile == 0)(lambda: start_stores(first, 0, 1))
            if index == steps // 2:

                @pl.when(tile == index)
                def _():
                    start_stores(second, 1, 1)
                    perform((("share_rows", slice(0, 4)),))

            if events:
                pl.when(tile == index)(functools.partial(perform, events))
        rows = rows_of(lax.rem(tile + steps // 2, steps))
        hidden = jnp.dot(u1[rows, :], in_vmem[...], preferred_element_type=F32)
        hidden = hidden + vectors_out[pl.ds(3, 1), pl.ds(0, 640)]
        norm, scale = norm_parts(hidden)
        act, slope = gelu_parts(norm * vectors_out[pl.ds(4, 1), pl.ds(0, 640)] + vectors_out[pl.ds(5, 1), pl.ds(0, 640)])
        u2[rows, :] = act.astype(BF16)
        slope2[rows, :] = slope.astype(BF16)
        xh2[rows, :] = norm.astype(BF16)
        scale2[rows, :] = jnp.broadcast_to(scale, (TILE, 128))
        return 0

    lax.fori_loop(0, steps, slim_tile, 0)
    start_stores(second, 1, 0)
    perform(GATHER_PLAN[2 * steps])
    for phase, pairs in enumerate((first, second)):
        for half in range(2):
            for copy in stores(pairs, phase, half):
                copy.wait()


def gather_stage(tokens, grads, vec, w_in, w_conv, w_out):
    rows = tokens.shape[0]
    shape = jax.ShapeDtypeStruct
    vmem = pl.BlockSpec(memory_space=pltpu.VMEM)
    wide, slim, column = (rows, 1280), (rows, 640), (rows, 128)
    *results, conv_full, out_full, s0, s1, s2, s3, s4, s5 = pl.pallas_call(
        gather_kernel,
        in_specs=[HBM] * 2 + [vmem] * 4,
        out_specs=[HBM] * 8 + [vmem] + [HBM] * 9,
        out_shape=[
            shape(wide, BF16), shape(wide, BF16), shape(wide, BF16), shape(column, F32),
            shape(slim, BF16), shape(slim, BF16), shape(column, F32), shape(slim, BF16),
            shape((16, 1280), F32),
            shape((1280, 640), BF16), shape((KSIZE, LEVELS, 4, 40, 640), BF16), shape((LEVELS, 4, 40, 1280), BF16),
            shape((1024, 640), BF16), shape((1024, 640), BF16), shape((1024, 640), BF16), shape((1024, 128), F32),
            shape((1024, 1280), BF16), shape((1024, 1280), BF16),
        ],
        scratch_shapes=[
            pltpu.VMEM((DEVICES, 2, 128), F32),
            pltpu.VMEM((1280, 640), BF16),
            pltpu.VMEM((KSIZE, 20, 640), BF16),
            pltpu.VMEM((20, 1280), BF16),
            pltpu.VMEM((KSIZE, 40, 640), BF16),
            pltpu.VMEM((40, 1280), BF16),
            pltpu.VMEM(wide, BF16),
            pltpu.VMEM(wide, BF16),
            pltpu.VMEM(wide, BF16),
            pltpu.VMEM(wide, BF16),
            pltpu.VMEM(column, F32),
            pltpu.VMEM(slim, BF16),
            pltpu.VMEM(slim, BF16),
            pltpu.VMEM(column, F32),
            pltpu.VMEM(slim, BF16),
            pltpu.SemaphoreType.DMA((rows // TILE,)),
            pltpu.SemaphoreType.DMA((2, 2, 4)),
            pltpu.SemaphoreType.DMA((6,)),
            pltpu.SemaphoreType.DMA((6,)),
            pltpu.SemaphoreType.DMA((3,)),
            pltpu.SemaphoreType.DMA((1 + LEVELS,)),
            pltpu.SemaphoreType.DMA((5, PART_COUNT)),
            pltpu.SemaphoreType.DMA((LEVELS, 4, PART_COUNT)),
            pltpu.SemaphoreType.DMA((4, PART_COUNT)),
            pltpu.SemaphoreType.DMA((2,)),
            pltpu.SemaphoreType.DMA((2,)),
            pltpu.SemaphoreType.DMA((PART_COUNT,)),
            pltpu.SemaphoreType.DMA((1,)),
        ],
        compiler_params=pltpu.CompilerParams(
            collective_id=0, has_side_effects=True, vmem_limit_bytes=VMEM_BYTES,
        ),
        name="gather_stage",
    )(tokens, grads, vec, w_in, w_conv, w_out)
    return *results, conv_full.reshape(KSIZE, 640, 640), out_full.reshape(640, 1280), (s0, s1, s2, s3, s4, s5)


def pack_vectors(ln1_gain, ln1_bias, b_in, ln2_gain, ln2_bias, b_conv, ln3_gain, ln3_bias, b_out, lengths):
    total = None
    for plane, pieces in enumerate(
        (
            zip((ln1_gain, ln1_bias, b_out, lengths), WIDE_OFFSETS + (LENGTH_LANE,)),
            zip((b_in, ln2_gain, ln2_bias, b_conv, ln3_gain, ln3_bias), SLIM_OFFSETS),
        )
    ):
        for piece, offset in pieces:
            line = piece[None]
            room = ((plane, 1 - plane, 0), (offset, 128 - offset - piece.shape[0], 0))
            placed = lax.pad(line, jnp.zeros((), line.dtype), room).astype(F32)
            total = placed if total is None else total + placed
    return total


PAD = 32
SPAN = 1024 + 2 * PAD
HALO = 16
UNIT = 128
LENGTH_LANE = 120


def unit_share(lengths):
    own_first, own_second, twin_first, twin_second = (lax.div(length + UNIT - 1, UNIT) for length in lengths)
    excess = own_first + own_second - twin_first - twin_second
    give = jnp.minimum(lax.div(jnp.maximum(excess, 0), 2), own_second)
    take = jnp.minimum(lax.div(jnp.maximum(-excess, 0), 2), twin_second)
    return own_first, own_second, twin_second, give, take


def read_lengths(vectors):
    lane = lax.broadcasted_iota(jnp.int32, (1, 128), 1)
    return [
        jnp.sum(jnp.where(lane == LENGTH_LANE + index, vectors[pl.ds(row, 1), pl.ds(0, 128)], 0.0)).astype(jnp.int32)
        for row in (9, 10)
        for index in range(2)
    ]


def middle_kernel(
    vectors, u2_hbm, xh2_hbm, slope2_hbm, scale2_hbm, grads_hbm, tokens_hbm, conv_hbm, last_hbm,
    u2_twin, xh2_twin, slope2_twin, scale2_twin, grads_twin, tokens_twin,
    out_hbm, dh1_hbm, out_twin, dh1_twin, d_conv_hbm, d_last_hbm, sums_out,
    conv, conv_t, last, last_t, u2, dh2, grads, tokens, xh2, slope2, scale2, d_conv, d_last, zeros,
    u2_sem, row_sem, back_sem, weight_sem, out_sem, dh1_sem, flush_sem,
):
    segments = 3
    tiles = 1024 // TILE
    wide, slim = 1280, 640
    lengths = read_lengths(vectors)
    first_units, second_units, twin_units, give, take = unit_share(lengths)

    def pick(segment, values):
        return jnp.where(segment == 0, values[0], jnp.where(segment == 1, values[1], values[2]))

    def bounds(segment):
        low = pick(segment, (0, 0, twin_units - take))
        high = pick(segment, (first_units, second_units - give, twin_units))
        before = jnp.logical_and(jnp.logical_and(segment == 2, low > 0), high > low).astype(jnp.int32)
        after = jnp.logical_and(jnp.logical_and(segment == 1, give > 0), high > 0).astype(jnp.int32)
        return low, high, before, after

    def tile_range(low, high):
        return lax.div(low, 2), jnp.where(high > low, lax.div(high + 1, 2), lax.div(low, 2))

    def worked_tiles(segment):
        low, high, _, _ = bounds(segment)
        return tile_range(low, high)

    def held_tiles(segment):
        low, high, before, after = bounds(segment)
        return tile_range(low - before, high + after)

    def live_units(segment):
        return pick(segment, (first_units, second_units, twin_units))

    def live_tiles(segment):
        return lax.div(live_units(segment) + 1, 2)

    def rows_of(segment, tile):
        return pl.ds(pl.multiple_of(segment * 1024 + tile * TILE, TILE), TILE)

    def padded(segment, row, count, shift=0):
        return pl.ds(pl.multiple_of(segment * SPAN + PAD + row, 8) + shift, count)

    def plain(row, count, shift=0):
        return pl.ds(pl.multiple_of(PAD + row, 8) + shift, count)

    def fetch(segment, tile, own, twin, target, rows, sem):
        @pl.when(segment < 2)
        def _():
            pltpu.make_async_copy(own.at[rows_of(segment, tile), :], target.at[rows, :], sem).start()

        @pl.when(segment == 2)
        def _():
            pltpu.make_async_copy(twin.at[rows_of(0, tile), :], target.at[rows, :], sem).start()

    def fetched(segment, tile, own, target, rows, sem):
        pltpu.make_async_copy(own.at[rows_of(0, tile), :], target.at[rows, :], sem).wait()

    def emit(tile, segment, source, own, twin, sem):
        @pl.when(segment < 2)
        def _():
            pltpu.make_async_copy(source, own.at[rows_of(segment, tile), :], sem).start()

        @pl.when(segment == 2)
        def _():
            pltpu.make_async_copy(source, twin.at[rows_of(0, tile), :], sem).start()

    def u2_at(segment, tile):
        return padded(segment, tile * TILE, TILE)

    row_arrays = ((grads_hbm, grads_twin, grads), (tokens_hbm, tokens_twin, tokens))
    back_arrays = ((xh2_hbm, xh2_twin, xh2), (slope2_hbm, slope2_twin, slope2), (scale2_hbm, scale2_twin, scale2))

    def fetch_rows(segment, tile, index):
        own, twin, target = row_arrays[index]
        fetch(segment, tile, own, twin, target, rows_of(segment, tile), row_sem.at[index, segment, tile])

    def rows_fetched(segment, tile, index):
        own, _, target = row_arrays[index]
        fetched(segment, tile, own, target, rows_of(segment, tile), row_sem.at[index, segment, tile])

    def fetch_u2(segment):
        low, high = held_tiles(segment)

        def one(tile, _):
            fetch(segment, tile, u2_hbm, u2_twin, u2, u2_at(segment, tile), u2_sem.at[segment, tile])
            return 0

        lax.fori_loop(low, high, one, 0)

    def out_store(segment, tile):
        emit(tile, segment, tokens.at[rows_of(segment, tile), :], out_hbm, out_twin, out_sem.at[segment, tile])

    def dh1_store(segment, tile, source):
        emit(tile, segment, source, dh1_hbm, dh1_twin, dh1_sem.at[segment, tile])

    conv_load = pltpu.make_async_copy(conv_hbm, conv, weight_sem.at[0])
    last_load = pltpu.make_async_copy(last_hbm, last, weight_sem.at[1])
    last_flush = pltpu.make_async_copy(last, d_last_hbm, flush_sem.at[0])

    fetch_u2(0)
    conv_load.start()
    last_load.start()

    def load_rows(segment, _):
        pl.when(segment > 0)(lambda: fetch_u2(segment))
        low, high = worked_tiles(segment)
        held = held_tiles(segment)

        def one(tile, _):
            fetch_rows(segment, tile, 0)
            pl.when(jnp.logical_and(tile >= low, tile < high))(lambda: fetch_rows(segment, tile, 1))
            return 0

        lax.fori_loop(held[0], held[1], one, 0)
        return 0

    def load_back(segment, _):
        low, high = worked_tiles(segment)

        def one(tile, _):
            for index, (own, twin, target) in enumerate(back_arrays):
                fetch(segment, tile, own, twin, target, rows_of(segment, tile), back_sem.at[index, segment, tile])
            return 0

        lax.fori_loop(low, high, one, 0)
        return 0

    lax.fori_loop(0, segments, load_rows, 0)
    lax.fori_loop(0, segments, load_back, 0)
    zeros[...] = jnp.zeros_like(zeros)

    def idle(segment, _):
        low, high = worked_tiles(segment)

        def one(tile, _):
            pl.when(jnp.logical_or(tile < low, tile >= high))(lambda: dh1_store(segment, tile, zeros))
            dead = jnp.logical_and(segment < 2, tile >= live_tiles(segment))
            pl.when(dead)(lambda: fetch_rows(segment, tile, 1))
            return 0

        lax.fori_loop(0, tiles, one, 0)
        return 0

    lax.fori_loop(0, segments, idle, 0)

    sums_out[...] = jnp.zeros_like(sums_out)

    def clear(index, _):
        rows = pl.ds(pl.multiple_of(index * 64, 64), 64)
        d_last[rows, :] = jnp.zeros((64, wide), F32)
        for tap in range(KSIZE):
            d_conv[tap, rows, :] = jnp.zeros((64, slim), F32)
        return 0

    lax.fori_loop(0, slim // 64, clear, 0)

    def vector(index, width=slim):
        return vectors[pl.ds(index, 1), pl.ds(0, width)]

    def add_sum(index, values):
        width = values.shape[1]
        sums_out[pl.ds(index * 8, 8), pl.ds(0, width)] += jnp.sum(
            values.reshape(values.shape[0] // 8, 8, width), axis=0
        )

    edge = jnp.zeros((PAD, slim), BF16)

    def one_segment(segment, _):
        low, high, before, after = bounds(segment)
        first_tile, end_tile = worked_tiles(segment)
        held = held_tiles(segment)
        count = live_units(segment)
        length = pick(segment, (lengths[0], lengths[1], lengths[3]))

        def live_rows(row, size):
            position = lax.broadcasted_iota(jnp.int32, (size, 128), 0) + row
            return (position < length).astype(F32)

        def prepare(tile, _):
            fetched(segment, tile, u2_hbm, u2, u2_at(segment, tile), u2_sem.at[segment, tile])
            return 0

        lax.fori_loop(held[0], held[1], prepare, 0)

        @pl.when(low == 0)
        def _():
            u2[padded(segment, -PAD, PAD), :] = edge

        dh2[plain(low * UNIT - PAD, PAD), :] = edge
        dh2[plain(high * UNIT, PAD), :] = edge

        @pl.when(jnp.logical_and(high > low, high + after == count))
        def _():
            tail = padded(segment, (count - 1) * UNIT, UNIT)
            u2[tail, :] = (u2[tail, :].astype(F32) * lanes(live_rows((count - 1) * UNIT, UNIT), slim)).astype(BF16)
            u2[padded(segment, count * UNIT, PAD), :] = edge

        @pl.when(segment == 0)
        def _():
            conv_load.wait()
            last_load.wait()
            last_t[...] = last[...].T

            def turn(tap, _):
                conv_t[tap] = conv[tap].T
                return 0

            lax.fori_loop(0, KSIZE, turn, 0)

        def forward_rows(row, size, whole):
            rows = pl.ds(pl.multiple_of(segment * 1024 + row, HALO), size)
            live = live_rows(row, size)
            hidden = jnp.dot(u2[padded(segment, row, size, -16), :], conv[0], preferred_element_type=F32)
            for tap in range(1, KSIZE):
                hidden += jnp.dot(
                    u2[padded(segment, row, size, (tap - 2) * DILATION), :], conv[tap], preferred_element_type=F32
                )
            gz = (grads[rows, :].astype(F32) * lanes(live, wide)).astype(BF16)
            back = jnp.dot(gz, last_t[...], preferred_element_type=F32)
            norm, scale = norm_parts(hidden + vector(6))
            act, slope = gelu_parts(norm * vector(7) + vector(8))
            slope_grad = back * slope
            err = slope_grad * vector(7)
            mean = jnp.sum(err, axis=1, keepdims=True) * (1.0 / slim)
            along = jnp.sum(err * norm, axis=1, keepdims=True) * (1.0 / slim)
            low_grad = (scale * (err - mean - norm * along)).astype(BF16)
            dh2[plain(row, size), :] = low_grad
            if whole:
                u3 = act.astype(BF16)
                branch = jnp.dot(u3, last[...], preferred_element_type=F32) + vector(2, wide)
                tokens[rows, :] = (tokens[rows, :].astype(F32) + lanes(live, wide) * branch).astype(BF16)
                d_last[...] += lax.dot_general(u3, gz, (((0,), (0,)), ((), ())), preferred_element_type=F32)
                add_sum(2, gz.astype(F32))
                add_sum(7, slope_grad * norm)
                add_sum(8, slope_grad)
                add_sum(6, low_grad.astype(F32))

        def by_size(tile, act):
            whole = jnp.logical_and(2 * tile >= low, 2 * tile + 2 <= high)
            pl.when(whole)(lambda: act(tile * TILE, TILE))
            pl.when(jnp.logical_not(whole))(lambda: act(jnp.maximum(2 * tile, low) * UNIT, UNIT))

        def forward(tile, _):
            rows_fetched(segment, tile, 0)
            rows_fetched(segment, tile, 1)
            by_size(tile, lambda row, size: forward_rows(row, size, True))
            out_store(segment, tile)
            return 0

        lax.fori_loop(first_tile, end_tile, forward, 0)

        @pl.when(before + after > 0)
        def _():
            tile = jnp.where(before > 0, held[0], held[1] - 1)
            pl.when(jnp.logical_or(tile < first_tile, tile >= end_tile))(lambda: rows_fetched(segment, tile, 0))
            forward_rows(jnp.where(before > 0, low * UNIT - HALO, high * UNIT), HALO, False)

        def dead_store(tile, _):
            rows_fetched(segment, tile, 1)
            out_store(segment, tile)
            return 0

        lax.fori_loop(jnp.where(segment < 2, live_tiles(segment), tiles), tiles, dead_store, 0)

        @pl.when(segment == segments - 1)
        def _():
            last[...] = d_last[...].astype(BF16)
            last_flush.start()

        def backward_rows(row, size):
            rows = pl.ds(pl.multiple_of(segment * 1024 + row, UNIT), size)
            live = lanes(live_rows(row, size), slim)
            source_t = u2[padded(segment, row, size), :].T
            total = None
            for tap in range(KSIZE):
                window = dh2[plain(row, size, (2 - tap) * DILATION), :]
                term = jnp.dot(window, conv_t[tap], preferred_element_type=F32)
                total = term if total is None else total + term
                d_conv[tap] += jnp.dot(source_t, window, preferred_element_type=F32)
            norm = xh2[rows, :].astype(F32)
            slope_grad = total * live * slope2[rows, :].astype(F32)
            add_sum(4, slope_grad * norm)
            add_sum(5, slope_grad)
            err = slope_grad * vector(4)
            mean = jnp.sum(err, axis=1, keepdims=True) * (1.0 / slim)
            along = jnp.sum(err * norm, axis=1, keepdims=True) * (1.0 / slim)
            low_grad = (lanes(scale2[rows, :], slim) * (err - mean - norm * along)).astype(BF16)
            add_sum(3, low_grad.astype(F32))
            slope2[rows, :] = low_grad
            if size == UNIT:
                other = 2 * lax.div(row, TILE) * TILE + UNIT - row
                slope2[pl.ds(pl.multiple_of(segment * 1024 + other, UNIT), UNIT), :] = jnp.zeros((UNIT, slim), BF16)

        def backward(tile, _):
            rows = rows_of(segment, tile)
            for index, (own, twin, target) in enumerate(back_arrays):
                fetched(segment, tile, own, target, rows, back_sem.at[index, segment, tile])
            by_size(tile, backward_rows)
            dh1_store(segment, tile, slope2.at[rows, :])
            return 0

        lax.fori_loop(first_tile, end_tile, backward, 0)
        return 0

    lax.fori_loop(0, segments, one_segment, 0)

    def conv_flush(tap):
        return pltpu.make_async_copy(conv.at[tap], d_conv_hbm.at[tap], flush_sem.at[tap + 1])

    def flush(tap, _):
        conv[tap] = d_conv[tap].astype(BF16)
        conv_flush(tap).start()
        return 0

    lax.fori_loop(0, KSIZE, flush, 0)

    def stored(segment, _):
        low, high = worked_tiles(segment)

        def one(tile, _):
            pltpu.make_async_copy(zeros, dh1_hbm.at[rows_of(0, tile), :], dh1_sem.at[segment, tile]).wait()
            worked = jnp.logical_and(tile >= low, tile < high)
            dead = jnp.logical_and(segment < 2, tile >= live_tiles(segment))

            @pl.when(jnp.logical_or(worked, dead))
            def _():
                pltpu.make_async_copy(
                    tokens.at[rows_of(0, tile), :], out_hbm.at[rows_of(0, tile), :], out_sem.at[segment, tile]
                ).wait()

            return 0

        lax.fori_loop(0, tiles, one, 0)
        return 0

    lax.fori_loop(0, segments, stored, 0)
    for copy in [last_flush] + [conv_flush(tap) for tap in range(KSIZE)]:
        copy.wait()


def middle_stage(vectors, u2, xh2, slope2, scale2, grads, tokens, w_conv, w_out, twins):
    rows = u2.shape[0]
    shape = jax.ShapeDtypeStruct
    vmem = pl.BlockSpec(memory_space=pltpu.VMEM)
    tiles = 1024 // TILE
    held = 3 * 1024
    return pl.pallas_call(
        middle_kernel,
        in_specs=[vmem] + [HBM] * 14,
        out_specs=[HBM] * 6 + [vmem],
        out_shape=[
            shape((rows, 1280), BF16), shape((rows, 640), BF16), shape((1024, 1280), BF16), shape((1024, 640), BF16),
            shape((KSIZE, 640, 640), BF16), shape((640, 1280), BF16), shape((72, 1280), F32),
        ],
        scratch_shapes=[
            pltpu.VMEM((KSIZE, 640, 640), BF16),
            pltpu.VMEM((KSIZE, 640, 640), BF16),
            pltpu.VMEM((640, 1280), BF16),
            pltpu.VMEM((1280, 640), BF16),
            pltpu.VMEM((3 * SPAN, 640), BF16),
            pltpu.VMEM((SPAN, 640), BF16),
            pltpu.VMEM((held, 1280), BF16),
            pltpu.VMEM((held, 1280), BF16),
            pltpu.VMEM((held, 640), BF16),
            pltpu.VMEM((held, 640), BF16),
            pltpu.VMEM((held, 128), F32),
            pltpu.VMEM((KSIZE, 640, 640), F32),
            pltpu.VMEM((640, 1280), F32),
            pltpu.VMEM((TILE, 640), BF16),
            pltpu.SemaphoreType.DMA((3, tiles)),
            pltpu.SemaphoreType.DMA((2, 3, tiles)),
            pltpu.SemaphoreType.DMA((3, 3, tiles)),
            pltpu.SemaphoreType.DMA((2,)),
            pltpu.SemaphoreType.DMA((3, tiles)),
            pltpu.SemaphoreType.DMA((3, tiles)),
            pltpu.SemaphoreType.DMA((6,)),
        ],
        compiler_params=pltpu.CompilerParams(vmem_limit_bytes=VMEM_BYTES),
        name="middle_stage",
    )(vectors, u2, xh2, slope2, scale2, grads, tokens, w_conv, w_out, *twins)


def pack_sums(plane, lines, offsets, packed_ref):
    width, chunk = ((1280, 40), (640, 20))[plane]
    owner, slot, row = chunk_masks(width, chunk)
    total = packed_ref[:, :, plane, :].reshape(DEVICES, 128)
    for line, offset in zip(lines, offsets):
        pick = (slot + offset == row).astype(F32).astype(BF16)
        spread = jnp.where(owner, jnp.broadcast_to(line, owner.shape), 0.0)
        for _ in range(3):
            term = spread.astype(BF16)
            spread = spread - term.astype(F32)
            total += lax.dot_general(term, pick, (((1,), (1,)), ((), ())), preferred_element_type=F32)
    packed_ref[:, :, plane, :] = total.reshape(LEVELS, 8, 128)


SCATTER_BY_Y = (False, True, False)
LINE_FIRST = (False, False, True)
SCATTER_PLAN = (
    (),
    (),
    (),
    (
        ("load", 1), ("twin", 1, "far"), ("first", 1, 1),
    ),
    (
        ("load", 2), ("twin", 2, "x"), ("line", 2, "x", 3), ("ready",), ("first", 1, 3), ("twin", 2, "far"),
        ("line", 2, "far", 3), ("twin", 2, "own"), ("line", 2, "own", 3),
    ),
    (
        ("first", 1, 2), ("line", 2, "x", 2), ("twin", 0, "far"), ("first", 0, 2), ("twin", 0, "x"), ("direct", 0, 0),
        ("twin", 1, "y"), ("direct", 1, 3), ("first", 0, 1), ("first", 0, 3), ("line", 2, "far", 2),
    ),
    (
        ("twin", 1, "x"), ("second", 1, 3), ("twin", 2, "y"), ("line", 2, "y", 3), ("direct", 1, 2),
        ("line", 2, "own", 2),
    ),
    (
        ("direct", 0, 3), ("line", 2, "x", 1), ("direct", 0, 1),
    ),
    (
        ("twin", 0, "y"), ("second", 0, 3), ("first", 1, 0), ("second", 1, 2), ("line", 2, "far", 1),
        ("direct", 0, 2), ("twin", 1, "own"), ("line", 1, "own", 3), ("line", 2, "y", 2), ("second", 0, 2),
        ("second", 1, 1), ("direct", 1, 1), ("plane", 2, "D"),
    ),
    (),
    (
        ("twin", 0, "own"), ("line", 0, "own", 3), ("plane", 2, "F"), ("line", 2, "own", 1), ("second", 0, 1),
        ("line", 1, "own", 2), ("line", 2, "y", 1),
    ),
    (),
    (
        ("direct", 1, 0), ("first", 0, 0), ("line", 0, "own", 2), ("vec_start",), ("line", 1, "own", 1),
        ("second", 1, 0), ("plane", 2, "S"), ("second", 0, 0), ("vec_middle",), ("line", 0, "own", 1), ("done", 2),
        ("done", 1), ("done", 0), ("vec_end",), ("finish",),
    ),
)


def scatter_kernel(
    u1_hbm, dh1_hbm, slope1_hbm, xh1_hbm, scale1_hbm, grads_hbm, w_in_hbm, vectors, sums, d_conv_hbm, d_last_hbm, d_conv_flat, d_last_flat, dh1_share, out_share,
    grad_tokens, g_in, g_conv, g_last, g_vec, out_back,
    u1, dh1, slope1, xh1, scale1, grads, w_in, w_in_t, dh1_back, d_in_sum, d_in, own_sums, packed, plane_box, level_box,
    conv_own, conv_twin, conv_far, conv_x, conv_y, conv_line, conv_done, conv_swap,
    last_own, last_twin, last_far, last_x, last_y, last_line, last_done, last_swap,
    in_twin, in_far, in_x, in_y, in_line,
    tile_sem, weight_sem, store_sem, vec_sem, load_sem, twin_send, twin_recv, send_sem, move_recv, line_recv,
    swap_send, swap_recv, back_send, back_recv,
):
    steps, weight_steps = 2048 // TILE, 4
    z, y, x, core = place()
    columns = {"own": 2 * y + x, "x": 2 * y + (1 - x), "y": 2 * (1 - y) + x, "far": 2 * (1 - y) + (1 - x)}
    boxes = {"far": (in_far, conv_far, last_far), "x": (in_x, conv_x, last_x), "y": (in_y, conv_y, last_y)}
    line_boxes = (in_line, conv_line, last_line)
    links = {
        "x": lambda: device(z, y, 1 - x, core), "y": lambda: device(z, 1 - y, x, core),
        "twin": lambda: device(z, y, x, 1 - core),
    }

    def remote(src, dst, send, recv, link):
        return pltpu.make_async_remote_copy(
            src_ref=src, dst_ref=dst, send_sem=send, recv_sem=recv, device_id=links[link]() if isinstance(link, str) else device(z + link, y, x, core), device_id_type=MESH
        )

    def cut(side, part):
        return (None, CONV_COLS[side], OUT_COLS[side])[part]

    def narrow(side, part):
        return pl.ds(0, 640 if part == 0 else cut(side, part)[1])

    def own_at(side, part, level, column):
        if part == 0:
            return d_in.at[level, column, side]
        if part == 1:
            return conv_own.at[:, level, column, :, narrow(side, part)]
        return last_own.at[level, column, :, narrow(side, part)]

    def twin_at(side, part, level, column):
        if part == 0:
            return in_twin.at[level, column]
        if part == 1:
            return conv_twin.at[:, level, column, :, narrow(side, part)]
        return last_twin.at[level, column, :, narrow(side, part)]

    def box_at(side, part, name, level):
        box = boxes[name][part]
        if part == 0:
            return box.at[level]
        if part == 1:
            return box.at[level, :, :, narrow(side, part)]
        return box.at[level, :, narrow(side, part)]

    def way_of(sign):
        return lax.shift_right_logical(1 - sign, 1) if not isinstance(sign, int) else (1 - sign) // 2

    def line_at(side, part, kind, sign, level):
        way = way_of(sign)
        if part == 0:
            return in_line.at[way, level]
        if part == 1:
            return conv_line.at[way, level, :, :, narrow(side, part)]
        return last_line.at[KINDS.index(kind), way, level, :, narrow(side, part)]

    def all_units(side, part, count):
        rows = pl.ds(0, 40 * count)
        if part == 0:
            return w_in_hbm.at[rows, :]
        if part == 1:
            return d_conv_flat.at[:, rows, pl.ds(*cut(side, part))]
        return d_last_flat.at[rows, pl.ds(*cut(side, part))]

    def load(side, part):
        source = (d_conv_hbm.at[:, :, :, :, pl.ds(*cut(side, 1))], d_last_hbm.at[:, :, :, pl.ds(*cut(side, 2))])
        target = (conv_own.at[:, :, :, :, narrow(side, 1)], last_own.at[:, :, :, narrow(side, 2)])
        return pltpu.make_async_copy(source[part - 1], target[part - 1], load_sem.at[part - 1])

    def twin_copy(part, kind, to_side):
        column = columns[kind]
        if part == 0:
            src, dst = d_in.at[:, column, to_side], in_twin.at[:, column]
        elif part == 1:
            src = d_conv_hbm.at[:, :, column, :, pl.ds(*cut(to_side, part))]
            dst = conv_twin.at[:, :, column, :, narrow(to_side, part)]
        else:
            src = d_last_hbm.at[:, column, :, pl.ds(*cut(to_side, part))]
            dst = last_twin.at[:, column, :, narrow(to_side, part)]
        return remote(src, dst, twin_send.at[part], twin_recv.at[part, KINDS.index(kind)], "twin")

    def exchange(side, part):
        for kind in ("far", "y", "x", "own"):
            twin_copy(part, kind, 1 - side).start()

    def take_twin(side, part, kind):
        twin_copy(part, kind, side).wait_recv()

    def move(side, part, kind, level, link, box):
        return remote(
            own_at(side, part, level, columns[kind]), box_at(side, part, box, level),
            send_sem.at[part], move_recv.at[("far", "x", "y").index(box), part, level], link,
        )

    def line(side, part, kind, level, sign):
        return remote(
            own_at(side, part, level, columns[kind]), line_at(side, part, kind, sign, level),
            send_sem.at[part], line_recv.at[KINDS.index(kind), way_of(sign), part, level], sign,
        )

    def read(ref):
        return ref[...].astype(F32)

    def each_level(distance, act):
        if distance == 0:
            act(z, 0)
            return

        def one(index, _):
            sign = 1 - 2 * index
            level = z + sign * distance
            pl.when(jnp.logical_and(level >= 0, level < LEVELS))(lambda: act(level, sign))
            return 0

        lax.fori_loop(0, 2, one, 0)

    def both_terms(side, part, level, kind):
        column = columns[kind]
        return read(own_at(side, part, level, column)) + read(twin_at(side, part, level, column))

    def put(side, part, level, kind, value):
        own_at(side, part, level, columns[kind])[...] = value.astype(BF16)

    def roles(part):
        return ("y", "x") if SCATTER_BY_Y[part] else ("x", "y")

    def first(side, part, distance):
        def one(level, sign):
            put(side, part, level, "far", both_terms(side, part, level, "far"))
            move(side, part, "far", level, roles(part)[0], "far").start()

        each_level(distance, one)

    def direct(side, part, distance):
        name = roles(part)[0]

        def one(level, sign):
            put(side, part, level, name, both_terms(side, part, level, name))
            move(side, part, name, level, name, name).start()

        each_level(distance, one)

    def second(side, part, distance):
        link, name = roles(part)

        def one(level, sign):
            move(side, part, "far", level, link, "far").wait_recv()
            put(side, part, level, name, both_terms(side, part, level, name) + read(box_at(side, part, "far", level)))
            move(side, part, name, level, name, name).start()

        each_level(distance, one)

    def line_hop(side, part, kind, distance):
        def one(level, sign):
            total = None
            if not LINE_FIRST[part]:
                for name in ("x", "y"):
                    move(side, part, name, level, name, name).wait_recv()
                total = read(box_at(side, part, "x", level)) + read(box_at(side, part, "y", level))
            terms = both_terms(side, part, level, kind)
            total = terms if total is None else terms + total
            behind = jnp.logical_and(z - sign >= 0, z - sign < LEVELS)

            @pl.when(behind)
            def _():
                line(side, part, kind, level, sign).wait_recv()
                put(side, part, level, kind, total + read(line_at(side, part, kind, sign, level)))

            @pl.when(jnp.logical_not(behind))
            def _():
                put(side, part, level, kind, total)

            line(side, part, kind, level, sign).start()

        each_level(distance, one)

    def add_lines(side, part, kind, target):
        for sign, guard in ((1, z > 0), (-1, z < LEVELS - 1)):

            @pl.when(guard)
            def _(sign=sign):
                line(side, part, kind, z, sign).wait_recv()
                target[...] = (
                    target[...].astype(F32) + read(line_at(side, part, kind, sign, z))
                ).astype(target.dtype)

    def plane(side, part, what):
        link, other = roles(part)
        kind = {"F": "far", "D": link, "S": other}[what]
        own = own_at(side, part, z, columns[kind])
        keep = last_done.at[:, narrow(side, part)]
        keep[...] = both_terms(side, part, z, kind)
        add_lines(side, part, kind, keep)
        if what == "S":
            move(side, part, "far", z, link, "far").wait_recv()
            keep[...] += read(box_at(side, part, "far", z))
        own[...] = keep[...].astype(BF16)
        if what == "F":
            move(side, part, "far", z, link, "far").start()
        else:
            move(side, part, kind, z, kind, kind).start()

    def done(side, part):
        if part == 0:
            target = g_in
        elif part == 1:
            target = conv_done.at[:, :, narrow(side, part)]
        else:
            target = last_done.at[:, narrow(side, part)]
        for name in ("x", "y"):
            move(side, part, name, z, name, name).wait_recv()
        target[...] = (
            both_terms(side, part, z, "own") + read(box_at(side, part, "x", z)) + read(box_at(side, part, "y", z))
        )
        add_lines(side, part, "own", target)
        if part:
            swap(part, side).start()

    def swap(part, from_side):
        lanes_ = narrow(from_side, part)
        if part == 1:
            src, dst = conv_done.at[:, :, lanes_], conv_swap.at[:, :, lanes_]
        else:
            src, dst = last_done.at[:, lanes_], last_swap.at[:, lanes_]
        return remote(src, dst, swap_send.at[part - 1], swap_recv.at[part - 1], "twin")

    def finish(side):
        first_row, count = side * 20, 20
        for part, mine, other, target in ((2, last_done, last_swap, g_last), (1, conv_done, conv_swap, g_conv)):
            swap(part, 1 - side).wait_recv()
            for refs, owner in ((mine, side), (other, 1 - side)):
                start, width = cut(owner, part)
                if part == 1:
                    target[:, :, pl.ds(start, width)] = refs[:, pl.ds(first_row, count), pl.ds(0, width)]
                else:
                    target[:, pl.ds(start, width)] = refs[pl.ds(first_row, count), pl.ds(0, width)]
        for part in range(3):
            if part:
                swap(part, side).wait_send()
            view = all_units(1 - side, part, CHIPS)
            remote(view, view, twin_send.at[part], twin_recv.at[part, 0], "twin").wait_send()
            view = all_units(side, part, CHIPS - 1)
            remote(view, view, send_sem.at[part], twin_recv.at[part, 0], "twin").wait_send()


    def in_plane():
        return y * 4 + x * 2 + core

    def plane_copy(offset):
        other, where = plane_peer(offset)
        return pltpu.make_async_remote_copy(
            src_ref=packed.at[:, other], dst_ref=plane_box.at[in_plane()], send_sem=vec_sem.at[0],
            recv_sem=vec_sem.at[1], device_id=where, device_id_type=MESH,
        )

    def level_copy(step):
        level = lax.rem(z + step, LEVELS)
        return pltpu.make_async_remote_copy(
            src_ref=plane_box.at[0, level], dst_ref=level_box.at[z], send_sem=vec_sem.at[2], recv_sem=vec_sem.at[3],
            device_id=device(level, y, x, core), device_id_type=MESH,
        )

    def sum_lines(ref, indices, width):
        return [jnp.sum(ref[pl.ds(8 * index, 8), pl.ds(0, width)], axis=0, keepdims=True) for index in indices]

    def vec_early():
        packed[...] = jnp.zeros_like(packed)
        pack_sums(0, sum_lines(sums, (2,), 1280), WIDE_OFFSETS[2:], packed)
        pack_sums(1, sum_lines(sums, range(3, 9), 640), SLIM_OFFSETS, packed)

    def vec_start(side):
        pack_sums(0, sum_lines(own_sums, (0, 1), 1280), WIDE_OFFSETS[:2], packed)
        for offset in range(1, 8):
            plane_copy(offset).start()
        for level in range(LEVELS):
            plane_box[pl.ds(in_plane(), 1), level] = packed[level, pl.ds(in_plane(), 1)]

    def vec_middle(side):
        view = plane_box.at[pl.ds(0, 7)]
        remote(view, view, vec_sem.at[0], vec_sem.at[1], "twin").wait()
        total = jnp.sum(plane_box[...], axis=0)
        plane_box[0] = total
        level_box[pl.ds(z, 1)] = plane_box[0, pl.ds(z, 1)]
        for step in range(1, LEVELS):
            level_copy(step).start()

    def vec_end(side):
        view = level_box.at[pl.ds(0, LEVELS - 1)]
        remote(view, view, vec_sem.at[2], vec_sem.at[3], "twin").wait()
        g_vec[...] = jnp.sum(level_box[...], axis=0)

    def ready(side):
        d_in[...] = d_in_sum[...].astype(BF16).reshape(d_in.shape)
        exchange(side, 0)

    actions = {
        "load": lambda side, part: load(side, part).wait(), "twin": take_twin, "first": first, "direct": direct,
        "second": second, "line": line_hop, "plane": plane, "done": done, "ready": ready, "vec_start": vec_start,
        "vec_middle": vec_middle, "vec_end": vec_end, "finish": finish,
    }

    def either(event):
        return event[0] in ("ready", "vec_start", "vec_middle", "vec_end") or event[1:2] == (0,)

    def perform(events):
        for alike, group in itertools.groupby(events, either):
            group = tuple(group)
            if alike:
                for event in group:
                    actions[event[0]](core, *event[1:])
                continue
            for side in range(2):

                @pl.when(core == side)
                def _(side=side, group=group):
                    for event in group:
                        actions[event[0]](side, *event[1:])

    def rows_of(tile):
        return pl.ds(pl.multiple_of(tile * TILE, TILE), TILE)

    tiles_of = ((u1, u1_hbm), (dh1, dh1_hbm), (slope1, slope1_hbm), (xh1, xh1_hbm), (scale1, scale1_hbm), (grads, grads_hbm))

    def half_load(index, half):
        target, source = tiles_of[index]
        rows = pl.ds(half * 1024, 1024)
        return pltpu.make_async_copy(source.at[rows, :], target.at[rows, :], tile_sem.at[index, half])

    def store(tile):
        return pltpu.make_async_copy(grads.at[rows_of(tile), :], grad_tokens.at[rows_of(tile), :], store_sem.at[tile])

    weight_load = pltpu.make_async_copy(w_in_hbm, w_in, weight_sem.at[0])

    barrier = pltpu.get_barrier_semaphore()
    for offset in range(1, 8):
        pl.semaphore_signal(barrier, inc=1, device_id=plane_peer(offset)[1], device_id_type=MESH)
    for step in range(1, LEVELS):
        pl.semaphore_signal(
            barrier, inc=1, device_id=device(lax.rem(z + step, LEVELS), y, x, core), device_id_type=MESH
        )
    for side in range(2):

        @pl.when(core == side)
        def _(side=side):
            for part in (1, 2):
                load(side, part).start()

    for half in range(2):
        half_load(0, half).start()
        half_load(1, half).start()
    weight_load.start()
    pl.semaphore_wait(barrier, 7 + LEVELS - 1)
    back_copies = [
        remote(dh1_share, dh1_back, back_send.at[0], back_recv.at[0], "twin"),
        remote(out_share, out_back, back_send.at[1], back_recv.at[1], "twin"),
    ]
    for side in range(2):

        @pl.when(core == side)
        def _(side=side):
            for kind in ("far", "y", "x", "own"):
                for part in (1, 2):
                    twin_copy(part, kind, 1 - side).start()
                if kind == "far":
                    back_copies[0].start()

    for half in range(2):
        for index in range(2, 6):
            half_load(index, half).start()
    own_sums[...] = jnp.zeros_like(own_sums)
    vec_early()

    def weight_tile(tile, _):
        for index in range(weight_steps):
            if SCATTER_PLAN[index]:
                pl.when(tile == index)(functools.partial(perform, SCATTER_PLAN[index]))
            if index in (0, weight_steps // 2):
                for array in range(2):
                    pl.when(tile == index)(half_load(array, 0 if index == 0 else 1).wait)
        rows = pl.ds(pl.multiple_of(tile * 512, 512), 512)
        pl.when(tile == weight_steps // 2)(back_copies[0].wait)

        @pl.when(tile >= weight_steps // 2)
        def _():
            again = pl.ds(pl.multiple_of(tile * 512 - 1024, 512), 512)
            dh1[rows, :] = dh1[rows, :] + dh1_back[again, :]

        term = lax.dot_general(u1[rows, :], dh1[rows, :], (((0,), (0,)), ((), ())), preferred_element_type=F32)

        @pl.when(tile == 0)
        def _():
            d_in_sum[...] = term

        @pl.when(tile > 0)
        def _():
            d_in_sum[...] += term

        return 0

    lax.fori_loop(0, weight_steps, weight_tile, 0)
    weight_load.wait()
    w_in_t[...] = w_in[...].T

    def token_tile(tile, _):
        for index in range(steps):
            if SCATTER_PLAN[weight_steps + index]:
                pl.when(tile == index)(functools.partial(perform, SCATTER_PLAN[weight_steps + index]))
            if index == 1:
                pl.when(tile == index)(back_copies[1].start)
            if index in (0, steps // 2):
                for array in range(2, 6):
                    pl.when(tile == index)(half_load(array, 0 if index == 0 else 1).wait)
        rows = rows_of(tile)
        back = jnp.dot(dh1[rows, :], w_in_t[...], preferred_element_type=F32)
        norm = xh1[rows, :].astype(F32)
        slope_grad = back * slope1[rows, :].astype(F32)
        for index, values in enumerate((slope_grad * norm, slope_grad)):
            own_sums[pl.ds(8 * index, 8), :] += jnp.sum(values.reshape(TILE // 8, 8, 1280), axis=0)
        err = slope_grad * vectors[pl.ds(0, 1), :]
        mean = jnp.sum(err, axis=1, keepdims=True) * (1.0 / 1280)
        along = jnp.sum(err * norm, axis=1, keepdims=True) * (1.0 / 1280)
        grads[rows, :] = (
            grads[rows, :].astype(F32) + lanes(scale1[rows, :], 1280) * (err - mean - norm * along)
        ).astype(BF16)
        store(tile).start()
        return 0

    lax.fori_loop(0, steps, token_tile, 0)
    perform(SCATTER_PLAN[weight_steps + steps])
    back_copies[1].wait()
    for tile in range(steps):
        store(tile).wait()


def scatter_stage(u1, dh1, slope1, xh1, scale1, grads, w_in, vectors, sums, d_conv, d_last, dh1_share, out_share):
    rows = u1.shape[0]
    steps = rows // TILE
    shape = jax.ShapeDtypeStruct
    vmem = pl.BlockSpec(memory_space=pltpu.VMEM)
    conv_box = (LEVELS, KSIZE, 40, 384)
    last_box = (LEVELS, 40, 896)
    in_box = (LEVELS, 40, 640)
    dma = pltpu.SemaphoreType.DMA
    return pl.pallas_call(
        scatter_kernel,
        in_specs=[HBM] * 7 + [vmem] * 2 + [HBM] * 6,
        out_specs=[HBM] + [vmem] * 4 + [HBM],
        out_shape=[
            shape((rows, 1280), BF16), shape((40, 640), F32), shape((KSIZE, 20, 640), F32), shape((20, 1280), F32),
            shape((2, 128), F32), shape((1024, 1280), BF16),
        ],
        scratch_shapes=[
            pltpu.VMEM((rows, 1280), BF16),
            pltpu.VMEM((rows, 640), BF16),
            pltpu.VMEM((rows, 1280), BF16),
            pltpu.VMEM((rows, 1280), BF16),
            pltpu.VMEM((rows, 128), F32),
            pltpu.VMEM((rows, 1280), BF16),
            pltpu.VMEM((1280, 640), BF16),
            pltpu.VMEM((640, 1280), BF16),
            pltpu.VMEM((1024, 640), BF16),
            pltpu.VMEM((1280, 640), F32),
            pltpu.VMEM((LEVELS, 4, 2, 40, 640), BF16),
            pltpu.VMEM((16, 1280), F32),
            pltpu.VMEM((LEVELS, 8, 2, 128), F32),
            pltpu.VMEM((8, LEVELS, 2, 128), F32),
            pltpu.VMEM((LEVELS, 2, 128), F32),
            pltpu.VMEM((KSIZE, LEVELS, 4, 40, 384), BF16),
            pltpu.VMEM((KSIZE, LEVELS, 4, 40, 384), BF16),
            pltpu.VMEM(conv_box, BF16),
            pltpu.VMEM(conv_box, BF16),
            pltpu.VMEM(conv_box, BF16),
            pltpu.VMEM((2,) + conv_box, BF16),
            pltpu.VMEM((KSIZE, 40, 384), F32),
            pltpu.VMEM((KSIZE, 40, 384), F32),
            pltpu.VMEM((LEVELS, 4, 40, 896), BF16),
            pltpu.VMEM((LEVELS, 4, 40, 896), BF16),
            pltpu.VMEM(last_box, BF16),
            pltpu.VMEM(last_box, BF16),
            pltpu.VMEM(last_box, BF16),
            pltpu.VMEM((4, 2) + last_box, BF16),
            pltpu.VMEM((40, 896), F32),
            pltpu.VMEM((40, 896), F32),
            pltpu.VMEM((LEVELS, 4, 40, 640), BF16),
            pltpu.VMEM(in_box, BF16),
            pltpu.VMEM(in_box, BF16),
            pltpu.VMEM(in_box, BF16),
            pltpu.VMEM((2,) + in_box, BF16),
            dma((6, 2)), dma((1,)), dma((steps,)), dma((4,)), dma((2,)), dma((3,)), dma((3, 4)),
            dma((3,)), dma((3, 3, LEVELS)), dma((4, 2, 3, LEVELS)), dma((2,)), dma((2,)), dma((2,)), dma((2,)),
        ],
        compiler_params=pltpu.CompilerParams(collective_id=1, has_side_effects=True, vmem_limit_bytes=VMEM_BYTES),
        name="scatter_stage",
    )(
        u1, dh1, slope1, xh1, scale1, grads, w_in, vectors, sums,
        d_conv.reshape(KSIZE, LEVELS, 4, 40, 640), d_last.reshape(LEVELS, 4, 40, 1280), d_conv, d_last, dh1_share, out_share,
    )


def settle_kernel(
    vectors, result_in, out_back, rows_hbm, g_in, g_conv, g_last, g_vec,
    result, rows_out, in_out, conv_out, last_out, *rest
):
    vectors_out, (buffer, moved, load_sem, store_sem, moved_sem) = rest[:9], rest[9:]
    count = buffer.shape[0]
    chunk = buffer.shape[1]
    loads = [
        pltpu.make_async_copy(rows_hbm.at[pl.ds(index * chunk, chunk), :], buffer.at[index], load_sem.at[index])
        for index in range(count)
    ]
    stores = [
        pltpu.make_async_copy(buffer.at[index], rows_out.at[pl.ds(index * chunk, chunk), :], store_sem.at[index])
        for index in range(count)
    ]
    for copy in loads:
        copy.start()
    in_out[...] = g_in[...]
    conv_out[...] = g_conv[...]
    last_out[...] = g_last[...]
    places = [(0, offset, 40) for offset in WIDE_OFFSETS] + [(1, offset, 20) for offset in SLIM_OFFSETS]
    for target, (plane, offset, width) in zip(vectors_out, places):
        target[...] = g_vec[pl.ds(plane, 1), pl.ds(offset, width)]
    _, second_units, _, give, _ = unit_share(read_lengths(vectors))
    kept = second_units - give
    end = jnp.where(give > 0, 2 * lax.div(second_units + 1, 2), kept)

    def moved_load(unit):
        rows = pl.ds(pl.multiple_of(unit * UNIT, UNIT), UNIT)
        return pltpu.make_async_copy(out_back.at[rows, :], moved.at[rows, :], moved_sem.at[0, unit])

    def moved_store(unit):
        rows = pl.ds(pl.multiple_of(unit * UNIT, UNIT), UNIT)
        target = pl.ds(pl.multiple_of(1024 + unit * UNIT, UNIT), UNIT)
        return pltpu.make_async_copy(moved.at[rows, :], result.at[target, :], moved_sem.at[1, unit])

    def each(act):
        def one(unit, _):
            act(unit)
            return 0

        lax.fori_loop(kept, end, one, 0)

    def pass_moved(unit):
        moved_load(unit).wait()
        moved_store(unit).start()

    each(lambda unit: moved_load(unit).start())
    for load, store in zip(loads, stores):
        load.wait()
        store.start()
    each(pass_moved)
    each(lambda unit: moved_store(unit).wait())
    for copy in stores:
        copy.wait()


def settle_stage(vectors, result, out_back, rows, g_in, g_conv, g_last, g_vec):
    chunks = 8
    shape = jax.ShapeDtypeStruct
    vmem = pl.BlockSpec(memory_space=pltpu.VMEM)
    return pl.pallas_call(
        settle_kernel,
        in_specs=[vmem] + [HBM] * 3 + [vmem] * 4,
        out_specs=[HBM] * 2 + [vmem] * 12,
        out_shape=[shape(v.shape, v.dtype) for v in (result, rows, g_in, g_conv, g_last)]
        + [shape((1, 40), F32)] * 3
        + [shape((1, 20), F32)] * 6,
        scratch_shapes=[
            pltpu.VMEM((chunks, rows.shape[0] // chunks, rows.shape[1]), rows.dtype),
            pltpu.VMEM((1024, 1280), BF16),
            pltpu.SemaphoreType.DMA((chunks,)),
            pltpu.SemaphoreType.DMA((chunks,)),
            pltpu.SemaphoreType.DMA((2, 1024 // UNIT)),
        ],
        input_output_aliases={1: 0},
        compiler_params=pltpu.CompilerParams(vmem_limit_bytes=VMEM_BYTES),
        name="settle_stage",
    )(vectors, result, out_back, rows, g_in, g_conv, g_last, g_vec)


def kernel_body(
    tokens, out_grad, lengths, ln1_gain, ln1_bias, w_in, b_in, ln2_gain, ln2_bias,
    w_conv, b_conv, ln3_gain, ln3_bias, w_out, b_out,
):
    proteins, length_pad, width = tokens.shape
    rows = tokens.reshape(proteins * length_pad, width)
    grads = out_grad.reshape(proteins * length_pad, width)
    vec = pack_vectors(
        ln1_gain, ln1_bias, b_in, ln2_gain, ln2_bias, b_conv, ln3_gain, ln3_bias, b_out, lengths
    )
    u1, slope1, xh1, scale1, xh2, slope2, scale2, u2, vectors, in_full, conv_full, out_full, twins = gather_stage(
        rows, grads, vec, w_in, w_conv, w_out
    )
    result, dh1, out_share, dh1_share, d_conv, d_last, sums = middle_stage(
        vectors, u2, xh2, slope2, scale2, grads, rows, conv_full, out_full, twins
    )
    *owned, out_back = scatter_stage(
        u1, dh1, slope1, xh1, scale1, grads, in_full, vectors, sums, d_conv, d_last, dh1_share, out_share
    )
    result, grad_rows, g_in, g_conv, g_last, *lines = settle_stage(vectors, result, out_back, *owned)
    lines = [line.reshape(line.shape[1]) for line in lines]
    wide, slim = lines[:3], lines[3:]
    return (
        result.reshape(tokens.shape), grad_rows.reshape(tokens.shape),
        wide[0], wide[1], g_in, slim[0], slim[1], slim[2], g_conv, slim[3], slim[4], slim[5], g_last, wide[2],
    )


def layer_norm(values, gain, bias):
    center = values - jnp.mean(values, axis=-1, keepdims=True)
    var_rows = jnp.mean(center * center, axis=-1, keepdims=True)
    return center * lax.rsqrt(var_rows + EPS) * gain + bias


def norm_gelu(values, gain, bias):
    return jax.nn.gelu(layer_norm(values, gain, bias), approximate=False)


def collect(
    ln1_gain,
    ln1_bias,
    w_in,
    b_in,
    ln2_gain,
    ln2_bias,
    w_conv,
    b_conv,
    ln3_gain,
    ln3_bias,
    w_out,
    b_out,
):
    return (
        lax.all_gather(ln1_gain, ("dp", "fsdp"), axis=0, tiled=True),
        lax.all_gather(ln1_bias, ("dp", "fsdp"), axis=0, tiled=True),
        lax.all_gather(w_in, ("dp", "fsdp"), axis=0, tiled=True),
        lax.all_gather(b_in, ("dp", "fsdp"), axis=0, tiled=True),
        lax.all_gather(ln2_gain, ("dp", "fsdp"), axis=0, tiled=True),
        lax.all_gather(ln2_bias, ("dp", "fsdp"), axis=0, tiled=True),
        lax.all_gather(w_conv, ("dp", "fsdp"), axis=1, tiled=True),
        lax.all_gather(b_conv, ("dp", "fsdp"), axis=0, tiled=True),
        lax.all_gather(ln3_gain, ("dp", "fsdp"), axis=0, tiled=True),
        lax.all_gather(ln3_bias, ("dp", "fsdp"), axis=0, tiled=True),
        lax.all_gather(w_out, ("dp", "fsdp"), axis=0, tiled=True),
        lax.all_gather(b_out, ("dp", "fsdp"), axis=0, tiled=True),
    )


def spread(
    term_g1,
    term_b1,
    term_wi,
    term_bi,
    term_g2,
    term_b2,
    term_wc,
    term_bc,
    term_g3,
    term_b3,
    term_wo,
    term_bo,
):
    return (
        lax.psum_scatter(term_g1, ("dp", "fsdp"), scatter_dimension=0, tiled=True),
        lax.psum_scatter(term_b1, ("dp", "fsdp"), scatter_dimension=0, tiled=True),
        lax.psum_scatter(term_wi, ("dp", "fsdp"), scatter_dimension=0, tiled=True),
        lax.psum_scatter(term_bi, ("dp", "fsdp"), scatter_dimension=0, tiled=True),
        lax.psum_scatter(term_g2, ("dp", "fsdp"), scatter_dimension=0, tiled=True),
        lax.psum_scatter(term_b2, ("dp", "fsdp"), scatter_dimension=0, tiled=True),
        lax.psum_scatter(term_wc, ("dp", "fsdp"), scatter_dimension=1, tiled=True),
        lax.psum_scatter(term_bc, ("dp", "fsdp"), scatter_dimension=0, tiled=True),
        lax.psum_scatter(term_g3, ("dp", "fsdp"), scatter_dimension=0, tiled=True),
        lax.psum_scatter(term_b3, ("dp", "fsdp"), scatter_dimension=0, tiled=True),
        lax.psum_scatter(term_wo, ("dp", "fsdp"), scatter_dimension=0, tiled=True),
        lax.psum_scatter(term_bo, ("dp", "fsdp"), scatter_dimension=0, tiled=True),
    )


def dilate(padded, kernel, length_pad):
    total = jnp.zeros((padded.shape[0], length_pad, kernel.shape[2]), jnp.float32)
    for kernel_tap in range(kernel.shape[0]):
        window = padded[:, kernel_tap * DILATION : kernel_tap * DILATION + length_pad]
        total = total + jnp.einsum(
            "pli,io->plo", window, kernel[kernel_tap], preferred_element_type=jnp.float32
        )
    return total


def plain_body(
    tokens,
    out_grad,
    lengths,
    ln1_gain,
    ln1_bias,
    w_in,
    b_in,
    ln2_gain,
    ln2_bias,
    w_conv,
    b_conv,
    ln3_gain,
    ln3_bias,
    w_out,
    b_out,
):
    proteins, length_pad, width = tokens.shape
    row_count = proteins * length_pad
    reach = KSIZE // 2 * DILATION
    positions = lax.broadcasted_iota(jnp.int32, (proteins, length_pad), 1)
    live = (positions < lengths[:, None]).astype(jnp.float32).reshape(row_count, 1)
    full = collect(
        ln1_gain,
        ln1_bias,
        w_in,
        b_in,
        ln2_gain,
        ln2_bias,
        w_conv,
        b_conv,
        ln3_gain,
        ln3_bias,
        w_out,
        b_out,
    )
    (
        gain_one,
        bias_one,
        first_matrix,
        first_bias,
        gain_two,
        bias_two,
        conv_kernel,
        conv_bias,
        gain_three,
        bias_three,
        last_matrix,
        last_bias,
    ) = full
    inner = first_matrix.shape[1]
    row_tokens = tokens.reshape(row_count, width).astype(jnp.float32)
    act_one, pull_one = jax.vjp(
        norm_gelu, row_tokens, gain_one.astype(jnp.float32), bias_one.astype(jnp.float32)
    )
    inner_one = act_one.astype(jnp.bfloat16)
    hidden_one = jnp.dot(
        inner_one, first_matrix, preferred_element_type=jnp.float32
    ) + first_bias.astype(jnp.float32)
    act_two, pull_two = jax.vjp(
        norm_gelu, hidden_one, gain_two.astype(jnp.float32), bias_two.astype(jnp.float32)
    )
    inner_two = (act_two * live).astype(jnp.bfloat16)
    padded_two = jnp.pad(
        inner_two.reshape(proteins, length_pad, inner), ((0, 0), (reach, reach), (0, 0))
    )
    hidden_two = dilate(padded_two, conv_kernel, length_pad).reshape(
        row_count, inner
    ) + conv_bias.astype(jnp.float32)
    act_three, pull_three = jax.vjp(
        norm_gelu, hidden_two, gain_three.astype(jnp.float32), bias_three.astype(jnp.float32)
    )
    inner_three = act_three.astype(jnp.bfloat16)
    branch = jnp.dot(
        inner_three, last_matrix, preferred_element_type=jnp.float32
    ) + last_bias.astype(jnp.float32)
    result = (row_tokens + live * branch).astype(jnp.bfloat16).reshape(proteins, length_pad, width)
    again = collect(
        ln1_gain,
        ln1_bias,
        w_in,
        b_in,
        ln2_gain,
        ln2_bias,
        w_conv,
        b_conv,
        ln3_gain,
        ln3_bias,
        w_out,
        b_out,
    )
    (
        again_g1,
        again_b1,
        back_first,
        again_bi,
        again_g2,
        again_b2,
        back_kernel,
        again_bc,
        again_g3,
        again_b3,
        back_last,
        again_bo,
    ) = again
    pull_one = jax.vjp(
        norm_gelu, row_tokens, again_g1.astype(jnp.float32), again_b1.astype(jnp.float32)
    )[1]
    pull_two = jax.vjp(
        norm_gelu, hidden_one, again_g2.astype(jnp.float32), again_b2.astype(jnp.float32)
    )[1]
    pull_three = jax.vjp(
        norm_gelu, hidden_two, again_g3.astype(jnp.float32), again_b3.astype(jnp.float32)
    )[1]
    grad_rows = out_grad.reshape(row_count, width)
    grad_branch = grad_rows * live.astype(jnp.bfloat16)
    term_wo = jnp.einsum("ri,rd->id", inner_three, grad_branch, preferred_element_type=jnp.float32)
    term_bo = jnp.sum(grad_branch.astype(jnp.float32), axis=0)
    grad_three = jnp.einsum("rd,id->ri", grad_branch, back_last, preferred_element_type=jnp.float32)
    d_hidden_two, term_g3, term_b3 = pull_three(grad_three)
    low_two = d_hidden_two.astype(jnp.bfloat16)
    term_bc = jnp.sum(low_two.astype(jnp.float32), axis=0)
    padded_grad = jnp.pad(
        low_two.reshape(proteins, length_pad, inner), ((0, 0), (reach, reach), (0, 0))
    )
    grad_view = low_two.reshape(proteins, length_pad, inner)
    kernel_terms = []
    grad_two = jnp.zeros((proteins, length_pad, inner), jnp.float32)
    taps = back_kernel.shape[0]
    for kernel_tap in range(taps):
        window = padded_two[:, kernel_tap * DILATION : kernel_tap * DILATION + length_pad]
        kernel_terms.append(
            jnp.einsum("pli,plo->io", window, grad_view, preferred_element_type=jnp.float32)
        )
        mirror = (taps - 1 - kernel_tap) * DILATION
        grad_window = padded_grad[:, mirror : mirror + length_pad]
        grad_two = grad_two + jnp.einsum(
            "plo,io->pli", grad_window, back_kernel[kernel_tap], preferred_element_type=jnp.float32
        )
    term_wc = jnp.stack(kernel_terms, axis=0)
    grad_two = grad_two.reshape(row_count, inner) * live
    d_hidden_one, term_g2, term_b2 = pull_two(grad_two)
    low_one = d_hidden_one.astype(jnp.bfloat16)
    term_wi = jnp.einsum("rd,ri->di", inner_one, low_one, preferred_element_type=jnp.float32)
    term_bi = jnp.sum(low_one.astype(jnp.float32), axis=0)
    grad_one = jnp.einsum("ri,di->rd", low_one, back_first, preferred_element_type=jnp.float32)
    d_tokens, term_g1, term_b1 = pull_one(grad_one)
    grad_tokens = (
        (grad_rows.astype(jnp.float32) + d_tokens)
        .astype(jnp.bfloat16)
        .reshape(proteins, length_pad, width)
    )
    owned = spread(
        term_g1,
        term_b1,
        term_wi,
        term_bi,
        term_g2,
        term_b2,
        term_wc,
        term_bc,
        term_g3,
        term_b3,
        term_wo,
        term_bo,
    )
    return (
        result,
        grad_tokens,
        owned[0],
        owned[1],
        owned[2],
        owned[3],
        owned[4],
        owned[5],
        owned[6],
        owned[7],
        owned[8],
        owned[9],
        owned[10],
        owned[11],
    )


def solution(mesh):
    both = ("dp", "fsdp")
    by_row = P(both)
    in_specs = (
        P(both, None, None), P(both, None, None), by_row, by_row, by_row, P(both, None), by_row, by_row, by_row,
        P(None, both, None), by_row, by_row, by_row, P(both, None), by_row,
    )
    out_specs = (
        P(both, None, None), P(both, None, None), by_row, by_row, P(both, None), by_row, by_row, by_row,
        P(None, both, None), by_row, by_row, by_row, P(both, None), by_row,
    )
    body = kernel_body if (mesh.shape["dp"], mesh.shape["fsdp"]) == (8, 4) else plain_body
    return jax.shard_map(body, mesh=mesh, in_specs=in_specs, out_specs=out_specs, check_vma=False)
```

```python
import functools
import itertools

import jax
import jax.numpy as jnp
from jax import lax
from jax.experimental import pallas as pl
from jax.experimental.pallas import tpu as pltpu
from jax.sharding import PartitionSpec as P

KSIZE = 5
DILATION = 8
EPS = 1e-05
HALF_ROOT = 0.7071067811865476
PHI_SCALE = 0.3989422804014327
F32 = jnp.float32
BF16 = jnp.bfloat16
MESH = pl.DeviceIdType.MESH
VMEM_BYTES = 62 * 2**20
HBM = pl.BlockSpec(memory_space=pl.ANY)
LEVELS = 4
CHIPS = 16
DEVICES = 32
TILE = 256
CONV_COLS = ((0, 384), (384, 256))
OUT_COLS = ((0, 384), (384, 896))
WIDE_OFFSETS = (0, 40, 80)
SLIM_OFFSETS = (0, 20, 40, 60, 80, 100)


def place():
    dp = lax.axis_index("dp")
    fs = lax.axis_index("fsdp")
    return lax.div(dp, 2), lax.rem(dp, 2), lax.div(fs, 2), lax.rem(fs, 2)


def device(z, y, x, core):
    return (z * 2 + y, x * 2 + core)


def chip(z, y, x):
    return (z * 2 + y) * 2 + x


def peer_of(step):
    mine = lax.axis_index("dp") * 4 + lax.axis_index("fsdp")
    other = lax.rem(mine + step, DEVICES)
    return mine, other, (lax.div(other, 4), lax.rem(other, 4))


def greet_all():
    barrier = pltpu.get_barrier_semaphore()

    def greet(step, _):
        _, _, target = peer_of(step)
        pl.semaphore_signal(barrier, inc=1, device_id=target, device_id_type=MESH)
        return 0

    lax.fori_loop(1, DEVICES, greet, 0)
    pl.semaphore_wait(barrier, DEVICES - 1)


def chunk_masks(width, chunk):
    scale = -(-65536 // chunk)
    column = lax.broadcasted_iota(jnp.int32, (DEVICES, width), 1)
    row = lax.broadcasted_iota(jnp.int32, (DEVICES, width), 0)
    owner = lax.shift_right_logical(column * scale, 16) == row
    place_col = lax.broadcasted_iota(jnp.int32, (128, width), 1)
    place_row = lax.broadcasted_iota(jnp.int32, (128, width), 0)
    slot = place_col - lax.shift_right_logical(place_col * scale, 16) * chunk
    return owner, slot, place_row


def unpack_vectors(packed_ref, vectors_ref):
    for plane, (width, chunk, offsets) in enumerate(
        ((1280, 40, WIDE_OFFSETS), (640, 20, SLIM_OFFSETS))
    ):
        owner, slot, row = chunk_masks(width, chunk)
        packed = packed_ref[:, plane, :].astype(BF16)
        for index, offset in enumerate(offsets):
            pick = (slot + offset == row).astype(F32).astype(BF16)
            spread = jnp.dot(packed, pick, preferred_element_type=F32)
            line = jnp.sum(jnp.where(owner, spread, 0.0), axis=0, keepdims=True)
            vectors_ref[pl.ds(plane * 3 + index, 1), pl.ds(0, width)] = line


def lanes(column, width):
    return jnp.concatenate([column] * (width // 128), axis=1)


def norm_parts(values):
    width = values.shape[1]
    mean = jnp.sum(values, axis=1, keepdims=True) * (1.0 / width)
    center = values - mean
    var = jnp.sum(center * center, axis=1, keepdims=True) * (1.0 / width)
    scale = lax.rsqrt(var + EPS)
    return center * scale, scale


def gelu_parts(arg):
    normal = 0.5 + 0.5 * lax.erf(arg * HALF_ROOT)
    slope = normal + arg * (PHI_SCALE * jnp.exp(-0.5 * (arg * arg)))
    return arg * normal, slope


PART_COUNT = 4
CONV_TAPS = {1: (0, 3), 2: (3, 2)}
BY_Y = (False, True, False, True)
PLANE_FIRST = (False, False, False, True)
KINDS = ("own", "x", "y", "far")
GATHER_PLAN = (
    (
        ("vec_begin",), ("send", 0), ("begin",), ("assemble",), ("send", 3), ("vec_plane",), ("y", 0, 0),
        ("own", 0, 1), ("send", 1), ("vec_pass", 1), ("own", 0, 2), ("send", 2), ("vec_pass", 2), ("y", 3, 0),
        ("x", 3, 0), ("x", 0, 0), ("own", 1, 1), ("own", 0, 3), ("share", "own", 0), ("y", 0, 1), ("vec_pass", 3),
        ("vectors",), ("x", 1, 0), ("x", 0, 1),
    ),
    (),
    (
        ("y", 0, 2), ("own", 2, 1), ("far", 3, 0),
    ),
    (),
    (
        ("y", 0, 3), ("share", "y", 0), ("x", 0, 2), ("own", 1, 2), ("y", 1, 0), ("y", 3, 1),
    ),
    (
        ("own", 2, 2), ("x", 3, 1), ("x", 2, 0),
    ),
    (),
    (
        ("y", 2, 0), ("own", 3, 1), ("x", 1, 1),
    ),
    (
        ("far", 3, 1), ("far", 0, 1), ("y", 1, 1), ("x", 0, 3), ("share", "x", 0), ("far", 0, 2), ("far", 0, 0),
        ("own", 1, 3), ("share", "own", 1), ("far", 0, 3), ("share", "far", 0), ("far", 1, 0), ("y", 2, 1),
        ("y", 3, 2), ("w_in",),
    ),
    (
        ("own", 2, 3), ("share", "own", 2),
    ),
    (),
    (
        ("x", 3, 2), ("x", 1, 2),
    ),
    (
        ("x", 2, 1), ("y", 1, 2), ("y", 2, 2), ("own", 3, 2), ("far", 3, 2), ("x", 1, 3), ("share", "x", 1),
        ("x", 2, 2), ("y", 2, 3), ("share", "y", 2),
    ),
    (),
    (
        ("y", 1, 3), ("share", "y", 1), ("far", 2, 0),
    ),
    (
        ("far", 1, 1), ("x", 2, 3), ("share", "x", 2),
    ),
    (
        ("y", 3, 3), ("share", "y", 3), ("far", 2, 1), ("own", 3, 3), ("share", "own", 3), ("far", 1, 2), ("x", 3, 3),
        ("share", "x", 3), ("far", 1, 3), ("share", "far", 1), ("far", 2, 2), ("far", 2, 3), ("share", "far", 2),
        ("far", 3, 3), ("share", "far", 3), ("finish",),
    ),
)


def plane_peer(offset):
    z, y, x, core = place()
    other = lax.rem(y * 4 + x * 2 + core + offset, 8)
    return other, (z * 2 + lax.div(other, 4), lax.rem(other, 4))


def greet_near(z, y, x, core):
    barrier = pltpu.get_barrier_semaphore()

    def greet(target):
        pl.semaphore_signal(barrier, inc=1, device_id=target, device_id_type=MESH)

    for offset in range(1, 8):
        greet(plane_peer(offset)[1])
    pl.when(z > 0)(lambda: greet(device(z - 1, y, x, core)))
    pl.when(z < LEVELS - 1)(lambda: greet(device(z + 1, y, x, core)))
    pl.semaphore_wait(barrier, 7 + (z > 0).astype(jnp.int32) + (z < LEVELS - 1).astype(jnp.int32))


def each_level(z, distance, act):
    if distance == 0:
        act(z, 0)
        return
    pl.when(z + distance < LEVELS)(lambda: act(z + distance, 1))
    pl.when(z - distance >= 0)(lambda: act(z - distance, -1))


def gather_kernel(
    tokens_hbm, grads_hbm, vec, w_in, w_conv, w_out,
    u1_hbm, slope1_hbm, xh1_hbm, scale1_hbm, xh2_hbm, slope2_hbm, scale2_hbm, u2_hbm, vectors_out,
    in_full, conv_full, out_full,
    u2_share, xh2_share, slope2_share, scale2_share, grads_share, tokens_share,
    packed, in_vmem, conv_twin, out_twin, conv_own, out_own,
    tokens, u1, slope1, xh1, scale1, xh2, slope2, scale2, u2, token_sem, store_sem, share_send, share_recv,
    vec_send, vec_recv, link_send, link_recv, twin_recv, pair_send, pair_recv, own_sem, load_sem,
):
    z, y, x, core = place()
    here = 2 * y + x
    steps = 2048 // TILE
    columns = {"own": here, "x": 2 * y + (1 - x), "y": 2 * (1 - y) + x, "far": 2 * (1 - y) + (1 - x)}

    def piece(part, level, column, side):
        if part == 0:
            return in_vmem.at[pl.ds(pl.multiple_of((level * 4 + column) * 80 + side * 40, 8), 40), :]
        if part in CONV_TAPS:
            return conv_full.at[pl.ds(*CONV_TAPS[part]), level, column, :, pl.ds(*CONV_COLS[side])]
        return out_full.at[level, column, :, pl.ds(*OUT_COLS[side])]

    def pieces(part, column, side):
        if part in CONV_TAPS:
            return conv_full.at[pl.ds(*CONV_TAPS[part]), :, column, :, pl.ds(*CONV_COLS[side])]
        return out_full.at[:, column, :, pl.ds(*OUT_COLS[side])]

    def span(part, side, count):
        if part == 0:
            return in_vmem.at[pl.ds(0, 40 * count), :]
        rows, columns_ = (LEVELS, count // LEVELS) if count % LEVELS == 0 else (count, 1)
        if part in CONV_TAPS:
            return conv_full.at[
                pl.ds(*CONV_TAPS[part]), pl.ds(0, rows), pl.ds(0, columns_), :, pl.ds(*CONV_COLS[side])
            ]
        return out_full.at[pl.ds(0, rows), pl.ds(0, columns_), :, pl.ds(*OUT_COLS[side])]

    def own_piece(part, side):
        if part == 0:
            return w_in
        if part in CONV_TAPS:
            return conv_own.at[pl.ds(*CONV_TAPS[part]), :, pl.ds(*CONV_COLS[side])]
        return out_own.at[:, pl.ds(*OUT_COLS[side])]

    def target(link, side):
        return (
            device(z, y, 1 - x, side),
            device(z, 1 - y, x, side),
            device(z + 1, y, x, side),
            device(z - 1, y, x, side),
            device(z, y, x, 1 - side),
        )[link]

    def remote(src, dst, send_sem, recv_sem, where):
        return pltpu.make_async_remote_copy(
            src_ref=src, dst_ref=dst, send_sem=send_sem, recv_sem=recv_sem, device_id=where, device_id_type=MESH
        )

    def wait_sent(side, part, link, count):
        view = span(part, side, count)
        remote(view, view, link_send.at[link, part], twin_recv.at[0, part], target(4, side)).wait_send()

    def guarded(link, act):
        if link == 2:
            pl.when(z < LEVELS - 1)(act)
        elif link == 3:
            pl.when(z > 0)(act)
        else:
            act()

    def forward(side, part, level, column, links, own=False):
        place_ref = piece(part, level, column, side)
        for link in links:

            def act(link=link):
                remote(
                    own_piece(part, side) if own else place_ref, place_ref,
                    link_send.at[link, part], link_recv.at[level, column, part], target(link, side),
                ).start()

            guarded(link, act)

    def pass_on(side, kind, part, distance):
        def act(level, sign):
            column = columns[kind]
            place_ref = piece(part, level, column, side)
            remote(
                place_ref, place_ref, link_send.at[4, part], link_recv.at[level, column, part], target(4, side)
            ).wait_recv()
            along = {1: (3,), -1: (2,), 0: (2, 3)}[sign]
            links = ()
            if kind == "own":
                links = along if PLANE_FIRST[part] else along + (0, 1)
            else:
                if kind == "x" and BY_Y[part] and (distance == 0 or not PLANE_FIRST[part]):
                    links += (1,)
                if kind == "y" and not BY_Y[part] and (distance == 0 or not PLANE_FIRST[part]):
                    links += (0,)
                if PLANE_FIRST[part]:
                    links += along
            forward(side, part, level, column, links)

        each_level(z, distance, act)

    def own_sends(side, part):
        forward(side, part, z, here, (0, 1, 2, 3), own=True)

    def twin_copy(side, kind, part, level=None):
        if level is None:
            view = pieces(part, columns[kind], side)
        else:
            view = piece(part, level, columns[kind], side)
        return remote(view, view, link_send.at[4, part], twin_recv.at[KINDS.index(kind), part], target(4, side))

    def share(side, kind, part):
        if kind == "own":
            own_copy(side, part).wait()
        if part:
            twin_copy(side, kind, part).start()
        else:
            for level in range(LEVELS):
                twin_copy(side, kind, part, level).start()

    def take_twin(side, part):
        for kind in KINDS:
            if part:
                twin_copy(1 - side, kind, part).wait_recv()
            else:
                view = span(part, side, LEVELS)
                remote(
                    view, view, link_send.at[4, part], twin_recv.at[KINDS.index(kind), part], target(4, side)
                ).wait_recv()

    def pair_copies(side):
        return [
            remote(src, dst, pair_send.at[index], pair_recv.at[index], target(4, side))
            for index, (src, dst) in enumerate(((w_conv, conv_twin), (w_out, out_twin)))
        ]

    def own_copy(side, part):
        return pltpu.make_async_copy(own_piece(part, side), piece(part, z, here, side), own_sem.at[part])

    def vec_copy(offset):
        mine = z * 8 + y * 4 + x * 2 + core
        return remote(vec, packed.at[mine], vec_send.at[0], vec_recv.at[0], plane_peer(offset)[1])

    def level_rows(level):
        return packed.at[pl.ds(pl.multiple_of(level * 8, 8), 8)]

    def vec_line(side, level, link):
        rows = level_rows(level)
        return remote(rows, rows, vec_send.at[link - 1], vec_recv.at[1 + level], target(link, side))

    def vec_begin(side):
        for offset in range(1, 8):
            vec_copy(offset).start()
        packed[pl.ds(z * 8 + y * 4 + x * 2 + side, 1)] = vec[...][None]

    def vec_plane(side):
        rows = packed.at[pl.ds(0, 7)]
        remote(rows, rows, vec_send.at[0], vec_recv.at[0], target(4, side)).wait()
        for link in (2, 3):
            guarded(link, lambda link=link: vec_line(side, z, link).start())

    def vec_pass(side, distance):
        def act(level, sign):
            link = 3 if sign > 0 else 2
            vec_line(side, level, link).wait_recv()
            guarded(link, lambda: vec_line(side, level, link).start())

        each_level(z, distance, act)

    def vec_finish(side):
        for level in range(LEVELS):

            @pl.when(z == level)
            def _(level=level):
                for link, count in ((2, level + 1 if level < LEVELS - 1 else 0), (3, LEVELS - level if level else 0)):
                    if count:
                        rows = packed.at[pl.ds(0, 8 * count)]
                        remote(rows, rows, vec_send.at[link - 1], vec_recv.at[0], target(4, side)).wait_send()

    def begin(side):
        own_copy(side, 0).start()
        for copy in pair_copies(side):
            copy.start()
        share_rows(side, slice(4, 6))

    def assemble(side):
        for copy in pair_copies(side):
            copy.wait()
        first_conv, second_conv = (w_conv, conv_twin) if side == 0 else (conv_twin, w_conv)
        first_out, second_out = (w_out, out_twin) if side == 0 else (out_twin, w_out)
        conv_own[...] = jnp.concatenate(
            [first_conv[...].astype(F32), second_conv[...].astype(F32)], axis=1
        ).astype(BF16)
        out_own[...] = jnp.concatenate(
            [first_out[...].astype(F32), second_out[...].astype(F32)], axis=0
        ).astype(BF16)
        for part in range(1, PART_COUNT):
            own_copy(side, part).start()

    def shares(side):
        half = pl.ds(1024, 1024)
        pairs = (
            (u2, u2_share), (xh2, xh2_share), (slope2, slope2_share), (scale2, scale2_share),
            (grads_hbm, grads_share), (tokens_hbm, tokens_share),
        )
        return [
            remote(source.at[half, :], target_, share_send.at[index], share_recv.at[index], target(4, side))
            for index, (source, target_) in enumerate(pairs)
        ]

    def share_rows(side, which):
        for copy in shares(side)[which]:
            copy.start()

    def save_in():
        return pltpu.make_async_copy(in_vmem, in_full, load_sem.at[0])

    def take_in(side):
        take_twin(side, 0)
        save_in().start()

    def finish(side):
        vec_finish(side)
        for part in range(1, PART_COUNT):
            take_twin(side, part)
        for part in range(PART_COUNT):
            plane, along = (1, 4) if PLANE_FIRST[part] else (4, 1)
            wait_sent(side, part, 0, plane if BY_Y[part] else 2 * plane)
            wait_sent(side, part, 1, 2 * plane if BY_Y[part] else plane)
            wait_sent(side, part, 4, CHIPS)
            for level in range(LEVELS):

                @pl.when(z == level)
                def _(part=part, along=along, level=level):
                    if level < LEVELS - 1:
                        wait_sent(side, part, 2, along * (level + 1))
                    if level > 0:
                        wait_sent(side, part, 3, along * (LEVELS - level))

        save_in().wait()
        for copy in shares(side):
            copy.wait()

    def take_vectors(side):
        unpack_vectors(packed, vectors_out)
        mine = z * 8 + y * 4 + x * 2
        for row, owner in ((9, mine + side), (10, mine + 1 - side)):
            vectors_out[pl.ds(row, 1), pl.ds(0, 128)] = packed[owner, pl.ds(0, 1), :]

    actions = {
        "share_rows": share_rows,
        "send": own_sends, "begin": begin, "assemble": assemble, "w_in": take_in, "finish": finish,
        "vec_begin": vec_begin, "vec_plane": vec_plane, "vec_pass": vec_pass,
        "vectors": take_vectors,
        "share": share,
    }

    def perform(events):
        for side in range(2):

            @pl.when(core == side)
            def _(side=side):
                for event in events:
                    if event[0] in actions:
                        actions[event[0]](side, *event[1:])
                    else:
                        pass_on(side, *event)

    def rows_of(tile, count=1):
        return pl.ds(pl.multiple_of(tile * TILE, TILE), count * TILE)

    def token_load(tile):
        return pltpu.make_async_copy(tokens_hbm.at[rows_of(tile), :], tokens.at[rows_of(tile), :], token_sem.at[tile])

    first = ((u1, u1_hbm), (slope1, slope1_hbm), (xh1, xh1_hbm), (scale1, scale1_hbm))
    second = ((u2, u2_hbm), (xh2, xh2_hbm), (slope2, slope2_hbm), (scale2, scale2_hbm))

    def stores(pairs, phase, half):
        rows = rows_of(half * (steps // 2), steps // 2)
        return [
            pltpu.make_async_copy(src.at[rows, :], dst.at[rows, :], store_sem.at[phase, half, index])
            for index, (src, dst) in enumerate(pairs)
        ]

    def start_stores(pairs, phase, half):
        for copy in stores(pairs, phase, half):
            copy.start()

    greet_near(z, y, x, core)
    for tile in range(steps):
        token_load(tile).start()

    def wide_tile(tile, _):
        for index in range(steps):
            if GATHER_PLAN[index]:
                pl.when(tile == index)(functools.partial(perform, GATHER_PLAN[index]))
        token_load(tile).wait()
        rows = rows_of(tile)
        gain, bias = vectors_out[pl.ds(0, 1), :], vectors_out[pl.ds(1, 1), :]
        norm, scale = norm_parts(tokens[rows, :].astype(F32))
        act, slope = gelu_parts(norm * gain + bias)
        u1[rows, :] = act.astype(BF16)
        slope1[rows, :] = slope.astype(BF16)
        xh1[rows, :] = norm.astype(BF16)
        scale1[rows, :] = jnp.broadcast_to(scale, (TILE, 128))
        return 0

    lax.fori_loop(0, steps, wide_tile, 0)

    def slim_tile(tile, _):
        for index in range(steps):
            events = GATHER_PLAN[steps + index]
            if index == 0:
                pl.when(tile == 0)(lambda: start_stores(first, 0, 0))
                pl.when(tile == 0)(lambda: start_stores(first, 0, 1))
            if index == steps // 2:

                @pl.when(tile == index)
                def _():
                    start_stores(second, 1, 1)
                    perform((("share_rows", slice(0, 4)),))

            if events:
                pl.when(tile == index)(functools.partial(perform, events))
        rows = rows_of(lax.rem(tile + steps // 2, steps))
        hidden = jnp.dot(u1[rows, :], in_vmem[...], preferred_element_type=F32)
        hidden = hidden + vectors_out[pl.ds(3, 1), pl.ds(0, 640)]
        norm, scale = norm_parts(hidden)
        act, slope = gelu_parts(norm * vectors_out[pl.ds(4, 1), pl.ds(0, 640)] + vectors_out[pl.ds(5, 1), pl.ds(0, 640)])
        u2[rows, :] = act.astype(BF16)
        slope2[rows, :] = slope.astype(BF16)
        xh2[rows, :] = norm.astype(BF16)
        scale2[rows, :] = jnp.broadcast_to(scale, (TILE, 128))
        return 0

    lax.fori_loop(0, steps, slim_tile, 0)
    start_stores(second, 1, 0)
    perform(GATHER_PLAN[2 * steps])
    for phase, pairs in enumerate((first, second)):
        for half in range(2):
            for copy in stores(pairs, phase, half):
                copy.wait()


def gather_stage(tokens, grads, vec, w_in, w_conv, w_out):
    rows = tokens.shape[0]
    shape = jax.ShapeDtypeStruct
    vmem = pl.BlockSpec(memory_space=pltpu.VMEM)
    wide, slim, column = (rows, 1280), (rows, 640), (rows, 128)
    *results, conv_full, out_full, s0, s1, s2, s3, s4, s5 = pl.pallas_call(
        gather_kernel,
        in_specs=[HBM] * 2 + [vmem] * 4,
        out_specs=[HBM] * 8 + [vmem] + [HBM] * 9,
        out_shape=[
            shape(wide, BF16), shape(wide, BF16), shape(wide, BF16), shape(column, F32),
            shape(slim, BF16), shape(slim, BF16), shape(column, F32), shape(slim, BF16),
            shape((16, 1280), F32),
            shape((1280, 640), BF16), shape((KSIZE, LEVELS, 4, 40, 640), BF16), shape((LEVELS, 4, 40, 1280), BF16),
            shape((1024, 640), BF16), shape((1024, 640), BF16), shape((1024, 640), BF16), shape((1024, 128), F32),
            shape((1024, 1280), BF16), shape((1024, 1280), BF16),
        ],
        scratch_shapes=[
            pltpu.VMEM((DEVICES, 2, 128), F32),
            pltpu.VMEM((1280, 640), BF16),
            pltpu.VMEM((KSIZE, 20, 640), BF16),
            pltpu.VMEM((20, 1280), BF16),
            pltpu.VMEM((KSIZE, 40, 640), BF16),
            pltpu.VMEM((40, 1280), BF16),
            pltpu.VMEM(wide, BF16),
            pltpu.VMEM(wide, BF16),
            pltpu.VMEM(wide, BF16),
            pltpu.VMEM(wide, BF16),
            pltpu.VMEM(column, F32),
            pltpu.VMEM(slim, BF16),
            pltpu.VMEM(slim, BF16),
            pltpu.VMEM(column, F32),
            pltpu.VMEM(slim, BF16),
            pltpu.SemaphoreType.DMA((rows // TILE,)),
            pltpu.SemaphoreType.DMA((2, 2, 4)),
            pltpu.SemaphoreType.DMA((6,)),
            pltpu.SemaphoreType.DMA((6,)),
            pltpu.SemaphoreType.DMA((3,)),
            pltpu.SemaphoreType.DMA((1 + LEVELS,)),
            pltpu.SemaphoreType.DMA((5, PART_COUNT)),
            pltpu.SemaphoreType.DMA((LEVELS, 4, PART_COUNT)),
            pltpu.SemaphoreType.DMA((4, PART_COUNT)),
            pltpu.SemaphoreType.DMA((2,)),
            pltpu.SemaphoreType.DMA((2,)),
            pltpu.SemaphoreType.DMA((PART_COUNT,)),
            pltpu.SemaphoreType.DMA((1,)),
        ],
        compiler_params=pltpu.CompilerParams(
            collective_id=0, has_side_effects=True, vmem_limit_bytes=VMEM_BYTES,
        ),
        name="gather_stage",
    )(tokens, grads, vec, w_in, w_conv, w_out)
    return *results, conv_full.reshape(KSIZE, 640, 640), out_full.reshape(640, 1280), (s0, s1, s2, s3, s4, s5)


def pack_vectors(ln1_gain, ln1_bias, b_in, ln2_gain, ln2_bias, b_conv, ln3_gain, ln3_bias, b_out, lengths):
    total = None
    for plane, pieces in enumerate(
        (
            zip((ln1_gain, ln1_bias, b_out, lengths), WIDE_OFFSETS + (LENGTH_LANE,)),
            zip((b_in, ln2_gain, ln2_bias, b_conv, ln3_gain, ln3_bias), SLIM_OFFSETS),
        )
    ):
        for piece, offset in pieces:
            line = piece[None]
            room = ((plane, 1 - plane, 0), (offset, 128 - offset - piece.shape[0], 0))
            placed = lax.pad(line, jnp.zeros((), line.dtype), room).astype(F32)
            total = placed if total is None else total + placed
    return total


PAD = 32
SPAN = 1024 + 2 * PAD
HALO = 16
UNIT = 128
LENGTH_LANE = 120


def unit_share(lengths):
    own_first, own_second, twin_first, twin_second = (lax.div(length + UNIT - 1, UNIT) for length in lengths)
    excess = own_first + own_second - twin_first - twin_second
    give = jnp.minimum(lax.div(jnp.maximum(excess, 0), 2), own_second)
    take = jnp.minimum(lax.div(jnp.maximum(-excess, 0), 2), twin_second)
    return own_first, own_second, twin_second, give, take


def read_lengths(vectors):
    lane = lax.broadcasted_iota(jnp.int32, (1, 128), 1)
    return [
        jnp.sum(jnp.where(lane == LENGTH_LANE + index, vectors[pl.ds(row, 1), pl.ds(0, 128)], 0.0)).astype(jnp.int32)
        for row in (9, 10)
        for index in range(2)
    ]


def middle_kernel(
    vectors, u2_hbm, xh2_hbm, slope2_hbm, scale2_hbm, grads_hbm, tokens_hbm, conv_hbm, last_hbm,
    u2_twin, xh2_twin, slope2_twin, scale2_twin, grads_twin, tokens_twin,
    out_hbm, dh1_hbm, out_twin, dh1_twin, d_conv_hbm, d_last_hbm, sums_out,
    conv, conv_t, last, last_t, u2, dh2, grads, tokens, xh2, slope2, scale2, d_conv, d_last, zeros,
    u2_sem, row_sem, back_sem, weight_sem, out_sem, dh1_sem, flush_sem,
):
    segments = 3
    tiles = 1024 // TILE
    wide, slim = 1280, 640
    lengths = read_lengths(vectors)
    first_units, second_units, twin_units, give, take = unit_share(lengths)

    def pick(segment, values):
        if isinstance(segment, int):
            return values[segment]
        return jnp.where(segment == 0, values[0], jnp.where(segment == 1, values[1], values[2]))

    def bounds(segment):
        low = pick(segment, (0, 0, twin_units - take))
        high = pick(segment, (first_units, second_units - give, twin_units))
        before = jnp.logical_and(jnp.logical_and(segment == 2, low > 0), high > low).astype(jnp.int32)
        after = jnp.logical_and(jnp.logical_and(segment == 1, give > 0), high > 0).astype(jnp.int32)
        return low, high, before, after

    def tile_range(low, high):
        return lax.div(low, 2), jnp.where(high > low, lax.div(high + 1, 2), lax.div(low, 2))

    def worked_tiles(segment):
        low, high, _, _ = bounds(segment)
        return tile_range(low, high)

    def held_tiles(segment):
        low, high, before, after = bounds(segment)
        return tile_range(low - before, high + after)

    def live_units(segment):
        return pick(segment, (first_units, second_units, twin_units))

    def live_tiles(segment):
        return lax.div(live_units(segment) + 1, 2)

    def rows_of(segment, tile):
        return pl.ds(pl.multiple_of(segment * 1024 + tile * TILE, TILE), TILE)

    def padded(segment, row, count, shift=0):
        return pl.ds(pl.multiple_of(segment * SPAN + PAD + row, 8) + shift, count)

    def plain(row, count, shift=0):
        return pl.ds(pl.multiple_of(PAD + row, 8) + shift, count)

    def fetch(segment, tile, own, twin, target, rows, sem):
        source = own.at[rows_of(segment, tile), :] if segment < 2 else twin.at[rows_of(0, tile), :]
        pltpu.make_async_copy(source, target.at[rows, :], sem).start()

    def fetched(segment, tile, own, target, rows, sem):
        pltpu.make_async_copy(own.at[rows_of(0, tile), :], target.at[rows, :], sem).wait()

    def emit(tile, segment, source, own, twin, sem):
        if isinstance(segment, int):
            target = own.at[rows_of(segment, tile), :] if segment < 2 else twin.at[rows_of(0, tile), :]
            pltpu.make_async_copy(source, target, sem).start()
            return

        @pl.when(segment < 2)
        def _():
            pltpu.make_async_copy(source, own.at[rows_of(segment, tile), :], sem).start()

        @pl.when(segment == 2)
        def _():
            pltpu.make_async_copy(source, twin.at[rows_of(0, tile), :], sem).start()

    def u2_at(segment, tile):
        return padded(segment, tile * TILE, TILE)

    row_arrays = ((grads_hbm, grads_twin, grads), (tokens_hbm, tokens_twin, tokens))
    back_arrays = ((xh2_hbm, xh2_twin, xh2), (slope2_hbm, slope2_twin, slope2), (scale2_hbm, scale2_twin, scale2))

    def fetch_rows(segment, tile, index):
        own, twin, target = row_arrays[index]
        fetch(segment, tile, own, twin, target, rows_of(segment, tile), row_sem.at[index, segment, tile])

    def rows_fetched(segment, tile, index):
        own, _, target = row_arrays[index]
        fetched(segment, tile, own, target, rows_of(segment, tile), row_sem.at[index, segment, tile])

    def fetch_u2(segment):
        low, high = held_tiles(segment)

        def one(tile, _):
            fetch(segment, tile, u2_hbm, u2_twin, u2, u2_at(segment, tile), u2_sem.at[segment, tile])
            return 0

        lax.fori_loop(low, high, one, 0)

    def out_store(segment, tile):
        emit(tile, segment, tokens.at[rows_of(segment, tile), :], out_hbm, out_twin, out_sem.at[segment, tile])

    def dh1_store(segment, tile, source):
        emit(tile, segment, source, dh1_hbm, dh1_twin, dh1_sem.at[segment, tile])

    conv_load = pltpu.make_async_copy(conv_hbm, conv, weight_sem.at[0])
    last_load = pltpu.make_async_copy(last_hbm, last, weight_sem.at[1])
    last_flush = pltpu.make_async_copy(last, d_last_hbm, flush_sem.at[0])

    fetch_u2(0)
    conv_load.start()
    last_load.start()

    def load_rows(segment):
        if segment:
            fetch_u2(segment)
        low, high = worked_tiles(segment)
        held = held_tiles(segment)

        def one(tile, _):
            fetch_rows(segment, tile, 0)
            pl.when(jnp.logical_and(tile >= low, tile < high))(lambda: fetch_rows(segment, tile, 1))
            return 0

        lax.fori_loop(held[0], held[1], one, 0)

    def load_back(segment):
        low, high = worked_tiles(segment)

        def one(tile, _):
            for index, (own, twin, target) in enumerate(back_arrays):
                fetch(segment, tile, own, twin, target, rows_of(segment, tile), back_sem.at[index, segment, tile])
            return 0

        lax.fori_loop(low, high, one, 0)

    load_rows(0)
    zeros[...] = jnp.zeros_like(zeros)

    def idle(segment):
        low, high = worked_tiles(segment)

        def one(tile, _):
            pl.when(jnp.logical_or(tile < low, tile >= high))(lambda: dh1_store(segment, tile, zeros))
            if segment < 2:
                pl.when(tile >= live_tiles(segment))(lambda: fetch_rows(segment, tile, 1))
            return 0

        lax.fori_loop(0, tiles, one, 0)

    def load_rest():
        for segment in range(segments):
            if segment:
                load_rows(segment)
            load_back(segment)
        for segment in range(segments):
            idle(segment)

    sums_out[...] = jnp.zeros_like(sums_out)

    def clear(index, _):
        rows = pl.ds(pl.multiple_of(index * 64, 64), 64)
        d_last[rows, :] = jnp.zeros((64, wide), F32)
        for tap in range(KSIZE):
            d_conv[tap, rows, :] = jnp.zeros((64, slim), F32)
        return 0

    lax.fori_loop(0, slim // 64, clear, 0)

    def vector(index, width=slim):
        return vectors[pl.ds(index, 1), pl.ds(0, width)]

    def add_sum(index, values):
        width = values.shape[1]
        sums_out[pl.ds(index * 8, 8), pl.ds(0, width)] += jnp.sum(
            values.reshape(values.shape[0] // 8, 8, width), axis=0
        )

    edge = jnp.zeros((PAD, slim), BF16)

    def one_segment(segment, _):
        low, high, before, after = bounds(segment)
        first_tile, end_tile = worked_tiles(segment)
        held = held_tiles(segment)
        count = live_units(segment)
        length = pick(segment, (lengths[0], lengths[1], lengths[3]))

        def live_rows(row, size):
            position = lax.broadcasted_iota(jnp.int32, (size, 128), 0) + row
            return (position < length).astype(F32)

        def prepare(tile, _):
            fetched(segment, tile, u2_hbm, u2, u2_at(segment, tile), u2_sem.at[segment, tile])
            return 0

        lax.fori_loop(held[0], held[1], prepare, 0)

        @pl.when(low == 0)
        def _():
            u2[padded(segment, -PAD, PAD), :] = edge

        dh2[plain(low * UNIT - PAD, PAD), :] = edge
        dh2[plain(high * UNIT, PAD), :] = edge

        @pl.when(jnp.logical_and(high > low, high + after == count))
        def _():
            tail = padded(segment, (count - 1) * UNIT, UNIT)
            u2[tail, :] = (u2[tail, :].astype(F32) * lanes(live_rows((count - 1) * UNIT, UNIT), slim)).astype(BF16)
            u2[padded(segment, count * UNIT, PAD), :] = edge

        @pl.when(segment == 0)
        def _():
            conv_load.wait()
            last_load.wait()
            load_rest()
            last_t[...] = last[...].T

            def turn(tap, _):
                conv_t[tap] = conv[tap].T
                return 0

            lax.fori_loop(0, KSIZE, turn, 0)

        def forward_rows(row, size, whole):
            rows = pl.ds(pl.multiple_of(segment * 1024 + row, HALO), size)
            live = live_rows(row, size)
            hidden = jnp.dot(u2[padded(segment, row, size, -16), :], conv[0], preferred_element_type=F32)
            for tap in range(1, KSIZE):
                hidden += jnp.dot(
                    u2[padded(segment, row, size, (tap - 2) * DILATION), :], conv[tap], preferred_element_type=F32
                )
            gz = (grads[rows, :].astype(F32) * lanes(live, wide)).astype(BF16)
            back = jnp.dot(gz, last_t[...], preferred_element_type=F32)
            norm, scale = norm_parts(hidden + vector(6))
            act, slope = gelu_parts(norm * vector(7) + vector(8))
            slope_grad = back * slope
            err = slope_grad * vector(7)
            mean = jnp.sum(err, axis=1, keepdims=True) * (1.0 / slim)
            along = jnp.sum(err * norm, axis=1, keepdims=True) * (1.0 / slim)
            low_grad = (scale * (err - mean - norm * along)).astype(BF16)
            dh2[plain(row, size), :] = low_grad
            if whole:
                u3 = act.astype(BF16)
                branch = jnp.dot(u3, last[...], preferred_element_type=F32) + vector(2, wide)
                tokens[rows, :] = (tokens[rows, :].astype(F32) + lanes(live, wide) * branch).astype(BF16)
                d_last[...] += lax.dot_general(u3, gz, (((0,), (0,)), ((), ())), preferred_element_type=F32)
                add_sum(2, gz.astype(F32))
                add_sum(7, slope_grad * norm)
                add_sum(8, slope_grad)
                add_sum(6, low_grad.astype(F32))

        def by_size(tile, act):
            whole = jnp.logical_and(2 * tile >= low, 2 * tile + 2 <= high)
            pl.when(whole)(lambda: act(tile * TILE, TILE))
            pl.when(jnp.logical_not(whole))(lambda: act(jnp.maximum(2 * tile, low) * UNIT, UNIT))

        def forward(tile, _):
            rows_fetched(segment, tile, 0)
            rows_fetched(segment, tile, 1)
            by_size(tile, lambda row, size: forward_rows(row, size, True))
            out_store(segment, tile)
            return 0

        lax.fori_loop(first_tile, end_tile, forward, 0)

        @pl.when(before + after > 0)
        def _():
            tile = jnp.where(before > 0, held[0], held[1] - 1)
            pl.when(jnp.logical_or(tile < first_tile, tile >= end_tile))(lambda: rows_fetched(segment, tile, 0))
            forward_rows(jnp.where(before > 0, low * UNIT - HALO, high * UNIT), HALO, False)

        def dead_store(tile, _):
            rows_fetched(segment, tile, 1)
            out_store(segment, tile)
            return 0

        lax.fori_loop(jnp.where(segment < 2, live_tiles(segment), tiles), tiles, dead_store, 0)

        @pl.when(segment == segments - 1)
        def _():
            last[...] = d_last[...].astype(BF16)
            last_flush.start()

        def backward_rows(row, size):
            rows = pl.ds(pl.multiple_of(segment * 1024 + row, UNIT), size)
            live = lanes(live_rows(row, size), slim)
            source_t = u2[padded(segment, row, size), :].T
            total = None
            for tap in range(KSIZE):
                window = dh2[plain(row, size, (2 - tap) * DILATION), :]
                term = jnp.dot(window, conv_t[tap], preferred_element_type=F32)
                total = term if total is None else total + term
                d_conv[tap] += jnp.dot(source_t, window, preferred_element_type=F32)
            norm = xh2[rows, :].astype(F32)
            slope_grad = total * live * slope2[rows, :].astype(F32)
            add_sum(4, slope_grad * norm)
            add_sum(5, slope_grad)
            err = slope_grad * vector(4)
            mean = jnp.sum(err, axis=1, keepdims=True) * (1.0 / slim)
            along = jnp.sum(err * norm, axis=1, keepdims=True) * (1.0 / slim)
            low_grad = (lanes(scale2[rows, :], slim) * (err - mean - norm * along)).astype(BF16)
            add_sum(3, low_grad.astype(F32))
            slope2[rows, :] = low_grad
            if size == UNIT:
                other = 2 * lax.div(row, TILE) * TILE + UNIT - row
                slope2[pl.ds(pl.multiple_of(segment * 1024 + other, UNIT), UNIT), :] = jnp.zeros((UNIT, slim), BF16)

        def backward(tile, _):
            rows = rows_of(segment, tile)
            for index, (own, twin, target) in enumerate(back_arrays):
                fetched(segment, tile, own, target, rows, back_sem.at[index, segment, tile])
            by_size(tile, backward_rows)
            dh1_store(segment, tile, slope2.at[rows, :])
            return 0

        lax.fori_loop(first_tile, end_tile, backward, 0)
        return 0

    lax.fori_loop(0, segments, one_segment, 0)

    def conv_flush(tap):
        return pltpu.make_async_copy(conv.at[tap], d_conv_hbm.at[tap], flush_sem.at[tap + 1])

    def flush(tap, _):
        conv[tap] = d_conv[tap].astype(BF16)
        conv_flush(tap).start()
        return 0

    lax.fori_loop(0, KSIZE, flush, 0)

    def stored(segment, _):
        low, high = worked_tiles(segment)

        def one(tile, _):
            pltpu.make_async_copy(zeros, dh1_hbm.at[rows_of(0, tile), :], dh1_sem.at[segment, tile]).wait()
            worked = jnp.logical_and(tile >= low, tile < high)
            dead = jnp.logical_and(segment < 2, tile >= live_tiles(segment))

            @pl.when(jnp.logical_or(worked, dead))
            def _():
                pltpu.make_async_copy(
                    tokens.at[rows_of(0, tile), :], out_hbm.at[rows_of(0, tile), :], out_sem.at[segment, tile]
                ).wait()

            return 0

        lax.fori_loop(0, tiles, one, 0)
        return 0

    lax.fori_loop(0, segments, stored, 0)
    for copy in [last_flush] + [conv_flush(tap) for tap in range(KSIZE)]:
        copy.wait()


def middle_stage(vectors, u2, xh2, slope2, scale2, grads, tokens, w_conv, w_out, twins):
    rows = u2.shape[0]
    shape = jax.ShapeDtypeStruct
    vmem = pl.BlockSpec(memory_space=pltpu.VMEM)
    tiles = 1024 // TILE
    held = 3 * 1024
    return pl.pallas_call(
        middle_kernel,
        in_specs=[vmem] + [HBM] * 14,
        out_specs=[HBM] * 6 + [vmem],
        out_shape=[
            shape((rows, 1280), BF16), shape((rows, 640), BF16), shape((1024, 1280), BF16), shape((1024, 640), BF16),
            shape((KSIZE, 640, 640), BF16), shape((640, 1280), BF16), shape((72, 1280), F32),
        ],
        scratch_shapes=[
            pltpu.VMEM((KSIZE, 640, 640), BF16),
            pltpu.VMEM((KSIZE, 640, 640), BF16),
            pltpu.VMEM((640, 1280), BF16),
            pltpu.VMEM((1280, 640), BF16),
            pltpu.VMEM((3 * SPAN, 640), BF16),
            pltpu.VMEM((SPAN, 640), BF16),
            pltpu.VMEM((held, 1280), BF16),
            pltpu.VMEM((held, 1280), BF16),
            pltpu.VMEM((held, 640), BF16),
            pltpu.VMEM((held, 640), BF16),
            pltpu.VMEM((held, 128), F32),
            pltpu.VMEM((KSIZE, 640, 640), F32),
            pltpu.VMEM((640, 1280), F32),
            pltpu.VMEM((TILE, 640), BF16),
            pltpu.SemaphoreType.DMA((3, tiles)),
            pltpu.SemaphoreType.DMA((2, 3, tiles)),
            pltpu.SemaphoreType.DMA((3, 3, tiles)),
            pltpu.SemaphoreType.DMA((2,)),
            pltpu.SemaphoreType.DMA((3, tiles)),
            pltpu.SemaphoreType.DMA((3, tiles)),
            pltpu.SemaphoreType.DMA((6,)),
        ],
        compiler_params=pltpu.CompilerParams(vmem_limit_bytes=VMEM_BYTES),
        name="middle_stage",
    )(vectors, u2, xh2, slope2, scale2, grads, tokens, w_conv, w_out, *twins)


def pack_sums(plane, lines, offsets, packed_ref):
    width, chunk = ((1280, 40), (640, 20))[plane]
    owner, slot, row = chunk_masks(width, chunk)
    total = packed_ref[:, :, plane, :].reshape(DEVICES, 128)
    for line, offset in zip(lines, offsets):
        pick = (slot + offset == row).astype(F32).astype(BF16)
        spread = jnp.where(owner, jnp.broadcast_to(line, owner.shape), 0.0)
        for _ in range(3):
            term = spread.astype(BF16)
            spread = spread - term.astype(F32)
            total += lax.dot_general(term, pick, (((1,), (1,)), ((), ())), preferred_element_type=F32)
    packed_ref[:, :, plane, :] = total.reshape(LEVELS, 8, 128)


SCATTER_BY_Y = (False, True, False)
LINE_FIRST = (False, False, True)
SCATTER_PLAN = (
    (),
    (),
    (),
    (
        ("load", 1), ("twin", 1, "far"), ("first", 1, 1),
    ),
    (
        ("load", 2), ("twin", 2, "x"), ("line", 2, "x", 3), ("ready",), ("first", 1, 3), ("twin", 2, "far"),
        ("line", 2, "far", 3), ("twin", 2, "own"), ("line", 2, "own", 3),
    ),
    (
        ("first", 1, 2), ("line", 2, "x", 2), ("twin", 0, "far"), ("first", 0, 2), ("twin", 0, "x"), ("direct", 0, 0),
        ("twin", 1, "y"), ("direct", 1, 3), ("first", 0, 1), ("first", 0, 3), ("line", 2, "far", 2),
    ),
    (
        ("twin", 1, "x"), ("second", 1, 3), ("twin", 2, "y"), ("line", 2, "y", 3), ("direct", 1, 2),
        ("line", 2, "own", 2),
    ),
    (
        ("direct", 0, 3), ("line", 2, "x", 1), ("direct", 0, 1),
    ),
    (
        ("twin", 0, "y"), ("second", 0, 3), ("first", 1, 0), ("second", 1, 2), ("line", 2, "far", 1),
        ("direct", 0, 2), ("twin", 1, "own"), ("line", 1, "own", 3), ("line", 2, "y", 2), ("second", 0, 2),
        ("second", 1, 1), ("direct", 1, 1), ("plane", 2, "D"),
    ),
    (),
    (
        ("twin", 0, "own"), ("line", 0, "own", 3), ("plane", 2, "F"), ("line", 2, "own", 1), ("second", 0, 1),
        ("line", 1, "own", 2), ("line", 2, "y", 1),
    ),
    (),
    (
        ("direct", 1, 0), ("first", 0, 0), ("line", 0, "own", 2), ("vec_start",), ("line", 1, "own", 1),
        ("second", 1, 0), ("plane", 2, "S"), ("second", 0, 0), ("vec_middle",), ("line", 0, "own", 1), ("done", 2),
        ("done", 1), ("done", 0), ("vec_end",), ("finish",),
    ),
)


def scatter_kernel(
    u1_hbm, dh1_hbm, slope1_hbm, xh1_hbm, scale1_hbm, grads_hbm, w_in_hbm, vectors, sums, d_conv_hbm, d_last_hbm, d_conv_flat, d_last_flat, dh1_share, out_share,
    grad_tokens, g_in, g_conv, g_last, g_vec, out_back,
    u1, dh1, slope1, xh1, scale1, grads, w_in, w_in_t, dh1_back, d_in_sum, d_in, own_sums, packed, plane_box, level_box,
    conv_own, conv_twin, conv_far, conv_x, conv_y, conv_line, conv_done, conv_swap,
    last_own, last_twin, last_far, last_x, last_y, last_line, last_done, last_swap,
    in_twin, in_far, in_x, in_y, in_line,
    tile_sem, weight_sem, store_sem, vec_sem, load_sem, twin_send, twin_recv, send_sem, move_recv, line_recv,
    swap_send, swap_recv, back_send, back_recv,
):
    steps, weight_steps = 2048 // TILE, 4
    z, y, x, core = place()
    columns = {"own": 2 * y + x, "x": 2 * y + (1 - x), "y": 2 * (1 - y) + x, "far": 2 * (1 - y) + (1 - x)}
    boxes = {"far": (in_far, conv_far, last_far), "x": (in_x, conv_x, last_x), "y": (in_y, conv_y, last_y)}
    line_boxes = (in_line, conv_line, last_line)
    links = {
        "x": lambda: device(z, y, 1 - x, core), "y": lambda: device(z, 1 - y, x, core),
        "twin": lambda: device(z, y, x, 1 - core),
    }

    def remote(src, dst, send, recv, link):
        return pltpu.make_async_remote_copy(
            src_ref=src, dst_ref=dst, send_sem=send, recv_sem=recv, device_id=links[link]() if isinstance(link, str) else device(z + link, y, x, core), device_id_type=MESH
        )

    def cut(side, part):
        return (None, CONV_COLS[side], OUT_COLS[side])[part]

    def narrow(side, part):
        return pl.ds(0, 640 if part == 0 else cut(side, part)[1])

    def own_at(side, part, level, column):
        if part == 0:
            return d_in.at[level, column, side]
        if part == 1:
            return conv_own.at[:, level, column, :, narrow(side, part)]
        return last_own.at[level, column, :, narrow(side, part)]

    def twin_at(side, part, level, column):
        if part == 0:
            return in_twin.at[level, column]
        if part == 1:
            return conv_twin.at[:, level, column, :, narrow(side, part)]
        return last_twin.at[level, column, :, narrow(side, part)]

    def box_at(side, part, name, level):
        box = boxes[name][part]
        if part == 0:
            return box.at[level]
        if part == 1:
            return box.at[level, :, :, narrow(side, part)]
        return box.at[level, :, narrow(side, part)]

    def way_of(sign):
        return lax.shift_right_logical(1 - sign, 1) if not isinstance(sign, int) else (1 - sign) // 2

    def line_at(side, part, kind, sign, level):
        way = way_of(sign)
        if part == 0:
            return in_line.at[way, level]
        if part == 1:
            return conv_line.at[way, level, :, :, narrow(side, part)]
        return last_line.at[KINDS.index(kind), way, level, :, narrow(side, part)]

    def all_units(side, part, count):
        rows = pl.ds(0, 40 * count)
        if part == 0:
            return w_in_hbm.at[rows, :]
        if part == 1:
            return d_conv_flat.at[:, rows, pl.ds(*cut(side, part))]
        return d_last_flat.at[rows, pl.ds(*cut(side, part))]

    def load(side, part):
        source = (d_conv_hbm.at[:, :, :, :, pl.ds(*cut(side, 1))], d_last_hbm.at[:, :, :, pl.ds(*cut(side, 2))])
        target = (conv_own.at[:, :, :, :, narrow(side, 1)], last_own.at[:, :, :, narrow(side, 2)])
        return pltpu.make_async_copy(source[part - 1], target[part - 1], load_sem.at[part - 1])

    def twin_copy(part, kind, to_side):
        column = columns[kind]
        if part == 0:
            src, dst = d_in.at[:, column, to_side], in_twin.at[:, column]
        elif part == 1:
            src = d_conv_hbm.at[:, :, column, :, pl.ds(*cut(to_side, part))]
            dst = conv_twin.at[:, :, column, :, narrow(to_side, part)]
        else:
            src = d_last_hbm.at[:, column, :, pl.ds(*cut(to_side, part))]
            dst = last_twin.at[:, column, :, narrow(to_side, part)]
        return remote(src, dst, twin_send.at[part], twin_recv.at[part, KINDS.index(kind)], "twin")

    def exchange(side, part):
        for kind in ("far", "y", "x", "own"):
            twin_copy(part, kind, 1 - side).start()

    def take_twin(side, part, kind):
        twin_copy(part, kind, side).wait_recv()

    def move(side, part, kind, level, link, box):
        return remote(
            own_at(side, part, level, columns[kind]), box_at(side, part, box, level),
            send_sem.at[part], move_recv.at[("far", "x", "y").index(box), part, level], link,
        )

    def line(side, part, kind, level, sign):
        return remote(
            own_at(side, part, level, columns[kind]), line_at(side, part, kind, sign, level),
            send_sem.at[part], line_recv.at[KINDS.index(kind), way_of(sign), part, level], sign,
        )

    def read(ref):
        return ref[...].astype(F32)

    def each_level(distance, act):
        if distance == 0:
            act(z, 0)
            return

        def one(index, _):
            sign = 1 - 2 * index
            level = z + sign * distance
            pl.when(jnp.logical_and(level >= 0, level < LEVELS))(lambda: act(level, sign))
            return 0

        lax.fori_loop(0, 2, one, 0)

    def both_terms(side, part, level, kind):
        column = columns[kind]
        return read(own_at(side, part, level, column)) + read(twin_at(side, part, level, column))

    def put(side, part, level, kind, value):
        own_at(side, part, level, columns[kind])[...] = value.astype(BF16)

    def roles(part):
        return ("y", "x") if SCATTER_BY_Y[part] else ("x", "y")

    def first(side, part, distance):
        def one(level, sign):
            put(side, part, level, "far", both_terms(side, part, level, "far"))
            move(side, part, "far", level, roles(part)[0], "far").start()

        each_level(distance, one)

    def direct(side, part, distance):
        name = roles(part)[0]

        def one(level, sign):
            put(side, part, level, name, both_terms(side, part, level, name))
            move(side, part, name, level, name, name).start()

        each_level(distance, one)

    def second(side, part, distance):
        link, name = roles(part)

        def one(level, sign):
            move(side, part, "far", level, link, "far").wait_recv()
            put(side, part, level, name, both_terms(side, part, level, name) + read(box_at(side, part, "far", level)))
            move(side, part, name, level, name, name).start()

        each_level(distance, one)

    def line_hop(side, part, kind, distance):
        def one(level, sign):
            total = None
            if not LINE_FIRST[part]:
                for name in ("x", "y"):
                    move(side, part, name, level, name, name).wait_recv()
                total = read(box_at(side, part, "x", level)) + read(box_at(side, part, "y", level))
            terms = both_terms(side, part, level, kind)
            total = terms if total is None else terms + total
            behind = jnp.logical_and(z - sign >= 0, z - sign < LEVELS)

            @pl.when(behind)
            def _():
                line(side, part, kind, level, sign).wait_recv()
                put(side, part, level, kind, total + read(line_at(side, part, kind, sign, level)))

            @pl.when(jnp.logical_not(behind))
            def _():
                put(side, part, level, kind, total)

            line(side, part, kind, level, sign).start()

        each_level(distance, one)

    def add_lines(side, part, kind, target):
        for sign, guard in ((1, z > 0), (-1, z < LEVELS - 1)):

            @pl.when(guard)
            def _(sign=sign):
                line(side, part, kind, z, sign).wait_recv()
                target[...] = (
                    target[...].astype(F32) + read(line_at(side, part, kind, sign, z))
                ).astype(target.dtype)

    def plane(side, part, what):
        link, other = roles(part)
        kind = {"F": "far", "D": link, "S": other}[what]
        own = own_at(side, part, z, columns[kind])
        keep = last_done.at[:, narrow(side, part)]
        keep[...] = both_terms(side, part, z, kind)
        add_lines(side, part, kind, keep)
        if what == "S":
            move(side, part, "far", z, link, "far").wait_recv()
            keep[...] += read(box_at(side, part, "far", z))
        own[...] = keep[...].astype(BF16)
        if what == "F":
            move(side, part, "far", z, link, "far").start()
        else:
            move(side, part, kind, z, kind, kind).start()

    def done(side, part):
        if part == 0:
            target = g_in
        elif part == 1:
            target = conv_done.at[:, :, narrow(side, part)]
        else:
            target = last_done.at[:, narrow(side, part)]
        for name in ("x", "y"):
            move(side, part, name, z, name, name).wait_recv()
        target[...] = (
            both_terms(side, part, z, "own") + read(box_at(side, part, "x", z)) + read(box_at(side, part, "y", z))
        )
        add_lines(side, part, "own", target)
        if part:
            swap(part, side).start()

    def swap(part, from_side):
        lanes_ = narrow(from_side, part)
        if part == 1:
            src, dst = conv_done.at[:, :, lanes_], conv_swap.at[:, :, lanes_]
        else:
            src, dst = last_done.at[:, lanes_], last_swap.at[:, lanes_]
        return remote(src, dst, swap_send.at[part - 1], swap_recv.at[part - 1], "twin")

    def finish(side):
        first_row, count = side * 20, 20
        for part, mine, other, target in ((2, last_done, last_swap, g_last), (1, conv_done, conv_swap, g_conv)):
            swap(part, 1 - side).wait_recv()
            for refs, owner in ((mine, side), (other, 1 - side)):
                start, width = cut(owner, part)
                if part == 1:
                    target[:, :, pl.ds(start, width)] = refs[:, pl.ds(first_row, count), pl.ds(0, width)]
                else:
                    target[:, pl.ds(start, width)] = refs[pl.ds(first_row, count), pl.ds(0, width)]
        for part in range(3):
            if part:
                swap(part, side).wait_send()
            view = all_units(1 - side, part, CHIPS)
            remote(view, view, twin_send.at[part], twin_recv.at[part, 0], "twin").wait_send()
            view = all_units(side, part, CHIPS - 1)
            remote(view, view, send_sem.at[part], twin_recv.at[part, 0], "twin").wait_send()


    def in_plane():
        return y * 4 + x * 2 + core

    def plane_copy(offset):
        other, where = plane_peer(offset)
        return pltpu.make_async_remote_copy(
            src_ref=packed.at[:, other], dst_ref=plane_box.at[in_plane()], send_sem=vec_sem.at[0],
            recv_sem=vec_sem.at[1], device_id=where, device_id_type=MESH,
        )

    def level_copy(step):
        level = lax.rem(z + step, LEVELS)
        return pltpu.make_async_remote_copy(
            src_ref=plane_box.at[0, level], dst_ref=level_box.at[z], send_sem=vec_sem.at[2], recv_sem=vec_sem.at[3],
            device_id=device(level, y, x, core), device_id_type=MESH,
        )

    def sum_lines(ref, indices, width):
        return [jnp.sum(ref[pl.ds(8 * index, 8), pl.ds(0, width)], axis=0, keepdims=True) for index in indices]

    def vec_early():
        packed[...] = jnp.zeros_like(packed)
        pack_sums(0, sum_lines(sums, (2,), 1280), WIDE_OFFSETS[2:], packed)
        pack_sums(1, sum_lines(sums, range(3, 9), 640), SLIM_OFFSETS, packed)

    def vec_start(side):
        pack_sums(0, sum_lines(own_sums, (0, 1), 1280), WIDE_OFFSETS[:2], packed)
        for offset in range(1, 8):
            plane_copy(offset).start()
        for level in range(LEVELS):
            plane_box[pl.ds(in_plane(), 1), level] = packed[level, pl.ds(in_plane(), 1)]

    def vec_middle(side):
        view = plane_box.at[pl.ds(0, 7)]
        remote(view, view, vec_sem.at[0], vec_sem.at[1], "twin").wait()
        total = jnp.sum(plane_box[...], axis=0)
        plane_box[0] = total
        level_box[pl.ds(z, 1)] = plane_box[0, pl.ds(z, 1)]
        for step in range(1, LEVELS):
            level_copy(step).start()

    def vec_end(side):
        view = level_box.at[pl.ds(0, LEVELS - 1)]
        remote(view, view, vec_sem.at[2], vec_sem.at[3], "twin").wait()
        g_vec[...] = jnp.sum(level_box[...], axis=0)

    def ready(side):
        d_in[...] = d_in_sum[...].astype(BF16).reshape(d_in.shape)
        exchange(side, 0)

    actions = {
        "load": lambda side, part: load(side, part).wait(), "twin": take_twin, "first": first, "direct": direct,
        "second": second, "line": line_hop, "plane": plane, "done": done, "ready": ready, "vec_start": vec_start,
        "vec_middle": vec_middle, "vec_end": vec_end, "finish": finish,
    }

    def either(event):
        return event[0] in ("ready", "vec_start", "vec_middle", "vec_end") or event[1:2] == (0,)

    def perform(events):
        for alike, group in itertools.groupby(events, either):
            group = tuple(group)
            if alike:
                for event in group:
                    actions[event[0]](core, *event[1:])
                continue
            for side in range(2):

                @pl.when(core == side)
                def _(side=side, group=group):
                    for event in group:
                        actions[event[0]](side, *event[1:])

    def rows_of(tile):
        return pl.ds(pl.multiple_of(tile * TILE, TILE), TILE)

    tiles_of = ((u1, u1_hbm), (dh1, dh1_hbm), (slope1, slope1_hbm), (xh1, xh1_hbm), (scale1, scale1_hbm), (grads, grads_hbm))

    def half_load(index, half):
        target, source = tiles_of[index]
        rows = pl.ds(half * 1024, 1024)
        return pltpu.make_async_copy(source.at[rows, :], target.at[rows, :], tile_sem.at[index, half])

    def store(tile):
        return pltpu.make_async_copy(grads.at[rows_of(tile), :], grad_tokens.at[rows_of(tile), :], store_sem.at[tile])

    weight_load = pltpu.make_async_copy(w_in_hbm, w_in, weight_sem.at[0])

    barrier = pltpu.get_barrier_semaphore()
    for offset in range(1, 8):
        pl.semaphore_signal(barrier, inc=1, device_id=plane_peer(offset)[1], device_id_type=MESH)
    for step in range(1, LEVELS):
        pl.semaphore_signal(
            barrier, inc=1, device_id=device(lax.rem(z + step, LEVELS), y, x, core), device_id_type=MESH
        )
    for side in range(2):

        @pl.when(core == side)
        def _(side=side):
            for part in (1, 2):
                load(side, part).start()

    for half in range(2):
        half_load(0, half).start()
        half_load(1, half).start()
    weight_load.start()
    pl.semaphore_wait(barrier, 7 + LEVELS - 1)
    back_copies = [
        remote(dh1_share, dh1_back, back_send.at[0], back_recv.at[0], "twin"),
        remote(out_share, out_back, back_send.at[1], back_recv.at[1], "twin"),
    ]
    for side in range(2):

        @pl.when(core == side)
        def _(side=side):
            for kind in ("far", "y", "x", "own"):
                for part in (1, 2):
                    twin_copy(part, kind, 1 - side).start()
                if kind == "far":
                    back_copies[0].start()

    for half in range(2):
        for index in range(2, 6):
            half_load(index, half).start()
    own_sums[...] = jnp.zeros_like(own_sums)
    vec_early()

    def weight_tile(tile, _):
        for index in range(weight_steps):
            if SCATTER_PLAN[index]:
                pl.when(tile == index)(functools.partial(perform, SCATTER_PLAN[index]))
            if index in (0, weight_steps // 2):
                for array in range(2):
                    pl.when(tile == index)(half_load(array, 0 if index == 0 else 1).wait)
        rows = pl.ds(pl.multiple_of(tile * 512, 512), 512)
        pl.when(tile == weight_steps // 2)(back_copies[0].wait)

        @pl.when(tile >= weight_steps // 2)
        def _():
            again = pl.ds(pl.multiple_of(tile * 512 - 1024, 512), 512)
            dh1[rows, :] = dh1[rows, :] + dh1_back[again, :]

        term = lax.dot_general(u1[rows, :], dh1[rows, :], (((0,), (0,)), ((), ())), preferred_element_type=F32)

        @pl.when(tile == 0)
        def _():
            d_in_sum[...] = term

        @pl.when(tile > 0)
        def _():
            d_in_sum[...] += term

        return 0

    lax.fori_loop(0, weight_steps, weight_tile, 0)
    weight_load.wait()
    w_in_t[...] = w_in[...].T

    def token_tile(tile, _):
        for index in range(steps):
            if SCATTER_PLAN[weight_steps + index]:
                pl.when(tile == index)(functools.partial(perform, SCATTER_PLAN[weight_steps + index]))
            if index == 1:
                pl.when(tile == index)(back_copies[1].start)
            if index in (0, steps // 2):
                for array in range(2, 6):
                    pl.when(tile == index)(half_load(array, 0 if index == 0 else 1).wait)
        rows = rows_of(tile)
        back = jnp.dot(dh1[rows, :], w_in_t[...], preferred_element_type=F32)
        norm = xh1[rows, :].astype(F32)
        slope_grad = back * slope1[rows, :].astype(F32)
        for index, values in enumerate((slope_grad * norm, slope_grad)):
            own_sums[pl.ds(8 * index, 8), :] += jnp.sum(values.reshape(TILE // 8, 8, 1280), axis=0)
        err = slope_grad * vectors[pl.ds(0, 1), :]
        mean = jnp.sum(err, axis=1, keepdims=True) * (1.0 / 1280)
        along = jnp.sum(err * norm, axis=1, keepdims=True) * (1.0 / 1280)
        grads[rows, :] = (
            grads[rows, :].astype(F32) + lanes(scale1[rows, :], 1280) * (err - mean - norm * along)
        ).astype(BF16)
        store(tile).start()
        return 0

    lax.fori_loop(0, steps, token_tile, 0)
    perform(SCATTER_PLAN[weight_steps + steps])
    back_copies[1].wait()
    for tile in range(steps):
        store(tile).wait()


def scatter_stage(u1, dh1, slope1, xh1, scale1, grads, w_in, vectors, sums, d_conv, d_last, dh1_share, out_share):
    rows = u1.shape[0]
    steps = rows // TILE
    shape = jax.ShapeDtypeStruct
    vmem = pl.BlockSpec(memory_space=pltpu.VMEM)
    conv_box = (LEVELS, KSIZE, 40, 384)
    last_box = (LEVELS, 40, 896)
    in_box = (LEVELS, 40, 640)
    dma = pltpu.SemaphoreType.DMA
    return pl.pallas_call(
        scatter_kernel,
        in_specs=[HBM] * 7 + [vmem] * 2 + [HBM] * 6,
        out_specs=[HBM] + [vmem] * 4 + [HBM],
        out_shape=[
            shape((rows, 1280), BF16), shape((40, 640), F32), shape((KSIZE, 20, 640), F32), shape((20, 1280), F32),
            shape((2, 128), F32), shape((1024, 1280), BF16),
        ],
        scratch_shapes=[
            pltpu.VMEM((rows, 1280), BF16),
            pltpu.VMEM((rows, 640), BF16),
            pltpu.VMEM((rows, 1280), BF16),
            pltpu.VMEM((rows, 1280), BF16),
            pltpu.VMEM((rows, 128), F32),
            pltpu.VMEM((rows, 1280), BF16),
            pltpu.VMEM((1280, 640), BF16),
            pltpu.VMEM((640, 1280), BF16),
            pltpu.VMEM((1024, 640), BF16),
            pltpu.VMEM((1280, 640), F32),
            pltpu.VMEM((LEVELS, 4, 2, 40, 640), BF16),
            pltpu.VMEM((16, 1280), F32),
            pltpu.VMEM((LEVELS, 8, 2, 128), F32),
            pltpu.VMEM((8, LEVELS, 2, 128), F32),
            pltpu.VMEM((LEVELS, 2, 128), F32),
            pltpu.VMEM((KSIZE, LEVELS, 4, 40, 384), BF16),
            pltpu.VMEM((KSIZE, LEVELS, 4, 40, 384), BF16),
            pltpu.VMEM(conv_box, BF16),
            pltpu.VMEM(conv_box, BF16),
            pltpu.VMEM(conv_box, BF16),
            pltpu.VMEM((2,) + conv_box, BF16),
            pltpu.VMEM((KSIZE, 40, 384), F32),
            pltpu.VMEM((KSIZE, 40, 384), F32),
            pltpu.VMEM((LEVELS, 4, 40, 896), BF16),
            pltpu.VMEM((LEVELS, 4, 40, 896), BF16),
            pltpu.VMEM(last_box, BF16),
            pltpu.VMEM(last_box, BF16),
            pltpu.VMEM(last_box, BF16),
            pltpu.VMEM((4, 2) + last_box, BF16),
            pltpu.VMEM((40, 896), F32),
            pltpu.VMEM((40, 896), F32),
            pltpu.VMEM((LEVELS, 4, 40, 640), BF16),
            pltpu.VMEM(in_box, BF16),
            pltpu.VMEM(in_box, BF16),
            pltpu.VMEM(in_box, BF16),
            pltpu.VMEM((2,) + in_box, BF16),
            dma((6, 2)), dma((1,)), dma((steps,)), dma((4,)), dma((2,)), dma((3,)), dma((3, 4)),
            dma((3,)), dma((3, 3, LEVELS)), dma((4, 2, 3, LEVELS)), dma((2,)), dma((2,)), dma((2,)), dma((2,)),
        ],
        compiler_params=pltpu.CompilerParams(collective_id=1, has_side_effects=True, vmem_limit_bytes=VMEM_BYTES),
        name="scatter_stage",
    )(
        u1, dh1, slope1, xh1, scale1, grads, w_in, vectors, sums,
        d_conv.reshape(KSIZE, LEVELS, 4, 40, 640), d_last.reshape(LEVELS, 4, 40, 1280), d_conv, d_last, dh1_share, out_share,
    )


def settle_kernel(
    vectors, result_in, out_back, rows_hbm, g_in, g_conv, g_last, g_vec,
    result, rows_out, in_out, conv_out, last_out, *rest
):
    vectors_out, (buffer, moved, load_sem, store_sem, moved_sem) = rest[:9], rest[9:]
    count = buffer.shape[0]
    chunk = buffer.shape[1]
    loads = [
        pltpu.make_async_copy(rows_hbm.at[pl.ds(index * chunk, chunk), :], buffer.at[index], load_sem.at[index])
        for index in range(count)
    ]
    stores = [
        pltpu.make_async_copy(buffer.at[index], rows_out.at[pl.ds(index * chunk, chunk), :], store_sem.at[index])
        for index in range(count)
    ]
    for copy in loads:
        copy.start()
    in_out[...] = g_in[...]
    conv_out[...] = g_conv[...]
    last_out[...] = g_last[...]
    places = [(0, offset, 40) for offset in WIDE_OFFSETS] + [(1, offset, 20) for offset in SLIM_OFFSETS]
    for target, (plane, offset, width) in zip(vectors_out, places):
        target[...] = g_vec[pl.ds(plane, 1), pl.ds(offset, width)]
    _, second_units, _, give, _ = unit_share(read_lengths(vectors))
    kept = second_units - give
    end = jnp.where(give > 0, 2 * lax.div(second_units + 1, 2), kept)

    def moved_load(unit):
        rows = pl.ds(pl.multiple_of(unit * UNIT, UNIT), UNIT)
        return pltpu.make_async_copy(out_back.at[rows, :], moved.at[rows, :], moved_sem.at[0, unit])

    def moved_store(unit):
        rows = pl.ds(pl.multiple_of(unit * UNIT, UNIT), UNIT)
        target = pl.ds(pl.multiple_of(1024 + unit * UNIT, UNIT), UNIT)
        return pltpu.make_async_copy(moved.at[rows, :], result.at[target, :], moved_sem.at[1, unit])

    def each(act):
        def one(unit, _):
            act(unit)
            return 0

        lax.fori_loop(kept, end, one, 0)

    def pass_moved(unit):
        moved_load(unit).wait()
        moved_store(unit).start()

    each(lambda unit: moved_load(unit).start())
    for load, store in zip(loads, stores):
        load.wait()
        store.start()
    each(pass_moved)
    each(lambda unit: moved_store(unit).wait())
    for copy in stores:
        copy.wait()


def settle_stage(vectors, result, out_back, rows, g_in, g_conv, g_last, g_vec):
    chunks = 8
    shape = jax.ShapeDtypeStruct
    vmem = pl.BlockSpec(memory_space=pltpu.VMEM)
    return pl.pallas_call(
        settle_kernel,
        in_specs=[vmem] + [HBM] * 3 + [vmem] * 4,
        out_specs=[HBM] * 2 + [vmem] * 12,
        out_shape=[shape(v.shape, v.dtype) for v in (result, rows, g_in, g_conv, g_last)]
        + [shape((1, 40), F32)] * 3
        + [shape((1, 20), F32)] * 6,
        scratch_shapes=[
            pltpu.VMEM((chunks, rows.shape[0] // chunks, rows.shape[1]), rows.dtype),
            pltpu.VMEM((1024, 1280), BF16),
            pltpu.SemaphoreType.DMA((chunks,)),
            pltpu.SemaphoreType.DMA((chunks,)),
            pltpu.SemaphoreType.DMA((2, 1024 // UNIT)),
        ],
        input_output_aliases={1: 0},
        compiler_params=pltpu.CompilerParams(vmem_limit_bytes=VMEM_BYTES),
        name="settle_stage",
    )(vectors, result, out_back, rows, g_in, g_conv, g_last, g_vec)


def kernel_body(
    tokens, out_grad, lengths, ln1_gain, ln1_bias, w_in, b_in, ln2_gain, ln2_bias,
    w_conv, b_conv, ln3_gain, ln3_bias, w_out, b_out,
):
    proteins, length_pad, width = tokens.shape
    rows = tokens.reshape(proteins * length_pad, width)
    grads = out_grad.reshape(proteins * length_pad, width)
    vec = pack_vectors(
        ln1_gain, ln1_bias, b_in, ln2_gain, ln2_bias, b_conv, ln3_gain, ln3_bias, b_out, lengths
    )
    u1, slope1, xh1, scale1, xh2, slope2, scale2, u2, vectors, in_full, conv_full, out_full, twins = gather_stage(
        rows, grads, vec, w_in, w_conv, w_out
    )
    result, dh1, out_share, dh1_share, d_conv, d_last, sums = middle_stage(
        vectors, u2, xh2, slope2, scale2, grads, rows, conv_full, out_full, twins
    )
    *owned, out_back = scatter_stage(
        u1, dh1, slope1, xh1, scale1, grads, in_full, vectors, sums, d_conv, d_last, dh1_share, out_share
    )
    result, grad_rows, g_in, g_conv, g_last, *lines = settle_stage(vectors, result, out_back, *owned)
    lines = [line.reshape(line.shape[1]) for line in lines]
    wide, slim = lines[:3], lines[3:]
    return (
        result.reshape(tokens.shape), grad_rows.reshape(tokens.shape),
        wide[0], wide[1], g_in, slim[0], slim[1], slim[2], g_conv, slim[3], slim[4], slim[5], g_last, wide[2],
    )


def layer_norm(values, gain, bias):
    center = values - jnp.mean(values, axis=-1, keepdims=True)
    var_rows = jnp.mean(center * center, axis=-1, keepdims=True)
    return center * lax.rsqrt(var_rows + EPS) * gain + bias


def norm_gelu(values, gain, bias):
    return jax.nn.gelu(layer_norm(values, gain, bias), approximate=False)


def collect(
    ln1_gain,
    ln1_bias,
    w_in,
    b_in,
    ln2_gain,
    ln2_bias,
    w_conv,
    b_conv,
    ln3_gain,
    ln3_bias,
    w_out,
    b_out,
):
    return (
        lax.all_gather(ln1_gain, ("dp", "fsdp"), axis=0, tiled=True),
        lax.all_gather(ln1_bias, ("dp", "fsdp"), axis=0, tiled=True),
        lax.all_gather(w_in, ("dp", "fsdp"), axis=0, tiled=True),
        lax.all_gather(b_in, ("dp", "fsdp"), axis=0, tiled=True),
        lax.all_gather(ln2_gain, ("dp", "fsdp"), axis=0, tiled=True),
        lax.all_gather(ln2_bias, ("dp", "fsdp"), axis=0, tiled=True),
        lax.all_gather(w_conv, ("dp", "fsdp"), axis=1, tiled=True),
        lax.all_gather(b_conv, ("dp", "fsdp"), axis=0, tiled=True),
        lax.all_gather(ln3_gain, ("dp", "fsdp"), axis=0, tiled=True),
        lax.all_gather(ln3_bias, ("dp", "fsdp"), axis=0, tiled=True),
        lax.all_gather(w_out, ("dp", "fsdp"), axis=0, tiled=True),
        lax.all_gather(b_out, ("dp", "fsdp"), axis=0, tiled=True),
    )


def spread(
    term_g1,
    term_b1,
    term_wi,
    term_bi,
    term_g2,
    term_b2,
    term_wc,
    term_bc,
    term_g3,
    term_b3,
    term_wo,
    term_bo,
):
    return (
        lax.psum_scatter(term_g1, ("dp", "fsdp"), scatter_dimension=0, tiled=True),
        lax.psum_scatter(term_b1, ("dp", "fsdp"), scatter_dimension=0, tiled=True),
        lax.psum_scatter(term_wi, ("dp", "fsdp"), scatter_dimension=0, tiled=True),
        lax.psum_scatter(term_bi, ("dp", "fsdp"), scatter_dimension=0, tiled=True),
        lax.psum_scatter(term_g2, ("dp", "fsdp"), scatter_dimension=0, tiled=True),
        lax.psum_scatter(term_b2, ("dp", "fsdp"), scatter_dimension=0, tiled=True),
        lax.psum_scatter(term_wc, ("dp", "fsdp"), scatter_dimension=1, tiled=True),
        lax.psum_scatter(term_bc, ("dp", "fsdp"), scatter_dimension=0, tiled=True),
        lax.psum_scatter(term_g3, ("dp", "fsdp"), scatter_dimension=0, tiled=True),
        lax.psum_scatter(term_b3, ("dp", "fsdp"), scatter_dimension=0, tiled=True),
        lax.psum_scatter(term_wo, ("dp", "fsdp"), scatter_dimension=0, tiled=True),
        lax.psum_scatter(term_bo, ("dp", "fsdp"), scatter_dimension=0, tiled=True),
    )


def dilate(padded, kernel, length_pad):
    total = jnp.zeros((padded.shape[0], length_pad, kernel.shape[2]), jnp.float32)
    for kernel_tap in range(kernel.shape[0]):
        window = padded[:, kernel_tap * DILATION : kernel_tap * DILATION + length_pad]
        total = total + jnp.einsum(
            "pli,io->plo", window, kernel[kernel_tap], preferred_element_type=jnp.float32
        )
    return total


def plain_body(
    tokens,
    out_grad,
    lengths,
    ln1_gain,
    ln1_bias,
    w_in,
    b_in,
    ln2_gain,
    ln2_bias,
    w_conv,
    b_conv,
    ln3_gain,
    ln3_bias,
    w_out,
    b_out,
):
    proteins, length_pad, width = tokens.shape
    row_count = proteins * length_pad
    reach = KSIZE // 2 * DILATION
    positions = lax.broadcasted_iota(jnp.int32, (proteins, length_pad), 1)
    live = (positions < lengths[:, None]).astype(jnp.float32).reshape(row_count, 1)
    full = collect(
        ln1_gain,
        ln1_bias,
        w_in,
        b_in,
        ln2_gain,
        ln2_bias,
        w_conv,
        b_conv,
        ln3_gain,
        ln3_bias,
        w_out,
        b_out,
    )
    (
        gain_one,
        bias_one,
        first_matrix,
        first_bias,
        gain_two,
        bias_two,
        conv_kernel,
        conv_bias,
        gain_three,
        bias_three,
        last_matrix,
        last_bias,
    ) = full
    inner = first_matrix.shape[1]
    row_tokens = tokens.reshape(row_count, width).astype(jnp.float32)
    act_one, pull_one = jax.vjp(
        norm_gelu, row_tokens, gain_one.astype(jnp.float32), bias_one.astype(jnp.float32)
    )
    inner_one = act_one.astype(jnp.bfloat16)
    hidden_one = jnp.dot(
        inner_one, first_matrix, preferred_element_type=jnp.float32
    ) + first_bias.astype(jnp.float32)
    act_two, pull_two = jax.vjp(
        norm_gelu, hidden_one, gain_two.astype(jnp.float32), bias_two.astype(jnp.float32)
    )
    inner_two = (act_two * live).astype(jnp.bfloat16)
    padded_two = jnp.pad(
        inner_two.reshape(proteins, length_pad, inner), ((0, 0), (reach, reach), (0, 0))
    )
    hidden_two = dilate(padded_two, conv_kernel, length_pad).reshape(
        row_count, inner
    ) + conv_bias.astype(jnp.float32)
    act_three, pull_three = jax.vjp(
        norm_gelu, hidden_two, gain_three.astype(jnp.float32), bias_three.astype(jnp.float32)
    )
    inner_three = act_three.astype(jnp.bfloat16)
    branch = jnp.dot(
        inner_three, last_matrix, preferred_element_type=jnp.float32
    ) + last_bias.astype(jnp.float32)
    result = (row_tokens + live * branch).astype(jnp.bfloat16).reshape(proteins, length_pad, width)
    again = collect(
        ln1_gain,
        ln1_bias,
        w_in,
        b_in,
        ln2_gain,
        ln2_bias,
        w_conv,
        b_conv,
        ln3_gain,
        ln3_bias,
        w_out,
        b_out,
    )
    (
        again_g1,
        again_b1,
        back_first,
        again_bi,
        again_g2,
        again_b2,
        back_kernel,
        again_bc,
        again_g3,
        again_b3,
        back_last,
        again_bo,
    ) = again
    pull_one = jax.vjp(
        norm_gelu, row_tokens, again_g1.astype(jnp.float32), again_b1.astype(jnp.float32)
    )[1]
    pull_two = jax.vjp(
        norm_gelu, hidden_one, again_g2.astype(jnp.float32), again_b2.astype(jnp.float32)
    )[1]
    pull_three = jax.vjp(
        norm_gelu, hidden_two, again_g3.astype(jnp.float32), again_b3.astype(jnp.float32)
    )[1]
    grad_rows = out_grad.reshape(row_count, width)
    grad_branch = grad_rows * live.astype(jnp.bfloat16)
    term_wo = jnp.einsum("ri,rd->id", inner_three, grad_branch, preferred_element_type=jnp.float32)
    term_bo = jnp.sum(grad_branch.astype(jnp.float32), axis=0)
    grad_three = jnp.einsum("rd,id->ri", grad_branch, back_last, preferred_element_type=jnp.float32)
    d_hidden_two, term_g3, term_b3 = pull_three(grad_three)
    low_two = d_hidden_two.astype(jnp.bfloat16)
    term_bc = jnp.sum(low_two.astype(jnp.float32), axis=0)
    padded_grad = jnp.pad(
        low_two.reshape(proteins, length_pad, inner), ((0, 0), (reach, reach), (0, 0))
    )
    grad_view = low_two.reshape(proteins, length_pad, inner)
    kernel_terms = []
    grad_two = jnp.zeros((proteins, length_pad, inner), jnp.float32)
    taps = back_kernel.shape[0]
    for kernel_tap in range(taps):
        window = padded_two[:, kernel_tap * DILATION : kernel_tap * DILATION + length_pad]
        kernel_terms.append(
            jnp.einsum("pli,plo->io", window, grad_view, preferred_element_type=jnp.float32)
        )
        mirror = (taps - 1 - kernel_tap) * DILATION
        grad_window = padded_grad[:, mirror : mirror + length_pad]
        grad_two = grad_two + jnp.einsum(
            "plo,io->pli", grad_window, back_kernel[kernel_tap], preferred_element_type=jnp.float32
        )
    term_wc = jnp.stack(kernel_terms, axis=0)
    grad_two = grad_two.reshape(row_count, inner) * live
    d_hidden_one, term_g2, term_b2 = pull_two(grad_two)
    low_one = d_hidden_one.astype(jnp.bfloat16)
    term_wi = jnp.einsum("rd,ri->di", inner_one, low_one, preferred_element_type=jnp.float32)
    term_bi = jnp.sum(low_one.astype(jnp.float32), axis=0)
    grad_one = jnp.einsum("ri,di->rd", low_one, back_first, preferred_element_type=jnp.float32)
    d_tokens, term_g1, term_b1 = pull_one(grad_one)
    grad_tokens = (
        (grad_rows.astype(jnp.float32) + d_tokens)
        .astype(jnp.bfloat16)
        .reshape(proteins, length_pad, width)
    )
    owned = spread(
        term_g1,
        term_b1,
        term_wi,
        term_bi,
        term_g2,
        term_b2,
        term_wc,
        term_bc,
        term_g3,
        term_b3,
        term_wo,
        term_bo,
    )
    return (
        result,
        grad_tokens,
        owned[0],
        owned[1],
        owned[2],
        owned[3],
        owned[4],
        owned[5],
        owned[6],
        owned[7],
        owned[8],
        owned[9],
        owned[10],
        owned[11],
    )


def solution(mesh):
    both = ("dp", "fsdp")
    by_row = P(both)
    in_specs = (
        P(both, None, None), P(both, None, None), by_row, by_row, by_row, P(both, None), by_row, by_row, by_row,
        P(None, both, None), by_row, by_row, by_row, P(both, None), by_row,
    )
    out_specs = (
        P(both, None, None), P(both, None, None), by_row, by_row, P(both, None), by_row, by_row, by_row,
        P(None, both, None), by_row, by_row, by_row, P(both, None), by_row,
    )
    body = kernel_body if (mesh.shape["dp"], mesh.shape["fsdp"]) == (8, 4) else plain_body
    return jax.shard_map(body, mesh=mesh, in_specs=in_specs, out_specs=out_specs, check_vma=False)
```
